32 devices in a mesh: row: 4 (over y, x), seq: 8 (over z, core).
Axes of the slice: x: 2, y: 2, z: 4, core: 2. Of those that a mesh axis runs over, the one named last changes fastest.
Arguments:
- tokens: bfloat16 [8, 512, 2048], P('row', 'seq'), may hold values from -6 to 6
- cotangent: bfloat16 [8, 512, 2048], P('row', 'seq'), may hold values from -6 to 6
- doc_lengths: int32 [8, 8], P('row'), may hold values from 1 to 256, 512 in all within a row
- attn_gain: bfloat16 [2048], P(('row', 'seq')), may hold values from 0.25 to 1.75
- w_query: bfloat16 [2048, 2048], P(('row', 'seq')), may hold values from -0.125 to 0.125
- w_key: bfloat16 [2048, 512], P(('row', 'seq')), may hold values from -0.125 to 0.125
- w_value: bfloat16 [2048, 512], P(('row', 'seq')), may hold values from -0.125 to 0.125
- w_out: bfloat16 [2048, 2048], P(('row', 'seq')), may hold values from -0.5 to 0.5
- mlp_gain: bfloat16 [2048], P(('row', 'seq')), may hold values from 0.25 to 1.75
- w_gate: bfloat16 [2048, 8192], P(('row', 'seq')), may hold values from -0.125 to 0.125
- w_up: bfloat16 [2048, 8192], P(('row', 'seq')), may hold values from -0.125 to 0.125
- w_down: bfloat16 [8192, 2048], P(('row', 'seq')), may hold values from -0.125 to 0.125
Outputs:
- output: bfloat16 [8, 512, 2048], P('row', 'seq')
- grad_tokens: float32 [8, 512, 2048], P('row', 'seq')
- grad_attn_gain: float32 [2048], P(('row', 'seq'))
- grad_query: float32 [2048, 2048], P(('row', 'seq'))
- grad_key: float32 [2048, 512], P(('row', 'seq'))
- grad_value: float32 [2048, 512], P(('row', 'seq'))
- grad_out: float32 [2048, 2048], P(('row', 'seq'))
- grad_mlp_gain: float32 [2048], P(('row', 'seq'))
- grad_gate: float32 [2048, 8192], P(('row', 'seq'))
- grad_up: float32 [2048, 8192], P(('row', 'seq'))
- grad_down: float32 [8192, 2048], P(('row', 'seq'))
The draws below stay inside these ranges and needn't reach their ends.
Inputs may be any that keep to these rules, and one draw needn't show every extreme that they name: `doc_lengths`: the 8 lengths of each row add up to 512, and the longest of each row is exactly 256.
All inputs are finite; a program needn't handle non-finite values.
Results may differ from the reference program's by a relative error of at most 0.017.
Values may be sent and summed in bfloat16 or wider, within the bound.
A program may use at most 640 MiB of HBM per device.

```python
import math
import jax
import jax.numpy as jnp
import numpy as np
from jax import lax

D = 2048
HEAD_DIM = 64
FF = 8192
DOCS = 8
ROWS = 8
LEN = 512
KVD = 512


def steps_of(key, shape, shards, least, high):
    def one(axis_at, shards_of):
        heights = jax.random.uniform(jax.random.fold_in(jax.random.fold_in(key, 6), axis_at), (shards_of,), jnp.float32, least / len(shards), high / len(shards))
        return jnp.repeat(jnp.exp(heights), shape[axis_at] // shards_of).reshape((-1,) + (1,) * (len(shape) - axis_at - 1))

    factor_of = one(*shards[0])
    for cut in shards[1:]:
        factor_of = factor_of * one(*cut)
    return factor_of


def length_profile(amount, total, limit, slope):
    weights = [(1 << 20) // math.isqrt(grade ** slope) + 1 for grade in range(2, amount + 1)]
    rest, holding = total - limit - (amount - 1), [1] * (amount - 1)
    while rest > 0:
        candidates = [i for i in range(amount - 1) if holding[i] < limit]
        mass, budget = sum([weights[i] for i in candidates]), rest
        for i in candidates:
            more = min(limit - holding[i], max(1, budget * weights[i] // mass), rest)
            holding[i] = holding[i] + more
            rest = rest - more
    return np.array([limit] + holding)


def ragged_sizes(stream_key, number_of, total, limit, slope):
    if number_of == 2:
        one = jax.random.randint(stream_key, (), max(1, total - limit), min(limit, total - 1) + 1)
        return jnp.stack([one, total - one])
    tallies = jnp.asarray(length_profile(number_of, total, limit, slope), jnp.int32)
    pairs = (number_of - 1) // 2
    source_of, taker = tallies[1:1 + 2 * pairs:2], tallies[2:2 + 2 * pairs:2]
    room = jnp.minimum(source_of - 1, limit - taker)
    passed = jax.random.randint(jax.random.fold_in(stream_key, 1), (pairs,), 0, 1 << 20) % (room + 1)
    tallies = tallies.at[1:1 + 2 * pairs:2].set(source_of - passed).at[2:2 + 2 * pairs:2].set(taker + passed)
    return tallies[jax.random.permutation(jax.random.fold_in(stream_key, 2), number_of)]


def scatter_about(stream_key, shape, spread, limit, pieces=(), kind=jnp.bfloat16):
    level = steps_of(stream_key, shape, pieces, -0.22, 0.18) if pieces else 1.0
    values = jax.random.normal(stream_key, shape, jnp.float32) * spread * level
    return jnp.minimum(jnp.maximum(values, -limit), limit).astype(kind)


def setup_inputs(seed: int = 0) -> dict:
    key_list = jax.random.split(jax.random.key(seed), 13)
    tokens = scatter_about(key_list[0], (ROWS, LEN, D), 1.0, 6.0, ((0, 4), (1, 8)))
    cotangent = scatter_about(key_list[1], (ROWS, LEN, D), 1.0, 6.0, ((0, 4), (1, 8)))
    doc_lengths = jax.vmap(lambda own: ragged_sizes(own, DOCS, LEN, LEN // 2, 2))(jax.random.split(key_list[2], ROWS)).reshape((ROWS, DOCS)).astype(jnp.int32)
    attn_gain = jnp.clip(1.0 + 0.15 * jax.random.normal(key_list[3], (D,), jnp.float32), 0.25, 1.75).astype(jnp.bfloat16)
    w_query = scatter_about(key_list[4], (D, D), D ** -0.5, 0.125, ((0, 32),))
    w_key = scatter_about(key_list[5], (D, KVD), D ** -0.5, 0.125, ((0, 32),))
    w_value = scatter_about(key_list[6], (D, KVD), D ** -0.5, 0.125, ((0, 32),))
    w_out = scatter_about(key_list[7], (D, D), (D // 16) ** -0.5, 0.5, ((0, 32),))
    mlp_gain = jnp.clip(1.0 + 0.15 * jax.random.normal(key_list[8], (D,), jnp.float32), 0.25, 1.75).astype(jnp.bfloat16)
    w_gate = scatter_about(key_list[9], (D, FF), D ** -0.5, 0.125, ((0, 32),))
    w_up = scatter_about(key_list[10], (D, FF), D ** -0.5, 0.125, ((0, 32),))
    w_down = scatter_about(key_list[11], (FF, D), (FF // 4) ** -0.5, 0.125, ((0, 32),))
    return {"tokens": tokens, "cotangent": cotangent, "doc_lengths": doc_lengths, "attn_gain": attn_gain, "w_query": w_query, "w_key": w_key, "w_value": w_value, "w_out": w_out, "mlp_gain": mlp_gain, "w_gate": w_gate, "w_up": w_up, "w_down": w_down}


EPSILON = 1e-05
THETA = 500000.0

@jax.custom_vjp
def low(v):
    return lax.optimization_barrier(v.astype(jnp.bfloat16)).astype(jnp.float32)

@jax.custom_vjp
def low_back(v):
    return v

def low_keep(v):
    return (low(v), None)

def low_pass(kept, grad):
    return (grad,)

def back_keep(v):
    return (v, None)

def back_low(kept, grad):
    return (low(grad),)
low.defvjp(low_keep, low_pass)
low_back.defvjp(back_keep, back_low)

def rope_table(head_size):
    half_size = head_size // 2
    plain = THETA ** (-(np.arange(half_size) * 2.0) / head_size)
    factor, low_factor, high_factor, old_span = (32.0, 1.0, 4.0, 8192.0)
    wavelength = 2.0 * math.pi / plain
    smooth = (old_span / wavelength - low_factor) / (high_factor - low_factor)
    blended = (1.0 - smooth) * plain / factor + smooth * plain
    return np.where(wavelength < old_span / high_factor, plain, np.where(wavelength > old_span / low_factor, plain / factor, blended))

def matmul(left, right):
    return jnp.dot(left, right, precision=lax.Precision.HIGHEST, preferred_element_type=jnp.float32)

def rotate(values, cosine, sine):
    half_size = values.shape[-1] // 2
    turned = jnp.concatenate([-values[..., half_size:], values[..., :half_size]], axis=-1)
    return values * cosine + turned * sine

def rms_scale(values):
    return values * lax.rsqrt(lax.optimization_barrier(jnp.mean(values * values, axis=-1, keepdims=True)) + EPSILON)

def attend(queries, keys, values, place, first):
    length, heads, head_size = queries.shape
    key_heads = keys.shape[1]
    groups = heads // key_heads
    block = math.gcd(length, 512)
    scale = head_size ** (-0.5)
    grouped = queries.reshape(length // block, block, key_heads, groups, head_size)
    place_blocks = place.reshape(length // block, block)
    first_blocks = first.reshape(length // block, block)

    def one_block(inputs):
        query_block, query_place, query_first = inputs
        raw = low_back(jnp.einsum('qhgd,khd->hgqk', query_block, keys, precision=lax.Precision.HIGHEST))
        allowed = (place[None, :] <= query_place[:, None]) & (place[None, :] >= query_first[:, None])
        scores = jnp.where(allowed[None, None], raw * scale, -1e+30)
        weights = jax.nn.softmax(scores, axis=-1)
        return jnp.einsum('hgqk,khd->qhgd', low(weights), values, precision=lax.Precision.HIGHEST)
    result = lax.map(jax.checkpoint(one_block), (grouped, place_blocks, first_blocks))
    return result.reshape(length, heads * head_size)

def layer(inputs, attn_gain, w_query, w_key, w_value, w_out, mlp_gain, w_gate, w_up, w_down, cosine, sine, place, first):
    length = inputs.shape[0]
    hidden_one = low(rms_scale(inputs) * attn_gain)
    queries = low_back(matmul(hidden_one, w_query)).reshape(length, -1, HEAD_DIM)
    keys = low_back(matmul(hidden_one, w_key)).reshape(length, -1, HEAD_DIM)
    values = low(low_back(matmul(hidden_one, w_value))).reshape(length, -1, HEAD_DIM)
    queries = low(rotate(queries, cosine[:, None, :], sine[:, None, :]))
    keys = low(rotate(keys, cosine[:, None, :], sine[:, None, :]))
    mixed = low(low_back(attend(queries, keys, values, place, first)))
    middle = inputs + low_back(matmul(mixed, w_out))
    hidden_two = low(rms_scale(middle) * mlp_gain)
    gate_out = low_back(matmul(hidden_two, w_gate))
    up_out = low_back(matmul(hidden_two, w_up))
    active = low(jax.nn.silu(gate_out) * up_out)
    return middle + low_back(matmul(active, w_down))

def reference(tokens, cotangent, doc_lengths, attn_gain, w_query, w_key, w_value, w_out, mlp_gain, w_gate, w_up, w_down):
    weights = tuple((item.astype(jnp.float32) for item in (attn_gain, w_query, w_key, w_value, w_out, mlp_gain, w_gate, w_up, w_down)))
    table = jnp.asarray(rope_table(HEAD_DIM), jnp.float32)
    place = jnp.arange(LEN, dtype=jnp.int32)

    def one_row(totals, inputs):
        row_in, row_cot, row_lengths = inputs
        ends = jnp.cumsum(row_lengths).astype(jnp.int32)
        first = lax.optimization_barrier(jnp.max(jnp.where(ends[None, :] <= place[:, None], ends[None, :], 0), axis=1)).astype(jnp.int32)
        angle = (place - first).astype(jnp.float32)[:, None] * table[None, :]
        cosine = jnp.concatenate([jnp.cos(angle), jnp.cos(angle)], axis=-1)
        sine = jnp.concatenate([jnp.sin(angle), jnp.sin(angle)], axis=-1)

        def forward(row_x, *params):
            return layer(row_x, *params, cosine, sine, place, first)
        result, pullback = jax.vjp(forward, row_in.astype(jnp.float32), *weights)
        grads = pullback(row_cot.astype(jnp.float32))
        totals = tuple((total + grad for total, grad in zip(totals, grads[1:])))
        return (totals, (result.astype(jnp.bfloat16), grads[0]))
    start_totals = tuple((jnp.zeros(item.shape, jnp.float32) for item in weights))
    totals, (output, grad_tokens) = lax.scan(one_row, start_totals, (tokens, cotangent, doc_lengths))
    return (output, grad_tokens, totals[0], totals[1], totals[2], totals[3], totals[4], totals[5], totals[6], totals[7], totals[8])
```

```python
import math

import jax
import jax.numpy as jnp
import numpy as np
from jax import lax
from jax.sharding import PartitionSpec as P

HEAD_DIM = 64


EPSILON = 1e-05
THETA = 500000.0


def rope_table(head_size):
    half_size = head_size // 2
    plain = THETA ** (-(np.arange(half_size) * 2.0) / head_size)
    factor, low_factor, high_factor, old_span = (32.0, 1.0, 4.0, 8192.0)
    wavelength = 2.0 * math.pi / plain
    smooth = (old_span / wavelength - low_factor) / (high_factor - low_factor)
    blended = (1.0 - smooth) * plain / factor + smooth * plain
    return np.where(
        wavelength < old_span / high_factor,
        plain,
        np.where(wavelength > old_span / low_factor, plain / factor, blended),
    )


def norm_scale(values):
    return lax.rsqrt(jnp.mean(values * values, axis=-1, keepdims=True) + EPSILON)


def norm_back(grad_normed, normed, scale):
    return scale * (grad_normed - normed * jnp.mean(grad_normed * normed, axis=-1, keepdims=True))


def rotate(values, cosine, sine):
    half_size = values.shape[-1] // 2
    turned = jnp.concatenate([-values[..., half_size:], values[..., :half_size]], axis=-1)
    return values * cosine + turned * sine


def rotate_back(grad, cosine, sine):
    half_size = grad.shape[-1] // 2
    turned = grad * sine
    return grad * cosine + jnp.concatenate(
        [turned[..., half_size:], -turned[..., :half_size]], axis=-1
    )


def contract_last(left, right):
    return lax.dot_general(
        left, right, (((1,), (1,)), ((), ())), preferred_element_type=jnp.float32
    )


def contract_first(left, right):
    return lax.dot_general(
        left, right, (((0,), (0,)), ((), ())), preferred_element_type=jnp.float32
    )


def gathered_layer(
    tokens,
    cotangent,
    doc_lengths,
    attn_gain,
    w_query,
    w_key,
    w_value,
    w_out,
    mlp_gain,
    w_gate,
    w_up,
    w_down,
):
    rows, stretch, width = tokens.shape
    count = rows * stretch
    key_width = w_key.shape[1]
    hidden_width = w_gate.shape[1]
    key_heads = key_width // HEAD_DIM
    heads = width // HEAD_DIM
    groups = heads // key_heads
    length = stretch * lax.axis_size("seq")
    block = math.gcd(length, 512)
    scale = HEAD_DIM ** (-0.5)
    table = jnp.asarray(rope_table(HEAD_DIM), jnp.float32)
    place = lax.axis_index("seq") * stretch + jnp.arange(stretch, dtype=jnp.int32)
    live_blocks = ((lax.axis_index("seq") + 1) * stretch + block - 1) // block
    ends = jnp.cumsum(doc_lengths, axis=1)
    first = jnp.max(
        jnp.where(ends[:, None, :] <= place[None, :, None], ends[:, None, :], 0), axis=2
    )
    angle = (place[None, :] - first).astype(jnp.float32)[..., None] * table
    cosine = jnp.concatenate([jnp.cos(angle), jnp.cos(angle)], axis=-1)[:, :, None, :]
    sine = jnp.concatenate([jnp.sin(angle), jnp.sin(angle)], axis=-1)[:, :, None, :]
    inputs = tokens.reshape(count, width).astype(jnp.float32)
    scale_one = norm_scale(inputs)
    normed_one = inputs * scale_one
    gain_piece = lax.all_gather(attn_gain, ("row", "seq"), axis=0, tiled=True)
    query_piece = lax.all_gather(w_query, ("row", "seq"), axis=0, tiled=True)
    key_piece = lax.all_gather(w_key, ("row", "seq"), axis=0, tiled=True)
    value_piece = lax.all_gather(w_value, ("row", "seq"), axis=0, tiled=True)
    hidden_piece = (normed_one * gain_piece.astype(jnp.float32)).astype(jnp.bfloat16)
    query_sum = jnp.dot(hidden_piece, query_piece, preferred_element_type=jnp.float32)
    key_sum = jnp.dot(hidden_piece, key_piece, preferred_element_type=jnp.float32)
    value_sum = jnp.dot(hidden_piece, value_piece, preferred_element_type=jnp.float32)
    hidden_one = hidden_piece
    queries = rotate(query_sum.reshape(rows, stretch, heads, HEAD_DIM), cosine, sine).astype(
        jnp.bfloat16
    )
    keys = rotate(key_sum.reshape(rows, stretch, key_heads, HEAD_DIM), cosine, sine).astype(
        jnp.bfloat16
    )
    values = value_sum.astype(jnp.bfloat16)
    query_grouped = queries.reshape(rows, stretch, key_heads, groups, HEAD_DIM)

    def gather_keys():
        return (
            lax.all_gather(keys.reshape(rows, stretch, key_width), "seq", axis=1, tiled=True),
            lax.all_gather(values.reshape(rows, stretch, key_width), "seq", axis=1, tiled=True),
        )

    key_all, value_all = gather_keys()

    def block_rows(source, index):
        return lax.dynamic_slice_in_dim(source, index * block, block, 1).reshape(
            rows, block, key_heads, HEAD_DIM
        )

    def block_scores(key_block, index):
        raw = jnp.einsum(
            "rqhgd,rkhd->rhgqk", query_grouped, key_block, preferred_element_type=jnp.float32
        )
        key_place = index * block + jnp.arange(block, dtype=jnp.int32)
        allowed = (key_place[None, None, :] <= place[None, :, None]) & (
            key_place[None, None, :] >= first[:, :, None]
        )
        return jnp.where(allowed[:, None, None], raw * scale, -1e30)

    def total_step(index, carry):
        running_max, running_total = carry
        scores = block_scores(block_rows(key_all, index), index)
        new_max = jnp.maximum(running_max, jnp.max(scores, axis=-1))
        new_total = running_total * jnp.exp(running_max - new_max) + jnp.sum(
            jnp.exp(scores - new_max[..., None]), axis=-1
        )
        return (new_max, new_total)

    stat_shape = (rows, key_heads, groups, stretch)
    running_max, running_total = lax.fori_loop(
        0,
        live_blocks,
        total_step,
        (jnp.full(stat_shape, -1e30, jnp.float32), jnp.zeros(stat_shape, jnp.float32)),
    )
    log_total = running_max + jnp.log(running_total)

    def mix_step(index, mixed_sum):
        probs = jnp.exp(block_scores(block_rows(key_all, index), index) - log_total[..., None])
        return mixed_sum + jnp.einsum(
            "rhgqk,rkhd->rqhgd",
            probs.astype(jnp.bfloat16),
            block_rows(value_all, index),
            preferred_element_type=jnp.float32,
        )

    mixed_sum = lax.fori_loop(
        0,
        live_blocks,
        mix_step,
        jnp.zeros((rows, stretch, key_heads, groups, HEAD_DIM), jnp.float32),
    )
    mixed = mixed_sum.reshape(count, width).astype(jnp.bfloat16)
    attn_branch = jnp.dot(
        mixed,
        lax.all_gather(w_out, ("row", "seq"), axis=0, tiled=True),
        preferred_element_type=jnp.float32,
    )
    middle = inputs + attn_branch
    scale_two = norm_scale(middle)
    normed_two = middle * scale_two
    gain_piece = lax.all_gather(mlp_gain, ("row", "seq"), axis=0, tiled=True)
    gate_piece = lax.all_gather(w_gate, ("row", "seq"), axis=0, tiled=True)
    up_piece = lax.all_gather(w_up, ("row", "seq"), axis=0, tiled=True)
    hidden_piece = (normed_two * gain_piece.astype(jnp.float32)).astype(jnp.bfloat16)
    gate_sum, up_sum, hidden_two = (
        jnp.dot(hidden_piece, gate_piece, preferred_element_type=jnp.float32),
        jnp.dot(hidden_piece, up_piece, preferred_element_type=jnp.float32),
        hidden_piece,
    )
    sigma = jax.nn.sigmoid(gate_sum)
    silu_value = gate_sum * sigma
    active = (silu_value * up_sum).astype(jnp.bfloat16)
    mlp_branch = jnp.dot(
        active,
        lax.all_gather(w_down, ("row", "seq"), axis=0, tiled=True),
        preferred_element_type=jnp.float32,
    )
    output = (middle + mlp_branch).astype(jnp.bfloat16).reshape(rows, stretch, width)
    grad_out_low = cotangent.reshape(count, width)
    grad_active = contract_last(
        grad_out_low, lax.all_gather(w_down, ("row", "seq"), axis=0, tiled=True)
    )
    grad_down = lax.psum_scatter(
        contract_first(active, grad_out_low), ("row", "seq"), scatter_dimension=0, tiled=True
    )
    grad_up_low = (grad_active * silu_value).astype(jnp.bfloat16)
    grad_gate_low = (grad_active * up_sum * sigma * (1.0 + gate_sum * (1.0 - sigma))).astype(
        jnp.bfloat16
    )
    both_grads = jnp.concatenate([grad_gate_low, grad_up_low], axis=1)
    gain_piece = lax.all_gather(mlp_gain, ("row", "seq"), axis=0, tiled=True)
    gate_piece = lax.all_gather(w_gate, ("row", "seq"), axis=0, tiled=True)
    up_piece = lax.all_gather(w_up, ("row", "seq"), axis=0, tiled=True)
    grad_piece = contract_last(grad_gate_low, gate_piece) + contract_last(grad_up_low, up_piece)
    normed_piece = normed_two
    grad_normed_two = grad_piece * gain_piece.astype(jnp.float32)
    grad_gain_two = jnp.sum(normed_piece * grad_piece, axis=0)
    grad_gate_up = lax.psum_scatter(
        contract_first(hidden_two, both_grads), ("row", "seq"), scatter_dimension=0, tiled=True
    )
    grad_gate = grad_gate_up[:, :hidden_width]
    grad_up = grad_gate_up[:, hidden_width:]
    grad_middle = grad_out_low.astype(jnp.float32) + norm_back(
        grad_normed_two, normed_two, scale_two
    )
    grad_branch_low = grad_middle.astype(jnp.bfloat16)
    grad_mixed = contract_last(
        grad_branch_low, lax.all_gather(w_out, ("row", "seq"), axis=0, tiled=True)
    ).astype(jnp.bfloat16)
    grad_out = lax.psum_scatter(
        contract_first(mixed, grad_branch_low), ("row", "seq"), scatter_dimension=0, tiled=True
    )
    grad_grouped = grad_mixed.reshape(rows, stretch, key_heads, groups, HEAD_DIM)
    key_back, value_back = gather_keys()

    def delta_step(index, total):
        probs = jnp.exp(block_scores(block_rows(key_back, index), index) - log_total[..., None])
        grad_probs = jnp.einsum(
            "rqhgd,rkhd->rhgqk",
            grad_grouped,
            block_rows(value_back, index),
            preferred_element_type=jnp.float32,
        )
        return total + jnp.sum(probs * grad_probs, axis=-1)

    delta = lax.fori_loop(0, live_blocks, delta_step, jnp.zeros(stat_shape, jnp.float32))

    def grad_step(index, carry):
        grad_queries, grad_key_all, grad_value_all = carry
        key_block = block_rows(key_back, index)
        probs = jnp.exp(block_scores(key_block, index) - log_total[..., None])
        grad_probs = jnp.einsum(
            "rqhgd,rkhd->rhgqk",
            grad_grouped,
            block_rows(value_back, index),
            preferred_element_type=jnp.float32,
        )
        grad_raw = (scale * probs * (grad_probs - delta[..., None])).astype(jnp.bfloat16)
        grad_queries = grad_queries + jnp.einsum(
            "rhgqk,rkhd->rqhgd", grad_raw, key_block, preferred_element_type=jnp.float32
        )
        key_part = jnp.einsum(
            "rhgqk,rqhgd->rkhd", grad_raw, query_grouped, preferred_element_type=jnp.float32
        ).reshape(rows, block, key_width)
        value_part = jnp.einsum(
            "rhgqk,rqhgd->rkhd",
            probs.astype(jnp.bfloat16),
            grad_grouped,
            preferred_element_type=jnp.float32,
        ).reshape(rows, block, key_width)
        return (
            grad_queries,
            lax.dynamic_update_slice_in_dim(grad_key_all, key_part, index * block, 1),
            lax.dynamic_update_slice_in_dim(grad_value_all, value_part, index * block, 1),
        )

    grad_queries, grad_key_all, grad_value_all = lax.fori_loop(
        0,
        live_blocks,
        grad_step,
        (
            jnp.zeros((rows, stretch, key_heads, groups, HEAD_DIM), jnp.float32),
            jnp.zeros((rows, length, key_width), jnp.float32),
            jnp.zeros((rows, length, key_width), jnp.float32),
        ),
    )
    grad_key_sum, grad_value_sum = (
        lax.psum_scatter(
            grad_key_all.astype(jnp.bfloat16), "seq", scatter_dimension=1, tiled=True
        ).astype(jnp.float32),
        lax.psum_scatter(
            grad_value_all.astype(jnp.bfloat16), "seq", scatter_dimension=1, tiled=True
        ).astype(jnp.float32),
    )
    grad_query_low = (
        rotate_back(grad_queries.reshape(rows, stretch, heads, HEAD_DIM), cosine, sine)
        .reshape(count, width)
        .astype(jnp.bfloat16)
    )
    grad_key_low = (
        rotate_back(grad_key_sum.reshape(rows, stretch, key_heads, HEAD_DIM), cosine, sine)
        .reshape(count, key_width)
        .astype(jnp.bfloat16)
    )
    grad_value_low = grad_value_sum.reshape(count, key_width).astype(jnp.bfloat16)
    gain_piece = lax.all_gather(attn_gain, ("row", "seq"), axis=0, tiled=True)
    query_piece = lax.all_gather(w_query, ("row", "seq"), axis=0, tiled=True)
    key_piece = lax.all_gather(w_key, ("row", "seq"), axis=0, tiled=True)
    value_piece = lax.all_gather(w_value, ("row", "seq"), axis=0, tiled=True)
    grad_piece = (
        contract_last(grad_query_low, query_piece)
        + contract_last(grad_key_low, key_piece)
        + contract_last(grad_value_low, value_piece)
    )
    normed_piece = normed_one
    grad_normed_one = grad_piece * gain_piece.astype(jnp.float32)
    grad_gain_one = jnp.sum(normed_piece * grad_piece, axis=0)
    grad_query, grad_key, grad_value, grad_attn_gain, grad_mlp_gain = (
        lax.psum_scatter(
            contract_first(hidden_one, grad_query_low),
            ("row", "seq"),
            scatter_dimension=0,
            tiled=True,
        ),
        lax.psum_scatter(
            contract_first(hidden_one, grad_key_low),
            ("row", "seq"),
            scatter_dimension=0,
            tiled=True,
        ),
        lax.psum_scatter(
            contract_first(hidden_one, grad_value_low),
            ("row", "seq"),
            scatter_dimension=0,
            tiled=True,
        ),
        lax.psum_scatter(grad_gain_one, ("row", "seq"), scatter_dimension=0, tiled=True),
        lax.psum_scatter(grad_gain_two, ("row", "seq"), scatter_dimension=0, tiled=True),
    )
    grad_tokens = (grad_middle + norm_back(grad_normed_one, normed_one, scale_one)).reshape(
        rows, stretch, width
    )
    return (
        output,
        grad_tokens,
        grad_attn_gain,
        grad_query,
        grad_key,
        grad_value,
        grad_out,
        grad_mlp_gain,
        grad_gate,
        grad_up,
        grad_down,
    )


BOTH = ("row", "seq")


def gather(piece, axis_name, axis):
    return lax.all_gather(piece, axis_name, axis=axis, tiled=True)


def scatter(whole, axis_name, axis):
    return lax.psum_scatter(whole, axis_name, scatter_dimension=axis, tiled=True)


def sharded_layer(
    tokens,
    cotangent,
    doc_lengths,
    attn_gain,
    w_query,
    w_key,
    w_value,
    w_out,
    mlp_gain,
    w_gate,
    w_up,
    w_down,
):
    row_size, seq_size = lax.axis_size("row"), lax.axis_size("seq")
    rows, stretch, width = tokens.shape
    length = stretch * seq_size
    count = rows * length
    piece_rows = w_query.shape[0]
    key_heads = w_key.shape[1] // HEAD_DIM // seq_size
    heads = w_query.shape[1] // HEAD_DIM // seq_size
    groups = heads // key_heads
    query_width, key_width = heads * HEAD_DIM, key_heads * HEAD_DIM
    unit_block = w_down.shape[0]
    units = unit_block * row_size
    scale = HEAD_DIM ** (-0.5)

    place = jnp.arange(length, dtype=jnp.int32)
    ends = jnp.cumsum(doc_lengths, axis=1)
    first = jnp.max(
        jnp.where(ends[:, None, :] <= place[None, :, None], ends[:, None, :], 0), axis=2
    )
    table = jnp.asarray(rope_table(HEAD_DIM), jnp.float32)
    angle = (place[None, :] - first).astype(jnp.float32)[..., None] * table
    cosine = jnp.concatenate([jnp.cos(angle), jnp.cos(angle)], axis=-1)[:, :, None, :]
    sine = jnp.concatenate([jnp.sin(angle), jnp.sin(angle)], axis=-1)[:, :, None, :]

    gains = gather(jnp.stack([attn_gain, mlp_gain]), BOTH, 1).astype(jnp.float32)

    def unit_columns(weight):
        split = weight.reshape(piece_rows, row_size, seq_size, unit_block)
        return split.transpose(0, 2, 1, 3).reshape(piece_rows, seq_size, units)

    def to_columns(*pieces):
        mine = jnp.concatenate(pieces, axis=2)
        mine = lax.all_to_all(mine, "seq", 1, 0, tiled=True)
        return gather(mine.reshape(piece_rows * seq_size, -1), "row", 0)

    total = row_size * seq_size
    shift = [(i, (i % row_size) * seq_size + i // row_size) for i in range(total)]
    shift_back = [(b, a) for a, b in shift]

    w_qkv = to_columns(
        w_query.reshape(piece_rows, seq_size, query_width),
        w_key.reshape(piece_rows, seq_size, key_width),
        w_value.reshape(piece_rows, seq_size, key_width),
    )
    out_part = gather(lax.ppermute(w_out, BOTH, shift), "row", 0)
    w_units = to_columns(unit_columns(w_gate), unit_columns(w_up))
    down_part = gather(w_down, "row", 0)

    all_tokens = gather(tokens, "seq", 1).reshape(count, width)
    all_cotangent = gather(cotangent, "seq", 1).reshape(count, width)

    inputs = all_tokens.astype(jnp.float32)
    hidden_one = (inputs * norm_scale(inputs) * gains[0]).astype(jnp.bfloat16)
    qkv = jnp.dot(hidden_one, w_qkv, preferred_element_type=jnp.float32)
    queries = rotate(
        qkv[:, :query_width].reshape(rows, length, heads, HEAD_DIM), cosine, sine
    ).astype(jnp.bfloat16).reshape(rows, length, key_heads, groups, HEAD_DIM)
    keys = rotate(
        qkv[:, query_width : query_width + key_width].reshape(rows, length, key_heads, HEAD_DIM),
        cosine,
        sine,
    ).astype(jnp.bfloat16)
    values = (
        qkv[:, query_width + key_width :]
        .astype(jnp.bfloat16)
        .reshape(rows, length, key_heads, HEAD_DIM)
    )
    raw = jnp.einsum("rqhgd,rkhd->rhgqk", queries, keys, preferred_element_type=jnp.float32)
    allowed = (place[None, None, :] <= place[None, :, None]) & (
        place[None, None, :] >= first[:, :, None]
    )
    probs = jax.nn.softmax(jnp.where(allowed[:, None, None], raw * scale, -1e30), axis=-1)
    probs_low = probs.astype(jnp.bfloat16)
    mixed = (
        jnp.einsum("rhgqk,rkhd->rqhgd", probs_low, values, preferred_element_type=jnp.float32)
        .astype(jnp.bfloat16)
        .reshape(count, query_width)
    )
    branch = jnp.dot(mixed, out_part, preferred_element_type=jnp.float32).astype(jnp.bfloat16)
    branch = scatter(branch.reshape(rows, length, width), "seq", 1)
    own_inputs = tokens.astype(jnp.float32)
    middle = own_inputs + branch.astype(jnp.float32)
    scale_two = norm_scale(middle)
    normed_two = middle * scale_two
    hidden_two = gather((normed_two * gains[1]).astype(jnp.bfloat16), "seq", 1)
    hidden_two = hidden_two.reshape(count, width)
    both = jnp.dot(hidden_two, w_units, preferred_element_type=jnp.float32)
    gate_sum, up_sum = both[:, :units], both[:, units:]
    sigma = jax.nn.sigmoid(gate_sum)
    silu_value = gate_sum * sigma
    active = (silu_value * up_sum).astype(jnp.bfloat16)
    mlp_branch = jnp.dot(active, down_part, preferred_element_type=jnp.float32)
    mlp_branch = scatter(mlp_branch.astype(jnp.bfloat16).reshape(rows, length, width), "seq", 1)
    output = (middle + mlp_branch.astype(jnp.float32)).astype(jnp.bfloat16)

    grad_active = contract_last(all_cotangent, down_part)
    grad_down = scatter(contract_first(active, all_cotangent).astype(jnp.bfloat16), "row", 0)
    grad_up_low = (grad_active * silu_value).astype(jnp.bfloat16)
    grad_gate_low = (grad_active * up_sum * sigma * (1.0 + gate_sum * (1.0 - sigma))).astype(
        jnp.bfloat16
    )
    both_grads = jnp.concatenate([grad_gate_low, grad_up_low], axis=1)
    grad_hidden = contract_last(both_grads, w_units).astype(jnp.bfloat16)
    grad_hidden = scatter(grad_hidden.reshape(rows, length, width), "seq", 1).astype(jnp.float32)
    grad_gain_two = jnp.sum(normed_two * grad_hidden, axis=(0, 1))
    grad_middle = cotangent.astype(jnp.float32) + norm_back(
        grad_hidden * gains[1], normed_two, scale_two
    )

    def from_columns(grad):
        mine = scatter(grad.astype(jnp.bfloat16), "row", 0)
        mine = mine.reshape(seq_size, piece_rows, -1)
        mine = lax.all_to_all(mine, "seq", 0, 0, tiled=True)
        return mine.transpose(1, 0, 2)

    def unit_rows(grad):
        split = grad.reshape(piece_rows, seq_size, row_size, unit_block)
        return split.transpose(0, 2, 1, 3).reshape(piece_rows, -1).astype(jnp.float32)

    grad_units = from_columns(contract_first(hidden_two, both_grads))
    grad_gate, grad_up = unit_rows(grad_units[:, :, :units]), unit_rows(grad_units[:, :, units:])

    grad_branch = gather(grad_middle.astype(jnp.bfloat16), "seq", 1).reshape(count, width)
    grad_mixed = contract_last(grad_branch, out_part).astype(jnp.bfloat16)
    grad_out = scatter(contract_first(mixed, grad_branch).astype(jnp.bfloat16), "row", 0)
    grad_out = lax.ppermute(grad_out, BOTH, shift_back).astype(jnp.float32)
    grad_grouped = grad_mixed.reshape(rows, length, key_heads, groups, HEAD_DIM)
    grad_probs = jnp.einsum(
        "rqhgd,rkhd->rhgqk", grad_grouped, values, preferred_element_type=jnp.float32
    )
    delta = jnp.sum(probs * grad_probs, axis=-1, keepdims=True)
    grad_raw = (scale * probs * (grad_probs - delta)).astype(jnp.bfloat16)
    grad_queries = jnp.einsum(
        "rhgqk,rkhd->rqhgd", grad_raw, keys, preferred_element_type=jnp.float32
    )
    grad_keys = jnp.einsum(
        "rhgqk,rqhgd->rkhd", grad_raw, queries, preferred_element_type=jnp.float32
    )
    grad_values = jnp.einsum(
        "rhgqk,rqhgd->rkhd", probs_low, grad_grouped, preferred_element_type=jnp.float32
    )
    grad_qkv_low = jnp.concatenate(
        [
            rotate_back(grad_queries.reshape(rows, length, heads, HEAD_DIM), cosine, sine).reshape(
                count, query_width
            ),
            rotate_back(grad_keys, cosine, sine).reshape(count, key_width),
            grad_values.reshape(count, key_width),
        ],
        axis=1,
    ).astype(jnp.bfloat16)
    grad_qkv = from_columns(contract_first(hidden_one, grad_qkv_low))

    def head_rows(grad):
        return grad.reshape(piece_rows, -1).astype(jnp.float32)

    grad_query = head_rows(grad_qkv[:, :, :query_width])
    grad_key = head_rows(grad_qkv[:, :, query_width : query_width + key_width])
    grad_value = head_rows(grad_qkv[:, :, query_width + key_width :])
    grad_hidden = contract_last(grad_qkv_low, w_qkv).astype(jnp.bfloat16)
    grad_hidden = scatter(grad_hidden.reshape(rows, length, width), "seq", 1).astype(jnp.float32)
    own_scale = norm_scale(own_inputs)
    own_normed = own_inputs * own_scale
    grad_gain_one = jnp.sum(own_normed * grad_hidden, axis=(0, 1))
    grad_tokens = grad_middle + norm_back(grad_hidden * gains[0], own_normed, own_scale)
    grad_gains = scatter(jnp.stack([grad_gain_one, grad_gain_two]), BOTH, 1)
    return (
        output,
        grad_tokens,
        grad_gains[0],
        grad_query,
        grad_key,
        grad_value,
        grad_out,
        grad_gains[1],
        grad_gate,
        grad_up,
        grad_down.astype(jnp.float32),
    )


def local(tokens, cotangent, doc_lengths, attn_gain, w_query, w_key, w_value, *rest):
    whole_heads = w_key.shape[1] % (HEAD_DIM * lax.axis_size("seq")) == 0
    layer = sharded_layer if whole_heads else gathered_layer
    return layer(tokens, cotangent, doc_lengths, attn_gain, w_query, w_key, w_value, *rest)


def solution(mesh):
    return jax.shard_map(
        local,
        mesh=mesh,
        in_specs=(
            P("row", "seq", None),
            P("row", "seq", None),
            P("row", None),
            P(("row", "seq")),
            P(("row", "seq"), None),
            P(("row", "seq"), None),
            P(("row", "seq"), None),
            P(("row", "seq"), None),
            P(("row", "seq")),
            P(("row", "seq"), None),
            P(("row", "seq"), None),
            P(("row", "seq"), None),
        ),
        out_specs=(
            P("row", "seq", None),
            P("row", "seq", None),
            P(("row", "seq")),
            P(("row", "seq"), None),
            P(("row", "seq"), None),
            P(("row", "seq"), None),
            P(("row", "seq"), None),
            P(("row", "seq")),
            P(("row", "seq"), None),
            P(("row", "seq"), None),
            P(("row", "seq"), None),
        ),
        check_vma=False,
    )
```

```python
import math

import jax
import jax.numpy as jnp
import numpy as np
from jax import lax
from jax.experimental import pallas as pl
from jax.experimental.pallas import tpu as pltpu
from jax.sharding import PartitionSpec as P

HEAD_DIM = 64


EPSILON = 1e-05
THETA = 500000.0


def rope_table(head_size):
    half_size = head_size // 2
    plain = THETA ** (-(np.arange(half_size) * 2.0) / head_size)
    factor, low_factor, high_factor, old_span = (32.0, 1.0, 4.0, 8192.0)
    wavelength = 2.0 * math.pi / plain
    smooth = (old_span / wavelength - low_factor) / (high_factor - low_factor)
    blended = (1.0 - smooth) * plain / factor + smooth * plain
    return np.where(
        wavelength < old_span / high_factor,
        plain,
        np.where(wavelength > old_span / low_factor, plain / factor, blended),
    )


def norm_scale(values):
    return lax.rsqrt(jnp.mean(values * values, axis=-1, keepdims=True) + EPSILON)


def norm_back(grad_normed, normed, scale):
    return scale * (grad_normed - normed * jnp.mean(grad_normed * normed, axis=-1, keepdims=True))


def rotate(values, cosine, sine):
    half_size = values.shape[-1] // 2
    turned = jnp.concatenate([-values[..., half_size:], values[..., :half_size]], axis=-1)
    return values * cosine + turned * sine


def rotate_back(grad, cosine, sine):
    half_size = grad.shape[-1] // 2
    turned = grad * sine
    return grad * cosine + jnp.concatenate(
        [turned[..., half_size:], -turned[..., :half_size]], axis=-1
    )


def contract_last(left, right):
    return lax.dot_general(
        left, right, (((1,), (1,)), ((), ())), preferred_element_type=jnp.float32
    )


def contract_first(left, right):
    return lax.dot_general(
        left, right, (((0,), (0,)), ((), ())), preferred_element_type=jnp.float32
    )


def gathered_layer(
    tokens,
    cotangent,
    doc_lengths,
    attn_gain,
    w_query,
    w_key,
    w_value,
    w_out,
    mlp_gain,
    w_gate,
    w_up,
    w_down,
):
    rows, stretch, width = tokens.shape
    count = rows * stretch
    key_width = w_key.shape[1]
    hidden_width = w_gate.shape[1]
    key_heads = key_width // HEAD_DIM
    heads = width // HEAD_DIM
    groups = heads // key_heads
    length = stretch * lax.axis_size("seq")
    block = math.gcd(length, 512)
    scale = HEAD_DIM ** (-0.5)
    table = jnp.asarray(rope_table(HEAD_DIM), jnp.float32)
    place = lax.axis_index("seq") * stretch + jnp.arange(stretch, dtype=jnp.int32)
    live_blocks = ((lax.axis_index("seq") + 1) * stretch + block - 1) // block
    ends = jnp.cumsum(doc_lengths, axis=1)
    first = jnp.max(
        jnp.where(ends[:, None, :] <= place[None, :, None], ends[:, None, :], 0), axis=2
    )
    angle = (place[None, :] - first).astype(jnp.float32)[..., None] * table
    cosine = jnp.concatenate([jnp.cos(angle), jnp.cos(angle)], axis=-1)[:, :, None, :]
    sine = jnp.concatenate([jnp.sin(angle), jnp.sin(angle)], axis=-1)[:, :, None, :]
    inputs = tokens.reshape(count, width).astype(jnp.float32)
    scale_one = norm_scale(inputs)
    normed_one = inputs * scale_one
    gain_piece = lax.all_gather(attn_gain, ("row", "seq"), axis=0, tiled=True)
    query_piece = lax.all_gather(w_query, ("row", "seq"), axis=0, tiled=True)
    key_piece = lax.all_gather(w_key, ("row", "seq"), axis=0, tiled=True)
    value_piece = lax.all_gather(w_value, ("row", "seq"), axis=0, tiled=True)
    hidden_piece = (normed_one * gain_piece.astype(jnp.float32)).astype(jnp.bfloat16)
    query_sum = jnp.dot(hidden_piece, query_piece, preferred_element_type=jnp.float32)
    key_sum = jnp.dot(hidden_piece, key_piece, preferred_element_type=jnp.float32)
    value_sum = jnp.dot(hidden_piece, value_piece, preferred_element_type=jnp.float32)
    hidden_one = hidden_piece
    queries = rotate(query_sum.reshape(rows, stretch, heads, HEAD_DIM), cosine, sine).astype(
        jnp.bfloat16
    )
    keys = rotate(key_sum.reshape(rows, stretch, key_heads, HEAD_DIM), cosine, sine).astype(
        jnp.bfloat16
    )
    values = value_sum.astype(jnp.bfloat16)
    query_grouped = queries.reshape(rows, stretch, key_heads, groups, HEAD_DIM)

    def gather_keys():
        return (
            lax.all_gather(keys.reshape(rows, stretch, key_width), "seq", axis=1, tiled=True),
            lax.all_gather(values.reshape(rows, stretch, key_width), "seq", axis=1, tiled=True),
        )

    key_all, value_all = gather_keys()

    def block_rows(source, index):
        return lax.dynamic_slice_in_dim(source, index * block, block, 1).reshape(
            rows, block, key_heads, HEAD_DIM
        )

    def block_scores(key_block, index):
        raw = jnp.einsum(
            "rqhgd,rkhd->rhgqk", query_grouped, key_block, preferred_element_type=jnp.float32
        )
        key_place = index * block + jnp.arange(block, dtype=jnp.int32)
        allowed = (key_place[None, None, :] <= place[None, :, None]) & (
            key_place[None, None, :] >= first[:, :, None]
        )
        return jnp.where(allowed[:, None, None], raw * scale, -1e30)

    def total_step(index, carry):
        running_max, running_total = carry
        scores = block_scores(block_rows(key_all, index), index)
        new_max = jnp.maximum(running_max, jnp.max(scores, axis=-1))
        new_total = running_total * jnp.exp(running_max - new_max) + jnp.sum(
            jnp.exp(scores - new_max[..., None]), axis=-1
        )
        return (new_max, new_total)

    stat_shape = (rows, key_heads, groups, stretch)
    running_max, running_total = lax.fori_loop(
        0,
        live_blocks,
        total_step,
        (jnp.full(stat_shape, -1e30, jnp.float32), jnp.zeros(stat_shape, jnp.float32)),
    )
    log_total = running_max + jnp.log(running_total)

    def mix_step(index, mixed_sum):
        probs = jnp.exp(block_scores(block_rows(key_all, index), index) - log_total[..., None])
        return mixed_sum + jnp.einsum(
            "rhgqk,rkhd->rqhgd",
            probs.astype(jnp.bfloat16),
            block_rows(value_all, index),
            preferred_element_type=jnp.float32,
        )

    mixed_sum = lax.fori_loop(
        0,
        live_blocks,
        mix_step,
        jnp.zeros((rows, stretch, key_heads, groups, HEAD_DIM), jnp.float32),
    )
    mixed = mixed_sum.reshape(count, width).astype(jnp.bfloat16)
    attn_branch = jnp.dot(
        mixed,
        lax.all_gather(w_out, ("row", "seq"), axis=0, tiled=True),
        preferred_element_type=jnp.float32,
    )
    middle = inputs + attn_branch
    scale_two = norm_scale(middle)
    normed_two = middle * scale_two
    gain_piece = lax.all_gather(mlp_gain, ("row", "seq"), axis=0, tiled=True)
    gate_piece = lax.all_gather(w_gate, ("row", "seq"), axis=0, tiled=True)
    up_piece = lax.all_gather(w_up, ("row", "seq"), axis=0, tiled=True)
    hidden_piece = (normed_two * gain_piece.astype(jnp.float32)).astype(jnp.bfloat16)
    gate_sum, up_sum, hidden_two = (
        jnp.dot(hidden_piece, gate_piece, preferred_element_type=jnp.float32),
        jnp.dot(hidden_piece, up_piece, preferred_element_type=jnp.float32),
        hidden_piece,
    )
    sigma = jax.nn.sigmoid(gate_sum)
    silu_value = gate_sum * sigma
    active = (silu_value * up_sum).astype(jnp.bfloat16)
    mlp_branch = jnp.dot(
        active,
        lax.all_gather(w_down, ("row", "seq"), axis=0, tiled=True),
        preferred_element_type=jnp.float32,
    )
    output = (middle + mlp_branch).astype(jnp.bfloat16).reshape(rows, stretch, width)
    grad_out_low = cotangent.reshape(count, width)
    grad_active = contract_last(
        grad_out_low, lax.all_gather(w_down, ("row", "seq"), axis=0, tiled=True)
    )
    grad_down = lax.psum_scatter(
        contract_first(active, grad_out_low), ("row", "seq"), scatter_dimension=0, tiled=True
    )
    grad_up_low = (grad_active * silu_value).astype(jnp.bfloat16)
    grad_gate_low = (grad_active * up_sum * sigma * (1.0 + gate_sum * (1.0 - sigma))).astype(
        jnp.bfloat16
    )
    both_grads = jnp.concatenate([grad_gate_low, grad_up_low], axis=1)
    gain_piece = lax.all_gather(mlp_gain, ("row", "seq"), axis=0, tiled=True)
    gate_piece = lax.all_gather(w_gate, ("row", "seq"), axis=0, tiled=True)
    up_piece = lax.all_gather(w_up, ("row", "seq"), axis=0, tiled=True)
    grad_piece = contract_last(grad_gate_low, gate_piece) + contract_last(grad_up_low, up_piece)
    normed_piece = normed_two
    grad_normed_two = grad_piece * gain_piece.astype(jnp.float32)
    grad_gain_two = jnp.sum(normed_piece * grad_piece, axis=0)
    grad_gate_up = lax.psum_scatter(
        contract_first(hidden_two, both_grads), ("row", "seq"), scatter_dimension=0, tiled=True
    )
    grad_gate = grad_gate_up[:, :hidden_width]
    grad_up = grad_gate_up[:, hidden_width:]
    grad_middle = grad_out_low.astype(jnp.float32) + norm_back(
        grad_normed_two, normed_two, scale_two
    )
    grad_branch_low = grad_middle.astype(jnp.bfloat16)
    grad_mixed = contract_last(
        grad_branch_low, lax.all_gather(w_out, ("row", "seq"), axis=0, tiled=True)
    ).astype(jnp.bfloat16)
    grad_out = lax.psum_scatter(
        contract_first(mixed, grad_branch_low), ("row", "seq"), scatter_dimension=0, tiled=True
    )
    grad_grouped = grad_mixed.reshape(rows, stretch, key_heads, groups, HEAD_DIM)
    key_back, value_back = gather_keys()

    def delta_step(index, total):
        probs = jnp.exp(block_scores(block_rows(key_back, index), index) - log_total[..., None])
        grad_probs = jnp.einsum(
            "rqhgd,rkhd->rhgqk",
            grad_grouped,
            block_rows(value_back, index),
            preferred_element_type=jnp.float32,
        )
        return total + jnp.sum(probs * grad_probs, axis=-1)

    delta = lax.fori_loop(0, live_blocks, delta_step, jnp.zeros(stat_shape, jnp.float32))

    def grad_step(index, carry):
        grad_queries, grad_key_all, grad_value_all = carry
        key_block = block_rows(key_back, index)
        probs = jnp.exp(block_scores(key_block, index) - log_total[..., None])
        grad_probs = jnp.einsum(
            "rqhgd,rkhd->rhgqk",
            grad_grouped,
            block_rows(value_back, index),
            preferred_element_type=jnp.float32,
        )
        grad_raw = (scale * probs * (grad_probs - delta[..., None])).astype(jnp.bfloat16)
        grad_queries = grad_queries + jnp.einsum(
            "rhgqk,rkhd->rqhgd", grad_raw, key_block, preferred_element_type=jnp.float32
        )
        key_part = jnp.einsum(
            "rhgqk,rqhgd->rkhd", grad_raw, query_grouped, preferred_element_type=jnp.float32
        ).reshape(rows, block, key_width)
        value_part = jnp.einsum(
            "rhgqk,rqhgd->rkhd",
            probs.astype(jnp.bfloat16),
            grad_grouped,
            preferred_element_type=jnp.float32,
        ).reshape(rows, block, key_width)
        return (
            grad_queries,
            lax.dynamic_update_slice_in_dim(grad_key_all, key_part, index * block, 1),
            lax.dynamic_update_slice_in_dim(grad_value_all, value_part, index * block, 1),
        )

    grad_queries, grad_key_all, grad_value_all = lax.fori_loop(
        0,
        live_blocks,
        grad_step,
        (
            jnp.zeros((rows, stretch, key_heads, groups, HEAD_DIM), jnp.float32),
            jnp.zeros((rows, length, key_width), jnp.float32),
            jnp.zeros((rows, length, key_width), jnp.float32),
        ),
    )
    grad_key_sum, grad_value_sum = (
        lax.psum_scatter(
            grad_key_all.astype(jnp.bfloat16), "seq", scatter_dimension=1, tiled=True
        ).astype(jnp.float32),
        lax.psum_scatter(
            grad_value_all.astype(jnp.bfloat16), "seq", scatter_dimension=1, tiled=True
        ).astype(jnp.float32),
    )
    grad_query_low = (
        rotate_back(grad_queries.reshape(rows, stretch, heads, HEAD_DIM), cosine, sine)
        .reshape(count, width)
        .astype(jnp.bfloat16)
    )
    grad_key_low = (
        rotate_back(grad_key_sum.reshape(rows, stretch, key_heads, HEAD_DIM), cosine, sine)
        .reshape(count, key_width)
        .astype(jnp.bfloat16)
    )
    grad_value_low = grad_value_sum.reshape(count, key_width).astype(jnp.bfloat16)
    gain_piece = lax.all_gather(attn_gain, ("row", "seq"), axis=0, tiled=True)
    query_piece = lax.all_gather(w_query, ("row", "seq"), axis=0, tiled=True)
    key_piece = lax.all_gather(w_key, ("row", "seq"), axis=0, tiled=True)
    value_piece = lax.all_gather(w_value, ("row", "seq"), axis=0, tiled=True)
    grad_piece = (
        contract_last(grad_query_low, query_piece)
        + contract_last(grad_key_low, key_piece)
        + contract_last(grad_value_low, value_piece)
    )
    normed_piece = normed_one
    grad_normed_one = grad_piece * gain_piece.astype(jnp.float32)
    grad_gain_one = jnp.sum(normed_piece * grad_piece, axis=0)
    grad_query, grad_key, grad_value, grad_attn_gain, grad_mlp_gain = (
        lax.psum_scatter(
            contract_first(hidden_one, grad_query_low),
            ("row", "seq"),
            scatter_dimension=0,
            tiled=True,
        ),
        lax.psum_scatter(
            contract_first(hidden_one, grad_key_low),
            ("row", "seq"),
            scatter_dimension=0,
            tiled=True,
        ),
        lax.psum_scatter(
            contract_first(hidden_one, grad_value_low),
            ("row", "seq"),
            scatter_dimension=0,
            tiled=True,
        ),
        lax.psum_scatter(grad_gain_one, ("row", "seq"), scatter_dimension=0, tiled=True),
        lax.psum_scatter(grad_gain_two, ("row", "seq"), scatter_dimension=0, tiled=True),
    )
    grad_tokens = (grad_middle + norm_back(grad_normed_one, normed_one, scale_one)).reshape(
        rows, stretch, width
    )
    return (
        output,
        grad_tokens,
        grad_attn_gain,
        grad_query,
        grad_key,
        grad_value,
        grad_out,
        grad_mlp_gain,
        grad_gate,
        grad_up,
        grad_down,
    )


MESH = pl.DeviceIdType.MESH
VMEM_LIMIT = 60 * 1024 * 1024


def neighbours():
    row, seq = lax.axis_index("row"), lax.axis_index("seq")
    row_size, seq_size = lax.axis_size("row"), lax.axis_size("seq")
    return dict(
        row=row,
        seq=seq,
        z=seq // 2,
        core=seq % 2,
        up=(row, (seq + 2) % seq_size),
        down=(row, (seq + seq_size - 2) % seq_size),
        pair=(row, seq + 1 - 2 * (seq % 2)),
        side=(row + 1 - 2 * (row % 2), seq),
        across=((row + row_size // 2) % row_size, seq),
        side_row=row + 1 - 2 * (row % 2),
        across_row=(row + row_size // 2) % row_size,
    )


def greet(peers):
    barrier = pltpu.get_barrier_semaphore()
    for peer in peers:
        pl.semaphore_signal(barrier, inc=1, device_id=peer, device_id_type=MESH)
    pl.semaphore_wait(barrier, len(peers))


def send(source, target, sems, index, peer):
    copy = pltpu.make_async_remote_copy(
        src_ref=source,
        dst_ref=target,
        send_sem=sems[0].at[index],
        recv_sem=sems[1].at[index],
        device_id=peer,
        device_id_type=MESH,
    )
    copy.start()
    return copy


def sem_pairs(amount):
    return [pltpu.SemaphoreType.DMA((amount,)), pltpu.SemaphoreType.DMA((amount,))]


def by_rows(amount, step, body):
    def one(i, carry):
        body(pl.ds(pl.multiple_of(i * step, step), step))
        return carry

    lax.fori_loop(0, amount // step, one, 0)


def copy_rows(target, source):
    def one(rows):
        target[rows] = source[rows]

    by_rows(source.shape[0], 16, one)


def gather_seq_steps(here, whole, stretch, pair_sems, ring_sems):
    seq, chips = here["seq"], lax.axis_size("seq") // 2
    seq_size = 2 * chips
    copies = []

    def spot(owner):
        return pl.ds(pl.multiple_of(owner * stretch, stretch), stretch)

    def ring(step):
        above = (seq + seq_size - 2 * step) % seq_size
        below = (seq + 2 * step) % seq_size
        up_view, down_view = whole.at[0, spot(above)], whole.at[1, spot(below)]
        moves = []
        if step < chips - 1:
            moves.append(send(up_view, up_view, ring_sems, 2 * step, here["up"]))
            moves.append(send(down_view, down_view, ring_sems, 2 * step + 1, here["down"]))
        if step == 0:
            own = whole.at[:, spot(seq)]
            copies.append(send(own, own, pair_sems, 0, here["pair"]))
        else:
            copies.append(send(up_view, up_view, pair_sems, 2 * step - 1, here["pair"]))
            copies.append(send(down_view, down_view, pair_sems, 2 * step, here["pair"]))
        return moves

    last = []

    def first_step():
        last.extend(ring(0))

    def next_step(step):
        def run():
            for copy in last:
                copy.wait()
            del last[:]
            last.extend(ring(step))

        return run

    def finish():
        for copy in copies:
            copy.wait()

    return [first_step] + [next_step(step) for step in range(1, chips)] + [finish]


def reduce_seq_steps(here, part, stretch, pair_in, total, ring_in, pair_sems, ring_sems, done):
    z, core, chips = here["z"], here["core"], lax.axis_size("seq") // 2
    order = [chips - 1, 1] + list(range(2, chips - 1)) + [0]
    copies, pair_copies = [], {}

    def spot(chip, side):
        return pl.ds(pl.multiple_of((2 * chip + side) * stretch, stretch), stretch)

    def pair_start():
        for index, far in enumerate(order):
            chip = (z + far) % chips
            pair_copies[far] = send(
                part.at[:, spot(chip, 1 - core)], pair_in.at[chip], pair_sems, index, here["pair"]
            )

    def pair_sum(far):
        chip = (z + far) % chips
        pair_copies[far].wait_recv()
        base = (2 * chip + core) * stretch

        for half in range(2):
            def add(rows):
                mine = part[half, pl.ds(pl.multiple_of(base + rows.start, 16), 16)]
                other = pair_in[chip, half, rows]
                total[chip, half, rows] = (
                    mine.astype(jnp.float32) + other.astype(jnp.float32)
                ).astype(jnp.bfloat16)

            by_rows(stretch, 16, add)

    last = {}

    def ring_send(step):
        for half, peer, chip in (
            (0, here["up"], (z + 2 * chips - 1 - step) % chips),
            (1, here["down"], (z + 1 + step) % chips),
        ):
            if step > 0:
                last[half].wait_recv()
                arrived = ring_in.at[step - 1, half]

                def add(rows):
                    total[chip, half, rows] = (
                        total[chip, half, rows].astype(jnp.float32)
                        + arrived[rows].astype(jnp.float32)
                    ).astype(jnp.bfloat16)

                by_rows(stretch, 16, add)
            last[half] = send(
                total.at[chip, half], ring_in.at[step, half], ring_sems, 2 * step + half, peer
            )
            copies.append(last[half])

    def first_step():
        pair_start()
        pair_sum(chips - 1)
        pair_sum(1)
        ring_send(0)
        for far in order[2:]:
            pair_sum(far)

    def next_step(step):
        def run():
            ring_send(step)

        return run

    def finish():
        for half in range(2):
            last[half].wait_recv()
            arrived = ring_in.at[chips - 2, half]

            def close(rows):
                done(
                    half,
                    rows,
                    total[z, half, rows].astype(jnp.float32) + arrived[rows].astype(jnp.float32),
                )

            by_rows(stretch, 16, close)

    def drain():
        for copy in list(pair_copies.values()) + copies:
            copy.wait_send()

    return [first_step] + [next_step(step) for step in range(1, chips - 1)] + [finish], drain


def gather_row_steps(here, own, whole, sems):
    half = whole.shape[1] // 2
    row, side, across = here["row"], here["side_row"], here["across_row"]
    state = []

    def first_step():
        state.append(send(own, whole.at[row], sems, 0, here["side"]))
        state.append(send(own, whole.at[row], sems, 1, here["across"]))

    def second_step():
        low, high = pl.ds(0, half), pl.ds(half, half)
        state[0].wait_recv()
        state.append(send(whole.at[side, low], whole.at[side, low], sems, 2, here["across"]))
        state[1].wait_recv()
        state.append(send(whole.at[across, high], whole.at[across, high], sems, 3, here["side"]))

    def finish():
        for copy in state[2:]:
            copy.wait_recv()
        for copy in state:
            copy.wait_send()

    return [first_step, second_step, finish]


def reduce_row_steps(here, part, inbox, sums, sems, done):
    half = part.shape[1] // 2
    row, side, across = here["row"], here["side_row"], here["across_row"]
    corner = (side + 2) % 4
    state = []

    def first_step():
        low, high = pl.ds(0, half), pl.ds(half, half)
        for index, (owner, rows, peer) in enumerate(
            (
                (corner, low, "side"),
                (corner, high, "across"),
                (side, low, "side"),
                (across, high, "across"),
            )
        ):
            state.append(send(part.at[owner, rows], inbox.at[index], sems, index, here[peer]))

    def add(owner, offset, index):
        def run(rows):
            spot = pl.ds(pl.multiple_of(offset + rows.start, 16), 16)
            sums[index, rows] = (
                part[owner, spot].astype(jnp.float32) + inbox[index, rows].astype(jnp.float32)
            ).astype(jnp.bfloat16)

        by_rows(half, 16, run)

    def second_step():
        state[0].wait_recv()
        add(across, 0, 0)
        state.append(send(sums.at[0], inbox.at[4], sems, 4, here["across"]))
        state[1].wait_recv()
        add(side, half, 1)
        state.append(send(sums.at[1], inbox.at[5], sems, 5, here["side"]))
        state[2].wait_recv()
        state[3].wait_recv()

    def finish():
        for offset, one, two in ((0, 2, 4), (half, 3, 5)):
            state[two].wait_recv()

            def close(rows):
                spot = pl.ds(pl.multiple_of(offset + rows.start, 16), 16)
                done(
                    spot,
                    part[row, spot].astype(jnp.float32)
                    + inbox[one, rows].astype(jnp.float32)
                    + inbox[two, rows].astype(jnp.float32),
                )

            by_rows(half, 16, close)
        for copy in state:
            copy.wait_send()

    return [first_step, second_step, finish]


def exchange_seq(here, source, target_of, sems):
    seq, seq_size = here["seq"], lax.axis_size("seq")
    copies = []
    for far in range(1, seq_size):
        dest = (seq + far) % seq_size
        copies.append(
            send(source.at[dest], target_of(seq), sems, far - 1, (here["row"], dest))
        )
    return copies


def seq_peers(here):
    seq_size = lax.axis_size("seq")
    return [(here["row"], (here["seq"] + far) % seq_size) for far in range(1, seq_size)]


def call(kernel, args, out_shape, scratch, collective_id):
    in_vmem = pl.BlockSpec(memory_space=pltpu.VMEM)
    return pl.pallas_call(
        kernel,
        out_shape=out_shape,
        in_specs=[in_vmem] * len(args),
        out_specs=[in_vmem] * len(out_shape),
        scratch_shapes=scratch,
        compiler_params=pltpu.CompilerParams(
            collective_id=collective_id, has_side_effects=True, vmem_limit_bytes=VMEM_LIMIT
        ),
    )(*args)


def low(*shape):
    return jax.ShapeDtypeStruct(shape, jnp.bfloat16)


def full(*shape):
    return jax.ShapeDtypeStruct(shape, jnp.float32)


def open_kernel(
    tokens, heads_pack, units_pack, out_piece, down_piece,
    all_tokens, heads_all, units_mine, out_all, down_all,
    pair_a, pair_b, ring_a, ring_b, heads_a, heads_b, units_a, units_b,
    row_a, row_b, out_a, out_b, down_a, down_b,
):
    here = neighbours()
    seq, row = here["seq"], here["row"]
    stretch = tokens.shape[1]
    piece = heads_pack.shape[1]
    greet(seq_peers(here) + [here["side"], here["across"]])

    def spot(owner):
        return pl.ds(pl.multiple_of(owner * piece, piece), piece)

    for half in range(2):
        own = pl.ds(pl.multiple_of(seq * stretch, stretch), stretch)
        copy_rows(all_tokens.at[half, own], tokens.at[half])
    heads = exchange_seq(here, heads_pack, lambda s: heads_all.at[row, spot(s)], (heads_a, heads_b))
    gather_down = gather_row_steps(here, down_piece, down_all, (down_a, down_b))
    gather_out = gather_row_steps(here, out_piece, out_all, (out_a, out_b))
    steps = gather_seq_steps(here, all_tokens, stretch, (pair_a, pair_b), (ring_a, ring_b))
    steps[0]()
    gather_out[0]()
    units = exchange_seq(here, units_pack, lambda s: units_mine.at[spot(s)], (units_a, units_b))
    copy_rows(heads_all.at[row, spot(seq)], heads_pack.at[seq])
    copy_rows(units_mine.at[spot(seq)], units_pack.at[seq])
    copy_rows(out_all.at[row], out_piece)
    copy_rows(down_all.at[row], down_piece)
    for copy in heads:
        copy.wait_recv()
    gather_heads = gather_row_steps(here, heads_all.at[row], heads_all, (row_a, row_b))
    gather_heads[0]()
    gather_out[1]()
    gather_down[0]()
    steps[1]()
    gather_heads[1]()
    steps[2]()
    gather_down[1]()
    for step in steps[3:]:
        step()
    gather_heads[2]()
    gather_out[2]()
    gather_down[2]()
    for copy in heads:
        copy.wait_send()
    for copy in units:
        copy.wait()


def middle_kernel(
    branch, tokens, gain, units_mine,
    middle, hidden, units_all,
    pair_in, total, ring_in, pair_a, pair_b, ring_a, ring_b,
    gpair_a, gpair_b, gring_a, gring_b, row_a, row_b,
):
    here = neighbours()
    seq = here["seq"]
    stretch = tokens.shape[1]
    greet([here["up"], here["down"], here["pair"], here["side"], here["across"]])

    def done(half, rows, value):
        value = tokens[half, rows].astype(jnp.float32) + value
        middle[half, rows] = value
        normed = value * norm_scale(value)
        spot = pl.ds(pl.multiple_of(seq * stretch + rows.start, 16), 16)
        hidden[half, spot] = (normed * gain[...]).astype(jnp.bfloat16)

    copy_rows(units_all.at[here["row"]], units_mine)
    reduce_steps, drain = reduce_seq_steps(
        here, branch, stretch, pair_in, total, ring_in, (pair_a, pair_b), (ring_a, ring_b), done
    )
    units = gather_row_steps(here, units_mine, units_all, (row_a, row_b))
    units[0]()
    for step in reduce_steps:
        step()
    gather_steps = gather_seq_steps(here, hidden, stretch, (gpair_a, gpair_b), (gring_a, gring_b))
    gather_steps[0]()
    gather_steps[1]()
    units[1]()
    for step in gather_steps[2:]:
        step()
    units[2]()
    drain()


def back_kernel(
    grad_part, cotangent, middle, gain, units_part,
    grad_middle, grad_low, gain_grad, units_out,
    pair_in, total, ring_in, inbox, sums, pair_a, pair_b, ring_a, ring_b,
    gpair_a, gpair_b, gring_a, gring_b, row_a, row_b,
):
    here = neighbours()
    seq = here["seq"]
    stretch = cotangent.shape[1]
    greet([here["up"], here["down"], here["pair"], here["side"], here["across"]])
    gain_grad[...] = jnp.zeros_like(gain_grad)

    def done(half, rows, grad):
        value = middle[half, rows]
        scale = norm_scale(value)
        normed = value * scale
        gain_grad[...] += jnp.sum(normed * grad, axis=0, keepdims=True)
        back = cotangent[half, rows].astype(jnp.float32) + norm_back(
            grad * gain[...], normed, scale
        )
        grad_middle[half, rows] = back
        spot = pl.ds(pl.multiple_of(seq * stretch + rows.start, 16), 16)
        grad_low[half, spot] = back.astype(jnp.bfloat16)

    def done_units(rows, value):
        units_out[rows] = value.astype(jnp.bfloat16)

    reduce_steps, drain = reduce_seq_steps(
        here, grad_part, stretch, pair_in, total, ring_in, (pair_a, pair_b), (ring_a, ring_b), done
    )
    units = reduce_row_steps(here, units_part, inbox, sums, (row_a, row_b), done_units)
    units[0]()
    for step in reduce_steps:
        step()
    gather_steps = gather_seq_steps(here, grad_low, stretch, (gpair_a, gpair_b), (gring_a, gring_b))
    gather_steps[0]()
    units[1]()
    for step in gather_steps[1:]:
        step()
    units[2]()
    drain()


def sum_small(here, mine, inbox, sems):
    chips = lax.axis_size("seq") // 2
    slot = 0
    stages = [[here["pair"]]]
    stages.append(
        [(here["row"], (here["seq"] + 2 * far) % (2 * chips)) for far in range(1, chips)]
    )
    stages += [[here["side"]], [here["across"]]]
    copies = []
    for number, stage in enumerate(stages):
        sent = [
            send(mine.at[number], inbox.at[slot + i], sems, slot + i, peer)
            for i, peer in enumerate(stage)
        ]
        value = mine[number]
        for i, copy in enumerate(sent):
            copy.wait_recv()
            value = value + inbox[slot + i]
        mine[number + 1] = value
        slot += len(stage)
        copies += sent
    for copy in copies:
        copy.wait_send()
    return slot


def close_kernel(
    grad_part, tokens, grad_middle, gain, gain_two, heads_part, units_mine,
    grad_tokens, gain_sums, heads_out, units_out,
    heads_mine, pair_in, total, ring_in, inbox, sums, small, small_in,
    pair_a, pair_b, ring_a, ring_b, row_a, row_b, heads_a, heads_b, units_a, units_b,
    small_a, small_b,
):
    here = neighbours()
    seq, chips = here["seq"], lax.axis_size("seq") // 2
    stretch = tokens.shape[1]
    greet(seq_peers(here) + [here["side"], here["across"]])
    small[0, 0:1] = jnp.zeros_like(small[0, 0:1])
    small[0, 1:2] = gain_two[...]

    def done(half, rows, grad):
        value = tokens[half, rows].astype(jnp.float32)
        scale = norm_scale(value)
        normed = value * scale
        small[0, 0:1] += jnp.sum(normed * grad, axis=0, keepdims=True)
        grad_tokens[half, rows] = grad_middle[half, rows] + norm_back(
            grad * gain[...], normed, scale
        )

    piece = heads_out.shape[1]

    def done_heads(rows, value):
        heads_mine[rows] = value.astype(jnp.bfloat16)

    reduce_steps, drain = reduce_seq_steps(
        here, grad_part, stretch, pair_in, total, ring_in, (pair_a, pair_b), (ring_a, ring_b), done
    )
    heads = reduce_row_steps(here, heads_part, inbox, sums, (row_a, row_b), done_heads)
    heads[0]()
    reduce_steps[0]()
    units = exchange_seq(here, units_mine, lambda s: units_out.at[s], (units_a, units_b))
    copy_rows(units_out.at[seq], units_mine.at[seq])
    heads[1]()
    heads[2]()

    copies = []
    for far in range(1, 2 * chips):
        dest = (seq + far) % (2 * chips)
        rows = pl.ds(pl.multiple_of(dest * piece, piece), piece)
        copies.append(
            send(
                heads_mine.at[rows], heads_out.at[seq], (heads_a, heads_b), far - 1,
                (here["row"], dest),
            )
        )
    copy_rows(heads_out.at[seq], heads_mine.at[pl.ds(pl.multiple_of(seq * piece, piece), piece)])
    for step in reduce_steps[1:]:
        step()
    sum_small(here, small, small_in, (small_a, small_b))
    gain_sums[...] = small[4]
    for copy in copies + units:
        copy.wait()
    drain()


def seq_scratch(chips, stretch, width):
    return [
        pltpu.VMEM((chips, 2, stretch, width), jnp.bfloat16),
        pltpu.VMEM((chips, 2, stretch, width), jnp.bfloat16),
        pltpu.VMEM((chips - 1, 2, stretch, width), jnp.bfloat16),
    ]


def row_scratch(pieces, columns):
    return [
        pltpu.VMEM((6, pieces // 2, columns), jnp.bfloat16),
        pltpu.VMEM((2, pieces // 2, columns), jnp.bfloat16),
    ]


BOTH = ("row", "seq")


def gather(piece, axis_name, axis):
    return lax.all_gather(piece, axis_name, axis=axis, tiled=True)


def scatter(whole, axis_name, axis):
    return lax.psum_scatter(whole, axis_name, scatter_dimension=axis, tiled=True)


def sharded_layer(
    tokens,
    cotangent,
    doc_lengths,
    attn_gain,
    w_query,
    w_key,
    w_value,
    w_out,
    mlp_gain,
    w_gate,
    w_up,
    w_down,
):
    row_size, seq_size = lax.axis_size("row"), lax.axis_size("seq")
    rows, stretch, width = tokens.shape
    length = stretch * seq_size
    count = rows * length
    piece_rows = w_query.shape[0]
    key_heads = w_key.shape[1] // HEAD_DIM // seq_size
    heads = w_query.shape[1] // HEAD_DIM // seq_size
    groups = heads // key_heads
    query_width, key_width = heads * HEAD_DIM, key_heads * HEAD_DIM
    unit_block = w_down.shape[0]
    units = unit_block * row_size
    scale = HEAD_DIM ** (-0.5)

    place = jnp.arange(length, dtype=jnp.int32)
    ends = jnp.cumsum(doc_lengths, axis=1)
    first = jnp.max(
        jnp.where(ends[:, None, :] <= place[None, :, None], ends[:, None, :], 0), axis=2
    )
    table = jnp.asarray(rope_table(HEAD_DIM), jnp.float32)
    angle = (place[None, :] - first).astype(jnp.float32)[..., None] * table
    cosine = jnp.concatenate([jnp.cos(angle), jnp.cos(angle)], axis=-1)[:, :, None, :]
    sine = jnp.concatenate([jnp.sin(angle), jnp.sin(angle)], axis=-1)[:, :, None, :]

    def unit_columns(weight):
        split = weight.reshape(piece_rows, row_size, seq_size, unit_block)
        return split.transpose(2, 0, 1, 3).reshape(seq_size, piece_rows, units)

    total = row_size * seq_size
    shift = [(i, (i % row_size) * seq_size + i // row_size) for i in range(total)]
    shift_back = [(b, a) for a, b in shift]

    def head_columns(weight, columns):
        return weight.reshape(piece_rows, seq_size, columns).transpose(1, 0, 2)

    head_width = query_width + 2 * key_width
    spare = -(head_width + 2) % 128
    gain_columns = jnp.stack([attn_gain, mlp_gain], axis=1)
    gain_columns = jnp.pad(gain_columns, ((0, 0), (0, spare)))
    heads_pack = jnp.concatenate(
        [
            head_columns(w_query, query_width),
            head_columns(w_key, key_width),
            head_columns(w_value, key_width),
            jnp.broadcast_to(gain_columns, (seq_size, piece_rows, spare + 2)),
        ],
        axis=2,
    )
    units_pack = jnp.concatenate([unit_columns(w_gate), unit_columns(w_up)], axis=2)
    pack_width = head_width + 2 + spare
    chips = seq_size // 2
    pieces = piece_rows * seq_size
    all_tokens, heads_all, units_mine, out_part, down_part = call(
        open_kernel,
        (tokens, heads_pack, units_pack, lax.ppermute(w_out, BOTH, shift), w_down),
        [
            low(rows, length, width),
            low(row_size, pieces, pack_width),
            low(pieces, 2 * units),
            low(row_size, piece_rows, width),
            low(row_size, unit_block, width),
        ],
        sem_pairs(2 * chips - 1)
        + sem_pairs(2 * chips - 2)
        + sem_pairs(seq_size - 1) * 2
        + sem_pairs(4) * 3,
        0,
    )
    all_tokens = all_tokens.reshape(count, width)
    heads_all = heads_all.reshape(width, pack_width)
    w_qkv = heads_all[:, :head_width]
    gains = heads_all[:, head_width : head_width + 2].astype(jnp.float32).T
    out_part = out_part.reshape(query_width, width)
    down_part = down_part.reshape(units, width)
    all_cotangent = gather(cotangent, "seq", 1).reshape(count, width)

    inputs = all_tokens.astype(jnp.float32)
    hidden_one = (inputs * norm_scale(inputs) * gains[0]).astype(jnp.bfloat16)
    qkv = jnp.dot(hidden_one, w_qkv, preferred_element_type=jnp.float32)
    queries = rotate(
        qkv[:, :query_width].reshape(rows, length, heads, HEAD_DIM), cosine, sine
    ).astype(jnp.bfloat16).reshape(rows, length, key_heads, groups, HEAD_DIM)
    keys = rotate(
        qkv[:, query_width : query_width + key_width].reshape(rows, length, key_heads, HEAD_DIM),
        cosine,
        sine,
    ).astype(jnp.bfloat16)
    values = (
        qkv[:, query_width + key_width :]
        .astype(jnp.bfloat16)
        .reshape(rows, length, key_heads, HEAD_DIM)
    )
    raw = jnp.einsum("rqhgd,rkhd->rhgqk", queries, keys, preferred_element_type=jnp.float32)
    allowed = (place[None, None, :] <= place[None, :, None]) & (
        place[None, None, :] >= first[:, :, None]
    )
    probs = jax.nn.softmax(jnp.where(allowed[:, None, None], raw * scale, -1e30), axis=-1)
    probs_low = probs.astype(jnp.bfloat16)
    mixed = (
        jnp.einsum("rhgqk,rkhd->rqhgd", probs_low, values, preferred_element_type=jnp.float32)
        .astype(jnp.bfloat16)
        .reshape(count, query_width)
    )
    branch = jnp.dot(mixed, out_part, preferred_element_type=jnp.float32).astype(jnp.bfloat16)
    middle, hidden_two, w_units = call(
        middle_kernel,
        (branch.reshape(rows, length, width), tokens, gains[1:2], units_mine),
        [full(rows, stretch, width), low(rows, length, width), low(row_size, pieces, 2 * units)],
        seq_scratch(chips, stretch, width)
        + sem_pairs(chips)
        + sem_pairs(2 * chips - 2)
        + sem_pairs(2 * chips - 1)
        + sem_pairs(2 * chips - 2)
        + sem_pairs(4),
        1,
    )
    hidden_two = hidden_two.reshape(count, width)
    w_units = w_units.reshape(width, 2 * units)
    both = jnp.dot(hidden_two, w_units, preferred_element_type=jnp.float32)
    gate_sum, up_sum = both[:, :units], both[:, units:]
    sigma = jax.nn.sigmoid(gate_sum)
    silu_value = gate_sum * sigma
    active = (silu_value * up_sum).astype(jnp.bfloat16)
    mlp_branch = jnp.dot(active, down_part, preferred_element_type=jnp.float32)
    mlp_branch = scatter(mlp_branch.astype(jnp.bfloat16).reshape(rows, length, width), "seq", 1)
    output = (middle + mlp_branch.astype(jnp.float32)).astype(jnp.bfloat16)

    grad_active = contract_last(all_cotangent, down_part)
    grad_down = scatter(contract_first(active, all_cotangent).astype(jnp.bfloat16), "row", 0)
    grad_up_low = (grad_active * silu_value).astype(jnp.bfloat16)
    grad_gate_low = (grad_active * up_sum * sigma * (1.0 + gate_sum * (1.0 - sigma))).astype(
        jnp.bfloat16
    )
    both_grads = jnp.concatenate([grad_gate_low, grad_up_low], axis=1)
    grad_hidden = contract_last(both_grads, w_units).astype(jnp.bfloat16)
    grad_units = contract_first(hidden_two, both_grads).astype(jnp.bfloat16)
    grad_middle, grad_branch, grad_gain_two, units_mine = call(
        back_kernel,
        (
            grad_hidden.reshape(rows, length, width),
            cotangent,
            middle,
            gains[1:2],
            grad_units.reshape(row_size, pieces, 2 * units),
        ),
        [
            full(rows, stretch, width),
            low(rows, length, width),
            full(1, width),
            low(pieces, 2 * units),
        ],
        seq_scratch(chips, stretch, width)
        + row_scratch(pieces, 2 * units)
        + sem_pairs(chips)
        + sem_pairs(2 * chips - 2)
        + sem_pairs(2 * chips - 1)
        + sem_pairs(2 * chips - 2)
        + sem_pairs(6),
        2,
    )
    grad_branch = grad_branch.reshape(count, width)
    grad_mixed = contract_last(grad_branch, out_part).astype(jnp.bfloat16)
    grad_out = scatter(contract_first(mixed, grad_branch).astype(jnp.bfloat16), "row", 0)
    grad_out = lax.ppermute(grad_out, BOTH, shift_back).astype(jnp.float32)
    grad_grouped = grad_mixed.reshape(rows, length, key_heads, groups, HEAD_DIM)
    grad_probs = jnp.einsum(
        "rqhgd,rkhd->rhgqk", grad_grouped, values, preferred_element_type=jnp.float32
    )
    delta = jnp.sum(probs * grad_probs, axis=-1, keepdims=True)
    grad_raw = (scale * probs * (grad_probs - delta)).astype(jnp.bfloat16)
    grad_queries = jnp.einsum(
        "rhgqk,rkhd->rqhgd", grad_raw, keys, preferred_element_type=jnp.float32
    )
    grad_keys = jnp.einsum(
        "rhgqk,rqhgd->rkhd", grad_raw, queries, preferred_element_type=jnp.float32
    )
    grad_values = jnp.einsum(
        "rhgqk,rqhgd->rkhd", probs_low, grad_grouped, preferred_element_type=jnp.float32
    )
    grad_qkv_low = jnp.concatenate(
        [
            rotate_back(grad_queries.reshape(rows, length, heads, HEAD_DIM), cosine, sine).reshape(
                count, query_width
            ),
            rotate_back(grad_keys, cosine, sine).reshape(count, key_width),
            grad_values.reshape(count, key_width),
        ],
        axis=1,
    ).astype(jnp.bfloat16)
    grad_qkv = contract_first(hidden_one, grad_qkv_low).astype(jnp.bfloat16)
    grad_hidden = contract_last(grad_qkv_low, w_qkv).astype(jnp.bfloat16)
    grad_tokens, gain_sums, grad_qkv, grad_units = call(
        close_kernel,
        (
            grad_hidden.reshape(rows, length, width),
            tokens,
            grad_middle,
            gains[0:1],
            grad_gain_two,
            grad_qkv.reshape(row_size, pieces, head_width),
            units_mine.reshape(seq_size, piece_rows, 2 * units),
        ),
        [
            full(rows, stretch, width),
            full(2, width),
            low(seq_size, piece_rows, head_width),
            low(seq_size, piece_rows, 2 * units),
        ],
        [pltpu.VMEM((pieces, head_width), jnp.bfloat16)]
        + seq_scratch(chips, stretch, width)
        + row_scratch(pieces, head_width)
        + [pltpu.VMEM((5, 2, width), jnp.float32), pltpu.VMEM((chips + 2, 2, width), jnp.float32)]
        + sem_pairs(chips)
        + sem_pairs(2 * chips - 2)
        + sem_pairs(6)
        + sem_pairs(seq_size - 1) * 2
        + sem_pairs(chips + 2),
        3,
    )

    def unit_rows(grad):
        split = grad.reshape(seq_size, piece_rows, row_size, unit_block)
        return split.transpose(1, 2, 0, 3).reshape(piece_rows, -1).astype(jnp.float32)

    def head_rows(grad):
        return grad.transpose(1, 0, 2).reshape(piece_rows, -1).astype(jnp.float32)

    grad_gate, grad_up = unit_rows(grad_units[:, :, :units]), unit_rows(grad_units[:, :, units:])
    grad_query = head_rows(grad_qkv[:, :, :query_width])
    grad_key = head_rows(grad_qkv[:, :, query_width : query_width + key_width])
    grad_value = head_rows(grad_qkv[:, :, query_width + key_width :])
    own = (lax.axis_index("row") * seq_size + lax.axis_index("seq")) * piece_rows
    grad_gains = lax.dynamic_slice_in_dim(gain_sums, own, piece_rows, 1)
    return (
        output,
        grad_tokens,
        grad_gains[0],
        grad_query,
        grad_key,
        grad_value,
        grad_out,
        grad_gains[1],
        grad_gate,
        grad_up,
        grad_down.astype(jnp.float32),
    )


def local(tokens, cotangent, doc_lengths, attn_gain, w_query, w_key, w_value, *rest):
    whole_heads = w_key.shape[1] % (HEAD_DIM * lax.axis_size("seq")) == 0
    layer = sharded_layer if whole_heads else gathered_layer
    return layer(tokens, cotangent, doc_lengths, attn_gain, w_query, w_key, w_value, *rest)


def solution(mesh):
    return jax.shard_map(
        local,
        mesh=mesh,
        in_specs=(
            P("row", "seq", None),
            P("row", "seq", None),
            P("row", None),
            P(("row", "seq")),
            P(("row", "seq"), None),
            P(("row", "seq"), None),
            P(("row", "seq"), None),
            P(("row", "seq"), None),
            P(("row", "seq")),
            P(("row", "seq"), None),
            P(("row", "seq"), None),
            P(("row", "seq"), None),
        ),
        out_specs=(
            P("row", "seq", None),
            P("row", "seq", None),
            P(("row", "seq")),
            P(("row", "seq"), None),
            P(("row", "seq"), None),
            P(("row", "seq"), None),
            P(("row", "seq"), None),
            P(("row", "seq")),
            P(("row", "seq"), None),
            P(("row", "seq"), None),
            P(("row", "seq"), None),
        ),
        check_vma=False,
    )
```

```python
import math

import jax
import jax.numpy as jnp
import numpy as np
from jax import lax
from jax.experimental import pallas as pl
from jax.experimental.pallas import tpu as pltpu
from jax.sharding import PartitionSpec as P

HEAD_DIM = 64


EPSILON = 1e-05
THETA = 500000.0


def rope_table(head_size):
    half_size = head_size // 2
    plain = THETA ** (-(np.arange(half_size) * 2.0) / head_size)
    factor, low_factor, high_factor, old_span = (32.0, 1.0, 4.0, 8192.0)
    wavelength = 2.0 * math.pi / plain
    smooth = (old_span / wavelength - low_factor) / (high_factor - low_factor)
    blended = (1.0 - smooth) * plain / factor + smooth * plain
    return np.where(
        wavelength < old_span / high_factor,
        plain,
        np.where(wavelength > old_span / low_factor, plain / factor, blended),
    )


def norm_scale(values):
    return lax.rsqrt(jnp.mean(values * values, axis=-1, keepdims=True) + EPSILON)


def norm_back(grad_normed, normed, scale):
    return scale * (grad_normed - normed * jnp.mean(grad_normed * normed, axis=-1, keepdims=True))


def rotate(values, cosine, sine):
    half_size = values.shape[-1] // 2
    turned = jnp.concatenate([-values[..., half_size:], values[..., :half_size]], axis=-1)
    return values * cosine + turned * sine


def rotate_back(grad, cosine, sine):
    half_size = grad.shape[-1] // 2
    turned = grad * sine
    return grad * cosine + jnp.concatenate(
        [turned[..., half_size:], -turned[..., :half_size]], axis=-1
    )


def contract_last(left, right):
    return lax.dot_general(
        left, right, (((1,), (1,)), ((), ())), preferred_element_type=jnp.float32
    )


def contract_first(left, right):
    return lax.dot_general(
        left, right, (((0,), (0,)), ((), ())), preferred_element_type=jnp.float32
    )


def gathered_layer(
    tokens,
    cotangent,
    doc_lengths,
    attn_gain,
    w_query,
    w_key,
    w_value,
    w_out,
    mlp_gain,
    w_gate,
    w_up,
    w_down,
):
    rows, stretch, width = tokens.shape
    count = rows * stretch
    key_width = w_key.shape[1]
    hidden_width = w_gate.shape[1]
    key_heads = key_width // HEAD_DIM
    heads = width // HEAD_DIM
    groups = heads // key_heads
    length = stretch * lax.axis_size("seq")
    block = math.gcd(length, 512)
    scale = HEAD_DIM ** (-0.5)
    table = jnp.asarray(rope_table(HEAD_DIM), jnp.float32)
    place = lax.axis_index("seq") * stretch + jnp.arange(stretch, dtype=jnp.int32)
    live_blocks = ((lax.axis_index("seq") + 1) * stretch + block - 1) // block
    ends = jnp.cumsum(doc_lengths, axis=1)
    first = jnp.max(
        jnp.where(ends[:, None, :] <= place[None, :, None], ends[:, None, :], 0), axis=2
    )
    angle = (place[None, :] - first).astype(jnp.float32)[..., None] * table
    cosine = jnp.concatenate([jnp.cos(angle), jnp.cos(angle)], axis=-1)[:, :, None, :]
    sine = jnp.concatenate([jnp.sin(angle), jnp.sin(angle)], axis=-1)[:, :, None, :]
    inputs = tokens.reshape(count, width).astype(jnp.float32)
    scale_one = norm_scale(inputs)
    normed_one = inputs * scale_one
    gain_piece = lax.all_gather(attn_gain, ("row", "seq"), axis=0, tiled=True)
    query_piece = lax.all_gather(w_query, ("row", "seq"), axis=0, tiled=True)
    key_piece = lax.all_gather(w_key, ("row", "seq"), axis=0, tiled=True)
    value_piece = lax.all_gather(w_value, ("row", "seq"), axis=0, tiled=True)
    hidden_piece = (normed_one * gain_piece.astype(jnp.float32)).astype(jnp.bfloat16)
    query_sum = jnp.dot(hidden_piece, query_piece, preferred_element_type=jnp.float32)
    key_sum = jnp.dot(hidden_piece, key_piece, preferred_element_type=jnp.float32)
    value_sum = jnp.dot(hidden_piece, value_piece, preferred_element_type=jnp.float32)
    hidden_one = hidden_piece
    queries = rotate(query_sum.reshape(rows, stretch, heads, HEAD_DIM), cosine, sine).astype(
        jnp.bfloat16
    )
    keys = rotate(key_sum.reshape(rows, stretch, key_heads, HEAD_DIM), cosine, sine).astype(
        jnp.bfloat16
    )
    values = value_sum.astype(jnp.bfloat16)
    query_grouped = queries.reshape(rows, stretch, key_heads, groups, HEAD_DIM)

    def gather_keys():
        return (
            lax.all_gather(keys.reshape(rows, stretch, key_width), "seq", axis=1, tiled=True),
            lax.all_gather(values.reshape(rows, stretch, key_width), "seq", axis=1, tiled=True),
        )

    key_all, value_all = gather_keys()

    def block_rows(source, index):
        return lax.dynamic_slice_in_dim(source, index * block, block, 1).reshape(
            rows, block, key_heads, HEAD_DIM
        )

    def block_scores(key_block, index):
        raw = jnp.einsum(
            "rqhgd,rkhd->rhgqk", query_grouped, key_block, preferred_element_type=jnp.float32
        )
        key_place = index * block + jnp.arange(block, dtype=jnp.int32)
        allowed = (key_place[None, None, :] <= place[None, :, None]) & (
            key_place[None, None, :] >= first[:, :, None]
        )
        return jnp.where(allowed[:, None, None], raw * scale, -1e30)

    def total_step(index, carry):
        running_max, running_total = carry
        scores = block_scores(block_rows(key_all, index), index)
        new_max = jnp.maximum(running_max, jnp.max(scores, axis=-1))
        new_total = running_total * jnp.exp(running_max - new_max) + jnp.sum(
            jnp.exp(scores - new_max[..., None]), axis=-1
        )
        return (new_max, new_total)

    stat_shape = (rows, key_heads, groups, stretch)
    running_max, running_total = lax.fori_loop(
        0,
        live_blocks,
        total_step,
        (jnp.full(stat_shape, -1e30, jnp.float32), jnp.zeros(stat_shape, jnp.float32)),
    )
    log_total = running_max + jnp.log(running_total)

    def mix_step(index, mixed_sum):
        probs = jnp.exp(block_scores(block_rows(key_all, index), index) - log_total[..., None])
        return mixed_sum + jnp.einsum(
            "rhgqk,rkhd->rqhgd",
            probs.astype(jnp.bfloat16),
            block_rows(value_all, index),
            preferred_element_type=jnp.float32,
        )

    mixed_sum = lax.fori_loop(
        0,
        live_blocks,
        mix_step,
        jnp.zeros((rows, stretch, key_heads, groups, HEAD_DIM), jnp.float32),
    )
    mixed = mixed_sum.reshape(count, width).astype(jnp.bfloat16)
    attn_branch = jnp.dot(
        mixed,
        lax.all_gather(w_out, ("row", "seq"), axis=0, tiled=True),
        preferred_element_type=jnp.float32,
    )
    middle = inputs + attn_branch
    scale_two = norm_scale(middle)
    normed_two = middle * scale_two
    gain_piece = lax.all_gather(mlp_gain, ("row", "seq"), axis=0, tiled=True)
    gate_piece = lax.all_gather(w_gate, ("row", "seq"), axis=0, tiled=True)
    up_piece = lax.all_gather(w_up, ("row", "seq"), axis=0, tiled=True)
    hidden_piece = (normed_two * gain_piece.astype(jnp.float32)).astype(jnp.bfloat16)
    gate_sum, up_sum, hidden_two = (
        jnp.dot(hidden_piece, gate_piece, preferred_element_type=jnp.float32),
        jnp.dot(hidden_piece, up_piece, preferred_element_type=jnp.float32),
        hidden_piece,
    )
    sigma = jax.nn.sigmoid(gate_sum)
    silu_value = gate_sum * sigma
    active = (silu_value * up_sum).astype(jnp.bfloat16)
    mlp_branch = jnp.dot(
        active,
        lax.all_gather(w_down, ("row", "seq"), axis=0, tiled=True),
        preferred_element_type=jnp.float32,
    )
    output = (middle + mlp_branch).astype(jnp.bfloat16).reshape(rows, stretch, width)
    grad_out_low = cotangent.reshape(count, width)
    grad_active = contract_last(
        grad_out_low, lax.all_gather(w_down, ("row", "seq"), axis=0, tiled=True)
    )
    grad_down = lax.psum_scatter(
        contract_first(active, grad_out_low), ("row", "seq"), scatter_dimension=0, tiled=True
    )
    grad_up_low = (grad_active * silu_value).astype(jnp.bfloat16)
    grad_gate_low = (grad_active * up_sum * sigma * (1.0 + gate_sum * (1.0 - sigma))).astype(
        jnp.bfloat16
    )
    both_grads = jnp.concatenate([grad_gate_low, grad_up_low], axis=1)
    gain_piece = lax.all_gather(mlp_gain, ("row", "seq"), axis=0, tiled=True)
    gate_piece = lax.all_gather(w_gate, ("row", "seq"), axis=0, tiled=True)
    up_piece = lax.all_gather(w_up, ("row", "seq"), axis=0, tiled=True)
    grad_piece = contract_last(grad_gate_low, gate_piece) + contract_last(grad_up_low, up_piece)
    normed_piece = normed_two
    grad_normed_two = grad_piece * gain_piece.astype(jnp.float32)
    grad_gain_two = jnp.sum(normed_piece * grad_piece, axis=0)
    grad_gate_up = lax.psum_scatter(
        contract_first(hidden_two, both_grads), ("row", "seq"), scatter_dimension=0, tiled=True
    )
    grad_gate = grad_gate_up[:, :hidden_width]
    grad_up = grad_gate_up[:, hidden_width:]
    grad_middle = grad_out_low.astype(jnp.float32) + norm_back(
        grad_normed_two, normed_two, scale_two
    )
    grad_branch_low = grad_middle.astype(jnp.bfloat16)
    grad_mixed = contract_last(
        grad_branch_low, lax.all_gather(w_out, ("row", "seq"), axis=0, tiled=True)
    ).astype(jnp.bfloat16)
    grad_out = lax.psum_scatter(
        contract_first(mixed, grad_branch_low), ("row", "seq"), scatter_dimension=0, tiled=True
    )
    grad_grouped = grad_mixed.reshape(rows, stretch, key_heads, groups, HEAD_DIM)
    key_back, value_back = gather_keys()

    def delta_step(index, total):
        probs = jnp.exp(block_scores(block_rows(key_back, index), index) - log_total[..., None])
        grad_probs = jnp.einsum(
            "rqhgd,rkhd->rhgqk",
            grad_grouped,
            block_rows(value_back, index),
            preferred_element_type=jnp.float32,
        )
        return total + jnp.sum(probs * grad_probs, axis=-1)

    delta = lax.fori_loop(0, live_blocks, delta_step, jnp.zeros(stat_shape, jnp.float32))

    def grad_step(index, carry):
        grad_queries, grad_key_all, grad_value_all = carry
        key_block = block_rows(key_back, index)
        probs = jnp.exp(block_scores(key_block, index) - log_total[..., None])
        grad_probs = jnp.einsum(
            "rqhgd,rkhd->rhgqk",
            grad_grouped,
            block_rows(value_back, index),
            preferred_element_type=jnp.float32,
        )
        grad_raw = (scale * probs * (grad_probs - delta[..., None])).astype(jnp.bfloat16)
        grad_queries = grad_queries + jnp.einsum(
            "rhgqk,rkhd->rqhgd", grad_raw, key_block, preferred_element_type=jnp.float32
        )
        key_part = jnp.einsum(
            "rhgqk,rqhgd->rkhd", grad_raw, query_grouped, preferred_element_type=jnp.float32
        ).reshape(rows, block, key_width)
        value_part = jnp.einsum(
            "rhgqk,rqhgd->rkhd",
            probs.astype(jnp.bfloat16),
            grad_grouped,
            preferred_element_type=jnp.float32,
        ).reshape(rows, block, key_width)
        return (
            grad_queries,
            lax.dynamic_update_slice_in_dim(grad_key_all, key_part, index * block, 1),
            lax.dynamic_update_slice_in_dim(grad_value_all, value_part, index * block, 1),
        )

    grad_queries, grad_key_all, grad_value_all = lax.fori_loop(
        0,
        live_blocks,
        grad_step,
        (
            jnp.zeros((rows, stretch, key_heads, groups, HEAD_DIM), jnp.float32),
            jnp.zeros((rows, length, key_width), jnp.float32),
            jnp.zeros((rows, length, key_width), jnp.float32),
        ),
    )
    grad_key_sum, grad_value_sum = (
        lax.psum_scatter(
            grad_key_all.astype(jnp.bfloat16), "seq", scatter_dimension=1, tiled=True
        ).astype(jnp.float32),
        lax.psum_scatter(
            grad_value_all.astype(jnp.bfloat16), "seq", scatter_dimension=1, tiled=True
        ).astype(jnp.float32),
    )
    grad_query_low = (
        rotate_back(grad_queries.reshape(rows, stretch, heads, HEAD_DIM), cosine, sine)
        .reshape(count, width)
        .astype(jnp.bfloat16)
    )
    grad_key_low = (
        rotate_back(grad_key_sum.reshape(rows, stretch, key_heads, HEAD_DIM), cosine, sine)
        .reshape(count, key_width)
        .astype(jnp.bfloat16)
    )
    grad_value_low = grad_value_sum.reshape(count, key_width).astype(jnp.bfloat16)
    gain_piece = lax.all_gather(attn_gain, ("row", "seq"), axis=0, tiled=True)
    query_piece = lax.all_gather(w_query, ("row", "seq"), axis=0, tiled=True)
    key_piece = lax.all_gather(w_key, ("row", "seq"), axis=0, tiled=True)
    value_piece = lax.all_gather(w_value, ("row", "seq"), axis=0, tiled=True)
    grad_piece = (
        contract_last(grad_query_low, query_piece)
        + contract_last(grad_key_low, key_piece)
        + contract_last(grad_value_low, value_piece)
    )
    normed_piece = normed_one
    grad_normed_one = grad_piece * gain_piece.astype(jnp.float32)
    grad_gain_one = jnp.sum(normed_piece * grad_piece, axis=0)
    grad_query, grad_key, grad_value, grad_attn_gain, grad_mlp_gain = (
        lax.psum_scatter(
            contract_first(hidden_one, grad_query_low),
            ("row", "seq"),
            scatter_dimension=0,
            tiled=True,
        ),
        lax.psum_scatter(
            contract_first(hidden_one, grad_key_low),
            ("row", "seq"),
            scatter_dimension=0,
            tiled=True,
        ),
        lax.psum_scatter(
            contract_first(hidden_one, grad_value_low),
            ("row", "seq"),
            scatter_dimension=0,
            tiled=True,
        ),
        lax.psum_scatter(grad_gain_one, ("row", "seq"), scatter_dimension=0, tiled=True),
        lax.psum_scatter(grad_gain_two, ("row", "seq"), scatter_dimension=0, tiled=True),
    )
    grad_tokens = (grad_middle + norm_back(grad_normed_one, normed_one, scale_one)).reshape(
        rows, stretch, width
    )
    return (
        output,
        grad_tokens,
        grad_attn_gain,
        grad_query,
        grad_key,
        grad_value,
        grad_out,
        grad_mlp_gain,
        grad_gate,
        grad_up,
        grad_down,
    )


MESH = pl.DeviceIdType.MESH
VMEM_LIMIT = 60 * 1024 * 1024


def neighbours():
    row, seq = lax.axis_index("row"), lax.axis_index("seq")
    row_size, seq_size = lax.axis_size("row"), lax.axis_size("seq")
    return dict(
        row=row,
        seq=seq,
        z=seq // 2,
        core=seq % 2,
        up=(row, (seq + 2) % seq_size),
        down=(row, (seq + seq_size - 2) % seq_size),
        pair=(row, seq + 1 - 2 * (seq % 2)),
        side=(row + 1 - 2 * (row % 2), seq),
        across=((row + row_size // 2) % row_size, seq),
        side_row=row + 1 - 2 * (row % 2),
        across_row=(row + row_size // 2) % row_size,
    )


def greet(peers):
    barrier = pltpu.get_barrier_semaphore()
    for peer in peers:
        pl.semaphore_signal(barrier, inc=1, device_id=peer, device_id_type=MESH)
    pl.semaphore_wait(barrier, len(peers))


def send(source, target, sems, index, peer):
    copy = pltpu.make_async_remote_copy(
        src_ref=source,
        dst_ref=target,
        send_sem=sems[0].at[index],
        recv_sem=sems[1].at[index],
        device_id=peer,
        device_id_type=MESH,
    )
    copy.start()
    return copy


def sem_pairs(amount):
    return [pltpu.SemaphoreType.DMA((amount,)), pltpu.SemaphoreType.DMA((amount,))]


def by_rows(amount, step, body):
    def one(i, carry):
        body(pl.ds(pl.multiple_of(i * step, step), step))
        return carry

    lax.fori_loop(0, amount // step, one, 0)


def copy_rows(target, source):
    def one(rows):
        target[rows] = source[rows]

    by_rows(source.shape[0], 16, one)


def gather_seq_steps(here, whole, stretch, pair_sems, ring_sems):
    seq, chips = here["seq"], lax.axis_size("seq") // 2
    seq_size = 2 * chips
    copies = []

    def spot(owner):
        return pl.ds(pl.multiple_of(owner * stretch, stretch), stretch)

    def ring(step):
        above = (seq + seq_size - 2 * step) % seq_size
        below = (seq + 2 * step) % seq_size
        up_view, down_view = whole.at[0, spot(above)], whole.at[1, spot(below)]
        moves = []
        if step < chips - 1:
            moves.append(send(up_view, up_view, ring_sems, 2 * step, here["up"]))
            moves.append(send(down_view, down_view, ring_sems, 2 * step + 1, here["down"]))
        if step == 0:
            own = whole.at[:, spot(seq)]
            copies.append(send(own, own, pair_sems, 0, here["pair"]))
        else:
            copies.append(send(up_view, up_view, pair_sems, 2 * step - 1, here["pair"]))
            copies.append(send(down_view, down_view, pair_sems, 2 * step, here["pair"]))
        return moves

    last = []

    def first_step():
        last.extend(ring(0))

    def next_step(step):
        def run():
            for copy in last:
                copy.wait()
            del last[:]
            last.extend(ring(step))

        return run

    def finish():
        for copy in copies:
            copy.wait()

    return [first_step] + [next_step(step) for step in range(1, chips)] + [finish]


def reduce_seq_steps(here, part, stretch, pair_in, total, ring_in, pair_sems, ring_sems, done):
    z, core, chips = here["z"], here["core"], lax.axis_size("seq") // 2
    order = [chips - 1, 1] + list(range(2, chips - 1)) + [0]
    copies, pair_copies = [], {}

    def spot(chip, side):
        return pl.ds(pl.multiple_of((2 * chip + side) * stretch, stretch), stretch)

    def pair_start():
        for index, far in enumerate(order):
            chip = (z + far) % chips
            pair_copies[far] = send(
                part.at[:, spot(chip, 1 - core)], pair_in.at[chip], pair_sems, index, here["pair"]
            )

    def pair_sum(far):
        chip = (z + far) % chips
        pair_copies[far].wait_recv()
        base = (2 * chip + core) * stretch

        for half in range(2):
            def add(rows):
                mine = part[half, pl.ds(pl.multiple_of(base + rows.start, 16), 16)]
                other = pair_in[chip, half, rows]
                total[chip, half, rows] = (
                    mine.astype(jnp.float32) + other.astype(jnp.float32)
                ).astype(jnp.bfloat16)

            by_rows(stretch, 16, add)

    last = {}

    def ring_send(step):
        for half, peer, chip in (
            (0, here["up"], (z + 2 * chips - 1 - step) % chips),
            (1, here["down"], (z + 1 + step) % chips),
        ):
            if step > 0:
                last[half].wait_recv()
                arrived = ring_in.at[step - 1, half]

                def add(rows):
                    total[chip, half, rows] = (
                        total[chip, half, rows].astype(jnp.float32)
                        + arrived[rows].astype(jnp.float32)
                    ).astype(jnp.bfloat16)

                by_rows(stretch, 16, add)
            last[half] = send(
                total.at[chip, half], ring_in.at[step, half], ring_sems, 2 * step + half, peer
            )
            copies.append(last[half])

    def first_step():
        pair_start()
        pair_sum(chips - 1)
        pair_sum(1)
        ring_send(0)
        for far in order[2:]:
            pair_sum(far)

    def next_step(step):
        def run():
            ring_send(step)

        return run

    def finish():
        for half in range(2):
            last[half].wait_recv()
            arrived = ring_in.at[chips - 2, half]

            def close(rows):
                done(
                    half,
                    rows,
                    total[z, half, rows].astype(jnp.float32) + arrived[rows].astype(jnp.float32),
                )

            by_rows(stretch, 16, close)

    def drain():
        for copy in list(pair_copies.values()) + copies:
            copy.wait_send()

    return [first_step] + [next_step(step) for step in range(1, chips - 1)] + [finish], drain


def gather_row_steps(here, own, whole, sems):
    half = whole.shape[1] // 2
    row, side, across = here["row"], here["side_row"], here["across_row"]
    state = []

    def first_step():
        state.append(send(own, whole.at[row], sems, 0, here["side"]))
        state.append(send(own, whole.at[row], sems, 1, here["across"]))

    def second_step():
        low, high = pl.ds(0, half), pl.ds(half, half)
        state[0].wait_recv()
        state.append(send(whole.at[side, low], whole.at[side, low], sems, 2, here["across"]))
        state[1].wait_recv()
        state.append(send(whole.at[across, high], whole.at[across, high], sems, 3, here["side"]))

    def finish():
        for copy in state[2:]:
            copy.wait_recv()
        for copy in state:
            copy.wait_send()

    return [first_step, second_step, finish]


def reduce_row_steps(here, part, inbox, sums, sems, done):
    half = part.shape[1] // 2
    row, side, across = here["row"], here["side_row"], here["across_row"]
    corner = (side + 2) % 4
    state = []

    def first_step():
        low, high = pl.ds(0, half), pl.ds(half, half)
        for index, (owner, rows, peer) in enumerate(
            (
                (corner, low, "side"),
                (corner, high, "across"),
                (side, low, "side"),
                (across, high, "across"),
            )
        ):
            state.append(send(part.at[owner, rows], inbox.at[index], sems, index, here[peer]))

    def add(owner, offset, index):
        def run(rows):
            spot = pl.ds(pl.multiple_of(offset + rows.start, 16), 16)
            sums[index, rows] = (
                part[owner, spot].astype(jnp.float32) + inbox[index, rows].astype(jnp.float32)
            ).astype(jnp.bfloat16)

        by_rows(half, 16, run)

    def second_step():
        state[0].wait_recv()
        add(across, 0, 0)
        state.append(send(sums.at[0], inbox.at[4], sems, 4, here["across"]))
        state[1].wait_recv()
        add(side, half, 1)
        state.append(send(sums.at[1], inbox.at[5], sems, 5, here["side"]))
        state[2].wait_recv()
        state[3].wait_recv()

    def finish():
        for offset, one, two in ((0, 2, 4), (half, 3, 5)):
            state[two].wait_recv()

            def close(rows):
                spot = pl.ds(pl.multiple_of(offset + rows.start, 16), 16)
                done(
                    spot,
                    part[row, spot].astype(jnp.float32)
                    + inbox[one, rows].astype(jnp.float32)
                    + inbox[two, rows].astype(jnp.float32),
                )

            by_rows(half, 16, close)
        for copy in state:
            copy.wait_send()

    return [first_step, second_step, finish]


def exchange_seq(here, source, target_of, sems):
    seq, seq_size = here["seq"], lax.axis_size("seq")
    copies = []
    for far in range(1, seq_size):
        dest = (seq + far) % seq_size
        copies.append(
            send(source.at[dest], target_of(seq), sems, far - 1, (here["row"], dest))
        )
    return copies


def seq_peers(here):
    seq_size = lax.axis_size("seq")
    return [(here["row"], (here["seq"] + far) % seq_size) for far in range(1, seq_size)]


def call(kernel, args, out_shape, scratch, collective_id):
    in_vmem = pl.BlockSpec(memory_space=pltpu.VMEM)
    return pl.pallas_call(
        kernel,
        out_shape=out_shape,
        in_specs=[in_vmem] * len(args),
        out_specs=[in_vmem] * len(out_shape),
        scratch_shapes=scratch,
        compiler_params=pltpu.CompilerParams(
            collective_id=collective_id, has_side_effects=True, vmem_limit_bytes=VMEM_LIMIT
        ),
    )(*args)


def low(*shape):
    return jax.ShapeDtypeStruct(shape, jnp.bfloat16)


def full(*shape):
    return jax.ShapeDtypeStruct(shape, jnp.float32)


def open_kernel(
    tokens, heads_pack, units_pack, out_piece, down_piece,
    all_tokens, heads_all, units_mine, out_all, down_all,
    pair_a, pair_b, ring_a, ring_b, heads_a, heads_b, units_a, units_b,
    row_a, row_b, out_a, out_b, down_a, down_b,
):
    here = neighbours()
    seq, row = here["seq"], here["row"]
    stretch = tokens.shape[1]
    piece = heads_pack.shape[1]
    greet(seq_peers(here) + [here["side"], here["across"]])

    def spot(owner):
        return pl.ds(pl.multiple_of(owner * piece, piece), piece)

    for half in range(2):
        own = pl.ds(pl.multiple_of(seq * stretch, stretch), stretch)
        copy_rows(all_tokens.at[half, own], tokens.at[half])
    heads = exchange_seq(here, heads_pack, lambda s: heads_all.at[row, spot(s)], (heads_a, heads_b))
    gather_down = gather_row_steps(here, down_piece, down_all, (down_a, down_b))
    gather_out = gather_row_steps(here, out_piece, out_all, (out_a, out_b))
    steps = gather_seq_steps(here, all_tokens, stretch, (pair_a, pair_b), (ring_a, ring_b))
    steps[0]()
    gather_out[0]()
    units = exchange_seq(here, units_pack, lambda s: units_mine.at[spot(s)], (units_a, units_b))
    copy_rows(heads_all.at[row, spot(seq)], heads_pack.at[seq])
    copy_rows(units_mine.at[spot(seq)], units_pack.at[seq])
    copy_rows(out_all.at[row], out_piece)
    copy_rows(down_all.at[row], down_piece)
    for copy in heads:
        copy.wait_recv()
    gather_heads = gather_row_steps(here, heads_all.at[row], heads_all, (row_a, row_b))
    gather_heads[0]()
    gather_out[1]()
    gather_down[0]()
    steps[1]()
    gather_heads[1]()
    steps[2]()
    gather_down[1]()
    for step in steps[3:]:
        step()
    gather_heads[2]()
    gather_out[2]()
    gather_down[2]()
    for copy in heads:
        copy.wait_send()
    for copy in units:
        copy.wait()


def middle_kernel(
    branch, tokens, gain, units_mine,
    middle, hidden, units_all,
    pair_in, total, ring_in, pair_a, pair_b, ring_a, ring_b,
    gpair_a, gpair_b, gring_a, gring_b, row_a, row_b,
):
    here = neighbours()
    seq = here["seq"]
    stretch = tokens.shape[1]
    greet([here["up"], here["down"], here["pair"], here["side"], here["across"]])

    def done(half, rows, value):
        value = tokens[half, rows].astype(jnp.float32) + value
        middle[half, rows] = value
        normed = value * norm_scale(value)
        spot = pl.ds(pl.multiple_of(seq * stretch + rows.start, 16), 16)
        hidden[half, spot] = (normed * gain[...]).astype(jnp.bfloat16)

    copy_rows(units_all.at[here["row"]], units_mine)
    reduce_steps, drain = reduce_seq_steps(
        here, branch, stretch, pair_in, total, ring_in, (pair_a, pair_b), (ring_a, ring_b), done
    )
    units = gather_row_steps(here, units_mine, units_all, (row_a, row_b))
    units[0]()
    for step in reduce_steps:
        step()
    gather_steps = gather_seq_steps(here, hidden, stretch, (gpair_a, gpair_b), (gring_a, gring_b))
    gather_steps[0]()
    gather_steps[1]()
    units[1]()
    for step in gather_steps[2:]:
        step()
    units[2]()
    drain()


def back_kernel(
    grad_part, cotangent, middle, gain, units_part,
    grad_middle, grad_low, gain_grad, units_out,
    pair_in, total, ring_in, inbox, sums, pair_a, pair_b, ring_a, ring_b,
    gpair_a, gpair_b, gring_a, gring_b, row_a, row_b,
):
    here = neighbours()
    seq = here["seq"]
    stretch = cotangent.shape[1]
    greet([here["up"], here["down"], here["pair"], here["side"], here["across"]])
    gain_grad[...] = jnp.zeros_like(gain_grad)

    def done(half, rows, grad):
        value = middle[half, rows]
        scale = norm_scale(value)
        normed = value * scale
        gain_grad[...] += jnp.sum(normed * grad, axis=0, keepdims=True)
        back = cotangent[half, rows].astype(jnp.float32) + norm_back(
            grad * gain[...], normed, scale
        )
        grad_middle[half, rows] = back
        spot = pl.ds(pl.multiple_of(seq * stretch + rows.start, 16), 16)
        grad_low[half, spot] = back.astype(jnp.bfloat16)

    def done_units(rows, value):
        units_out[rows] = value.astype(jnp.bfloat16)

    reduce_steps, drain = reduce_seq_steps(
        here, grad_part, stretch, pair_in, total, ring_in, (pair_a, pair_b), (ring_a, ring_b), done
    )
    units = reduce_row_steps(here, units_part, inbox, sums, (row_a, row_b), done_units)
    units[0]()
    for step in reduce_steps:
        step()
    gather_steps = gather_seq_steps(here, grad_low, stretch, (gpair_a, gpair_b), (gring_a, gring_b))
    gather_steps[0]()
    units[1]()
    for step in gather_steps[1:]:
        step()
    units[2]()
    drain()


def sum_small(here, mine, inbox, sems):
    chips = lax.axis_size("seq") // 2
    slot = 0
    stages = [[here["pair"]]]
    stages.append(
        [(here["row"], (here["seq"] + 2 * far) % (2 * chips)) for far in range(1, chips)]
    )
    stages += [[here["side"]], [here["across"]]]
    copies = []
    for number, stage in enumerate(stages):
        sent = [
            send(mine.at[number], inbox.at[slot + i], sems, slot + i, peer)
            for i, peer in enumerate(stage)
        ]
        value = mine[number]
        for i, copy in enumerate(sent):
            copy.wait_recv()
            value = value + inbox[slot + i]
        mine[number + 1] = value
        slot += len(stage)
        copies += sent
    for copy in copies:
        copy.wait_send()
    return slot


def close_kernel(
    grad_part, tokens, grad_middle, gain, gain_two, heads_part,
    grad_tokens, gain_sums, heads_out,
    heads_mine, pair_in, total, ring_in, inbox, sums, small, small_in,
    pair_a, pair_b, ring_a, ring_b, row_a, row_b, heads_a, heads_b, small_a, small_b,
):
    here = neighbours()
    seq, chips = here["seq"], lax.axis_size("seq") // 2
    stretch = tokens.shape[1]
    greet(seq_peers(here) + [here["side"], here["across"]])
    small[0, 0:1] = jnp.zeros_like(small[0, 0:1])
    small[0, 1:2] = gain_two[...]

    def done(half, rows, grad):
        value = tokens[half, rows].astype(jnp.float32)
        scale = norm_scale(value)
        normed = value * scale
        small[0, 0:1] += jnp.sum(normed * grad, axis=0, keepdims=True)
        grad_tokens[half, rows] = grad_middle[half, rows] + norm_back(
            grad * gain[...], normed, scale
        )

    piece = heads_out.shape[1]

    def done_heads(rows, value):
        heads_mine[rows] = value.astype(jnp.bfloat16)

    reduce_steps, drain = reduce_seq_steps(
        here, grad_part, stretch, pair_in, total, ring_in, (pair_a, pair_b), (ring_a, ring_b), done
    )
    heads = reduce_row_steps(here, heads_part, inbox, sums, (row_a, row_b), done_heads)
    heads[0]()
    reduce_steps[0]()
    heads[1]()
    heads[2]()

    copies = []
    for far in range(1, 2 * chips):
        dest = (seq + far) % (2 * chips)
        rows = pl.ds(pl.multiple_of(dest * piece, piece), piece)
        copies.append(
            send(
                heads_mine.at[rows], heads_out.at[seq], (heads_a, heads_b), far - 1,
                (here["row"], dest),
            )
        )
    copy_rows(heads_out.at[seq], heads_mine.at[pl.ds(pl.multiple_of(seq * piece, piece), piece)])
    for step in reduce_steps[1:]:
        step()
    sum_small(here, small, small_in, (small_a, small_b))
    gain_sums[...] = small[4]
    for copy in copies:
        copy.wait()
    drain()


def seq_scratch(chips, stretch, width):
    return [
        pltpu.VMEM((chips, 2, stretch, width), jnp.bfloat16),
        pltpu.VMEM((chips, 2, stretch, width), jnp.bfloat16),
        pltpu.VMEM((chips - 1, 2, stretch, width), jnp.bfloat16),
    ]


def row_scratch(pieces, columns):
    return [
        pltpu.VMEM((6, pieces // 2, columns), jnp.bfloat16),
        pltpu.VMEM((2, pieces // 2, columns), jnp.bfloat16),
    ]


def unpack_units(grads, row_size):
    seq_size, rows, columns = grads.shape
    block = columns // 2 // row_size

    def kernel(gate, up, gate_out, up_out):
        for source, target in ((gate, gate_out), (up, up_out)):
            for s in range(seq_size):
                target[:, s * block : (s + 1) * block] = source[s].astype(jnp.float32)

    whole = full(rows, seq_size * columns // 2)
    return pl.pallas_call(
        kernel,
        grid=(row_size,),
        out_shape=[whole, whole],
        in_specs=[
            pl.BlockSpec((seq_size, rows, block), lambda r: (0, 0, r)),
            pl.BlockSpec((seq_size, rows, block), lambda r: (0, 0, row_size + r)),
        ],
        out_specs=[pl.BlockSpec((rows, seq_size * block), lambda r: (0, r))] * 2,
    )(grads, grads)


def unpack_heads(grads, query_width, key_width):
    seq_size, rows, _ = grads.shape

    def kernel(source, query, key, value):
        start = 0
        for target, width in ((query, query_width), (key, key_width), (value, key_width)):
            target[...] = jnp.concatenate(
                [source[s, :, start : start + width].astype(jnp.float32) for s in range(seq_size)],
                axis=1,
            )
            start += width

    return pl.pallas_call(
        kernel,
        out_shape=[full(rows, seq_size * w) for w in (query_width, key_width, key_width)],
    )(grads)


BOTH = ("row", "seq")


def gather(piece, axis_name, axis):
    return lax.all_gather(piece, axis_name, axis=axis, tiled=True)


def scatter(whole, axis_name, axis):
    return lax.psum_scatter(whole, axis_name, scatter_dimension=axis, tiled=True)


def sharded_layer(
    tokens,
    cotangent,
    doc_lengths,
    attn_gain,
    w_query,
    w_key,
    w_value,
    w_out,
    mlp_gain,
    w_gate,
    w_up,
    w_down,
):
    row_size, seq_size = lax.axis_size("row"), lax.axis_size("seq")
    rows, stretch, width = tokens.shape
    length = stretch * seq_size
    count = rows * length
    piece_rows = w_query.shape[0]
    key_heads = w_key.shape[1] // HEAD_DIM // seq_size
    heads = w_query.shape[1] // HEAD_DIM // seq_size
    groups = heads // key_heads
    query_width, key_width = heads * HEAD_DIM, key_heads * HEAD_DIM
    unit_block = w_down.shape[0]
    units = unit_block * row_size
    scale = HEAD_DIM ** (-0.5)

    place = jnp.arange(length, dtype=jnp.int32)
    ends = jnp.cumsum(doc_lengths, axis=1)
    first = jnp.max(
        jnp.where(ends[:, None, :] <= place[None, :, None], ends[:, None, :], 0), axis=2
    )
    table = jnp.asarray(rope_table(HEAD_DIM), jnp.float32)
    angle = (place[None, :] - first).astype(jnp.float32)[..., None] * table
    cosine = jnp.concatenate([jnp.cos(angle), jnp.cos(angle)], axis=-1)[:, :, None, :]
    sine = jnp.concatenate([jnp.sin(angle), jnp.sin(angle)], axis=-1)[:, :, None, :]

    def unit_columns(weight):
        split = weight.reshape(piece_rows, row_size, seq_size, unit_block)
        return split.transpose(2, 0, 1, 3).reshape(seq_size, piece_rows, units)

    total = row_size * seq_size
    shift = [(i, (i % row_size) * seq_size + i // row_size) for i in range(total)]
    shift_back = [(b, a) for a, b in shift]

    def head_columns(weight, columns):
        return weight.reshape(piece_rows, seq_size, columns).transpose(1, 0, 2)

    head_width = query_width + 2 * key_width
    spare = -(head_width + 2) % 128
    gain_columns = jnp.stack([attn_gain, mlp_gain], axis=1)
    gain_columns = jnp.pad(gain_columns, ((0, 0), (0, spare)))
    heads_pack = jnp.concatenate(
        [
            head_columns(w_query, query_width),
            head_columns(w_key, key_width),
            head_columns(w_value, key_width),
            jnp.broadcast_to(gain_columns, (seq_size, piece_rows, spare + 2)),
        ],
        axis=2,
    )
    units_pack = jnp.concatenate([unit_columns(w_gate), unit_columns(w_up)], axis=2)
    pack_width = head_width + 2 + spare
    chips = seq_size // 2
    pieces = piece_rows * seq_size
    all_tokens, heads_all, units_mine, out_part, down_part = call(
        open_kernel,
        (tokens, heads_pack, units_pack, lax.ppermute(w_out, BOTH, shift), w_down),
        [
            low(rows, length, width),
            low(row_size, pieces, pack_width),
            low(pieces, 2 * units),
            low(row_size, piece_rows, width),
            low(row_size, unit_block, width),
        ],
        sem_pairs(2 * chips - 1)
        + sem_pairs(2 * chips - 2)
        + sem_pairs(seq_size - 1) * 2
        + sem_pairs(4) * 3,
        0,
    )
    all_tokens = all_tokens.reshape(count, width)
    heads_all = heads_all.reshape(width, pack_width)
    w_qkv = heads_all[:, :head_width]
    gains = heads_all[:, head_width : head_width + 2].astype(jnp.float32).T
    out_part = out_part.reshape(query_width, width)
    down_part = down_part.reshape(units, width)
    late_cotangent, all_tokens = lax.optimization_barrier((cotangent, all_tokens))
    all_cotangent = gather(late_cotangent, "seq", 1).reshape(count, width)

    inputs = all_tokens.astype(jnp.float32)
    hidden_one = (inputs * norm_scale(inputs) * gains[0]).astype(jnp.bfloat16)
    qkv = jnp.dot(hidden_one, w_qkv, preferred_element_type=jnp.float32)
    queries = rotate(
        qkv[:, :query_width].reshape(rows, length, heads, HEAD_DIM), cosine, sine
    ).astype(jnp.bfloat16).reshape(rows, length, key_heads, groups, HEAD_DIM)
    keys = rotate(
        qkv[:, query_width : query_width + key_width].reshape(rows, length, key_heads, HEAD_DIM),
        cosine,
        sine,
    ).astype(jnp.bfloat16)
    values = (
        qkv[:, query_width + key_width :]
        .astype(jnp.bfloat16)
        .reshape(rows, length, key_heads, HEAD_DIM)
    )
    raw = jnp.einsum("rqhgd,rkhd->rhgqk", queries, keys, preferred_element_type=jnp.float32)
    allowed = (place[None, None, :] <= place[None, :, None]) & (
        place[None, None, :] >= first[:, :, None]
    )
    probs = jax.nn.softmax(jnp.where(allowed[:, None, None], raw * scale, -1e30), axis=-1)
    probs_low = probs.astype(jnp.bfloat16)
    mixed = (
        jnp.einsum("rhgqk,rkhd->rqhgd", probs_low, values, preferred_element_type=jnp.float32)
        .astype(jnp.bfloat16)
        .reshape(count, query_width)
    )
    branch = jnp.dot(mixed, out_part, preferred_element_type=jnp.float32).astype(jnp.bfloat16)
    middle, hidden_two, w_units = call(
        middle_kernel,
        (branch.reshape(rows, length, width), tokens, gains[1:2], units_mine),
        [full(rows, stretch, width), low(rows, length, width), low(row_size, pieces, 2 * units)],
        seq_scratch(chips, stretch, width)
        + sem_pairs(chips)
        + sem_pairs(2 * chips - 2)
        + sem_pairs(2 * chips - 1)
        + sem_pairs(2 * chips - 2)
        + sem_pairs(4),
        1,
    )
    hidden_two = hidden_two.reshape(count, width)
    w_units = w_units.reshape(width, 2 * units)
    both = jnp.dot(hidden_two, w_units, preferred_element_type=jnp.float32)
    gate_sum, up_sum = both[:, :units], both[:, units:]
    sigma = jax.nn.sigmoid(gate_sum)
    silu_value = gate_sum * sigma
    active = (silu_value * up_sum).astype(jnp.bfloat16)
    mlp_branch = jnp.dot(active, down_part, preferred_element_type=jnp.float32)
    mlp_branch, down_part = lax.optimization_barrier((mlp_branch.astype(jnp.bfloat16), down_part))
    mlp_branch = scatter(mlp_branch.reshape(rows, length, width), "seq", 1)
    output = (middle + mlp_branch.astype(jnp.float32)).astype(jnp.bfloat16)

    grad_active = contract_last(all_cotangent, down_part)
    grad_down = contract_first(active, all_cotangent).astype(jnp.bfloat16)
    grad_up_low = (grad_active * silu_value).astype(jnp.bfloat16)
    grad_gate_low = (grad_active * up_sum * sigma * (1.0 + gate_sum * (1.0 - sigma))).astype(
        jnp.bfloat16
    )
    both_grads = jnp.concatenate([grad_gate_low, grad_up_low], axis=1)
    grad_hidden = contract_last(both_grads, w_units).astype(jnp.bfloat16)
    grad_units = contract_first(hidden_two, both_grads).astype(jnp.bfloat16)
    grad_hidden, mlp_branch, grad_down = lax.optimization_barrier(
        (grad_hidden, mlp_branch, grad_down)
    )
    grad_middle, grad_branch, grad_gain_two, units_mine = call(
        back_kernel,
        (
            grad_hidden.reshape(rows, length, width),
            cotangent,
            middle,
            gains[1:2],
            grad_units.reshape(row_size, pieces, 2 * units),
        ),
        [
            full(rows, stretch, width),
            low(rows, length, width),
            full(1, width),
            low(pieces, 2 * units),
        ],
        seq_scratch(chips, stretch, width)
        + row_scratch(pieces, 2 * units)
        + sem_pairs(chips)
        + sem_pairs(2 * chips - 2)
        + sem_pairs(2 * chips - 1)
        + sem_pairs(2 * chips - 2)
        + sem_pairs(6),
        2,
    )
    grad_branch, grad_down = lax.optimization_barrier((grad_branch, grad_down))
    grad_down = scatter(grad_down, "row", 0)
    grad_units = lax.all_to_all(
        units_mine.reshape(seq_size, piece_rows, 2 * units), "seq", 0, 0, tiled=True
    )
    grad_branch = grad_branch.reshape(count, width)
    grad_mixed = contract_last(grad_branch, out_part).astype(jnp.bfloat16)
    grad_out = scatter(contract_first(mixed, grad_branch).astype(jnp.bfloat16), "row", 0)
    grad_out = lax.ppermute(grad_out, BOTH, shift_back).astype(jnp.float32)
    grad_grouped = grad_mixed.reshape(rows, length, key_heads, groups, HEAD_DIM)
    grad_probs = jnp.einsum(
        "rqhgd,rkhd->rhgqk", grad_grouped, values, preferred_element_type=jnp.float32
    )
    delta = jnp.sum(probs * grad_probs, axis=-1, keepdims=True)
    grad_raw = (scale * probs * (grad_probs - delta)).astype(jnp.bfloat16)
    grad_queries = jnp.einsum(
        "rhgqk,rkhd->rqhgd", grad_raw, keys, preferred_element_type=jnp.float32
    )
    grad_keys = jnp.einsum(
        "rhgqk,rqhgd->rkhd", grad_raw, queries, preferred_element_type=jnp.float32
    )
    grad_values = jnp.einsum(
        "rhgqk,rqhgd->rkhd", probs_low, grad_grouped, preferred_element_type=jnp.float32
    )
    grad_qkv_low = jnp.concatenate(
        [
            rotate_back(grad_queries.reshape(rows, length, heads, HEAD_DIM), cosine, sine).reshape(
                count, query_width
            ),
            rotate_back(grad_keys, cosine, sine).reshape(count, key_width),
            grad_values.reshape(count, key_width),
        ],
        axis=1,
    ).astype(jnp.bfloat16)
    grad_qkv = contract_first(hidden_one, grad_qkv_low).astype(jnp.bfloat16)
    grad_hidden = contract_last(grad_qkv_low, w_qkv).astype(jnp.bfloat16)
    grad_tokens, gain_sums, grad_qkv = call(
        close_kernel,
        (
            grad_hidden.reshape(rows, length, width),
            tokens,
            grad_middle,
            gains[0:1],
            grad_gain_two,
            grad_qkv.reshape(row_size, pieces, head_width),
        ),
        [
            full(rows, stretch, width),
            full(2, width),
            low(seq_size, piece_rows, head_width),
        ],
        [pltpu.VMEM((pieces, head_width), jnp.bfloat16)]
        + seq_scratch(chips, stretch, width)
        + row_scratch(pieces, head_width)
        + [pltpu.VMEM((5, 2, width), jnp.float32), pltpu.VMEM((chips + 2, 2, width), jnp.float32)]
        + sem_pairs(chips)
        + sem_pairs(2 * chips - 2)
        + sem_pairs(6)
        + sem_pairs(seq_size - 1)
        + sem_pairs(chips + 2),
        3,
    )

    grad_gate, grad_up = unpack_units(grad_units, row_size)
    grad_query, grad_key, grad_value = unpack_heads(grad_qkv, query_width, key_width)
    own = (lax.axis_index("row") * seq_size + lax.axis_index("seq")) * piece_rows
    grad_gains = lax.dynamic_slice_in_dim(gain_sums, own, piece_rows, 1)
    return (
        output,
        grad_tokens,
        grad_gains[0],
        grad_query,
        grad_key,
        grad_value,
        grad_out,
        grad_gains[1],
        grad_gate,
        grad_up,
        grad_down.astype(jnp.float32),
    )


def local(tokens, cotangent, doc_lengths, attn_gain, w_query, w_key, w_value, *rest):
    whole_heads = w_key.shape[1] % (HEAD_DIM * lax.axis_size("seq")) == 0
    layer = sharded_layer if whole_heads else gathered_layer
    return layer(tokens, cotangent, doc_lengths, attn_gain, w_query, w_key, w_value, *rest)


def solution(mesh):
    return jax.shard_map(
        local,
        mesh=mesh,
        in_specs=(
            P("row", "seq", None),
            P("row", "seq", None),
            P("row", None),
            P(("row", "seq")),
            P(("row", "seq"), None),
            P(("row", "seq"), None),
            P(("row", "seq"), None),
            P(("row", "seq"), None),
            P(("row", "seq")),
            P(("row", "seq"), None),
            P(("row", "seq"), None),
            P(("row", "seq"), None),
        ),
        out_specs=(
            P("row", "seq", None),
            P("row", "seq", None),
            P(("row", "seq")),
            P(("row", "seq"), None),
            P(("row", "seq"), None),
            P(("row", "seq"), None),
            P(("row", "seq"), None),
            P(("row", "seq")),
            P(("row", "seq"), None),
            P(("row", "seq"), None),
            P(("row", "seq"), None),
        ),
        check_vma=False,
    )
```

```python
import math

import jax
import jax.numpy as jnp
import numpy as np
from jax import lax
from jax.experimental import pallas as pl
from jax.experimental.pallas import tpu as pltpu
from jax.sharding import PartitionSpec as P

HEAD_DIM = 64


EPSILON = 1e-05
THETA = 500000.0


def rope_table(head_size):
    half_size = head_size // 2
    plain = THETA ** (-(np.arange(half_size) * 2.0) / head_size)
    factor, low_factor, high_factor, old_span = (32.0, 1.0, 4.0, 8192.0)
    wavelength = 2.0 * math.pi / plain
    smooth = (old_span / wavelength - low_factor) / (high_factor - low_factor)
    blended = (1.0 - smooth) * plain / factor + smooth * plain
    return np.where(
        wavelength < old_span / high_factor,
        plain,
        np.where(wavelength > old_span / low_factor, plain / factor, blended),
    )


def norm_scale(values):
    return lax.rsqrt(jnp.mean(values * values, axis=-1, keepdims=True) + EPSILON)


def norm_back(grad_normed, normed, scale):
    return scale * (grad_normed - normed * jnp.mean(grad_normed * normed, axis=-1, keepdims=True))


def rotate(values, cosine, sine):
    half_size = values.shape[-1] // 2
    turned = jnp.concatenate([-values[..., half_size:], values[..., :half_size]], axis=-1)
    return values * cosine + turned * sine


def rotate_back(grad, cosine, sine):
    half_size = grad.shape[-1] // 2
    turned = grad * sine
    return grad * cosine + jnp.concatenate(
        [turned[..., half_size:], -turned[..., :half_size]], axis=-1
    )


def contract_last(left, right):
    return lax.dot_general(
        left, right, (((1,), (1,)), ((), ())), preferred_element_type=jnp.float32
    )


def contract_first(left, right):
    return lax.dot_general(
        left, right, (((0,), (0,)), ((), ())), preferred_element_type=jnp.float32
    )


def gathered_layer(
    tokens,
    cotangent,
    doc_lengths,
    attn_gain,
    w_query,
    w_key,
    w_value,
    w_out,
    mlp_gain,
    w_gate,
    w_up,
    w_down,
):
    rows, stretch, width = tokens.shape
    count = rows * stretch
    key_width = w_key.shape[1]
    hidden_width = w_gate.shape[1]
    key_heads = key_width // HEAD_DIM
    heads = width // HEAD_DIM
    groups = heads // key_heads
    length = stretch * lax.axis_size("seq")
    block = math.gcd(length, 512)
    scale = HEAD_DIM ** (-0.5)
    table = jnp.asarray(rope_table(HEAD_DIM), jnp.float32)
    place = lax.axis_index("seq") * stretch + jnp.arange(stretch, dtype=jnp.int32)
    live_blocks = ((lax.axis_index("seq") + 1) * stretch + block - 1) // block
    ends = jnp.cumsum(doc_lengths, axis=1)
    first = jnp.max(
        jnp.where(ends[:, None, :] <= place[None, :, None], ends[:, None, :], 0), axis=2
    )
    angle = (place[None, :] - first).astype(jnp.float32)[..., None] * table
    cosine = jnp.concatenate([jnp.cos(angle), jnp.cos(angle)], axis=-1)[:, :, None, :]
    sine = jnp.concatenate([jnp.sin(angle), jnp.sin(angle)], axis=-1)[:, :, None, :]
    inputs = tokens.reshape(count, width).astype(jnp.float32)
    scale_one = norm_scale(inputs)
    normed_one = inputs * scale_one
    gain_piece = lax.all_gather(attn_gain, ("row", "seq"), axis=0, tiled=True)
    query_piece = lax.all_gather(w_query, ("row", "seq"), axis=0, tiled=True)
    key_piece = lax.all_gather(w_key, ("row", "seq"), axis=0, tiled=True)
    value_piece = lax.all_gather(w_value, ("row", "seq"), axis=0, tiled=True)
    hidden_piece = (normed_one * gain_piece.astype(jnp.float32)).astype(jnp.bfloat16)
    query_sum = jnp.dot(hidden_piece, query_piece, preferred_element_type=jnp.float32)
    key_sum = jnp.dot(hidden_piece, key_piece, preferred_element_type=jnp.float32)
    value_sum = jnp.dot(hidden_piece, value_piece, preferred_element_type=jnp.float32)
    hidden_one = hidden_piece
    queries = rotate(query_sum.reshape(rows, stretch, heads, HEAD_DIM), cosine, sine).astype(
        jnp.bfloat16
    )
    keys = rotate(key_sum.reshape(rows, stretch, key_heads, HEAD_DIM), cosine, sine).astype(
        jnp.bfloat16
    )
    values = value_sum.astype(jnp.bfloat16)
    query_grouped = queries.reshape(rows, stretch, key_heads, groups, HEAD_DIM)

    def gather_keys():
        return (
            lax.all_gather(keys.reshape(rows, stretch, key_width), "seq", axis=1, tiled=True),
            lax.all_gather(values.reshape(rows, stretch, key_width), "seq", axis=1, tiled=True),
        )

    key_all, value_all = gather_keys()

    def block_rows(source, index):
        return lax.dynamic_slice_in_dim(source, index * block, block, 1).reshape(
            rows, block, key_heads, HEAD_DIM
        )

    def block_scores(key_block, index):
        raw = jnp.einsum(
            "rqhgd,rkhd->rhgqk", query_grouped, key_block, preferred_element_type=jnp.float32
        )
        key_place = index * block + jnp.arange(block, dtype=jnp.int32)
        allowed = (key_place[None, None, :] <= place[None, :, None]) & (
            key_place[None, None, :] >= first[:, :, None]
        )
        return jnp.where(allowed[:, None, None], raw * scale, -1e30)

    def total_step(index, carry):
        running_max, running_total = carry
        scores = block_scores(block_rows(key_all, index), index)
        new_max = jnp.maximum(running_max, jnp.max(scores, axis=-1))
        new_total = running_total * jnp.exp(running_max - new_max) + jnp.sum(
            jnp.exp(scores - new_max[..., None]), axis=-1
        )
        return (new_max, new_total)

    stat_shape = (rows, key_heads, groups, stretch)
    running_max, running_total = lax.fori_loop(
        0,
        live_blocks,
        total_step,
        (jnp.full(stat_shape, -1e30, jnp.float32), jnp.zeros(stat_shape, jnp.float32)),
    )
    log_total = running_max + jnp.log(running_total)

    def mix_step(index, mixed_sum):
        probs = jnp.exp(block_scores(block_rows(key_all, index), index) - log_total[..., None])
        return mixed_sum + jnp.einsum(
            "rhgqk,rkhd->rqhgd",
            probs.astype(jnp.bfloat16),
            block_rows(value_all, index),
            preferred_element_type=jnp.float32,
        )

    mixed_sum = lax.fori_loop(
        0,
        live_blocks,
        mix_step,
        jnp.zeros((rows, stretch, key_heads, groups, HEAD_DIM), jnp.float32),
    )
    mixed = mixed_sum.reshape(count, width).astype(jnp.bfloat16)
    attn_branch = jnp.dot(
        mixed,
        lax.all_gather(w_out, ("row", "seq"), axis=0, tiled=True),
        preferred_element_type=jnp.float32,
    )
    middle = inputs + attn_branch
    scale_two = norm_scale(middle)
    normed_two = middle * scale_two
    gain_piece = lax.all_gather(mlp_gain, ("row", "seq"), axis=0, tiled=True)
    gate_piece = lax.all_gather(w_gate, ("row", "seq"), axis=0, tiled=True)
    up_piece = lax.all_gather(w_up, ("row", "seq"), axis=0, tiled=True)
    hidden_piece = (normed_two * gain_piece.astype(jnp.float32)).astype(jnp.bfloat16)
    gate_sum, up_sum, hidden_two = (
        jnp.dot(hidden_piece, gate_piece, preferred_element_type=jnp.float32),
        jnp.dot(hidden_piece, up_piece, preferred_element_type=jnp.float32),
        hidden_piece,
    )
    sigma = jax.nn.sigmoid(gate_sum)
    silu_value = gate_sum * sigma
    active = (silu_value * up_sum).astype(jnp.bfloat16)
    mlp_branch = jnp.dot(
        active,
        lax.all_gather(w_down, ("row", "seq"), axis=0, tiled=True),
        preferred_element_type=jnp.float32,
    )
    output = (middle + mlp_branch).astype(jnp.bfloat16).reshape(rows, stretch, width)
    grad_out_low = cotangent.reshape(count, width)
    grad_active = contract_last(
        grad_out_low, lax.all_gather(w_down, ("row", "seq"), axis=0, tiled=True)
    )
    grad_down = lax.psum_scatter(
        contract_first(active, grad_out_low), ("row", "seq"), scatter_dimension=0, tiled=True
    )
    grad_up_low = (grad_active * silu_value).astype(jnp.bfloat16)
    grad_gate_low = (grad_active * up_sum * sigma * (1.0 + gate_sum * (1.0 - sigma))).astype(
        jnp.bfloat16
    )
    both_grads = jnp.concatenate([grad_gate_low, grad_up_low], axis=1)
    gain_piece = lax.all_gather(mlp_gain, ("row", "seq"), axis=0, tiled=True)
    gate_piece = lax.all_gather(w_gate, ("row", "seq"), axis=0, tiled=True)
    up_piece = lax.all_gather(w_up, ("row", "seq"), axis=0, tiled=True)
    grad_piece = contract_last(grad_gate_low, gate_piece) + contract_last(grad_up_low, up_piece)
    normed_piece = normed_two
    grad_normed_two = grad_piece * gain_piece.astype(jnp.float32)
    grad_gain_two = jnp.sum(normed_piece * grad_piece, axis=0)
    grad_gate_up = lax.psum_scatter(
        contract_first(hidden_two, both_grads), ("row", "seq"), scatter_dimension=0, tiled=True
    )
    grad_gate = grad_gate_up[:, :hidden_width]
    grad_up = grad_gate_up[:, hidden_width:]
    grad_middle = grad_out_low.astype(jnp.float32) + norm_back(
        grad_normed_two, normed_two, scale_two
    )
    grad_branch_low = grad_middle.astype(jnp.bfloat16)
    grad_mixed = contract_last(
        grad_branch_low, lax.all_gather(w_out, ("row", "seq"), axis=0, tiled=True)
    ).astype(jnp.bfloat16)
    grad_out = lax.psum_scatter(
        contract_first(mixed, grad_branch_low), ("row", "seq"), scatter_dimension=0, tiled=True
    )
    grad_grouped = grad_mixed.reshape(rows, stretch, key_heads, groups, HEAD_DIM)
    key_back, value_back = gather_keys()

    def delta_step(index, total):
        probs = jnp.exp(block_scores(block_rows(key_back, index), index) - log_total[..., None])
        grad_probs = jnp.einsum(
            "rqhgd,rkhd->rhgqk",
            grad_grouped,
            block_rows(value_back, index),
            preferred_element_type=jnp.float32,
        )
        return total + jnp.sum(probs * grad_probs, axis=-1)

    delta = lax.fori_loop(0, live_blocks, delta_step, jnp.zeros(stat_shape, jnp.float32))

    def grad_step(index, carry):
        grad_queries, grad_key_all, grad_value_all = carry
        key_block = block_rows(key_back, index)
        probs = jnp.exp(block_scores(key_block, index) - log_total[..., None])
        grad_probs = jnp.einsum(
            "rqhgd,rkhd->rhgqk",
            grad_grouped,
            block_rows(value_back, index),
            preferred_element_type=jnp.float32,
        )
        grad_raw = (scale * probs * (grad_probs - delta[..., None])).astype(jnp.bfloat16)
        grad_queries = grad_queries + jnp.einsum(
            "rhgqk,rkhd->rqhgd", grad_raw, key_block, preferred_element_type=jnp.float32
        )
        key_part = jnp.einsum(
            "rhgqk,rqhgd->rkhd", grad_raw, query_grouped, preferred_element_type=jnp.float32
        ).reshape(rows, block, key_width)
        value_part = jnp.einsum(
            "rhgqk,rqhgd->rkhd",
            probs.astype(jnp.bfloat16),
            grad_grouped,
            preferred_element_type=jnp.float32,
        ).reshape(rows, block, key_width)
        return (
            grad_queries,
            lax.dynamic_update_slice_in_dim(grad_key_all, key_part, index * block, 1),
            lax.dynamic_update_slice_in_dim(grad_value_all, value_part, index * block, 1),
        )

    grad_queries, grad_key_all, grad_value_all = lax.fori_loop(
        0,
        live_blocks,
        grad_step,
        (
            jnp.zeros((rows, stretch, key_heads, groups, HEAD_DIM), jnp.float32),
            jnp.zeros((rows, length, key_width), jnp.float32),
            jnp.zeros((rows, length, key_width), jnp.float32),
        ),
    )
    grad_key_sum, grad_value_sum = (
        lax.psum_scatter(
            grad_key_all.astype(jnp.bfloat16), "seq", scatter_dimension=1, tiled=True
        ).astype(jnp.float32),
        lax.psum_scatter(
            grad_value_all.astype(jnp.bfloat16), "seq", scatter_dimension=1, tiled=True
        ).astype(jnp.float32),
    )
    grad_query_low = (
        rotate_back(grad_queries.reshape(rows, stretch, heads, HEAD_DIM), cosine, sine)
        .reshape(count, width)
        .astype(jnp.bfloat16)
    )
    grad_key_low = (
        rotate_back(grad_key_sum.reshape(rows, stretch, key_heads, HEAD_DIM), cosine, sine)
        .reshape(count, key_width)
        .astype(jnp.bfloat16)
    )
    grad_value_low = grad_value_sum.reshape(count, key_width).astype(jnp.bfloat16)
    gain_piece = lax.all_gather(attn_gain, ("row", "seq"), axis=0, tiled=True)
    query_piece = lax.all_gather(w_query, ("row", "seq"), axis=0, tiled=True)
    key_piece = lax.all_gather(w_key, ("row", "seq"), axis=0, tiled=True)
    value_piece = lax.all_gather(w_value, ("row", "seq"), axis=0, tiled=True)
    grad_piece = (
        contract_last(grad_query_low, query_piece)
        + contract_last(grad_key_low, key_piece)
        + contract_last(grad_value_low, value_piece)
    )
    normed_piece = normed_one
    grad_normed_one = grad_piece * gain_piece.astype(jnp.float32)
    grad_gain_one = jnp.sum(normed_piece * grad_piece, axis=0)
    grad_query, grad_key, grad_value, grad_attn_gain, grad_mlp_gain = (
        lax.psum_scatter(
            contract_first(hidden_one, grad_query_low),
            ("row", "seq"),
            scatter_dimension=0,
            tiled=True,
        ),
        lax.psum_scatter(
            contract_first(hidden_one, grad_key_low),
            ("row", "seq"),
            scatter_dimension=0,
            tiled=True,
        ),
        lax.psum_scatter(
            contract_first(hidden_one, grad_value_low),
            ("row", "seq"),
            scatter_dimension=0,
            tiled=True,
        ),
        lax.psum_scatter(grad_gain_one, ("row", "seq"), scatter_dimension=0, tiled=True),
        lax.psum_scatter(grad_gain_two, ("row", "seq"), scatter_dimension=0, tiled=True),
    )
    grad_tokens = (grad_middle + norm_back(grad_normed_one, normed_one, scale_one)).reshape(
        rows, stretch, width
    )
    return (
        output,
        grad_tokens,
        grad_attn_gain,
        grad_query,
        grad_key,
        grad_value,
        grad_out,
        grad_mlp_gain,
        grad_gate,
        grad_up,
        grad_down,
    )


MESH = pl.DeviceIdType.MESH
VMEM_LIMIT = 60 * 1024 * 1024
PARTS = 2


def neighbours():
    row, seq = lax.axis_index("row"), lax.axis_index("seq")
    row_size, seq_size = lax.axis_size("row"), lax.axis_size("seq")
    return dict(
        row=row,
        seq=seq,
        z=seq // 2,
        core=seq % 2,
        up=(row, (seq + 2) % seq_size),
        down=(row, (seq + seq_size - 2) % seq_size),
        pair=(row, seq + 1 - 2 * (seq % 2)),
        side=(row + 1 - 2 * (row % 2), seq),
        across=((row + row_size // 2) % row_size, seq),
        side_row=row + 1 - 2 * (row % 2),
        across_row=(row + row_size // 2) % row_size,
    )


def greet(peers):
    barrier = pltpu.get_barrier_semaphore()
    for peer in peers:
        pl.semaphore_signal(barrier, inc=1, device_id=peer, device_id_type=MESH)
    return lambda more=0: pl.semaphore_wait(barrier, len(peers) + more)


def send(source, target, sems, index, peer):
    copy = pltpu.make_async_remote_copy(
        src_ref=source,
        dst_ref=target,
        send_sem=sems[0].at[index],
        recv_sem=sems[1].at[index],
        device_id=peer,
        device_id_type=MESH,
    )
    copy.start()
    return copy


def sem_pairs(amount):
    return [pltpu.SemaphoreType.DMA((amount,)), pltpu.SemaphoreType.DMA((amount,))]


def by_rows(amount, step, body):
    def one(i, carry):
        body(pl.ds(pl.multiple_of(i * step, step), step))
        return carry

    lax.fori_loop(0, amount // step, one, 0)


def copy_rows(target, source):
    def one(rows):
        target[rows] = source[rows]

    by_rows(source.shape[0], 16, one)


def gather_seq_steps(here, whole, stretch, pair_sems, ring_sems):
    seq, chips = here["seq"], lax.axis_size("seq") // 2
    seq_size = 2 * chips
    piece = stretch // PARTS
    rings, pairs, last = [], [], {}

    def spot(owner, part):
        return pl.ds(pl.multiple_of(owner * stretch + part * piece, piece), piece)

    def ring(step):
        owners = (seq + seq_size - 2 * step) % seq_size, (seq + 2 * step) % seq_size
        for part in range(PARTS):
            for half, peer in ((0, "up"), (1, "down")):
                view = whole.at[half, spot(owners[half], part)]
                slot = (step * PARTS + part) * 2 + half
                if step > 0:
                    last[half, part].wait_recv()
                if step < chips - 1:
                    last[half, part] = send(view, view, ring_sems, slot, here[peer])
                    rings.append(last[half, part])
                pairs.append(send(view, view, pair_sems, slot, here["pair"]))

    def finish():
        for copy in pairs:
            copy.wait()
        for copy in rings:
            copy.wait_send()

    return [lambda step=step: ring(step) for step in range(chips)] + [finish]


def reduce_seq_steps(here, part, stretch, pair_in, total, ring_in, pair_sems, ring_sems, done):
    z, core, chips = here["z"], here["core"], lax.axis_size("seq") // 2
    order = [chips - 1, 1] + list(range(2, chips - 1)) + [0]
    copies, pair_copies = [], {}

    def spot(chip, side):
        return pl.ds(pl.multiple_of((2 * chip + side) * stretch, stretch), stretch)

    def pair_start():
        for index, far in enumerate(order):
            chip = (z + far) % chips
            pair_copies[far] = send(
                part.at[:, spot(chip, 1 - core)], pair_in.at[chip], pair_sems, index, here["pair"]
            )

    def pair_sum(far):
        chip = (z + far) % chips
        pair_copies[far].wait_recv()
        base = (2 * chip + core) * stretch

        for half in range(2):
            def add(rows):
                mine = part[half, pl.ds(pl.multiple_of(base + rows.start, 16), 16)]
                other = pair_in[chip, half, rows]
                total[chip, half, rows] = (
                    mine.astype(jnp.float32) + other.astype(jnp.float32)
                ).astype(jnp.bfloat16)

            by_rows(stretch, 16, add)

    last = {}

    def ring_send(step):
        for half, peer, chip in (
            (0, here["up"], (z + 2 * chips - 1 - step) % chips),
            (1, here["down"], (z + 1 + step) % chips),
        ):
            if step > 0:
                last[half].wait_recv()
                arrived = ring_in.at[step - 1, half]

                def add(rows):
                    total[chip, half, rows] = (
                        total[chip, half, rows].astype(jnp.float32)
                        + arrived[rows].astype(jnp.float32)
                    ).astype(jnp.bfloat16)

                by_rows(stretch, 16, add)
            last[half] = send(
                total.at[chip, half], ring_in.at[step, half], ring_sems, 2 * step + half, peer
            )
            copies.append(last[half])

    def first_step():
        pair_start()
        pair_sum(chips - 1)
        pair_sum(1)
        ring_send(0)
        for far in order[2:]:
            pair_sum(far)

    def next_step(step):
        def run():
            ring_send(step)

        return run

    def finish():
        for half in range(2):
            last[half].wait_recv()
            arrived = ring_in.at[chips - 2, half]

            def close(rows):
                done(
                    half,
                    rows,
                    total[z, half, rows].astype(jnp.float32) + arrived[rows].astype(jnp.float32),
                )

            by_rows(stretch, 16, close)

    def drain():
        for copy in list(pair_copies.values()) + copies:
            copy.wait_send()

    return [first_step] + [next_step(step) for step in range(1, chips - 1)] + [finish], drain


def gather_row_steps(here, own, whole, sems):
    half = whole.shape[1] // 2
    row, side, across = here["row"], here["side_row"], here["across_row"]
    state = []

    def first_step():
        state.append(send(own, whole.at[row], sems, 0, here["side"]))
        state.append(send(own, whole.at[row], sems, 1, here["across"]))

    def second_step():
        low, high = pl.ds(0, half), pl.ds(half, half)
        state[0].wait_recv()
        state.append(send(whole.at[side, low], whole.at[side, low], sems, 2, here["across"]))
        state[1].wait_recv()
        state.append(send(whole.at[across, high], whole.at[across, high], sems, 3, here["side"]))

    def finish():
        for copy in state[2:]:
            copy.wait_recv()
        for copy in state:
            copy.wait_send()

    return [first_step, second_step, finish]


def reduce_row_steps(here, part, inbox, sums, sems, done):
    half = part.shape[1] // 2
    row, side, across = here["row"], here["side_row"], here["across_row"]
    corner = (side + 2) % 4
    state = []

    def first_step():
        low, high = pl.ds(0, half), pl.ds(half, half)
        for index, (owner, rows, peer) in enumerate(
            (
                (corner, low, "side"),
                (corner, high, "across"),
                (side, low, "side"),
                (across, high, "across"),
            )
        ):
            state.append(send(part.at[owner, rows], inbox.at[index], sems, index, here[peer]))

    def add(owner, offset, index):
        def run(rows):
            spot = pl.ds(pl.multiple_of(offset + rows.start, 16), 16)
            sums[index, rows] = (
                part[owner, spot].astype(jnp.float32) + inbox[index, rows].astype(jnp.float32)
            ).astype(jnp.bfloat16)

        by_rows(half, 16, run)

    def second_step():
        state[0].wait_recv()
        add(across, 0, 0)
        state.append(send(sums.at[0], inbox.at[4], sems, 4, here["across"]))
        state[1].wait_recv()
        add(side, half, 1)
        state.append(send(sums.at[1], inbox.at[5], sems, 5, here["side"]))
        state[2].wait_recv()
        state[3].wait_recv()

    def finish():
        for offset, one, two in ((0, 2, 4), (half, 3, 5)):
            state[two].wait_recv()

            def close(rows):
                spot = pl.ds(pl.multiple_of(offset + rows.start, 16), 16)
                done(
                    spot,
                    part[row, spot].astype(jnp.float32)
                    + inbox[one, rows].astype(jnp.float32)
                    + inbox[two, rows].astype(jnp.float32),
                )

            by_rows(half, 16, close)
        for copy in state:
            copy.wait_send()

    return [first_step, second_step, finish]


def exchange_seq(here, source, target_of, sems):
    seq, seq_size = here["seq"], lax.axis_size("seq")
    copies = []
    for far in range(1, seq_size):
        dest = (seq + far) % seq_size
        copies.append(
            send(source.at[dest], target_of(seq), sems, far - 1, (here["row"], dest))
        )
    return copies


def seq_peers(here):
    seq_size = lax.axis_size("seq")
    return [(here["row"], (here["seq"] + far) % seq_size) for far in range(1, seq_size)]


def call(kernel, args, out_shape, scratch, collective_id):
    in_vmem = pl.BlockSpec(memory_space=pltpu.VMEM)
    return pl.pallas_call(
        kernel,
        out_shape=out_shape,
        in_specs=[in_vmem] * len(args),
        out_specs=[in_vmem] * len(out_shape),
        scratch_shapes=scratch,
        compiler_params=pltpu.CompilerParams(
            collective_id=collective_id, has_side_effects=True, vmem_limit_bytes=VMEM_LIMIT
        ),
    )(*args)


def low(*shape):
    return jax.ShapeDtypeStruct(shape, jnp.bfloat16)


def full(*shape):
    return jax.ShapeDtypeStruct(shape, jnp.float32)


def shift_route(here):
    row_size, seq_size = lax.axis_size("row"), lax.axis_size("seq")
    index = here["row"] * seq_size + here["seq"]
    origin = here["seq"] * row_size + here["row"]
    target = index % row_size, index // row_size
    return target, (origin // seq_size, origin % seq_size), index != origin


def open_kernel(
    tokens, heads_pack, w_gate, w_up, out_piece,
    all_tokens, heads_all, units_pack, out_all,
    pair_a, pair_b, ring_a, ring_b, heads_a, heads_b, row_a, row_b, out_a, out_b, shift_a, shift_b,
):
    here = neighbours()
    seq, row = here["seq"], here["row"]
    stretch = tokens.shape[1]
    piece = heads_pack.shape[1]
    target, origin, moves = shift_route(here)
    barrier_wait = greet(seq_peers(here) + [here["side"], here["across"]])

    @pl.when(moves)
    def _():
        for peer in (target, origin):
            pl.semaphore_signal(
                pltpu.get_barrier_semaphore(), inc=1, device_id=peer, device_id_type=MESH
            )

    barrier_wait(jnp.where(moves, 2, 0))

    def spot(owner):
        return pl.ds(pl.multiple_of(owner * piece, piece), piece)

    def shift():
        return pltpu.make_async_remote_copy(
            src_ref=out_piece,
            dst_ref=out_all.at[target[0]],
            send_sem=shift_a.at[0],
            recv_sem=shift_b.at[0],
            device_id=target,
            device_id_type=MESH,
        )

    heads = exchange_seq(here, heads_pack, lambda s: heads_all.at[row, spot(s)], (heads_a, heads_b))

    @pl.when(moves)
    def _():
        shift().start()

    for half in range(2):
        own = pl.ds(pl.multiple_of(seq * stretch, stretch), stretch)
        copy_rows(all_tokens.at[half, own], tokens.at[half])
    gather_out = gather_row_steps(here, out_all.at[row], out_all, (out_a, out_b))
    gather_heads = gather_row_steps(here, heads_all.at[row], heads_all, (row_a, row_b))
    steps = gather_seq_steps(here, all_tokens, stretch, (pair_a, pair_b), (ring_a, ring_b))
    steps[0]()
    copy_rows(heads_all.at[row, spot(seq)], heads_pack.at[seq])

    @pl.when(jnp.logical_not(moves))
    def _():
        copy_rows(out_all.at[row], out_piece)

    for copy in heads:
        copy.wait_recv()
    gather_heads[0]()

    @pl.when(moves)
    def _():
        shift().wait()

    gather_out[0]()
    seq_size, row_size = lax.axis_size("seq"), lax.axis_size("row")
    block = w_gate.shape[1] // (seq_size * row_size)
    for number, weight in enumerate((w_gate, w_up)):
        for r in range(row_size):
            for s in range(seq_size):
                source = (r * seq_size + s) * block
                place = (number * row_size + r) * block
                units_pack[s, :, place : place + block] = weight[:, source : source + block]
    steps[1]()
    gather_heads[1]()
    gather_out[1]()
    for step in steps[2:]:
        step()
    gather_heads[2]()
    gather_out[2]()
    for copy in heads:
        copy.wait_send()


def middle_kernel(
    branch, tokens, gain, units_mine,
    middle, hidden, units_all,
    pair_in, total, ring_in, pair_a, pair_b, ring_a, ring_b,
    gpair_a, gpair_b, gring_a, gring_b, row_a, row_b,
):
    here = neighbours()
    seq = here["seq"]
    stretch = tokens.shape[1]
    greet([here["up"], here["down"], here["pair"], here["side"], here["across"]])()

    def done(half, rows, value):
        value = tokens[half, rows].astype(jnp.float32) + value
        middle[half, rows] = value
        normed = value * norm_scale(value)
        spot = pl.ds(pl.multiple_of(seq * stretch + rows.start, 16), 16)
        hidden[half, spot] = (normed * gain[...]).astype(jnp.bfloat16)

    copy_rows(units_all.at[here["row"]], units_mine)
    reduce_steps, drain = reduce_seq_steps(
        here, branch, stretch, pair_in, total, ring_in, (pair_a, pair_b), (ring_a, ring_b), done
    )
    units = gather_row_steps(here, units_mine, units_all, (row_a, row_b))
    units[0]()
    for step in reduce_steps:
        step()
    gather_steps = gather_seq_steps(here, hidden, stretch, (gpair_a, gpair_b), (gring_a, gring_b))
    gather_steps[0]()
    gather_steps[1]()
    units[1]()
    for step in gather_steps[2:]:
        step()
    units[2]()
    drain()


def back_kernel(
    grad_part, cotangent, middle, gain, units_part,
    grad_middle, grad_low, gain_grad, units_out,
    pair_in, total, ring_in, inbox, sums, pair_a, pair_b, ring_a, ring_b,
    gpair_a, gpair_b, gring_a, gring_b, row_a, row_b,
):
    here = neighbours()
    seq = here["seq"]
    stretch = cotangent.shape[1]
    greet([here["up"], here["down"], here["pair"], here["side"], here["across"]])()
    gain_grad[...] = jnp.zeros_like(gain_grad)

    def done(half, rows, grad):
        value = middle[half, rows]
        scale = norm_scale(value)
        normed = value * scale
        gain_grad[...] += jnp.sum(normed * grad, axis=0, keepdims=True)
        back = cotangent[half, rows].astype(jnp.float32) + norm_back(
            grad * gain[...], normed, scale
        )
        grad_middle[half, rows] = back
        spot = pl.ds(pl.multiple_of(seq * stretch + rows.start, 16), 16)
        grad_low[half, spot] = back.astype(jnp.bfloat16)

    def done_units(rows, value):
        units_out[rows] = value.astype(jnp.bfloat16)

    reduce_steps, drain = reduce_seq_steps(
        here, grad_part, stretch, pair_in, total, ring_in, (pair_a, pair_b), (ring_a, ring_b), done
    )
    units = reduce_row_steps(here, units_part, inbox, sums, (row_a, row_b), done_units)
    units[0]()
    for step in reduce_steps:
        step()
    gather_steps = gather_seq_steps(here, grad_low, stretch, (gpair_a, gpair_b), (gring_a, gring_b))
    gather_steps[0]()
    units[1]()
    for step in gather_steps[1:]:
        step()
    units[2]()
    drain()


def sum_small(here, mine, inbox, sems):
    chips = lax.axis_size("seq") // 2
    slot = 0
    stages = [[here["pair"]]]
    stages.append(
        [(here["row"], (here["seq"] + 2 * far) % (2 * chips)) for far in range(1, chips)]
    )
    stages += [[here["side"]], [here["across"]]]
    copies = []
    for number, stage in enumerate(stages):
        sent = [
            send(mine.at[number], inbox.at[slot + i], sems, slot + i, peer)
            for i, peer in enumerate(stage)
        ]
        value = mine[number]
        for i, copy in enumerate(sent):
            copy.wait_recv()
            value = value + inbox[slot + i]
        mine[number + 1] = value
        slot += len(stage)
        copies += sent
    for copy in copies:
        copy.wait_send()
    return slot


def close_kernel(
    grad_part, tokens, grad_middle, gain, gain_two, heads_part,
    grad_tokens, gain_sums, heads_out,
    heads_mine, pair_in, total, ring_in, inbox, sums, small, small_in,
    pair_a, pair_b, ring_a, ring_b, row_a, row_b, heads_a, heads_b, small_a, small_b,
):
    here = neighbours()
    seq, chips = here["seq"], lax.axis_size("seq") // 2
    stretch = tokens.shape[1]
    greet(seq_peers(here) + [here["side"], here["across"]])()
    small[0, 0:1] = jnp.zeros_like(small[0, 0:1])
    small[0, 1:2] = gain_two[...]

    def done(half, rows, grad):
        value = tokens[half, rows].astype(jnp.float32)
        scale = norm_scale(value)
        normed = value * scale
        small[0, 0:1] += jnp.sum(normed * grad, axis=0, keepdims=True)
        grad_tokens[half, rows] = grad_middle[half, rows] + norm_back(
            grad * gain[...], normed, scale
        )

    piece = heads_out.shape[1]

    def done_heads(rows, value):
        heads_mine[rows] = value.astype(jnp.bfloat16)

    reduce_steps, drain = reduce_seq_steps(
        here, grad_part, stretch, pair_in, total, ring_in, (pair_a, pair_b), (ring_a, ring_b), done
    )
    heads = reduce_row_steps(here, heads_part, inbox, sums, (row_a, row_b), done_heads)
    heads[0]()
    reduce_steps[0]()
    heads[1]()
    for step in reduce_steps[1:-1]:
        step()
    heads[2]()
    copies = []
    for far in range(1, 2 * chips):
        dest = (seq + far) % (2 * chips)
        rows = pl.ds(pl.multiple_of(dest * piece, piece), piece)
        copies.append(
            send(
                heads_mine.at[rows], heads_out.at[seq], (heads_a, heads_b), far - 1,
                (here["row"], dest),
            )
        )
    reduce_steps[-1]()
    copy_rows(heads_out.at[seq], heads_mine.at[pl.ds(pl.multiple_of(seq * piece, piece), piece)])
    sum_small(here, small, small_in, (small_a, small_b))
    gain_sums[...] = small[4]
    for copy in copies:
        copy.wait()
    drain()


def seq_scratch(chips, stretch, width):
    return [
        pltpu.VMEM((chips, 2, stretch, width), jnp.bfloat16),
        pltpu.VMEM((chips, 2, stretch, width), jnp.bfloat16),
        pltpu.VMEM((chips - 1, 2, stretch, width), jnp.bfloat16),
    ]


def row_scratch(pieces, columns):
    return [
        pltpu.VMEM((6, pieces // 2, columns), jnp.bfloat16),
        pltpu.VMEM((2, pieces // 2, columns), jnp.bfloat16),
    ]


def unpack_units(grads, row_size):
    seq_size, rows, columns = grads.shape
    block = columns // 2 // row_size

    def kernel(gate, up, gate_out, up_out):
        for source, target in ((gate, gate_out), (up, up_out)):
            for s in range(seq_size):
                target[:, s * block : (s + 1) * block] = source[s].astype(jnp.float32)

    whole = full(rows, seq_size * columns // 2)
    return pl.pallas_call(
        kernel,
        grid=(row_size,),
        out_shape=[whole, whole],
        in_specs=[
            pl.BlockSpec((seq_size, rows, block), lambda r: (0, 0, r)),
            pl.BlockSpec((seq_size, rows, block), lambda r: (0, 0, row_size + r)),
        ],
        out_specs=[pl.BlockSpec((rows, seq_size * block), lambda r: (0, r))] * 2,
    )(grads, grads)


def unpack_heads(grads, query_width, key_width):
    seq_size, rows, _ = grads.shape

    def kernel(source, query, key, value):
        start = 0
        for target, width in ((query, query_width), (key, key_width), (value, key_width)):
            target[...] = jnp.concatenate(
                [source[s, :, start : start + width].astype(jnp.float32) for s in range(seq_size)],
                axis=1,
            )
            start += width

    return pl.pallas_call(
        kernel,
        out_shape=[full(rows, seq_size * w) for w in (query_width, key_width, key_width)],
    )(grads)


BOTH = ("row", "seq")


def gather(piece, axis_name, axis):
    return lax.all_gather(piece, axis_name, axis=axis, tiled=True)


def scatter(whole, axis_name, axis):
    return lax.psum_scatter(whole, axis_name, scatter_dimension=axis, tiled=True)


def sharded_layer(
    tokens,
    cotangent,
    doc_lengths,
    attn_gain,
    w_query,
    w_key,
    w_value,
    w_out,
    mlp_gain,
    w_gate,
    w_up,
    w_down,
):
    row_size, seq_size = lax.axis_size("row"), lax.axis_size("seq")
    rows, stretch, width = tokens.shape
    length = stretch * seq_size
    count = rows * length
    piece_rows = w_query.shape[0]
    key_heads = w_key.shape[1] // HEAD_DIM // seq_size
    heads = w_query.shape[1] // HEAD_DIM // seq_size
    groups = heads // key_heads
    query_width, key_width = heads * HEAD_DIM, key_heads * HEAD_DIM
    unit_block = w_down.shape[0]
    units = unit_block * row_size
    scale = HEAD_DIM ** (-0.5)

    place = jnp.arange(length, dtype=jnp.int32)
    ends = jnp.cumsum(doc_lengths, axis=1)
    first = jnp.max(
        jnp.where(ends[:, None, :] <= place[None, :, None], ends[:, None, :], 0), axis=2
    )
    table = jnp.asarray(rope_table(HEAD_DIM), jnp.float32)
    angle = (place[None, :] - first).astype(jnp.float32)[..., None] * table
    cosine = jnp.concatenate([jnp.cos(angle), jnp.cos(angle)], axis=-1)[:, :, None, :]
    sine = jnp.concatenate([jnp.sin(angle), jnp.sin(angle)], axis=-1)[:, :, None, :]

    total = row_size * seq_size
    shift_back = [((i % row_size) * seq_size + i // row_size, i) for i in range(total)]

    def head_columns(weight, columns):
        return weight.reshape(piece_rows, seq_size, columns).transpose(1, 0, 2)

    head_width = query_width + 2 * key_width
    spare = -(head_width + 2) % 128
    gain_columns = jnp.stack([attn_gain, mlp_gain], axis=1)
    gain_columns = jnp.pad(gain_columns, ((0, 0), (0, spare)))
    heads_pack = jnp.concatenate(
        [
            head_columns(w_query, query_width),
            head_columns(w_key, key_width),
            head_columns(w_value, key_width),
            jnp.broadcast_to(gain_columns, (seq_size, piece_rows, spare + 2)),
        ],
        axis=2,
    )
    pack_width = head_width + 2 + spare
    chips = seq_size // 2
    pieces = piece_rows * seq_size
    early_cotangent = gather(cotangent[:1], "seq", 1)
    all_tokens, heads_all, units_pack, out_part = call(
        open_kernel,
        (tokens, heads_pack, w_gate, w_up, w_out),
        [
            low(rows, length, width),
            low(row_size, pieces, pack_width),
            low(seq_size, piece_rows, 2 * units),
            low(row_size, piece_rows, width),
        ],
        sem_pairs(2 * chips * PARTS) * 2 + sem_pairs(seq_size - 1) + sem_pairs(4) * 2 + sem_pairs(1),
        0,
    )
    units_mine = lax.all_to_all(units_pack, "seq", 0, 0, tiled=True).reshape(pieces, 2 * units)
    late_down, all_tokens = lax.optimization_barrier((w_down, all_tokens))
    down_part = gather(late_down, "row", 0)
    all_tokens = all_tokens.reshape(count, width)
    heads_all = heads_all.reshape(width, pack_width)
    w_qkv = heads_all[:, :head_width]
    gains = heads_all[:, head_width : head_width + 2].astype(jnp.float32).T
    out_part = out_part.reshape(query_width, width)

    inputs = all_tokens.astype(jnp.float32)
    hidden_one = (inputs * norm_scale(inputs) * gains[0]).astype(jnp.bfloat16)
    qkv = jnp.dot(hidden_one, w_qkv, preferred_element_type=jnp.float32)
    queries = rotate(
        qkv[:, :query_width].reshape(rows, length, heads, HEAD_DIM), cosine, sine
    ).astype(jnp.bfloat16).reshape(rows, length, key_heads, groups, HEAD_DIM)
    keys = rotate(
        qkv[:, query_width : query_width + key_width].reshape(rows, length, key_heads, HEAD_DIM),
        cosine,
        sine,
    ).astype(jnp.bfloat16)
    values = (
        qkv[:, query_width + key_width :]
        .astype(jnp.bfloat16)
        .reshape(rows, length, key_heads, HEAD_DIM)
    )
    raw = jnp.einsum("rqhgd,rkhd->rhgqk", queries, keys, preferred_element_type=jnp.float32)
    allowed = (place[None, None, :] <= place[None, :, None]) & (
        place[None, None, :] >= first[:, :, None]
    )
    probs = jax.nn.softmax(jnp.where(allowed[:, None, None], raw * scale, -1e30), axis=-1)
    probs_low = probs.astype(jnp.bfloat16)
    mixed = (
        jnp.einsum("rhgqk,rkhd->rqhgd", probs_low, values, preferred_element_type=jnp.float32)
        .astype(jnp.bfloat16)
        .reshape(count, query_width)
    )
    branch = jnp.dot(mixed, out_part, preferred_element_type=jnp.float32).astype(jnp.bfloat16)
    middle, hidden_two, w_units = call(
        middle_kernel,
        (branch.reshape(rows, length, width), tokens, gains[1:2], units_mine),
        [full(rows, stretch, width), low(rows, length, width), low(row_size, pieces, 2 * units)],
        seq_scratch(chips, stretch, width)
        + sem_pairs(chips)
        + sem_pairs(2 * chips - 2)
        + sem_pairs(2 * chips * PARTS) * 2
        + sem_pairs(4),
        1,
    )
    late_cotangent, hidden_two = lax.optimization_barrier((cotangent[1:], hidden_two))
    all_cotangent = jnp.concatenate([early_cotangent, gather(late_cotangent, "seq", 1)])
    all_cotangent = all_cotangent.reshape(count, width)
    hidden_two = hidden_two.reshape(count, width)
    w_units = w_units.reshape(width, 2 * units)
    both = jnp.dot(hidden_two, w_units, preferred_element_type=jnp.float32)
    gate_sum, up_sum = both[:, :units], both[:, units:]
    sigma = jax.nn.sigmoid(gate_sum)
    silu_value = gate_sum * sigma
    active = (silu_value * up_sum).astype(jnp.bfloat16)
    mlp_branch = jnp.dot(active, down_part, preferred_element_type=jnp.float32)
    mlp_branch, down_part = lax.optimization_barrier((mlp_branch.astype(jnp.bfloat16), down_part))
    mlp_branch = scatter(mlp_branch.reshape(rows, length, width), "seq", 1)
    output = (middle + mlp_branch.astype(jnp.float32)).astype(jnp.bfloat16)

    grad_active = contract_last(all_cotangent, down_part)
    grad_down = contract_first(active, all_cotangent).astype(jnp.bfloat16)
    grad_up_low = (grad_active * silu_value).astype(jnp.bfloat16)
    grad_gate_low = (grad_active * up_sum * sigma * (1.0 + gate_sum * (1.0 - sigma))).astype(
        jnp.bfloat16
    )
    both_grads = jnp.concatenate([grad_gate_low, grad_up_low], axis=1)
    grad_hidden = contract_last(both_grads, w_units).astype(jnp.bfloat16)
    grad_units = contract_first(hidden_two, both_grads).astype(jnp.bfloat16)
    grad_hidden, mlp_branch, grad_down = lax.optimization_barrier(
        (grad_hidden, mlp_branch, grad_down)
    )
    grad_middle, grad_branch, grad_gain_two, units_mine = call(
        back_kernel,
        (
            grad_hidden.reshape(rows, length, width),
            cotangent,
            middle,
            gains[1:2],
            grad_units.reshape(row_size, pieces, 2 * units),
        ),
        [
            full(rows, stretch, width),
            low(rows, length, width),
            full(1, width),
            low(pieces, 2 * units),
        ],
        seq_scratch(chips, stretch, width)
        + row_scratch(pieces, 2 * units)
        + sem_pairs(chips)
        + sem_pairs(2 * chips - 2)
        + sem_pairs(2 * chips * PARTS) * 2
        + sem_pairs(6),
        2,
    )
    grad_branch, grad_down = lax.optimization_barrier((grad_branch, grad_down))
    grad_down = scatter(grad_down, "row", 0)
    grad_units = lax.all_to_all(
        units_mine.reshape(seq_size, piece_rows, 2 * units), "seq", 0, 0, tiled=True
    )
    grad_branch = grad_branch.reshape(count, width)
    grad_mixed = contract_last(grad_branch, out_part).astype(jnp.bfloat16)
    grad_grouped = grad_mixed.reshape(rows, stretch, key_heads, groups, HEAD_DIM)
    key_back, value_back = gather_keys()

    def delta_step(index, total):
        probs = jnp.exp(block_scores(block_rows(key_back, index), index) - log_total[..., None])
        grad_probs = jnp.einsum(
            "rqhgd,rkhd->rhgqk",
            grad_grouped,
            block_rows(value_back, index),
            preferred_element_type=jnp.float32,
        )
        return total + jnp.sum(probs * grad_probs, axis=-1)

    delta = lax.fori_loop(0, live_blocks, delta_step, jnp.zeros(stat_shape, jnp.float32))

    def grad_step(index, carry):
        grad_queries, grad_key_all, grad_value_all = carry
        key_block = block_rows(key_back, index)
        probs = jnp.exp(block_scores(key_block, index) - log_total[..., None])
        grad_probs = jnp.einsum(
            "rqhgd,rkhd->rhgqk",
            grad_grouped,
            block_rows(value_back, index),
            preferred_element_type=jnp.float32,
        )
        grad_raw = (scale * probs * (grad_probs - delta[..., None])).astype(jnp.bfloat16)
        grad_queries = grad_queries + jnp.einsum(
            "rhgqk,rkhd->rqhgd", grad_raw, key_block, preferred_element_type=jnp.float32
        )
        key_part = jnp.einsum(
            "rhgqk,rqhgd->rkhd", grad_raw, query_grouped, preferred_element_type=jnp.float32
        ).reshape(rows, block, key_width)
        value_part = jnp.einsum(
            "rhgqk,rqhgd->rkhd",
            probs.astype(jnp.bfloat16),
            grad_grouped,
            preferred_element_type=jnp.float32,
        ).reshape(rows, block, key_width)
        return (
            grad_queries,
            lax.dynamic_update_slice_in_dim(grad_key_all, key_part, index * block, 1),
            lax.dynamic_update_slice_in_dim(grad_value_all, value_part, index * block, 1),
        )

    grad_queries, grad_key_all, grad_value_all = lax.fori_loop(
        0,
        live_blocks,
        grad_step,
        (
            jnp.zeros((rows, stretch, key_heads, groups, HEAD_DIM), jnp.float32),
            jnp.zeros((rows, length, key_width), jnp.float32),
            jnp.zeros((rows, length, key_width), jnp.float32),
        ),
    )
    grad_key_sum, grad_value_sum = (
        lax.psum_scatter(
            grad_key_all.astype(jnp.bfloat16), "seq", scatter_dimension=1, tiled=True
        ).astype(jnp.float32),
        lax.psum_scatter(
            grad_value_all.astype(jnp.bfloat16), "seq", scatter_dimension=1, tiled=True
        ).astype(jnp.float32),
    )
    grad_query_low = (
        rotate_back(grad_queries.reshape(rows, stretch, heads, HEAD_DIM), cosine, sine)
        .reshape(count, width)
        .astype(jnp.bfloat16)
    )
    grad_key_low = (
        rotate_back(grad_key_sum.reshape(rows, stretch, key_heads, HEAD_DIM), cosine, sine)
        .reshape(count, key_width)
        .astype(jnp.bfloat16)
    )
    grad_value_low = grad_value_sum.reshape(count, key_width).astype(jnp.bfloat16)
    gain_piece = lax.all_gather(attn_gain, ("row", "seq"), axis=0, tiled=True)
    query_piece = lax.all_gather(w_query, ("row", "seq"), axis=0, tiled=True)
    key_piece = lax.all_gather(w_key, ("row", "seq"), axis=0, tiled=True)
    value_piece = lax.all_gather(w_value, ("row", "seq"), axis=0, tiled=True)
    grad_piece = (
        contract_last(grad_query_low, query_piece)
        + contract_last(grad_key_low, key_piece)
        + contract_last(grad_value_low, value_piece)
    )
    normed_piece = normed_one
    grad_normed_one = grad_piece * gain_piece.astype(jnp.float32)
    grad_gain_one = jnp.sum(normed_piece * grad_piece, axis=0)
    grad_query, grad_key, grad_value, grad_attn_gain, grad_mlp_gain = (
        lax.psum_scatter(
            contract_first(hidden_one, grad_query_low),
            ("row", "seq"),
            scatter_dimension=0,
            tiled=True,
        ),
        lax.psum_scatter(
            contract_first(hidden_one, grad_key_low),
            ("row", "seq"),
            scatter_dimension=0,
            tiled=True,
        ),
        lax.psum_scatter(
            contract_first(hidden_one, grad_value_low),
            ("row", "seq"),
            scatter_dimension=0,
            tiled=True,
        ),
        lax.psum_scatter(grad_gain_one, ("row", "seq"), scatter_dimension=0, tiled=True),
        lax.psum_scatter(grad_gain_two, ("row", "seq"), scatter_dimension=0, tiled=True),
    )
    grad_tokens = (grad_middle + norm_back(grad_normed_one, normed_one, scale_one)).reshape(
        rows, stretch, width
    )
    return (
        output,
        grad_tokens,
        grad_attn_gain,
        grad_query,
        grad_key,
        grad_value,
        grad_out,
        grad_mlp_gain,
        grad_gate,
        grad_up,
        grad_down,
    )


MESH = pl.DeviceIdType.MESH
VMEM_LIMIT = 60 * 1024 * 1024
PARTS = 2


def neighbours():
    row, seq = lax.axis_index("row"), lax.axis_index("seq")
    row_size, seq_size = lax.axis_size("row"), lax.axis_size("seq")
    return dict(
        row=row,
        seq=seq,
        z=seq // 2,
        core=seq % 2,
        up=(row, (seq + 2) % seq_size),
        down=(row, (seq + seq_size - 2) % seq_size),
        pair=(row, seq + 1 - 2 * (seq % 2)),
        side=(row + 1 - 2 * (row % 2), seq),
        across=((row + row_size // 2) % row_size, seq),
        side_row=row + 1 - 2 * (row % 2),
        across_row=(row + row_size // 2) % row_size,
    )


def greet(peers):
    barrier = pltpu.get_barrier_semaphore()
    for peer in peers:
        pl.semaphore_signal(barrier, inc=1, device_id=peer, device_id_type=MESH)
    return lambda more=0: pl.semaphore_wait(barrier, len(peers) + more)


def send(source, target, sems, index, peer):
    copy = pltpu.make_async_remote_copy(
        src_ref=source,
        dst_ref=target,
        send_sem=sems[0].at[index],
        recv_sem=sems[1].at[index],
        device_id=peer,
        device_id_type=MESH,
    )
    copy.start()
    return copy


def sem_pairs(amount):
    return [pltpu.SemaphoreType.DMA((amount,)), pltpu.SemaphoreType.DMA((amount,))]


def by_rows(amount, step, body):
    def one(i, carry):
        body(pl.ds(pl.multiple_of(i * step, step), step))
        return carry

    lax.fori_loop(0, amount // step, one, 0)


def copy_rows(target, source):
    def one(rows):
        target[rows] = source[rows]

    by_rows(source.shape[0], 16, one)


def gather_seq_steps(here, whole, stretch, pair_sems, ring_sems):
    seq, chips = here["seq"], lax.axis_size("seq") // 2
    seq_size = 2 * chips
    piece = stretch // PARTS
    rings, pairs, last = [], [], {}

    def spot(owner, part):
        return pl.ds(pl.multiple_of(owner * stretch + part * piece, piece), piece)

    def ring(step):
        owners = (seq + seq_size - 2 * step) % seq_size, (seq + 2 * step) % seq_size
        for part in range(PARTS):
            for half, peer in ((0, "up"), (1, "down")):
                view = whole.at[half, spot(owners[half], part)]
                slot = (step * PARTS + part) * 2 + half
                if step > 0:
                    last[half, part].wait_recv()
                if step < chips - 1:
                    last[half, part] = send(view, view, ring_sems, slot, here[peer])
                    rings.append(last[half, part])
                pairs.append(send(view, view, pair_sems, slot, here["pair"]))

    def finish():
        for copy in pairs:
            copy.wait()
        for copy in rings:
            copy.wait_send()

    return [lambda step=step: ring(step) for step in range(chips)] + [finish]


def reduce_seq_steps(here, part, stretch, pair_in, total, ring_in, pair_sems, ring_sems, done):
    z, core, chips = here["z"], here["core"], lax.axis_size("seq") // 2
    order = [chips - 1, 1] + list(range(2, chips - 1)) + [0]
    copies, pair_copies = [], {}

    def spot(chip, side):
        return pl.ds(pl.multiple_of((2 * chip + side) * stretch, stretch), stretch)

    def pair_start():
        for index, far in enumerate(order):
            chip = (z + far) % chips
            pair_copies[far] = send(
                part.at[:, spot(chip, 1 - core)], pair_in.at[chip], pair_sems, index, here["pair"]
            )

    def pair_sum(far):
        chip = (z + far) % chips
        pair_copies[far].wait_recv()
        base = (2 * chip + core) * stretch

        for half in range(2):
            def add(rows):
                mine = part[half, pl.ds(pl.multiple_of(base + rows.start, 16), 16)]
                other = pair_in[chip, half, rows]
                total[chip, half, rows] = (
                    mine.astype(jnp.float32) + other.astype(jnp.float32)
                ).astype(jnp.bfloat16)

            by_rows(stretch, 16, add)

    last = {}

    def ring_send(step):
        for half, peer, chip in (
            (0, here["up"], (z + 2 * chips - 1 - step) % chips),
            (1, here["down"], (z + 1 + step) % chips),
        ):
            if step > 0:
                last[half].wait_recv()
                arrived = ring_in.at[step - 1, half]

                def add(rows):
                    total[chip, half, rows] = (
                        total[chip, half, rows].astype(jnp.float32)
                        + arrived[rows].astype(jnp.float32)
                    ).astype(jnp.bfloat16)

                by_rows(stretch, 16, add)
            last[half] = send(
                total.at[chip, half], ring_in.at[step, half], ring_sems, 2 * step + half, peer
            )
            copies.append(last[half])

    def first_step():
        pair_start()
        pair_sum(chips - 1)
        pair_sum(1)
        ring_send(0)
        for far in order[2:]:
            pair_sum(far)

    def next_step(step):
        def run():
            ring_send(step)

        return run

    def finish():
        for half in range(2):
            last[half].wait_recv()
            arrived = ring_in.at[chips - 2, half]

            def close(rows):
                done(
                    half,
                    rows,
                    total[z, half, rows].astype(jnp.float32) + arrived[rows].astype(jnp.float32),
                )

            by_rows(stretch, 16, close)

    def drain():
        for copy in list(pair_copies.values()) + copies:
            copy.wait_send()

    return [first_step] + [next_step(step) for step in range(1, chips - 1)] + [finish], drain


def gather_row_steps(here, own, whole, sems):
    half = whole.shape[1] // 2
    row, side, across = here["row"], here["side_row"], here["across_row"]
    state = []

    def first_step():
        state.append(send(own, whole.at[row], sems, 0, here["side"]))
        state.append(send(own, whole.at[row], sems, 1, here["across"]))

    def second_step():
        low, high = pl.ds(0, half), pl.ds(half, half)
        state[0].wait_recv()
        state.append(send(whole.at[side, low], whole.at[side, low], sems, 2, here["across"]))
        state[1].wait_recv()
        state.append(send(whole.at[across, high], whole.at[across, high], sems, 3, here["side"]))

    def finish():
        for copy in state[2:]:
            copy.wait_recv()
        for copy in state:
            copy.wait_send()

    return [first_step, second_step, finish]


def reduce_row_steps(here, part, inbox, sums, sems, done):
    half = part.shape[1] // 2
    row, side, across = here["row"], here["side_row"], here["across_row"]
    corner = (side + 2) % 4
    state = []

    def first_step():
        low, high = pl.ds(0, half), pl.ds(half, half)
        for index, (owner, rows, peer) in enumerate(
            (
                (corner, low, "side"),
                (corner, high, "across"),
                (side, low, "side"),
                (across, high, "across"),
            )
        ):
            state.append(send(part.at[owner, rows], inbox.at[index], sems, index, here[peer]))

    def add(owner, offset, index):
        def run(rows):
            spot = pl.ds(pl.multiple_of(offset + rows.start, 16), 16)
            sums[index, rows] = (
                part[owner, spot].astype(jnp.float32) + inbox[index, rows].astype(jnp.float32)
            ).astype(jnp.bfloat16)

        by_rows(half, 16, run)

    def second_step():
        state[0].wait_recv()
        add(across, 0, 0)
        state.append(send(sums.at[0], inbox.at[4], sems, 4, here["across"]))
        state[1].wait_recv()
        add(side, half, 1)
        state.append(send(sums.at[1], inbox.at[5], sems, 5, here["side"]))
        state[2].wait_recv()
        state[3].wait_recv()

    def finish():
        for offset, one, two in ((0, 2, 4), (half, 3, 5)):
            state[two].wait_recv()

            def close(rows):
                spot = pl.ds(pl.multiple_of(offset + rows.start, 16), 16)
                done(
                    spot,
                    part[row, spot].astype(jnp.float32)
                    + inbox[one, rows].astype(jnp.float32)
                    + inbox[two, rows].astype(jnp.float32),
                )

            by_rows(half, 16, close)
        for copy in state:
            copy.wait_send()

    return [first_step, second_step, finish]


def exchange_seq(here, source, target_of, sems):
    seq, seq_size = here["seq"], lax.axis_size("seq")
    copies = []
    for far in range(1, seq_size):
        dest = (seq + far) % seq_size
        copies.append(
            send(source.at[dest], target_of(seq), sems, far - 1, (here["row"], dest))
        )
    return copies


def seq_peers(here):
    seq_size = lax.axis_size("seq")
    return [(here["row"], (here["seq"] + far) % seq_size) for far in range(1, seq_size)]


def call(kernel, args, out_shape, scratch, collective_id):
    in_vmem = pl.BlockSpec(memory_space=pltpu.VMEM)
    return pl.pallas_call(
        kernel,
        out_shape=out_shape,
        in_specs=[in_vmem] * len(args),
        out_specs=[in_vmem] * len(out_shape),
        scratch_shapes=scratch,
        compiler_params=pltpu.CompilerParams(
            collective_id=collective_id, has_side_effects=True, vmem_limit_bytes=VMEM_LIMIT
        ),
    )(*args)


def low(*shape):
    return jax.ShapeDtypeStruct(shape, jnp.bfloat16)


def full(*shape):
    return jax.ShapeDtypeStruct(shape, jnp.float32)


def shift_route(here):
    row_size, seq_size = lax.axis_size("row"), lax.axis_size("seq")
    index = here["row"] * seq_size + here["seq"]
    origin = here["seq"] * row_size + here["row"]
    target = index % row_size, index // row_size
    return target, (origin // seq_size, origin % seq_size), index != origin


def open_kernel(
    tokens, heads_pack, w_gate, w_up, out_piece,
    all_tokens, heads_all, units_pack, out_all,
    pair_a, pair_b, ring_a, ring_b, heads_a, heads_b, row_a, row_b, out_a, out_b, shift_a, shift_b,
):
    here = neighbours()
    seq, row = here["seq"], here["row"]
    stretch = tokens.shape[1]
    piece = heads_pack.shape[1]
    target, origin, moves = shift_route(here)
    barrier_wait = greet(seq_peers(here) + [here["side"], here["across"]])

    @pl.when(moves)
    def _():
        for peer in (target, origin):
            pl.semaphore_signal(
                pltpu.get_barrier_semaphore(), inc=1, device_id=peer, device_id_type=MESH
            )

    barrier_wait(jnp.where(moves, 2, 0))

    def spot(owner):
        return pl.ds(pl.multiple_of(owner * piece, piece), piece)

    def shift():
        return pltpu.make_async_remote_copy(
            src_ref=out_piece,
            dst_ref=out_all.at[target[0]],
            send_sem=shift_a.at[0],
            recv_sem=shift_b.at[0],
            device_id=target,
            device_id_type=MESH,
        )

    heads = exchange_seq(here, heads_pack, lambda s: heads_all.at[row, spot(s)], (heads_a, heads_b))

    @pl.when(moves)
    def _():
        shift().start()

    for half in range(2):
        own = pl.ds(pl.multiple_of(seq * stretch, stretch), stretch)
        copy_rows(all_tokens.at[half, own], tokens.at[half])
    gather_out = gather_row_steps(here, out_all.at[row], out_all, (out_a, out_b))
    gather_heads = gather_row_steps(here, heads_all.at[row], heads_all, (row_a, row_b))
    steps = gather_seq_steps(here, all_tokens, stretch, (pair_a, pair_b), (ring_a, ring_b))
    steps[0]()
    copy_rows(heads_all.at[row, spot(seq)], heads_pack.at[seq])

    @pl.when(jnp.logical_not(moves))
    def _():
        copy_rows(out_all.at[row], out_piece)

    for copy in heads:
        copy.wait_recv()
    gather_heads[0]()

    @pl.when(moves)
    def _():
        shift().wait()

    gather_out[0]()
    seq_size, row_size = lax.axis_size("seq"), lax.axis_size("row")
    block = w_gate.shape[1] // (seq_size * row_size)
    for number, weight in enumerate((w_gate, w_up)):
        for r in range(row_size):
            for s in range(seq_size):
                source = (r * seq_size + s) * block
                place = (number * row_size + r) * block
                units_pack[s, :, place : place + block] = weight[:, source : source + block]
    steps[1]()
    gather_heads[1]()
    gather_out[1]()
    for step in steps[2:]:
        step()
    gather_heads[2]()
    gather_out[2]()
    for copy in heads:
        copy.wait_send()


def middle_kernel(
    branch, tokens, gain, units_mine,
    middle, hidden, units_all,
    pair_in, total, ring_in, pair_a, pair_b, ring_a, ring_b,
    gpair_a, gpair_b, gring_a, gring_b, row_a, row_b,
):
    here = neighbours()
    seq = here["seq"]
    stretch = tokens.shape[1]
    greet([here["up"], here["down"], here["pair"], here["side"], here["across"]])()

    def done(half, rows, value):
        value = tokens[half, rows].astype(jnp.float32) + value
        middle[half, rows] = value
        normed = value * norm_scale(value)
        spot = pl.ds(pl.multiple_of(seq * stretch + rows.start, 16), 16)
        hidden[half, spot] = (normed * gain[...]).astype(jnp.bfloat16)

    copy_rows(units_all.at[here["row"]], units_mine)
    reduce_steps, drain = reduce_seq_steps(
        here, branch, stretch, pair_in, total, ring_in, (pair_a, pair_b), (ring_a, ring_b), done
    )
    units = gather_row_steps(here, units_mine, units_all, (row_a, row_b))
    units[0]()
    for step in reduce_steps:
        step()
    gather_steps = gather_seq_steps(here, hidden, stretch, (gpair_a, gpair_b), (gring_a, gring_b))
    gather_steps[0]()
    gather_steps[1]()
    units[1]()
    for step in gather_steps[2:]:
        step()
    units[2]()
    drain()


def back_kernel(
    grad_part, cotangent, middle, gain, units_part,
    grad_middle, grad_low, gain_grad, units_out,
    pair_in, total, ring_in, inbox, sums, pair_a, pair_b, ring_a, ring_b,
    gpair_a, gpair_b, gring_a, gring_b, row_a, row_b,
):
    here = neighbours()
    seq = here["seq"]
    stretch = cotangent.shape[1]
    greet([here["up"], here["down"], here["pair"], here["side"], here["across"]])()
    gain_grad[...] = jnp.zeros_like(gain_grad)

    def done(half, rows, grad):
        value = middle[half, rows]
        scale = norm_scale(value)
        normed = value * scale
        gain_grad[...] += jnp.sum(normed * grad, axis=0, keepdims=True)
        back = cotangent[half, rows].astype(jnp.float32) + norm_back(
            grad * gain[...], normed, scale
        )
        grad_middle[half, rows] = back
        spot = pl.ds(pl.multiple_of(seq * stretch + rows.start, 16), 16)
        grad_low[half, spot] = back.astype(jnp.bfloat16)

    def done_units(rows, value):
        units_out[rows] = value.astype(jnp.bfloat16)

    reduce_steps, drain = reduce_seq_steps(
        here, grad_part, stretch, pair_in, total, ring_in, (pair_a, pair_b), (ring_a, ring_b), done
    )
    units = reduce_row_steps(here, units_part, inbox, sums, (row_a, row_b), done_units)
    units[0]()
    for step in reduce_steps:
        step()
    gather_steps = gather_seq_steps(here, grad_low, stretch, (gpair_a, gpair_b), (gring_a, gring_b))
    gather_steps[0]()
    units[1]()
    for step in gather_steps[1:]:
        step()
    units[2]()
    drain()


def sum_small(here, mine, inbox, sems):
    chips = lax.axis_size("seq") // 2
    slot = 0
    stages = [[here["pair"]]]
    stages.append(
        [(here["row"], (here["seq"] + 2 * far) % (2 * chips)) for far in range(1, chips)]
    )
    stages += [[here["side"]], [here["across"]]]
    copies = []
    for number, stage in enumerate(stages):
        sent = [
            send(mine.at[number], inbox.at[slot + i], sems, slot + i, peer)
            for i, peer in enumerate(stage)
        ]
        value = mine[number]
        for i, copy in enumerate(sent):
            copy.wait_recv()
            value = value + inbox[slot + i]
        mine[number + 1] = value
        slot += len(stage)
        copies += sent
    for copy in copies:
        copy.wait_send()
    return slot


def close_kernel(
    grad_part, tokens, grad_middle, gain, gain_two, heads_part,
    grad_tokens, gain_sums, heads_out,
    heads_mine, pair_in, total, ring_in, inbox, sums, small, small_in,
    pair_a, pair_b, ring_a, ring_b, row_a, row_b, heads_a, heads_b, small_a, small_b,
):
    here = neighbours()
    seq, chips = here["seq"], lax.axis_size("seq") // 2
    stretch = tokens.shape[1]
    greet(seq_peers(here) + [here["side"], here["across"]])()
    small[0, 0:1] = jnp.zeros_like(small[0, 0:1])
    small[0, 1:2] = gain_two[...]

    def done(half, rows, grad):
        value = tokens[half, rows].astype(jnp.float32)
        scale = norm_scale(value)
        normed = value * scale
        small[0, 0:1] += jnp.sum(normed * grad, axis=0, keepdims=True)
        grad_tokens[half, rows] = grad_middle[half, rows] + norm_back(
            grad * gain[...], normed, scale
        )

    piece = heads_out.shape[1]

    def done_heads(rows, value):
        heads_mine[rows] = value.astype(jnp.bfloat16)

    reduce_steps, drain = reduce_seq_steps(
        here, grad_part, stretch, pair_in, total, ring_in, (pair_a, pair_b), (ring_a, ring_b), done
    )
    heads = reduce_row_steps(here, heads_part, inbox, sums, (row_a, row_b), done_heads)
    heads[0]()
    reduce_steps[0]()
    heads[1]()
    for step in reduce_steps[1:-1]:
        step()
    heads[2]()
    copies = []
    for far in range(1, 2 * chips):
        dest = (seq + far) % (2 * chips)
        rows = pl.ds(pl.multiple_of(dest * piece, piece), piece)
        copies.append(
            send(
                heads_mine.at[rows], heads_out.at[seq], (heads_a, heads_b), far - 1,
                (here["row"], dest),
            )
        )
    reduce_steps[-1]()
    copy_rows(heads_out.at[seq], heads_mine.at[pl.ds(pl.multiple_of(seq * piece, piece), piece)])
    sum_small(here, small, small_in, (small_a, small_b))
    gain_sums[...] = small[4]
    for copy in copies:
        copy.wait()
    drain()


def seq_scratch(chips, stretch, width):
    return [
        pltpu.VMEM((chips, 2, stretch, width), jnp.bfloat16),
        pltpu.VMEM((chips, 2, stretch, width), jnp.bfloat16),
        pltpu.VMEM((chips - 1, 2, stretch, width), jnp.bfloat16),
    ]


def row_scratch(pieces, columns):
    return [
        pltpu.VMEM((6, pieces // 2, columns), jnp.bfloat16),
        pltpu.VMEM((2, pieces // 2, columns), jnp.bfloat16),
    ]


def unpack_units(grads, row_size):
    seq_size, rows, columns = grads.shape
    block = columns // 2 // row_size

    def kernel(gate, up, gate_out, up_out):
        for source, target in ((gate, gate_out), (up, up_out)):
            for s in range(seq_size):
                target[:, s * block : (s + 1) * block] = source[s].astype(jnp.float32)

    whole = full(rows, seq_size * columns // 2)
    return pl.pallas_call(
        kernel,
        grid=(row_size,),
        out_shape=[whole, whole],
        in_specs=[
            pl.BlockSpec((seq_size, rows, block), lambda r: (0, 0, r)),
            pl.BlockSpec((seq_size, rows, block), lambda r: (0, 0, row_size + r)),
        ],
        out_specs=[pl.BlockSpec((rows, seq_size * block), lambda r: (0, r))] * 2,
    )(grads, grads)


def unpack_heads(grads, query_width, key_width):
    seq_size, rows, _ = grads.shape

    def kernel(source, query, key, value):
        start = 0
        for target, width in ((query, query_width), (key, key_width), (value, key_width)):
            target[...] = jnp.concatenate(
                [source[s, :, start : start + width].astype(jnp.float32) for s in range(seq_size)],
                axis=1,
            )
            start += width

    return pl.pallas_call(
        kernel,
        out_shape=[full(rows, seq_size * w) for w in (query_width, key_width, key_width)],
    )(grads)


BOTH = ("row", "seq")


def gather(piece, axis_name, axis):
    return lax.all_gather(piece, axis_name, axis=axis, tiled=True)


def scatter(whole, axis_name, axis):
    return lax.psum_scatter(whole, axis_name, scatter_dimension=axis, tiled=True)


def sharded_layer(
    tokens,
    cotangent,
    doc_lengths,
    attn_gain,
    w_query,
    w_key,
    w_value,
    w_out,
    mlp_gain,
    w_gate,
    w_up,
    w_down,
):
    row_size, seq_size = lax.axis_size("row"), lax.axis_size("seq")
    rows, stretch, width = tokens.shape
    length = stretch * seq_size
    count = rows * length
    piece_rows = w_query.shape[0]
    key_heads = w_key.shape[1] // HEAD_DIM // seq_size
    heads = w_query.shape[1] // HEAD_DIM // seq_size
    groups = heads // key_heads
    query_width, key_width = heads * HEAD_DIM, key_heads * HEAD_DIM
    unit_block = w_down.shape[0]
    units = unit_block * row_size
    scale = HEAD_DIM ** (-0.5)

    place = jnp.arange(length, dtype=jnp.int32)
    ends = jnp.cumsum(doc_lengths, axis=1)
    first = jnp.max(
        jnp.where(ends[:, None, :] <= place[None, :, None], ends[:, None, :], 0), axis=2
    )
    table = jnp.asarray(rope_table(HEAD_DIM), jnp.float32)
    angle = (place[None, :] - first).astype(jnp.float32)[..., None] * table
    cosine = jnp.concatenate([jnp.cos(angle), jnp.cos(angle)], axis=-1)[:, :, None, :]
    sine = jnp.concatenate([jnp.sin(angle), jnp.sin(angle)], axis=-1)[:, :, None, :]

    total = row_size * seq_size
    shift_back = [((i % row_size) * seq_size + i // row_size, i) for i in range(total)]

    def head_columns(weight, columns):
        return weight.reshape(piece_rows, seq_size, columns).transpose(1, 0, 2)

    head_width = query_width + 2 * key_width
    spare = -(head_width + 2) % 128
    gain_columns = jnp.stack([attn_gain, mlp_gain], axis=1)
    gain_columns = jnp.pad(gain_columns, ((0, 0), (0, spare)))
    heads_pack = jnp.concatenate(
        [
            head_columns(w_query, query_width),
            head_columns(w_key, key_width),
            head_columns(w_value, key_width),
            jnp.broadcast_to(gain_columns, (seq_size, piece_rows, spare + 2)),
        ],
        axis=2,
    )
    pack_width = head_width + 2 + spare
    chips = seq_size // 2
    pieces = piece_rows * seq_size
    early_cotangent = gather(cotangent[:1], "seq", 1)
    all_tokens, heads_all, units_pack, out_part = call(
        open_kernel,
        (tokens, heads_pack, w_gate, w_up, w_out),
        [
            low(rows, length, width),
            low(row_size, pieces, pack_width),
            low(seq_size, piece_rows, 2 * units),
            low(row_size, piece_rows, width),
        ],
        sem_pairs(2 * chips * PARTS) * 2 + sem_pairs(seq_size - 1) + sem_pairs(4) * 2 + sem_pairs(1),
        0,
    )
    units_mine = lax.all_to_all(units_pack, "seq", 0, 0, tiled=True).reshape(pieces, 2 * units)
    late_down, all_tokens = lax.optimization_barrier((w_down, all_tokens))
    down_part = gather(late_down, "row", 0)
    all_tokens = all_tokens.reshape(count, width)
    heads_all = heads_all.reshape(width, pack_width)
    w_qkv = heads_all[:, :head_width]
    gains = heads_all[:, head_width : head_width + 2].astype(jnp.float32).T
    out_part = out_part.reshape(query_width, width)

    inputs = all_tokens.astype(jnp.float32)
    hidden_one = (inputs * norm_scale(inputs) * gains[0]).astype(jnp.bfloat16)
    qkv = jnp.dot(hidden_one, w_qkv, preferred_element_type=jnp.float32)
    queries = rotate(
        qkv[:, :query_width].reshape(rows, length, heads, HEAD_DIM), cosine, sine
    ).astype(jnp.bfloat16).reshape(rows, length, key_heads, groups, HEAD_DIM)
    keys = rotate(
        qkv[:, query_width : query_width + key_width].reshape(rows, length, key_heads, HEAD_DIM),
        cosine,
        sine,
    ).astype(jnp.bfloat16)
    values = (
        qkv[:, query_width + key_width :]
        .astype(jnp.bfloat16)
        .reshape(rows, length, key_heads, HEAD_DIM)
    )
    raw = jnp.einsum("rqhgd,rkhd->rhgqk", queries, keys, preferred_element_type=jnp.float32)
    allowed = (place[None, None, :] <= place[None, :, None]) & (
        place[None, None, :] >= first[:, :, None]
    )
    probs = jax.nn.softmax(jnp.where(allowed[:, None, None], raw * scale, -1e30), axis=-1)
    probs_low = probs.astype(jnp.bfloat16)
    mixed = (
        jnp.einsum("rhgqk,rkhd->rqhgd", probs_low, values, preferred_element_type=jnp.float32)
        .astype(jnp.bfloat16)
        .reshape(count, query_width)
    )
    branch = jnp.dot(mixed, out_part, preferred_element_type=jnp.float32).astype(jnp.bfloat16)
    middle, hidden_two, w_units = call(
        middle_kernel,
        (branch.reshape(rows, length, width), tokens, gains[1:2], units_mine),
        [full(rows, stretch, width), low(rows, length, width), low(row_size, pieces, 2 * units)],
        seq_scratch(chips, stretch, width)
        + sem_pairs(chips)
        + sem_pairs(2 * chips - 2)
        + sem_pairs(2 * chips * PARTS) * 2
        + sem_pairs(4),
        1,
    )
    late_cotangent, hidden_two = lax.optimization_barrier((cotangent[1:], hidden_two))
    all_cotangent = jnp.concatenate([early_cotangent, gather(late_cotangent, "seq", 1)])
    all_cotangent = all_cotangent.reshape(count, width)
    hidden_two = hidden_two.reshape(count, width)
    w_units = w_units.reshape(width, 2 * units)
    both = jnp.dot(hidden_two, w_units, preferred_element_type=jnp.float32)
    gate_sum, up_sum = both[:, :units], both[:, units:]
    sigma = jax.nn.sigmoid(gate_sum)
    silu_value = gate_sum * sigma
    active = (silu_value * up_sum).astype(jnp.bfloat16)
    mlp_branch = jnp.dot(active, down_part, preferred_element_type=jnp.float32)
    mlp_branch, down_part = lax.optimization_barrier((mlp_branch.astype(jnp.bfloat16), down_part))
    mlp_branch = scatter(mlp_branch.reshape(rows, length, width), "seq", 1)
    output = (middle + mlp_branch.astype(jnp.float32)).astype(jnp.bfloat16)

    grad_active = contract_last(all_cotangent, down_part)
    grad_down = contract_first(active, all_cotangent).astype(jnp.bfloat16)
    grad_up_low = (grad_active * silu_value).astype(jnp.bfloat16)
    grad_gate_low = (grad_active * up_sum * sigma * (1.0 + gate_sum * (1.0 - sigma))).astype(
        jnp.bfloat16
    )
    both_grads = jnp.concatenate([grad_gate_low, grad_up_low], axis=1)
    grad_hidden = contract_last(both_grads, w_units).astype(jnp.bfloat16)
    grad_units = contract_first(hidden_two, both_grads).astype(jnp.bfloat16)
    grad_hidden, mlp_branch, grad_down = lax.optimization_barrier(
        (grad_hidden, mlp_branch, grad_down)
    )
    grad_middle, grad_branch, grad_gain_two, units_mine = call(
        back_kernel,
        (
            grad_hidden.reshape(rows, length, width),
            cotangent,
            middle,
            gains[1:2],
            grad_units.reshape(row_size, pieces, 2 * units),
        ),
        [
            full(rows, stretch, width),
            low(rows, length, width),
            full(1, width),
            low(pieces, 2 * units),
        ],
        seq_scratch(chips, stretch, width)
        + row_scratch(pieces, 2 * units)
        + sem_pairs(chips)
        + sem_pairs(2 * chips - 2)
        + sem_pairs(2 * chips * PARTS) * 2
        + sem_pairs(6),
        2,
    )
    grad_branch, grad_down = lax.optimization_barrier((grad_branch, grad_down))
    grad_down = scatter(grad_down, "row", 0)
    grad_units = lax.all_to_all(
        units_mine.reshape(seq_size, piece_rows, 2 * units), "seq", 0, 0, tiled=True
    )
    grad_branch = grad_branch.reshape(count, width)
    grad_mixed = contract_last(grad_branch, out_part).astype(jnp.bfloat16)
    grad_out = scatter(contract_first(mixed, grad_branch).astype(jnp.bfloat16), "row", 0)
    grad_out = lax.ppermute(grad_out, BOTH, shift_back).astype(jnp.float32)
    grad_grouped = grad_mixed.reshape(rows, length, key_heads, groups, HEAD_DIM)
    grad_probs = jnp.einsum(
        "rqhgd,rkhd->rhgqk", grad_grouped, values, preferred_element_type=jnp.float32
    )
    delta = jnp.sum(probs * grad_probs, axis=-1, keepdims=True)
    grad_raw = (scale * probs * (grad_probs - delta)).astype(jnp.bfloat16)
    grad_queries = jnp.einsum(
        "rhgqk,rkhd->rqhgd", grad_raw, keys, preferred_element_type=jnp.float32
    )
    grad_keys = jnp.einsum(
        "rhgqk,rqhgd->rkhd", grad_raw, queries, preferred_element_type=jnp.float32
    )
    grad_values = jnp.einsum(
        "rhgqk,rqhgd->rkhd", probs_low, grad_grouped, preferred_element_type=jnp.float32
    )
    mixed, grad_keys = lax.optimization_barrier((mixed, grad_keys))
    grad_qkv_low = jnp.concatenate(
        [
            rotate_back(grad_queries.reshape(rows, length, heads, HEAD_DIM), cosine, sine).reshape(
                count, query_width
            ),
            rotate_back(grad_keys, cosine, sine).reshape(count, key_width),
            grad_values.reshape(count, key_width),
        ],
        axis=1,
    ).astype(jnp.bfloat16)
    grad_qkv = contract_first(hidden_one, grad_qkv_low).astype(jnp.bfloat16)
    grad_hidden = contract_last(grad_qkv_low, w_qkv).astype(jnp.bfloat16)
    grad_hidden, grad_units = lax.optimization_barrier((grad_hidden, grad_units))
    grad_tokens, gain_sums, grad_qkv = call(
        close_kernel,
        (
            grad_hidden.reshape(rows, length, width),
            tokens,
            grad_middle,
            gains[0:1],
            grad_gain_two,
            grad_qkv.reshape(row_size, pieces, head_width),
        ),
        [
            full(rows, stretch, width),
            full(2, width),
            low(seq_size, piece_rows, head_width),
        ],
        [pltpu.VMEM((pieces, head_width), jnp.bfloat16)]
        + seq_scratch(chips, stretch, width)
        + row_scratch(pieces, head_width)
        + [pltpu.VMEM((5, 2, width), jnp.float32), pltpu.VMEM((chips + 2, 2, width), jnp.float32)]
        + sem_pairs(chips)
        + sem_pairs(2 * chips - 2)
        + sem_pairs(6)
        + sem_pairs(seq_size - 1)
        + sem_pairs(chips + 2),
        3,
    )

    grad_gate, grad_up = unpack_units(grad_units, row_size)
    grad_query, grad_key, grad_value = unpack_heads(grad_qkv, query_width, key_width)
    own = (lax.axis_index("row") * seq_size + lax.axis_index("seq")) * piece_rows
    grad_gains = lax.dynamic_slice_in_dim(gain_sums, own, piece_rows, 1)
    return (
        output,
        grad_tokens,
        grad_gains[0],
        grad_query,
        grad_key,
        grad_value,
        grad_out,
        grad_gains[1],
        grad_gate,
        grad_up,
        grad_down.astype(jnp.float32),
    )


def local(tokens, cotangent, doc_lengths, attn_gain, w_query, w_key, w_value, *rest):
    whole_heads = w_key.shape[1] % (HEAD_DIM * lax.axis_size("seq")) == 0
    layer = sharded_layer if whole_heads else gathered_layer
    return layer(tokens, cotangent, doc_lengths, attn_gain, w_query, w_key, w_value, *rest)


def solution(mesh):
    return jax.shard_map(
        local,
        mesh=mesh,
        in_specs=(
            P("row", "seq", None),
            P("row", "seq", None),
            P("row", None),
            P(("row", "seq")),
            P(("row", "seq"), None),
            P(("row", "seq"), None),
            P(("row", "seq"), None),
            P(("row", "seq"), None),
            P(("row", "seq")),
            P(("row", "seq"), None),
            P(("row", "seq"), None),
            P(("row", "seq"), None),
        ),
        out_specs=(
            P("row", "seq", None),
            P("row", "seq", None),
            P(("row", "seq")),
            P(("row", "seq"), None),
            P(("row", "seq"), None),
            P(("row", "seq"), None),
            P(("row", "seq"), None),
            P(("row", "seq")),
            P(("row", "seq"), None),
            P(("row", "seq"), None),
            P(("row", "seq"), None),
        ),
        check_vma=False,
    )
```

```python
import math

import jax
import jax.numpy as jnp
import numpy as np
from jax import lax
from jax.experimental import pallas as pl
from jax.experimental.pallas import tpu as pltpu
from jax.sharding import PartitionSpec as P

HEAD_DIM = 64


EPSILON = 1e-05
THETA = 500000.0


def rope_table(head_size):
    half_size = head_size // 2
    plain = THETA ** (-(np.arange(half_size) * 2.0) / head_size)
    factor, low_factor, high_factor, old_span = (32.0, 1.0, 4.0, 8192.0)
    wavelength = 2.0 * math.pi / plain
    smooth = (old_span / wavelength - low_factor) / (high_factor - low_factor)
    blended = (1.0 - smooth) * plain / factor + smooth * plain
    return np.where(
        wavelength < old_span / high_factor,
        plain,
        np.where(wavelength > old_span / low_factor, plain / factor, blended),
    )


def norm_scale(values):
    return lax.rsqrt(jnp.mean(values * values, axis=-1, keepdims=True) + EPSILON)


def norm_back(grad_normed, normed, scale):
    return scale * (grad_normed - normed * jnp.mean(grad_normed * normed, axis=-1, keepdims=True))


def rotate(values, cosine, sine):
    half_size = values.shape[-1] // 2
    turned = jnp.concatenate([-values[..., half_size:], values[..., :half_size]], axis=-1)
    return values * cosine + turned * sine


def rotate_back(grad, cosine, sine):
    half_size = grad.shape[-1] // 2
    turned = grad * sine
    return grad * cosine + jnp.concatenate(
        [turned[..., half_size:], -turned[..., :half_size]], axis=-1
    )


def contract_last(left, right):
    return lax.dot_general(
        left, right, (((1,), (1,)), ((), ())), preferred_element_type=jnp.float32
    )


def contract_first(left, right):
    return lax.dot_general(
        left, right, (((0,), (0,)), ((), ())), preferred_element_type=jnp.float32
    )


def gathered_layer(
    tokens,
    cotangent,
    doc_lengths,
    attn_gain,
    w_query,
    w_key,
    w_value,
    w_out,
    mlp_gain,
    w_gate,
    w_up,
    w_down,
):
    rows, stretch, width = tokens.shape
    count = rows * stretch
    key_width = w_key.shape[1]
    hidden_width = w_gate.shape[1]
    key_heads = key_width // HEAD_DIM
    heads = width // HEAD_DIM
    groups = heads // key_heads
    length = stretch * lax.axis_size("seq")
    block = math.gcd(length, 512)
    scale = HEAD_DIM ** (-0.5)
    table = jnp.asarray(rope_table(HEAD_DIM), jnp.float32)
    place = lax.axis_index("seq") * stretch + jnp.arange(stretch, dtype=jnp.int32)
    live_blocks = ((lax.axis_index("seq") + 1) * stretch + block - 1) // block
    ends = jnp.cumsum(doc_lengths, axis=1)
    first = jnp.max(
        jnp.where(ends[:, None, :] <= place[None, :, None], ends[:, None, :], 0), axis=2
    )
    angle = (place[None, :] - first).astype(jnp.float32)[..., None] * table
    cosine = jnp.concatenate([jnp.cos(angle), jnp.cos(angle)], axis=-1)[:, :, None, :]
    sine = jnp.concatenate([jnp.sin(angle), jnp.sin(angle)], axis=-1)[:, :, None, :]
    inputs = tokens.reshape(count, width).astype(jnp.float32)
    scale_one = norm_scale(inputs)
    normed_one = inputs * scale_one
    gain_piece = lax.all_gather(attn_gain, ("row", "seq"), axis=0, tiled=True)
    query_piece = lax.all_gather(w_query, ("row", "seq"), axis=0, tiled=True)
    key_piece = lax.all_gather(w_key, ("row", "seq"), axis=0, tiled=True)
    value_piece = lax.all_gather(w_value, ("row", "seq"), axis=0, tiled=True)
    hidden_piece = (normed_one * gain_piece.astype(jnp.float32)).astype(jnp.bfloat16)
    query_sum = jnp.dot(hidden_piece, query_piece, preferred_element_type=jnp.float32)
    key_sum = jnp.dot(hidden_piece, key_piece, preferred_element_type=jnp.float32)
    value_sum = jnp.dot(hidden_piece, value_piece, preferred_element_type=jnp.float32)
    hidden_one = hidden_piece
    queries = rotate(query_sum.reshape(rows, stretch, heads, HEAD_DIM), cosine, sine).astype(
        jnp.bfloat16
    )
    keys = rotate(key_sum.reshape(rows, stretch, key_heads, HEAD_DIM), cosine, sine).astype(
        jnp.bfloat16
    )
    values = value_sum.astype(jnp.bfloat16)
    query_grouped = queries.reshape(rows, stretch, key_heads, groups, HEAD_DIM)

    def gather_keys():
        return (
            lax.all_gather(keys.reshape(rows, stretch, key_width), "seq", axis=1, tiled=True),
            lax.all_gather(values.reshape(rows, stretch, key_width), "seq", axis=1, tiled=True),
        )

    key_all, value_all = gather_keys()

    def block_rows(source, index):
        return lax.dynamic_slice_in_dim(source, index * block, block, 1).reshape(
            rows, block, key_heads, HEAD_DIM
        )

    def block_scores(key_block, index):
        raw = jnp.einsum(
            "rqhgd,rkhd->rhgqk", query_grouped, key_block, preferred_element_type=jnp.float32
        )
        key_place = index * block + jnp.arange(block, dtype=jnp.int32)
        allowed = (key_place[None, None, :] <= place[None, :, None]) & (
            key_place[None, None, :] >= first[:, :, None]
        )
        return jnp.where(allowed[:, None, None], raw * scale, -1e30)

    def total_step(index, carry):
        running_max, running_total = carry
        scores = block_scores(block_rows(key_all, index), index)
        new_max = jnp.maximum(running_max, jnp.max(scores, axis=-1))
        new_total = running_total * jnp.exp(running_max - new_max) + jnp.sum(
            jnp.exp(scores - new_max[..., None]), axis=-1
        )
        return (new_max, new_total)

    stat_shape = (rows, key_heads, groups, stretch)
    running_max, running_total = lax.fori_loop(
        0,
        live_blocks,
        total_step,
        (jnp.full(stat_shape, -1e30, jnp.float32), jnp.zeros(stat_shape, jnp.float32)),
    )
    log_total = running_max + jnp.log(running_total)

    def mix_step(index, mixed_sum):
        probs = jnp.exp(block_scores(block_rows(key_all, index), index) - log_total[..., None])
        return mixed_sum + jnp.einsum(
            "rhgqk,rkhd->rqhgd",
            probs.astype(jnp.bfloat16),
            block_rows(value_all, index),
            preferred_element_type=jnp.float32,
        )

    mixed_sum = lax.fori_loop(
        0,
        live_blocks,
        mix_step,
        jnp.zeros((rows, stretch, key_heads, groups, HEAD_DIM), jnp.float32),
    )
    mixed = mixed_sum.reshape(count, width).astype(jnp.bfloat16)
    attn_branch = jnp.dot(
        mixed,
        lax.all_gather(w_out, ("row", "seq"), axis=0, tiled=True),
        preferred_element_type=jnp.float32,
    )
    middle = inputs + attn_branch
    scale_two = norm_scale(middle)
    normed_two = middle * scale_two
    gain_piece = lax.all_gather(mlp_gain, ("row", "seq"), axis=0, tiled=True)
    gate_piece = lax.all_gather(w_gate, ("row", "seq"), axis=0, tiled=True)
    up_piece = lax.all_gather(w_up, ("row", "seq"), axis=0, tiled=True)
    hidden_piece = (normed_two * gain_piece.astype(jnp.float32)).astype(jnp.bfloat16)
    gate_sum, up_sum, hidden_two = (
        jnp.dot(hidden_piece, gate_piece, preferred_element_type=jnp.float32),
        jnp.dot(hidden_piece, up_piece, preferred_element_type=jnp.float32),
        hidden_piece,
    )
    sigma = jax.nn.sigmoid(gate_sum)
    silu_value = gate_sum * sigma
    active = (silu_value * up_sum).astype(jnp.bfloat16)
    mlp_branch = jnp.dot(
        active,
        lax.all_gather(w_down, ("row", "seq"), axis=0, tiled=True),
        preferred_element_type=jnp.float32,
    )
    output = (middle + mlp_branch).astype(jnp.bfloat16).reshape(rows, stretch, width)
    grad_out_low = cotangent.reshape(count, width)
    grad_active = contract_last(
        grad_out_low, lax.all_gather(w_down, ("row", "seq"), axis=0, tiled=True)
    )
    grad_down = lax.psum_scatter(
        contract_first(active, grad_out_low), ("row", "seq"), scatter_dimension=0, tiled=True
    )
    grad_up_low = (grad_active * silu_value).astype(jnp.bfloat16)
    grad_gate_low = (grad_active * up_sum * sigma * (1.0 + gate_sum * (1.0 - sigma))).astype(
        jnp.bfloat16
    )
    both_grads = jnp.concatenate([grad_gate_low, grad_up_low], axis=1)
    gain_piece = lax.all_gather(mlp_gain, ("row", "seq"), axis=0, tiled=True)
    gate_piece = lax.all_gather(w_gate, ("row", "seq"), axis=0, tiled=True)
    up_piece = lax.all_gather(w_up, ("row", "seq"), axis=0, tiled=True)
    grad_piece = contract_last(grad_gate_low, gate_piece) + contract_last(grad_up_low, up_piece)
    normed_piece = normed_two
    grad_normed_two = grad_piece * gain_piece.astype(jnp.float32)
    grad_gain_two = jnp.sum(normed_piece * grad_piece, axis=0)
    grad_gate_up = lax.psum_scatter(
        contract_first(hidden_two, both_grads), ("row", "seq"), scatter_dimension=0, tiled=True
    )
    grad_gate = grad_gate_up[:, :hidden_width]
    grad_up = grad_gate_up[:, hidden_width:]
    grad_middle = grad_out_low.astype(jnp.float32) + norm_back(
        grad_normed_two, normed_two, scale_two
    )
    grad_branch_low = grad_middle.astype(jnp.bfloat16)
    grad_mixed = contract_last(
        grad_branch_low, lax.all_gather(w_out, ("row", "seq"), axis=0, tiled=True)
    ).astype(jnp.bfloat16)
    grad_out = lax.psum_scatter(
        contract_first(mixed, grad_branch_low), ("row", "seq"), scatter_dimension=0, tiled=True
    )
    grad_grouped = grad_mixed.reshape(rows, stretch, key_heads, groups, HEAD_DIM)
    key_back, value_back = gather_keys()

    def delta_step(index, total):
        probs = jnp.exp(block_scores(block_rows(key_back, index), index) - log_total[..., None])
        grad_probs = jnp.einsum(
            "rqhgd,rkhd->rhgqk",
            grad_grouped,
            block_rows(value_back, index),
            preferred_element_type=jnp.float32,
        )
        return total + jnp.sum(probs * grad_probs, axis=-1)

    delta = lax.fori_loop(0, live_blocks, delta_step, jnp.zeros(stat_shape, jnp.float32))

    def grad_step(index, carry):
        grad_queries, grad_key_all, grad_value_all = carry
        key_block = block_rows(key_back, index)
        probs = jnp.exp(block_scores(key_block, index) - log_total[..., None])
        grad_probs = jnp.einsum(
            "rqhgd,rkhd->rhgqk",
            grad_grouped,
            block_rows(value_back, index),
            preferred_element_type=jnp.float32,
        )
        grad_raw = (scale * probs * (grad_probs - delta[..., None])).astype(jnp.bfloat16)
        grad_queries = grad_queries + jnp.einsum(
            "rhgqk,rkhd->rqhgd", grad_raw, key_block, preferred_element_type=jnp.float32
        )
        key_part = jnp.einsum(
            "rhgqk,rqhgd->rkhd", grad_raw, query_grouped, preferred_element_type=jnp.float32
        ).reshape(rows, block, key_width)
        value_part = jnp.einsum(
            "rhgqk,rqhgd->rkhd",
            probs.astype(jnp.bfloat16),
            grad_grouped,
            preferred_element_type=jnp.float32,
        ).reshape(rows, block, key_width)
        return (
            grad_queries,
            lax.dynamic_update_slice_in_dim(grad_key_all, key_part, index * block, 1),
            lax.dynamic_update_slice_in_dim(grad_value_all, value_part, index * block, 1),
        )

    grad_queries, grad_key_all, grad_value_all = lax.fori_loop(
        0,
        live_blocks,
        grad_step,
        (
            jnp.zeros((rows, stretch, key_heads, groups, HEAD_DIM), jnp.float32),
            jnp.zeros((rows, length, key_width), jnp.float32),
            jnp.zeros((rows, length, key_width), jnp.float32),
        ),
    )
    grad_key_sum, grad_value_sum = (
        lax.psum_scatter(
            grad_key_all.astype(jnp.bfloat16), "seq", scatter_dimension=1, tiled=True
        ).astype(jnp.float32),
        lax.psum_scatter(
            grad_value_all.astype(jnp.bfloat16), "seq", scatter_dimension=1, tiled=True
        ).astype(jnp.float32),
    )
    grad_query_low = (
        rotate_back(grad_queries.reshape(rows, stretch, heads, HEAD_DIM), cosine, sine)
        .reshape(count, width)
        .astype(jnp.bfloat16)
    )
    grad_key_low = (
        rotate_back(grad_key_sum.reshape(rows, stretch, key_heads, HEAD_DIM), cosine, sine)
        .reshape(count, key_width)
        .astype(jnp.bfloat16)
    )
    grad_value_low = grad_value_sum.reshape(count, key_width).astype(jnp.bfloat16)
    gain_piece = lax.all_gather(attn_gain, ("row", "seq"), axis=0, tiled=True)
    query_piece = lax.all_gather(w_query, ("row", "seq"), axis=0, tiled=True)
    key_piece = lax.all_gather(w_key, ("row", "seq"), axis=0, tiled=True)
    value_piece = lax.all_gather(w_value, ("row", "seq"), axis=0, tiled=True)
    grad_piece = (
        contract_last(grad_query_low, query_piece)
        + contract_last(grad_key_low, key_piece)
        + contract_last(grad_value_low, value_piece)
    )
    normed_piece = normed_one
    grad_normed_one = grad_piece * gain_piece.astype(jnp.float32)
    grad_gain_one = jnp.sum(normed_piece * grad_piece, axis=0)
    grad_query, grad_key, grad_value, grad_attn_gain, grad_mlp_gain = (
        lax.psum_scatter(
            contract_first(hidden_one, grad_query_low),
            ("row", "seq"),
            scatter_dimension=0,
            tiled=True,
        ),
        lax.psum_scatter(
            contract_first(hidden_one, grad_key_low),
            ("row", "seq"),
            scatter_dimension=0,
            tiled=True,
        ),
        lax.psum_scatter(
            contract_first(hidden_one, grad_value_low),
            ("row", "seq"),
            scatter_dimension=0,
            tiled=True,
        ),
        lax.psum_scatter(grad_gain_one, ("row", "seq"), scatter_dimension=0, tiled=True),
        lax.psum_scatter(grad_gain_two, ("row", "seq"), scatter_dimension=0, tiled=True),
    )
    grad_tokens = (grad_middle + norm_back(grad_normed_one, normed_one, scale_one)).reshape(
        rows, stretch, width
    )
    return (
        output,
        grad_tokens,
        grad_attn_gain,
        grad_query,
        grad_key,
        grad_value,
        grad_out,
        grad_mlp_gain,
        grad_gate,
        grad_up,
        grad_down,
    )


MESH = pl.DeviceIdType.MESH
VMEM_LIMIT = 60 * 1024 * 1024
PARTS = 2


def neighbours():
    row, seq = lax.axis_index("row"), lax.axis_index("seq")
    row_size, seq_size = lax.axis_size("row"), lax.axis_size("seq")
    return dict(
        row=row,
        seq=seq,
        z=seq // 2,
        core=seq % 2,
        up=(row, (seq + 2) % seq_size),
        down=(row, (seq + seq_size - 2) % seq_size),
        pair=(row, seq + 1 - 2 * (seq % 2)),
        side=(row + 1 - 2 * (row % 2), seq),
        across=((row + row_size // 2) % row_size, seq),
        corner=((row + 1 - 2 * (row % 2) + row_size // 2) % row_size, seq),
        side_row=row + 1 - 2 * (row % 2),
        across_row=(row + row_size // 2) % row_size,
    )


def greet(peers, route=None):
    barrier = pltpu.get_barrier_semaphore()
    for peer in peers:
        pl.semaphore_signal(barrier, inc=1, device_id=peer, device_id_type=MESH)
    amount = len(peers)
    if route is not None:
        moves, *ends = route

        @pl.when(moves)
        def _():
            for peer in ends:
                pl.semaphore_signal(barrier, inc=1, device_id=peer, device_id_type=MESH)

        amount = amount + jnp.where(moves, len(ends), 0)
    pl.semaphore_wait(barrier, amount)


def send(source, target, sems, index, peer):
    copy = pltpu.make_async_remote_copy(
        src_ref=source,
        dst_ref=target,
        send_sem=sems[0].at[index],
        recv_sem=sems[1].at[index],
        device_id=peer,
        device_id_type=MESH,
    )
    copy.start()
    return copy


def sem_pairs(amount):
    return [pltpu.SemaphoreType.DMA((amount,)), pltpu.SemaphoreType.DMA((amount,))]


def by_rows(amount, step, body):
    def one(i, carry):
        body(pl.ds(pl.multiple_of(i * step, step), step))
        return carry

    lax.fori_loop(0, amount // step, one, 0)


def copy_rows(target, source):
    def one(rows):
        target[rows] = source[rows]

    by_rows(source.shape[0], 16, one)


def gather_seq_steps(here, whole, stretch, pair_sems, ring_sems):
    seq, chips = here["seq"], lax.axis_size("seq") // 2
    seq_size = 2 * chips
    piece = stretch // PARTS
    rings, pairs, last = [], [], {}

    def spot(owner, part):
        return pl.ds(pl.multiple_of(owner * stretch + part * piece, piece), piece)

    def ring(step, part):
        owners = (seq + seq_size - 2 * step) % seq_size, (seq + 2 * step) % seq_size
        for half, peer in ((0, "up"), (1, "down")):
            view = whole.at[half, spot(owners[half], part)]
            slot = (step * PARTS + part) * 2 + half
            if step > 0:
                last[half, part].wait_recv()
            if step < chips - 1:
                last[half, part] = send(view, view, ring_sems, slot, here[peer])
                rings.append(last[half, part])
            pairs.append(send(view, view, pair_sems, slot, here["pair"]))

    def both(step):
        for part in range(PARTS):
            ring(step, part)

    def finish():
        for copy in pairs:
            copy.wait()
        for copy in rings:
            copy.wait_send()

    return ring, [lambda step=step: both(step) for step in range(chips)] + [finish]


def reduce_seq_steps(here, part, stretch, pair_in, total, ring_in, pair_sems, ring_sems, done):
    z, core, chips = here["z"], here["core"], lax.axis_size("seq") // 2
    piece = stretch // PARTS
    copies, pair_copies, last = [], {}, {}
    order = [spot for t in range(chips - 1) for spot in ((chips - 1 - t, 0), (1 + t, 1))]
    order += [(0, 0), (0, 1)]

    def place(far):
        return (z + far) % chips

    def each(number, body):
        def one(rows):
            body(pl.ds(pl.multiple_of(number * piece + rows.start, 16), 16))

        by_rows(piece, 16, one)

    def pair_sum(far, half, number):
        chip = place(far)
        base = (2 * chip + core) * stretch
        if number == 0:
            pair_copies[far, half].wait_recv()

        def add(rows):
            mine = part[half, pl.ds(pl.multiple_of(base + rows.start, 16), 16)]
            other = pair_in[chip, half, rows]
            total[chip, half, rows] = (
                mine.astype(jnp.float32) + other.astype(jnp.float32)
            ).astype(jnp.bfloat16)

        each(number, add)

    def ring_send(step, half, number):
        far, peer = ((chips - 1 - step, "up"), (1 + step, "down"))[half]
        chip = place(far)
        if step == 0:
            pair_sum(far, half, number)
        else:
            last[half, number].wait_recv()
            arrived = ring_in.at[step - 1, half]

            def add(rows):
                total[chip, half, rows] = (
                    total[chip, half, rows].astype(jnp.float32)
                    + arrived[rows].astype(jnp.float32)
                ).astype(jnp.bfloat16)

            each(number, add)
        rows = pl.ds(number * piece, piece)
        last[half, number] = send(
            total.at[chip, half, rows],
            ring_in.at[step, half, rows],
            ring_sems,
            (step * PARTS + number) * 2 + half,
            here[peer],
        )
        copies.append(last[half, number])

    def ring(step):
        for number in range(PARTS):
            for half in range(2):
                ring_send(step, half, number)

    def first_step():
        for index, (far, half) in enumerate(order):
            chip = place(far)
            spot = pl.ds(pl.multiple_of((2 * chip + 1 - core) * stretch, stretch), stretch)
            pair_copies[far, half] = send(
                part.at[half, spot], pair_in.at[chip, half], pair_sems, index, here["pair"]
            )
        ring(0)
        for far, half in order[2:]:
            for number in range(PARTS):
                pair_sum(far, half, number)

    def finish(number):
        for half in range(2):
            last[half, number].wait_recv()
            arrived = ring_in.at[chips - 2, half]

            def close(rows):
                done(
                    half,
                    rows,
                    total[z, half, rows].astype(jnp.float32) + arrived[rows].astype(jnp.float32),
                )

            each(number, close)

    def drain():
        for copy in list(pair_copies.values()) + copies:
            copy.wait_send()

    steps = [first_step] + [lambda step=step: ring(step) for step in range(1, chips - 1)]
    return steps, finish, drain


def gather_row_steps(here, own, whole, sems):
    half = whole.shape[1] // 2
    row, side, across = here["row"], here["side_row"], here["across_row"]
    state = []

    def first_step():
        state.append(send(own, whole.at[row], sems, 0, here["side"]))
        state.append(send(own, whole.at[row], sems, 1, here["across"]))

    def second_step():
        low, high = pl.ds(0, half), pl.ds(half, half)
        state[0].wait_recv()
        state.append(send(whole.at[side, low], whole.at[side, low], sems, 2, here["across"]))
        state[1].wait_recv()
        state.append(send(whole.at[across, high], whole.at[across, high], sems, 3, here["side"]))

    def finish():
        for copy in state[2:]:
            copy.wait_recv()
        for copy in state:
            copy.wait_send()

    return [first_step, second_step, finish]


def reduce_row_steps(here, source, part, inbox, sums, sems, done):
    half = part.shape[1] // 2
    row, side, across = here["row"], here["side_row"], here["across_row"]
    corner = (side + 2) % 4
    state = []

    def first_step():
        low, high = pl.ds(0, half), pl.ds(half, half)
        for index, (owner, rows, peer) in enumerate(
            (
                (corner, low, "side"),
                (corner, high, "across"),
                (side, low, "side"),
                (across, high, "across"),
            )
        ):
            state.append(send(source.at[owner, rows], inbox.at[index], sems, index, here[peer]))

    def add(owner, offset, index):
        def run(rows):
            spot = pl.ds(pl.multiple_of(offset + rows.start, 16), 16)
            sums[index, rows] = (
                part[owner, spot].astype(jnp.float32) + inbox[index, rows].astype(jnp.float32)
            ).astype(jnp.bfloat16)

        by_rows(half, 16, run)

    def second_step():
        state[0].wait_recv()
        add(across, 0, 0)
        state.append(send(sums.at[0], inbox.at[4], sems, 4, here["across"]))
        state[1].wait_recv()
        add(side, half, 1)
        state.append(send(sums.at[1], inbox.at[5], sems, 5, here["side"]))
        state[2].wait_recv()
        state[3].wait_recv()

    def finish():
        for offset, one, two in ((0, 2, 4), (half, 3, 5)):
            state[two].wait_recv()

            def close(rows):
                spot = pl.ds(pl.multiple_of(offset + rows.start, 16), 16)
                done(
                    spot,
                    part[row, spot].astype(jnp.float32)
                    + inbox[one, rows].astype(jnp.float32)
                    + inbox[two, rows].astype(jnp.float32),
                )

            by_rows(half, 16, close)
        for copy in state:
            copy.wait_send()

    return [first_step, second_step, finish]


def exchange_seq(here, source, target_of, sems):
    seq, seq_size = here["seq"], lax.axis_size("seq")
    copies = []
    for far in range(1, seq_size):
        dest = (seq + far) % seq_size
        copies.append(
            send(source.at[dest], target_of(seq), sems, far - 1, (here["row"], dest))
        )
    return copies


def seq_peers(here):
    seq_size = lax.axis_size("seq")
    return [(here["row"], (here["seq"] + far) % seq_size) for far in range(1, seq_size)]


def call(kernel, args, out_shape, scratch, collective_id, far_in=(), far_out=()):
    near, far = (pl.BlockSpec(memory_space=space) for space in (pltpu.VMEM, pl.ANY))
    return pl.pallas_call(
        kernel,
        out_shape=out_shape,
        in_specs=[far if i in far_in else near for i in range(len(args))],
        out_specs=[far if i in far_out else near for i in range(len(out_shape))],
        scratch_shapes=scratch,
        compiler_params=pltpu.CompilerParams(
            collective_id=collective_id, has_side_effects=True, vmem_limit_bytes=VMEM_LIMIT
        ),
    )(*args)


def low(*shape):
    return jax.ShapeDtypeStruct(shape, jnp.bfloat16)


def full(*shape):
    return jax.ShapeDtypeStruct(shape, jnp.float32)


def shift_route(here):
    row_size, seq_size = lax.axis_size("row"), lax.axis_size("seq")
    index = here["row"] * seq_size + here["seq"]
    origin = here["seq"] * row_size + here["row"]
    target = index % row_size, index // row_size
    return target, (origin // seq_size, origin % seq_size), index != origin


def open_kernel(
    tokens, heads_pack, w_gate, w_up, out_piece,
    all_tokens, heads_all, units_pack, out_all,
    pair_a, pair_b, ring_a, ring_b, heads_a, heads_b, row_a, row_b, out_a, out_b, shift_a, shift_b,
):
    here = neighbours()
    seq, row = here["seq"], here["row"]
    stretch = tokens.shape[1]
    piece = heads_pack.shape[1]
    target, origin, moves = shift_route(here)
    greet(seq_peers(here) + [here["side"], here["across"]], (moves, target, origin))

    def spot(owner):
        return pl.ds(pl.multiple_of(owner * piece, piece), piece)

    def shift():
        return pltpu.make_async_remote_copy(
            src_ref=out_piece,
            dst_ref=out_all.at[target[0]],
            send_sem=shift_a.at[0],
            recv_sem=shift_b.at[0],
            device_id=target,
            device_id_type=MESH,
        )

    heads = exchange_seq(here, heads_pack, lambda s: heads_all.at[row, spot(s)], (heads_a, heads_b))

    @pl.when(moves)
    def _():
        shift().start()

    for half in range(2):
        own = pl.ds(pl.multiple_of(seq * stretch, stretch), stretch)
        copy_rows(all_tokens.at[half, own], tokens.at[half])
    gather_out = gather_row_steps(here, out_all.at[row], out_all, (out_a, out_b))
    gather_heads = gather_row_steps(here, heads_all.at[row], heads_all, (row_a, row_b))
    _, steps = gather_seq_steps(here, all_tokens, stretch, (pair_a, pair_b), (ring_a, ring_b))
    steps[0]()
    copy_rows(heads_all.at[row, spot(seq)], heads_pack.at[seq])

    @pl.when(jnp.logical_not(moves))
    def _():
        copy_rows(out_all.at[row], out_piece)

    for copy in heads:
        copy.wait_recv()
    gather_heads[0]()

    @pl.when(moves)
    def _():
        shift().wait()

    gather_out[0]()
    seq_size, row_size = lax.axis_size("seq"), lax.axis_size("row")
    block = w_gate.shape[1] // (seq_size * row_size)
    for number, weight in enumerate((w_gate, w_up)):
        for r in range(row_size):
            for s in range(seq_size):
                source = (r * seq_size + s) * block
                place = (number * row_size + r) * block
                units_pack[s, :, place : place + block] = weight[:, source : source + block]
    steps[1]()
    gather_heads[1]()
    gather_out[1]()
    for step in steps[2:]:
        step()
    gather_heads[2]()
    gather_out[2]()
    for copy in heads:
        copy.wait_send()


def middle_kernel(
    branch, tokens, gain, units_mine,
    middle, hidden, units_all,
    pair_in, total, ring_in, pair_a, pair_b, ring_a, ring_b,
    gpair_a, gpair_b, gring_a, gring_b, row_a, row_b, own_sem,
):
    here = neighbours()
    seq = here["seq"]
    stretch = tokens.shape[1]
    own_copy = pltpu.make_async_copy(units_mine, units_all.at[here["row"]], own_sem)
    own_copy.start()
    greet([here["up"], here["down"], here["pair"], here["side"], here["across"]])

    def done(half, rows, value):
        value = tokens[half, rows].astype(jnp.float32) + value
        middle[half, rows] = value
        normed = value * norm_scale(value)
        spot = pl.ds(pl.multiple_of(seq * stretch + rows.start, 16), 16)
        hidden[half, spot] = (normed * gain[...]).astype(jnp.bfloat16)

    reduce_steps, finish, drain = reduce_seq_steps(
        here, branch, stretch, pair_in, total, ring_in, (pair_a, pair_b), (ring_a, ring_b), done
    )
    units = gather_row_steps(here, units_mine, units_all, (row_a, row_b))
    units[0]()
    for step in reduce_steps:
        step()
    ring, gather_steps = gather_seq_steps(
        here, hidden, stretch, (gpair_a, gpair_b), (gring_a, gring_b)
    )
    for number in range(PARTS):
        finish(number)
        ring(0, number)
    gather_steps[1]()
    units[1]()
    for step in gather_steps[2:]:
        step()
    units[2]()
    drain()
    own_copy.wait()


def back_kernel(
    grad_part, cotangent, middle, gain, units_part,
    grad_middle, grad_low, gain_grad, units_out,
    pair_in, total, ring_in, inbox, sums, units_near, pair_a, pair_b, ring_a, ring_b,
    gpair_a, gpair_b, gring_a, gring_b, row_a, row_b, near_sem,
):
    here = neighbours()
    seq = here["seq"]
    stretch = cotangent.shape[1]
    near_copy = pltpu.make_async_copy(units_part, units_near, near_sem)
    near_copy.start()
    greet([here["up"], here["down"], here["pair"], here["side"], here["across"]])
    gain_grad[...] = jnp.zeros_like(gain_grad)

    def done(half, rows, grad):
        value = middle[half, rows]
        scale = norm_scale(value)
        normed = value * scale
        gain_grad[...] += jnp.sum(normed * grad, axis=0, keepdims=True)
        back = cotangent[half, rows].astype(jnp.float32) + norm_back(
            grad * gain[...], normed, scale
        )
        grad_middle[half, rows] = back
        spot = pl.ds(pl.multiple_of(seq * stretch + rows.start, 16), 16)
        grad_low[half, spot] = back.astype(jnp.bfloat16)

    def done_units(rows, value):
        units_out[rows] = value.astype(jnp.bfloat16)

    reduce_steps, finish, drain = reduce_seq_steps(
        here, grad_part, stretch, pair_in, total, ring_in, (pair_a, pair_b), (ring_a, ring_b), done
    )
    units = reduce_row_steps(
        here, units_part, units_near, inbox, sums, (row_a, row_b), done_units
    )
    units[0]()
    for step in reduce_steps:
        step()
    ring, gather_steps = gather_seq_steps(
        here, grad_low, stretch, (gpair_a, gpair_b), (gring_a, gring_b)
    )
    for number in range(PARTS):
        finish(number)
        ring(0, number)
    near_copy.wait()
    units[1]()
    for step in gather_steps[1:]:
        step()
    units[2]()
    drain()


def sum_small(here, mine, inbox, sems):
    slot = 0
    stages = [seq_peers(here), [here["side"], here["across"], here["corner"]]]
    copies = []
    for number, stage in enumerate(stages):
        sent = [
            send(mine.at[number], inbox.at[slot + i], sems, slot + i, peer)
            for i, peer in enumerate(stage)
        ]
        value = mine[number]
        for i, copy in enumerate(sent):
            copy.wait_recv()
            value = value + inbox[slot + i]
        mine[number + 1] = value
        slot += len(stage)
        copies += sent
    for copy in copies:
        copy.wait_send()
    return slot


def close_kernel(
    grad_part, tokens, grad_middle, gain, gain_two, heads_part,
    grad_tokens, gain_sums, heads_out,
    heads_mine, pair_in, total, ring_in, inbox, sums, small, small_in,
    pair_a, pair_b, ring_a, ring_b, row_a, row_b, heads_a, heads_b, small_a, small_b,
):
    here = neighbours()
    seq, chips = here["seq"], lax.axis_size("seq") // 2
    stretch = tokens.shape[1]
    greet(seq_peers(here) + [here["side"], here["across"], here["corner"]])
    small[0, 0:1] = jnp.zeros_like(small[0, 0:1])
    small[0, 1:2] = gain_two[...]

    def done(half, rows, grad):
        value = tokens[half, rows].astype(jnp.float32)
        scale = norm_scale(value)
        normed = value * scale
        small[0, 0:1] += jnp.sum(normed * grad, axis=0, keepdims=True)
        grad_tokens[half, rows] = grad_middle[half, rows] + norm_back(
            grad * gain[...], normed, scale
        )

    piece = heads_out.shape[1]

    def done_heads(rows, value):
        heads_mine[rows] = value.astype(jnp.bfloat16)

    reduce_steps, finish, drain = reduce_seq_steps(
        here, grad_part, stretch, pair_in, total, ring_in, (pair_a, pair_b), (ring_a, ring_b), done
    )
    heads = reduce_row_steps(here, heads_part, heads_part, inbox, sums, (row_a, row_b), done_heads)
    heads[0]()
    reduce_steps[0]()
    heads[1]()
    for step in reduce_steps[1:]:
        step()
    heads[2]()
    copies = []
    for far in range(1, 2 * chips):
        dest = (seq + far) % (2 * chips)
        rows = pl.ds(pl.multiple_of(dest * piece, piece), piece)
        copies.append(
            send(
                heads_mine.at[rows], heads_out.at[seq], (heads_a, heads_b), far - 1,
                (here["row"], dest),
            )
        )
    for number in range(PARTS):
        finish(number)
    copy_rows(heads_out.at[seq], heads_mine.at[pl.ds(pl.multiple_of(seq * piece, piece), piece)])
    sum_small(here, small, small_in, (small_a, small_b))
    gain_sums[...] = small[2]
    for copy in copies:
        copy.wait()
    drain()


def seq_scratch(chips, stretch, width):
    return [
        pltpu.VMEM((chips, 2, stretch, width), jnp.bfloat16),
        pltpu.VMEM((chips, 2, stretch, width), jnp.bfloat16),
        pltpu.VMEM((chips - 1, 2, stretch, width), jnp.bfloat16),
    ]


def row_scratch(pieces, columns):
    return [
        pltpu.VMEM((6, pieces // 2, columns), jnp.bfloat16),
        pltpu.VMEM((2, pieces // 2, columns), jnp.bfloat16),
    ]


def unpack_units(grads, row_size):
    seq_size, rows, columns = grads.shape
    block = columns // 2 // row_size

    def kernel(gate, up, gate_out, up_out):
        for source, target in ((gate, gate_out), (up, up_out)):
            for s in range(seq_size):
                target[:, s * block : (s + 1) * block] = source[s].astype(jnp.float32)

    whole = full(rows, seq_size * columns // 2)
    return pl.pallas_call(
        kernel,
        grid=(row_size,),
        out_shape=[whole, whole],
        in_specs=[
            pl.BlockSpec((seq_size, rows, block), lambda r: (0, 0, r)),
            pl.BlockSpec((seq_size, rows, block), lambda r: (0, 0, row_size + r)),
        ],
        out_specs=[pl.BlockSpec((rows, seq_size * block), lambda r: (0, r))] * 2,
    )(grads, grads)


def unpack_heads(grads, query_width, key_width):
    seq_size, rows, _ = grads.shape

    def kernel(source, query, key, value):
        start = 0
        for target, width in ((query, query_width), (key, key_width), (value, key_width)):
            target[...] = jnp.concatenate(
                [source[s, :, start : start + width].astype(jnp.float32) for s in range(seq_size)],
                axis=1,
            )
            start += width

    return pl.pallas_call(
        kernel,
        out_shape=[full(rows, seq_size * w) for w in (query_width, key_width, key_width)],
    )(grads)


BOTH = ("row", "seq")


def gather(piece, axis_name, axis):
    return lax.all_gather(piece, axis_name, axis=axis, tiled=True)


def scatter(whole, axis_name, axis):
    return lax.psum_scatter(whole, axis_name, scatter_dimension=axis, tiled=True)


def sharded_layer(
    tokens,
    cotangent,
    doc_lengths,
    attn_gain,
    w_query,
    w_key,
    w_value,
    w_out,
    mlp_gain,
    w_gate,
    w_up,
    w_down,
):
    row_size, seq_size = lax.axis_size("row"), lax.axis_size("seq")
    rows, stretch, width = tokens.shape
    length = stretch * seq_size
    count = rows * length
    piece_rows = w_query.shape[0]
    key_heads = w_key.shape[1] // HEAD_DIM // seq_size
    heads = w_query.shape[1] // HEAD_DIM // seq_size
    groups = heads // key_heads
    query_width, key_width = heads * HEAD_DIM, key_heads * HEAD_DIM
    unit_block = w_down.shape[0]
    units = unit_block * row_size
    scale = HEAD_DIM ** (-0.5)

    place = jnp.arange(length, dtype=jnp.int32)
    ends = jnp.cumsum(doc_lengths, axis=1)
    first = jnp.max(
        jnp.where(ends[:, None, :] <= place[None, :, None], ends[:, None, :], 0), axis=2
    )
    table = jnp.asarray(rope_table(HEAD_DIM), jnp.float32)
    angle = (place[None, :] - first).astype(jnp.float32)[..., None] * table
    cosine = jnp.concatenate([jnp.cos(angle), jnp.cos(angle)], axis=-1)[:, :, None, :]
    sine = jnp.concatenate([jnp.sin(angle), jnp.sin(angle)], axis=-1)[:, :, None, :]

    total = row_size * seq_size
    shift_back = [((i % row_size) * seq_size + i // row_size, i) for i in range(total)]

    def head_columns(weight, columns):
        return weight.reshape(piece_rows, seq_size, columns).transpose(1, 0, 2)

    head_width = query_width + 2 * key_width
    spare = -(head_width + 2) % 128
    gain_columns = jnp.stack([attn_gain, mlp_gain], axis=1)
    gain_columns = jnp.pad(gain_columns, ((0, 0), (0, spare)))
    heads_pack = jnp.concatenate(
        [
            head_columns(w_query, query_width),
            head_columns(w_key, key_width),
            head_columns(w_value, key_width),
            jnp.broadcast_to(gain_columns, (seq_size, piece_rows, spare + 2)),
        ],
        axis=2,
    )
    pack_width = head_width + 2 + spare
    chips = seq_size // 2
    pieces = piece_rows * seq_size
    early_cotangent = gather(cotangent[:1], "seq", 1)
    all_tokens, heads_all, units_pack, out_part = call(
        open_kernel,
        (tokens, heads_pack, w_gate, w_up, w_out),
        [
            low(rows, length, width),
            low(row_size, pieces, pack_width),
            low(seq_size, piece_rows, 2 * units),
            low(row_size, piece_rows, width),
        ],
        sem_pairs(2 * chips * PARTS) * 2 + sem_pairs(seq_size - 1) + sem_pairs(4) * 2 + sem_pairs(1),
        0,
    )
    units_mine = lax.all_to_all(units_pack, "seq", 0, 0, tiled=True).reshape(pieces, 2 * units)
    late_down, all_tokens = lax.optimization_barrier((w_down, all_tokens))
    down_part = gather(late_down, "row", 0)
    all_tokens = all_tokens.reshape(count, width)
    heads_all = heads_all.reshape(width, pack_width)
    w_qkv = heads_all[:, :head_width]
    gains = heads_all[:, head_width : head_width + 2].astype(jnp.float32).T
    out_part = out_part.reshape(query_width, width)

    inputs = all_tokens.astype(jnp.float32)
    hidden_one = (inputs * norm_scale(inputs) * gains[0]).astype(jnp.bfloat16)
    qkv = jnp.dot(hidden_one, w_qkv, preferred_element_type=jnp.float32)
    queries = rotate(
        qkv[:, :query_width].reshape(rows, length, heads, HEAD_DIM), cosine, sine
    ).astype(jnp.bfloat16).reshape(rows, length, key_heads, groups, HEAD_DIM)
    keys = rotate(
        qkv[:, query_width : query_width + key_width].reshape(rows, length, key_heads, HEAD_DIM),
        cosine,
        sine,
    ).astype(jnp.bfloat16)
    values = (
        qkv[:, query_width + key_width :]
        .astype(jnp.bfloat16)
        .reshape(rows, length, key_heads, HEAD_DIM)
    )
    raw = jnp.einsum("rqhgd,rkhd->rhgqk", queries, keys, preferred_element_type=jnp.float32)
    allowed = (place[None, None, :] <= place[None, :, None]) & (
        place[None, None, :] >= first[:, :, None]
    )
    probs = jax.nn.softmax(jnp.where(allowed[:, None, None], raw * scale, -1e30), axis=-1)
    probs_low = probs.astype(jnp.bfloat16)
    mixed = (
        jnp.einsum("rhgqk,rkhd->rqhgd", probs_low, values, preferred_element_type=jnp.float32)
        .astype(jnp.bfloat16)
        .reshape(count, query_width)
    )
    branch = jnp.dot(mixed, out_part, preferred_element_type=jnp.float32).astype(jnp.bfloat16)
    middle, hidden_two, w_units = call(
        middle_kernel,
        (branch.reshape(rows, length, width), tokens, gains[1:2], units_mine),
        [full(rows, stretch, width), low(rows, length, width), low(row_size, pieces, 2 * units)],
        seq_scratch(chips, stretch, width)
        + sem_pairs(2 * chips)
        + sem_pairs(2 * PARTS * (chips - 1))
        + sem_pairs(2 * chips * PARTS) * 2
        + sem_pairs(4)
        + [pltpu.SemaphoreType.DMA],
        1,
        far_out=(2,),
    )
    late_cotangent, hidden_two = lax.optimization_barrier((cotangent[1:], hidden_two))
    all_cotangent = jnp.concatenate([early_cotangent, gather(late_cotangent, "seq", 1)])
    all_cotangent = all_cotangent.reshape(count, width)
    hidden_two = hidden_two.reshape(count, width)
    w_units = w_units.reshape(width, 2 * units)
    both = jnp.dot(hidden_two, w_units, preferred_element_type=jnp.float32)
    gate_sum, up_sum = both[:, :units], both[:, units:]
    sigma = jax.nn.sigmoid(gate_sum)
    silu_value = gate_sum * sigma
    active = (silu_value * up_sum).astype(jnp.bfloat16)
    mlp_branch = jnp.dot(active, down_part, preferred_element_type=jnp.float32)
    mlp_branch, down_part = lax.optimization_barrier((mlp_branch.astype(jnp.bfloat16), down_part))
    mlp_branch = scatter(mlp_branch.reshape(rows, length, width), "seq", 1)
    output = (middle + mlp_branch.astype(jnp.float32)).astype(jnp.bfloat16)

    grad_active = contract_last(all_cotangent, down_part)
    grad_down = contract_first(active, all_cotangent).astype(jnp.bfloat16)
    grad_up_low = (grad_active * silu_value).astype(jnp.bfloat16)
    grad_gate_low = (grad_active * up_sum * sigma * (1.0 + gate_sum * (1.0 - sigma))).astype(
        jnp.bfloat16
    )
    both_grads = jnp.concatenate([grad_gate_low, grad_up_low], axis=1)
    grad_hidden = contract_last(both_grads, w_units).astype(jnp.bfloat16)
    grad_units = contract_first(hidden_two, both_grads).astype(jnp.bfloat16)
    grad_hidden, mlp_branch, grad_down = lax.optimization_barrier(
        (grad_hidden, mlp_branch, grad_down)
    )
    grad_middle, grad_branch, grad_gain_two, units_mine = call(
        back_kernel,
        (
            grad_hidden.reshape(rows, length, width),
            cotangent,
            middle,
            gains[1:2],
            grad_units.reshape(row_size, pieces, 2 * units),
        ),
        [
            full(rows, stretch, width),
            low(rows, length, width),
            full(1, width),
            low(pieces, 2 * units),
        ],
        seq_scratch(chips, stretch, width)
        + row_scratch(pieces, 2 * units)
        + [pltpu.VMEM((row_size, pieces, 2 * units), jnp.bfloat16)]
        + sem_pairs(2 * chips)
        + sem_pairs(2 * PARTS * (chips - 1))
        + sem_pairs(2 * chips * PARTS) * 2
        + sem_pairs(6)
        + [pltpu.SemaphoreType.DMA],
        2,
        far_in=(4,),
    )
    grad_branch, grad_down = lax.optimization_barrier((grad_branch, grad_down))
    grad_down = scatter(grad_down, "row", 0)
    grad_units = lax.all_to_all(
        units_mine.reshape(seq_size, piece_rows, 2 * units), "seq", 0, 0, tiled=True
    )
    grad_branch = grad_branch.reshape(count, width)
    grad_mixed = contract_last(grad_branch, out_part).astype(jnp.bfloat16)
    grad_out = scatter(contract_first(mixed, grad_branch).astype(jnp.bfloat16), "row", 0)
    grad_out = lax.ppermute(grad_out, BOTH, shift_back).astype(jnp.float32)
    grad_grouped = grad_mixed.reshape(rows, length, key_heads, groups, HEAD_DIM)
    grad_probs = jnp.einsum(
        "rqhgd,rkhd->rhgqk", grad_grouped, values, preferred_element_type=jnp.float32
    )
    delta = jnp.sum(probs * grad_probs, axis=-1, keepdims=True)
    grad_raw = (scale * probs * (grad_probs - delta)).astype(jnp.bfloat16)
    grad_queries = jnp.einsum(
        "rhgqk,rkhd->rqhgd", grad_raw, keys, preferred_element_type=jnp.float32
    )
    grad_keys = jnp.einsum(
        "rhgqk,rqhgd->rkhd", grad_raw, queries, preferred_element_type=jnp.float32
    )
    grad_values = jnp.einsum(
        "rhgqk,rqhgd->rkhd", probs_low, grad_grouped, preferred_element_type=jnp.float32
    )
    grad_qkv_low = jnp.concatenate(
        [
            rotate_back(grad_queries.reshape(rows, length, heads, HEAD_DIM), cosine, sine).reshape(
                count, query_width
            ),
            rotate_back(grad_keys, cosine, sine).reshape(count, key_width),
            grad_values.reshape(count, key_width),
        ],
        axis=1,
    ).astype(jnp.bfloat16)
    grad_qkv = contract_first(hidden_one, grad_qkv_low).astype(jnp.bfloat16)
    grad_hidden = contract_last(grad_qkv_low, w_qkv).astype(jnp.bfloat16)
    grad_hidden, grad_units = lax.optimization_barrier((grad_hidden, grad_units))
    grad_tokens, gain_sums, grad_qkv = call(
        close_kernel,
        (
            grad_hidden.reshape(rows, length, width),
            tokens,
            grad_middle,
            gains[0:1],
            grad_gain_two,
            grad_qkv.reshape(row_size, pieces, head_width),
        ),
        [
            full(rows, stretch, width),
            full(2, width),
            low(seq_size, piece_rows, head_width),
        ],
        [pltpu.VMEM((pieces, head_width), jnp.bfloat16)]
        + seq_scratch(chips, stretch, width)
        + row_scratch(pieces, head_width)
        + [pltpu.VMEM((3, 2, width), jnp.float32)]
        + [pltpu.VMEM((seq_size + row_size - 2, 2, width), jnp.float32)]
        + sem_pairs(2 * chips)
        + sem_pairs(2 * PARTS * (chips - 1))
        + sem_pairs(6)
        + sem_pairs(seq_size - 1)
        + sem_pairs(seq_size + row_size - 2),
        3,
    )

    grad_gate, grad_up = unpack_units(grad_units, row_size)
    grad_query, grad_key, grad_value = unpack_heads(grad_qkv, query_width, key_width)
    own = (lax.axis_index("row") * seq_size + lax.axis_index("seq")) * piece_rows
    grad_gains = lax.dynamic_slice_in_dim(gain_sums, own, piece_rows, 1)
    return (
        output,
        grad_tokens,
        grad_gains[0],
        grad_query,
        grad_key,
        grad_value,
        grad_out,
        grad_gains[1],
        grad_gate,
        grad_up,
        grad_down.astype(jnp.float32),
    )


def local(tokens, cotangent, doc_lengths, attn_gain, w_query, w_key, w_value, *rest):
    whole_heads = w_key.shape[1] % (HEAD_DIM * lax.axis_size("seq")) == 0
    layer = sharded_layer if whole_heads else gathered_layer
    return layer(tokens, cotangent, doc_lengths, attn_gain, w_query, w_key, w_value, *rest)


def solution(mesh):
    return jax.shard_map(
        local,
        mesh=mesh,
        in_specs=(
            P("row", "seq", None),
            P("row", "seq", None),
            P("row", None),
            P(("row", "seq")),
            P(("row", "seq"), None),
            P(("row", "seq"), None),
            P(("row", "seq"), None),
            P(("row", "seq"), None),
            P(("row", "seq")),
            P(("row", "seq"), None),
            P(("row", "seq"), None),
            P(("row", "seq"), None),
        ),
        out_specs=(
            P("row", "seq", None),
            P("row", "seq", None),
            P(("row", "seq")),
            P(("row", "seq"), None),
            P(("row", "seq"), None),
            P(("row", "seq"), None),
            P(("row", "seq"), None),
            P(("row", "seq")),
            P(("row", "seq"), None),
            P(("row", "seq"), None),
            P(("row", "seq"), None),
        ),
        check_vma=False,
    )
```

```python
import math

import jax
import jax.numpy as jnp
import numpy as np
from jax import lax
from jax.experimental import pallas as pl
from jax.experimental.pallas import tpu as pltpu
from jax.sharding import PartitionSpec as P

HEAD_DIM = 64


EPSILON = 1e-05
THETA = 500000.0


def rope_table(head_size):
    half_size = head_size // 2
    plain = THETA ** (-(np.arange(half_size) * 2.0) / head_size)
    factor, low_factor, high_factor, old_span = (32.0, 1.0, 4.0, 8192.0)
    wavelength = 2.0 * math.pi / plain
    smooth = (old_span / wavelength - low_factor) / (high_factor - low_factor)
    blended = (1.0 - smooth) * plain / factor + smooth * plain
    return np.where(
        wavelength < old_span / high_factor,
        plain,
        np.where(wavelength > old_span / low_factor, plain / factor, blended),
    )


def norm_scale(values):
    return lax.rsqrt(jnp.mean(values * values, axis=-1, keepdims=True) + EPSILON)


def norm_back(grad_normed, normed, scale):
    return scale * (grad_normed - normed * jnp.mean(grad_normed * normed, axis=-1, keepdims=True))


def rotate(values, cosine, sine):
    half_size = values.shape[-1] // 2
    turned = jnp.concatenate([-values[..., half_size:], values[..., :half_size]], axis=-1)
    return values * cosine + turned * sine


def rotate_back(grad, cosine, sine):
    half_size = grad.shape[-1] // 2
    turned = grad * sine
    return grad * cosine + jnp.concatenate(
        [turned[..., half_size:], -turned[..., :half_size]], axis=-1
    )


def contract_last(left, right):
    return lax.dot_general(
        left, right, (((1,), (1,)), ((), ())), preferred_element_type=jnp.float32
    )


def contract_first(left, right):
    return lax.dot_general(
        left, right, (((0,), (0,)), ((), ())), preferred_element_type=jnp.float32
    )


def gathered_layer(
    tokens,
    cotangent,
    doc_lengths,
    attn_gain,
    w_query,
    w_key,
    w_value,
    w_out,
    mlp_gain,
    w_gate,
    w_up,
    w_down,
):
    rows, stretch, width = tokens.shape
    count = rows * stretch
    key_width = w_key.shape[1]
    hidden_width = w_gate.shape[1]
    key_heads = key_width // HEAD_DIM
    heads = width // HEAD_DIM
    groups = heads // key_heads
    length = stretch * lax.axis_size("seq")
    block = math.gcd(length, 512)
    scale = HEAD_DIM ** (-0.5)
    table = jnp.asarray(rope_table(HEAD_DIM), jnp.float32)
    place = lax.axis_index("seq") * stretch + jnp.arange(stretch, dtype=jnp.int32)
    live_blocks = ((lax.axis_index("seq") + 1) * stretch + block - 1) // block
    ends = jnp.cumsum(doc_lengths, axis=1)
    first = jnp.max(
        jnp.where(ends[:, None, :] <= place[None, :, None], ends[:, None, :], 0), axis=2
    )
    angle = (place[None, :] - first).astype(jnp.float32)[..., None] * table
    cosine = jnp.concatenate([jnp.cos(angle), jnp.cos(angle)], axis=-1)[:, :, None, :]
    sine = jnp.concatenate([jnp.sin(angle), jnp.sin(angle)], axis=-1)[:, :, None, :]
    inputs = tokens.reshape(count, width).astype(jnp.float32)
    scale_one = norm_scale(inputs)
    normed_one = inputs * scale_one
    gain_piece = lax.all_gather(attn_gain, ("row", "seq"), axis=0, tiled=True)
    query_piece = lax.all_gather(w_query, ("row", "seq"), axis=0, tiled=True)
    key_piece = lax.all_gather(w_key, ("row", "seq"), axis=0, tiled=True)
    value_piece = lax.all_gather(w_value, ("row", "seq"), axis=0, tiled=True)
    hidden_piece = (normed_one * gain_piece.astype(jnp.float32)).astype(jnp.bfloat16)
    query_sum = jnp.dot(hidden_piece, query_piece, preferred_element_type=jnp.float32)
    key_sum = jnp.dot(hidden_piece, key_piece, preferred_element_type=jnp.float32)
    value_sum = jnp.dot(hidden_piece, value_piece, preferred_element_type=jnp.float32)
    hidden_one = hidden_piece
    queries = rotate(query_sum.reshape(rows, stretch, heads, HEAD_DIM), cosine, sine).astype(
        jnp.bfloat16
    )
    keys = rotate(key_sum.reshape(rows, stretch, key_heads, HEAD_DIM), cosine, sine).astype(
        jnp.bfloat16
    )
    values = value_sum.astype(jnp.bfloat16)
    query_grouped = queries.reshape(rows, stretch, key_heads, groups, HEAD_DIM)

    def gather_keys():
        return (
            lax.all_gather(keys.reshape(rows, stretch, key_width), "seq", axis=1, tiled=True),
            lax.all_gather(values.reshape(rows, stretch, key_width), "seq", axis=1, tiled=True),
        )

    key_all, value_all = gather_keys()

    def block_rows(source, index):
        return lax.dynamic_slice_in_dim(source, index * block, block, 1).reshape(
            rows, block, key_heads, HEAD_DIM
        )

    def block_scores(key_block, index):
        raw = jnp.einsum(
            "rqhgd,rkhd->rhgqk", query_grouped, key_block, preferred_element_type=jnp.float32
        )
        key_place = index * block + jnp.arange(block, dtype=jnp.int32)
        allowed = (key_place[None, None, :] <= place[None, :, None]) & (
            key_place[None, None, :] >= first[:, :, None]
        )
        return jnp.where(allowed[:, None, None], raw * scale, -1e30)

    def total_step(index, carry):
        running_max, running_total = carry
        scores = block_scores(block_rows(key_all, index), index)
        new_max = jnp.maximum(running_max, jnp.max(scores, axis=-1))
        new_total = running_total * jnp.exp(running_max - new_max) + jnp.sum(
            jnp.exp(scores - new_max[..., None]), axis=-1
        )
        return (new_max, new_total)

    stat_shape = (rows, key_heads, groups, stretch)
    running_max, running_total = lax.fori_loop(
        0,
        live_blocks,
        total_step,
        (jnp.full(stat_shape, -1e30, jnp.float32), jnp.zeros(stat_shape, jnp.float32)),
    )
    log_total = running_max + jnp.log(running_total)

    def mix_step(index, mixed_sum):
        probs = jnp.exp(block_scores(block_rows(key_all, index), index) - log_total[..., None])
        return mixed_sum + jnp.einsum(
            "rhgqk,rkhd->rqhgd",
            probs.astype(jnp.bfloat16),
            block_rows(value_all, index),
            preferred_element_type=jnp.float32,
        )

    mixed_sum = lax.fori_loop(
        0,
        live_blocks,
        mix_step,
        jnp.zeros((rows, stretch, key_heads, groups, HEAD_DIM), jnp.float32),
    )
    mixed = mixed_sum.reshape(count, width).astype(jnp.bfloat16)
    attn_branch = jnp.dot(
        mixed,
        lax.all_gather(w_out, ("row", "seq"), axis=0, tiled=True),
        preferred_element_type=jnp.float32,
    )
    middle = inputs + attn_branch
    scale_two = norm_scale(middle)
    normed_two = middle * scale_two
    gain_piece = lax.all_gather(mlp_gain, ("row", "seq"), axis=0, tiled=True)
    gate_piece = lax.all_gather(w_gate, ("row", "seq"), axis=0, tiled=True)
    up_piece = lax.all_gather(w_up, ("row", "seq"), axis=0, tiled=True)
    hidden_piece = (normed_two * gain_piece.astype(jnp.float32)).astype(jnp.bfloat16)
    gate_sum, up_sum, hidden_two = (
        jnp.dot(hidden_piece, gate_piece, preferred_element_type=jnp.float32),
        jnp.dot(hidden_piece, up_piece, preferred_element_type=jnp.float32),
        hidden_piece,
    )
    sigma = jax.nn.sigmoid(gate_sum)
    silu_value = gate_sum * sigma
    active = (silu_value * up_sum).astype(jnp.bfloat16)
    mlp_branch = jnp.dot(
        active,
        lax.all_gather(w_down, ("row", "seq"), axis=0, tiled=True),
        preferred_element_type=jnp.float32,
    )
    output = (middle + mlp_branch).astype(jnp.bfloat16).reshape(rows, stretch, width)
    grad_out_low = cotangent.reshape(count, width)
    grad_active = contract_last(
        grad_out_low, lax.all_gather(w_down, ("row", "seq"), axis=0, tiled=True)
    )
    grad_down = lax.psum_scatter(
        contract_first(active, grad_out_low), ("row", "seq"), scatter_dimension=0, tiled=True
    )
    grad_up_low = (grad_active * silu_value).astype(jnp.bfloat16)
    grad_gate_low = (grad_active * up_sum * sigma * (1.0 + gate_sum * (1.0 - sigma))).astype(
        jnp.bfloat16
    )
    both_grads = jnp.concatenate([grad_gate_low, grad_up_low], axis=1)
    gain_piece = lax.all_gather(mlp_gain, ("row", "seq"), axis=0, tiled=True)
    gate_piece = lax.all_gather(w_gate, ("row", "seq"), axis=0, tiled=True)
    up_piece = lax.all_gather(w_up, ("row", "seq"), axis=0, tiled=True)
    grad_piece = contract_last(grad_gate_low, gate_piece) + contract_last(grad_up_low, up_piece)
    normed_piece = normed_two
    grad_normed_two = grad_piece * gain_piece.astype(jnp.float32)
    grad_gain_two = jnp.sum(normed_piece * grad_piece, axis=0)
    grad_gate_up = lax.psum_scatter(
        contract_first(hidden_two, both_grads), ("row", "seq"), scatter_dimension=0, tiled=True
    )
    grad_gate = grad_gate_up[:, :hidden_width]
    grad_up = grad_gate_up[:, hidden_width:]
    grad_middle = grad_out_low.astype(jnp.float32) + norm_back(
        grad_normed_two, normed_two, scale_two
    )
    grad_branch_low = grad_middle.astype(jnp.bfloat16)
    grad_mixed = contract_last(
        grad_branch_low, lax.all_gather(w_out, ("row", "seq"), axis=0, tiled=True)
    ).astype(jnp.bfloat16)
    grad_out = lax.psum_scatter(
        contract_first(mixed, grad_branch_low), ("row", "seq"), scatter_dimension=0, tiled=True
    )
    grad_grouped = grad_mixed.reshape(rows, stretch, key_heads, groups, HEAD_DIM)
    key_back, value_back = gather_keys()

    def delta_step(index, total):
        probs = jnp.exp(block_scores(block_rows(key_back, index), index) - log_total[..., None])
        grad_probs = jnp.einsum(
            "rqhgd,rkhd->rhgqk",
            grad_grouped,
            block_rows(value_back, index),
            preferred_element_type=jnp.float32,
        )
        return total + jnp.sum(probs * grad_probs, axis=-1)

    delta = lax.fori_loop(0, live_blocks, delta_step, jnp.zeros(stat_shape, jnp.float32))

    def grad_step(index, carry):
        grad_queries, grad_key_all, grad_value_all = carry
        key_block = block_rows(key_back, index)
        probs = jnp.exp(block_scores(key_block, index) - log_total[..., None])
        grad_probs = jnp.einsum(
            "rqhgd,rkhd->rhgqk",
            grad_grouped,
            block_rows(value_back, index),
            preferred_element_type=jnp.float32,
        )
        grad_raw = (scale * probs * (grad_probs - delta[..., None])).astype(jnp.bfloat16)
        grad_queries = grad_queries + jnp.einsum(
            "rhgqk,rkhd->rqhgd", grad_raw, key_block, preferred_element_type=jnp.float32
        )
        key_part = jnp.einsum(
            "rhgqk,rqhgd->rkhd", grad_raw, query_grouped, preferred_element_type=jnp.float32
        ).reshape(rows, block, key_width)
        value_part = jnp.einsum(
            "rhgqk,rqhgd->rkhd",
            probs.astype(jnp.bfloat16),
            grad_grouped,
            preferred_element_type=jnp.float32,
        ).reshape(rows, block, key_width)
        return (
            grad_queries,
            lax.dynamic_update_slice_in_dim(grad_key_all, key_part, index * block, 1),
            lax.dynamic_update_slice_in_dim(grad_value_all, value_part, index * block, 1),
        )

    grad_queries, grad_key_all, grad_value_all = lax.fori_loop(
        0,
        live_blocks,
        grad_step,
        (
            jnp.zeros((rows, stretch, key_heads, groups, HEAD_DIM), jnp.float32),
            jnp.zeros((rows, length, key_width), jnp.float32),
            jnp.zeros((rows, length, key_width), jnp.float32),
        ),
    )
    grad_key_sum, grad_value_sum = (
        lax.psum_scatter(
            grad_key_all.astype(jnp.bfloat16), "seq", scatter_dimension=1, tiled=True
        ).astype(jnp.float32),
        lax.psum_scatter(
            grad_value_all.astype(jnp.bfloat16), "seq", scatter_dimension=1, tiled=True
        ).astype(jnp.float32),
    )
    grad_query_low = (
        rotate_back(grad_queries.reshape(rows, stretch, heads, HEAD_DIM), cosine, sine)
        .reshape(count, width)
        .astype(jnp.bfloat16)
    )
    grad_key_low = (
        rotate_back(grad_key_sum.reshape(rows, stretch, key_heads, HEAD_DIM), cosine, sine)
        .reshape(count, key_width)
        .astype(jnp.bfloat16)
    )
    grad_value_low = grad_value_sum.reshape(count, key_width).astype(jnp.bfloat16)
    gain_piece = lax.all_gather(attn_gain, ("row", "seq"), axis=0, tiled=True)
    query_piece = lax.all_gather(w_query, ("row", "seq"), axis=0, tiled=True)
    key_piece = lax.all_gather(w_key, ("row", "seq"), axis=0, tiled=True)
    value_piece = lax.all_gather(w_value, ("row", "seq"), axis=0, tiled=True)
    grad_piece = (
        contract_last(grad_query_low, query_piece)
        + contract_last(grad_key_low, key_piece)
        + contract_last(grad_value_low, value_piece)
    )
    normed_piece = normed_one
    grad_normed_one = grad_piece * gain_piece.astype(jnp.float32)
    grad_gain_one = jnp.sum(normed_piece * grad_piece, axis=0)
    grad_query, grad_key, grad_value, grad_attn_gain, grad_mlp_gain = (
        lax.psum_scatter(
            contract_first(hidden_one, grad_query_low),
            ("row", "seq"),
            scatter_dimension=0,
            tiled=True,
        ),
        lax.psum_scatter(
            contract_first(hidden_one, grad_key_low),
            ("row", "seq"),
            scatter_dimension=0,
            tiled=True,
        ),
        lax.psum_scatter(
            contract_first(hidden_one, grad_value_low),
            ("row", "seq"),
            scatter_dimension=0,
            tiled=True,
        ),
        lax.psum_scatter(grad_gain_one, ("row", "seq"), scatter_dimension=0, tiled=True),
        lax.psum_scatter(grad_gain_two, ("row", "seq"), scatter_dimension=0, tiled=True),
    )
    grad_tokens = (grad_middle + norm_back(grad_normed_one, normed_one, scale_one)).reshape(
        rows, stretch, width
    )
    return (
        output,
        grad_tokens,
        grad_attn_gain,
        grad_query,
        grad_key,
        grad_value,
        grad_out,
        grad_mlp_gain,
        grad_gate,
        grad_up,
        grad_down,
    )


MESH = pl.DeviceIdType.MESH
VMEM_LIMIT = 60 * 1024 * 1024
PARTS = 2


def neighbours():
    row, seq = lax.axis_index("row"), lax.axis_index("seq")
    row_size, seq_size = lax.axis_size("row"), lax.axis_size("seq")
    return dict(
        row=row,
        seq=seq,
        z=seq // 2,
        core=seq % 2,
        up=(row, (seq + 2) % seq_size),
        down=(row, (seq + seq_size - 2) % seq_size),
        pair=(row, seq + 1 - 2 * (seq % 2)),
        side=(row + 1 - 2 * (row % 2), seq),
        across=((row + row_size // 2) % row_size, seq),
        corner=((row + 1 - 2 * (row % 2) + row_size // 2) % row_size, seq),
        side_row=row + 1 - 2 * (row % 2),
        across_row=(row + row_size // 2) % row_size,
    )


def greet(peers, route=None):
    barrier = pltpu.get_barrier_semaphore()
    for peer in peers:
        pl.semaphore_signal(barrier, inc=1, device_id=peer, device_id_type=MESH)
    amount = len(peers)
    if route is not None:
        moves, *ends = route

        @pl.when(moves)
        def _():
            for peer in ends:
                pl.semaphore_signal(barrier, inc=1, device_id=peer, device_id_type=MESH)

        amount = amount + jnp.where(moves, len(ends), 0)
    pl.semaphore_wait(barrier, amount)


def send(source, target, sems, index, peer):
    copy = pltpu.make_async_remote_copy(
        src_ref=source,
        dst_ref=target,
        send_sem=sems[0].at[index],
        recv_sem=sems[1].at[index],
        device_id=peer,
        device_id_type=MESH,
    )
    copy.start()
    return copy


def sem_pairs(amount):
    return [pltpu.SemaphoreType.DMA((amount,)), pltpu.SemaphoreType.DMA((amount,))]


def by_rows(amount, step, body):
    def one(i, carry):
        body(pl.ds(pl.multiple_of(i * step, step), step))
        return carry

    lax.fori_loop(0, amount // step, one, 0)


def copy_rows(target, source):
    def one(rows):
        target[rows] = source[rows]

    by_rows(source.shape[0], 16, one)


def gather_seq_steps(here, whole, stretch, pair_sems, ring_sems):
    seq, chips = here["seq"], lax.axis_size("seq") // 2
    seq_size = 2 * chips
    piece = stretch // PARTS
    rings, pairs, last = [], [], {}

    def spot(owner, part):
        return pl.ds(pl.multiple_of(owner * stretch + part * piece, piece), piece)

    def ring(step, part):
        owners = (seq + seq_size - 2 * step) % seq_size, (seq + 2 * step) % seq_size
        for half, peer in ((0, "up"), (1, "down")):
            view = whole.at[half, spot(owners[half], part)]
            slot = (step * PARTS + part) * 2 + half
            if step > 0:
                last[half, part].wait_recv()
            if step < chips - 1:
                last[half, part] = send(view, view, ring_sems, slot, here[peer])
                rings.append(last[half, part])
            pairs.append(send(view, view, pair_sems, slot, here["pair"]))

    def both(step):
        for part in range(PARTS):
            ring(step, part)

    def finish():
        for copy in pairs:
            copy.wait()
        for copy in rings:
            copy.wait_send()

    return ring, [lambda step=step: both(step) for step in range(chips)] + [finish]


def reduce_seq_steps(here, part, stretch, pair_in, total, ring_in, pair_sems, ring_sems, done):
    z, core, chips = here["z"], here["core"], lax.axis_size("seq") // 2
    piece = stretch // PARTS
    copies, pair_copies, last = [], {}, {}
    order = [spot for t in range(chips - 1) for spot in ((chips - 1 - t, 0), (1 + t, 1))]
    order += [(0, 0), (0, 1)]

    def place(far):
        return (z + far) % chips

    def each(number, body):
        def one(rows):
            body(pl.ds(pl.multiple_of(number * piece + rows.start, 16), 16))

        by_rows(piece, 16, one)

    def pair_sum(far, half, number):
        chip = place(far)
        base = (2 * chip + core) * stretch
        if number == 0:
            pair_copies[far, half].wait_recv()

        def add(rows):
            mine = part[half, pl.ds(pl.multiple_of(base + rows.start, 16), 16)]
            other = pair_in[chip, half, rows]
            total[chip, half, rows] = (
                mine.astype(jnp.float32) + other.astype(jnp.float32)
            ).astype(jnp.bfloat16)

        each(number, add)

    def ring_send(step, half, number):
        far, peer = ((chips - 1 - step, "up"), (1 + step, "down"))[half]
        chip = place(far)
        if step == 0:
            pair_sum(far, half, number)
        else:
            last[half, number].wait_recv()
            arrived = ring_in.at[step - 1, half]

            def add(rows):
                total[chip, half, rows] = (
                    total[chip, half, rows].astype(jnp.float32)
                    + arrived[rows].astype(jnp.float32)
                ).astype(jnp.bfloat16)

            each(number, add)
        rows = pl.ds(number * piece, piece)
        last[half, number] = send(
            total.at[chip, half, rows],
            ring_in.at[step, half, rows],
            ring_sems,
            (step * PARTS + number) * 2 + half,
            here[peer],
        )
        copies.append(last[half, number])

    def ring(step):
        for number in range(PARTS):
            for half in range(2):
                ring_send(step, half, number)

    def first_step():
        for index, (far, half) in enumerate(order):
            chip = place(far)
            spot = pl.ds(pl.multiple_of((2 * chip + 1 - core) * stretch, stretch), stretch)
            pair_copies[far, half] = send(
                part.at[half, spot], pair_in.at[chip, half], pair_sems, index, here["pair"]
            )
        ring(0)
        for far, half in order[2:]:
            for number in range(PARTS):
                pair_sum(far, half, number)

    def finish(number):
        for half in range(2):
            last[half, number].wait_recv()
            arrived = ring_in.at[chips - 2, half]

            def close(rows):
                done(
                    half,
                    rows,
                    total[z, half, rows].astype(jnp.float32) + arrived[rows].astype(jnp.float32),
                )

            each(number, close)

    def drain():
        for copy in list(pair_copies.values()) + copies:
            copy.wait_send()

    steps = [first_step] + [lambda step=step: ring(step) for step in range(1, chips - 1)]
    return steps, finish, drain


def gather_row_steps(here, own, whole, sems):
    half = whole.shape[1] // 2
    row, side, across = here["row"], here["side_row"], here["across_row"]
    state = []

    def first_step():
        state.append(send(own, whole.at[row], sems, 0, here["side"]))
        state.append(send(own, whole.at[row], sems, 1, here["across"]))

    def second_step():
        low, high = pl.ds(0, half), pl.ds(half, half)
        state[0].wait_recv()
        state.append(send(whole.at[side, low], whole.at[side, low], sems, 2, here["across"]))
        state[1].wait_recv()
        state.append(send(whole.at[across, high], whole.at[across, high], sems, 3, here["side"]))

    def finish():
        for copy in state[2:]:
            copy.wait_recv()
        for copy in state:
            copy.wait_send()

    return [first_step, second_step, finish]


def reduce_row_steps(here, source, part, inbox, sums, sems, done):
    half = part.shape[1] // 2
    row, side, across = here["row"], here["side_row"], here["across_row"]
    corner = (side + 2) % 4
    state = []

    def first_step():
        low, high = pl.ds(0, half), pl.ds(half, half)
        for index, (owner, rows, peer) in enumerate(
            (
                (corner, low, "side"),
                (corner, high, "across"),
                (side, low, "side"),
                (across, high, "across"),
            )
        ):
            state.append(send(source.at[owner, rows], inbox.at[index], sems, index, here[peer]))

    def add(owner, offset, index):
        def run(rows):
            spot = pl.ds(pl.multiple_of(offset + rows.start, 16), 16)
            sums[index, rows] = (
                part[owner, spot].astype(jnp.float32) + inbox[index, rows].astype(jnp.float32)
            ).astype(jnp.bfloat16)

        by_rows(half, 16, run)

    def second_step():
        state[0].wait_recv()
        add(across, 0, 0)
        state.append(send(sums.at[0], inbox.at[4], sems, 4, here["across"]))
        state[1].wait_recv()
        add(side, half, 1)
        state.append(send(sums.at[1], inbox.at[5], sems, 5, here["side"]))
        state[2].wait_recv()
        state[3].wait_recv()

    def finish():
        for offset, one, two in ((0, 2, 4), (half, 3, 5)):
            state[two].wait_recv()

            def close(rows):
                spot = pl.ds(pl.multiple_of(offset + rows.start, 16), 16)
                done(
                    spot,
                    part[row, spot].astype(jnp.float32)
                    + inbox[one, rows].astype(jnp.float32)
                    + inbox[two, rows].astype(jnp.float32),
                )

            by_rows(half, 16, close)
        for copy in state:
            copy.wait_send()

    return [first_step, second_step, finish]


def exchange_seq(here, source, target_of, sems):
    seq, seq_size = here["seq"], lax.axis_size("seq")
    copies = []
    for far in range(1, seq_size):
        dest = (seq + far) % seq_size
        copies.append(
            send(source.at[dest], target_of(seq), sems, far - 1, (here["row"], dest))
        )
    return copies


def seq_peers(here):
    seq_size = lax.axis_size("seq")
    return [(here["row"], (here["seq"] + far) % seq_size) for far in range(1, seq_size)]


def call(kernel, args, out_shape, scratch, collective_id, far_in=(), far_out=()):
    near, far = (pl.BlockSpec(memory_space=space) for space in (pltpu.VMEM, pl.ANY))
    return pl.pallas_call(
        kernel,
        out_shape=out_shape,
        in_specs=[far if i in far_in else near for i in range(len(args))],
        out_specs=[far if i in far_out else near for i in range(len(out_shape))],
        scratch_shapes=scratch,
        compiler_params=pltpu.CompilerParams(
            collective_id=collective_id, has_side_effects=True, vmem_limit_bytes=VMEM_LIMIT
        ),
    )(*args)


def low(*shape):
    return jax.ShapeDtypeStruct(shape, jnp.bfloat16)


def full(*shape):
    return jax.ShapeDtypeStruct(shape, jnp.float32)


def shift_route(here):
    row_size, seq_size = lax.axis_size("row"), lax.axis_size("seq")
    index = here["row"] * seq_size + here["seq"]
    origin = here["seq"] * row_size + here["row"]
    target = index % row_size, index // row_size
    return target, (origin // seq_size, origin % seq_size), index != origin


def open_kernel(
    tokens, heads_pack, w_gate, w_up, out_piece,
    all_tokens, heads_all, units_pack, out_all,
    pair_a, pair_b, ring_a, ring_b, heads_a, heads_b, row_a, row_b, out_a, out_b, shift_a, shift_b,
):
    here = neighbours()
    seq, row = here["seq"], here["row"]
    stretch = tokens.shape[1]
    piece = heads_pack.shape[1]
    target, origin, moves = shift_route(here)
    greet(seq_peers(here) + [here["side"], here["across"]], (moves, target, origin))

    def spot(owner):
        return pl.ds(pl.multiple_of(owner * piece, piece), piece)

    def shift():
        return pltpu.make_async_remote_copy(
            src_ref=out_piece,
            dst_ref=out_all.at[target[0]],
            send_sem=shift_a.at[0],
            recv_sem=shift_b.at[0],
            device_id=target,
            device_id_type=MESH,
        )

    heads = exchange_seq(here, heads_pack, lambda s: heads_all.at[row, spot(s)], (heads_a, heads_b))

    @pl.when(moves)
    def _():
        shift().start()

    for half in range(2):
        own = pl.ds(pl.multiple_of(seq * stretch, stretch), stretch)
        copy_rows(all_tokens.at[half, own], tokens.at[half])
    gather_out = gather_row_steps(here, out_all.at[row], out_all, (out_a, out_b))
    gather_heads = gather_row_steps(here, heads_all.at[row], heads_all, (row_a, row_b))
    _, steps = gather_seq_steps(here, all_tokens, stretch, (pair_a, pair_b), (ring_a, ring_b))
    steps[0]()
    copy_rows(heads_all.at[row, spot(seq)], heads_pack.at[seq])

    @pl.when(jnp.logical_not(moves))
    def _():
        copy_rows(out_all.at[row], out_piece)

    for copy in heads:
        copy.wait_recv()
    gather_heads[0]()

    @pl.when(moves)
    def _():
        shift().wait()

    gather_out[0]()
    seq_size, row_size = lax.axis_size("seq"), lax.axis_size("row")
    block = w_gate.shape[1] // (seq_size * row_size)
    for number, weight in enumerate((w_gate, w_up)):
        for r in range(row_size):
            for s in range(seq_size):
                source = (r * seq_size + s) * block
                place = (number * row_size + r) * block
                units_pack[s, :, place : place + block] = weight[:, source : source + block]
    steps[1]()
    gather_heads[1]()
    gather_out[1]()
    for step in steps[2:]:
        step()
    gather_heads[2]()
    gather_out[2]()
    for copy in heads:
        copy.wait_send()


def middle_kernel(
    branch, tokens, gain, units_mine,
    middle, hidden, units_all,
    pair_in, total, ring_in, pair_a, pair_b, ring_a, ring_b,
    gpair_a, gpair_b, gring_a, gring_b, row_a, row_b, own_sem,
):
    here = neighbours()
    seq = here["seq"]
    stretch = tokens.shape[1]
    own_copy = pltpu.make_async_copy(units_mine, units_all.at[here["row"]], own_sem)
    own_copy.start()
    greet([here["up"], here["down"], here["pair"], here["side"], here["across"]])

    def done(half, rows, value):
        value = tokens[half, rows].astype(jnp.float32) + value
        middle[half, rows] = value
        normed = value * norm_scale(value)
        spot = pl.ds(pl.multiple_of(seq * stretch + rows.start, 16), 16)
        hidden[half, spot] = (normed * gain[...]).astype(jnp.bfloat16)

    reduce_steps, finish, drain = reduce_seq_steps(
        here, branch, stretch, pair_in, total, ring_in, (pair_a, pair_b), (ring_a, ring_b), done
    )
    units = gather_row_steps(here, units_mine, units_all, (row_a, row_b))
    units[0]()
    for step in reduce_steps:
        step()
    ring, gather_steps = gather_seq_steps(
        here, hidden, stretch, (gpair_a, gpair_b), (gring_a, gring_b)
    )
    for number in range(PARTS):
        finish(number)
        ring(0, number)
    gather_steps[1]()
    units[1]()
    for step in gather_steps[2:]:
        step()
    units[2]()
    drain()
    own_copy.wait()


def back_kernel(
    grad_part, cotangent, middle, gain, units_part,
    grad_middle, grad_low, gain_grad, units_out,
    pair_in, total, ring_in, inbox, sums, units_near, pair_a, pair_b, ring_a, ring_b,
    gpair_a, gpair_b, gring_a, gring_b, row_a, row_b, near_sem,
):
    here = neighbours()
    seq = here["seq"]
    stretch = cotangent.shape[1]
    near_copy = pltpu.make_async_copy(units_part, units_near, near_sem)
    near_copy.start()
    greet([here["up"], here["down"], here["pair"], here["side"], here["across"]])
    gain_grad[...] = jnp.zeros_like(gain_grad)

    def done(half, rows, grad):
        value = middle[half, rows]
        scale = norm_scale(value)
        normed = value * scale
        gain_grad[...] += jnp.sum(normed * grad, axis=0, keepdims=True)
        back = cotangent[half, rows].astype(jnp.float32) + norm_back(
            grad * gain[...], normed, scale
        )
        grad_middle[half, rows] = back
        spot = pl.ds(pl.multiple_of(seq * stretch + rows.start, 16), 16)
        grad_low[half, spot] = back.astype(jnp.bfloat16)

    def done_units(rows, value):
        units_out[rows] = value.astype(jnp.bfloat16)

    reduce_steps, finish, drain = reduce_seq_steps(
        here, grad_part, stretch, pair_in, total, ring_in, (pair_a, pair_b), (ring_a, ring_b), done
    )
    units = reduce_row_steps(
        here, units_part, units_near, inbox, sums, (row_a, row_b), done_units
    )
    units[0]()
    for step in reduce_steps:
        step()
    ring, gather_steps = gather_seq_steps(
        here, grad_low, stretch, (gpair_a, gpair_b), (gring_a, gring_b)
    )
    for number in range(PARTS):
        finish(number)
        ring(0, number)
    near_copy.wait()
    units[1]()
    for step in gather_steps[1:]:
        step()
    units[2]()
    drain()


def sum_small(here, mine, inbox, sems):
    slot = 0
    stages = [seq_peers(here), [here["side"], here["across"], here["corner"]]]
    copies = []
    for number, stage in enumerate(stages):
        sent = [
            send(mine.at[number], inbox.at[slot + i], sems, slot + i, peer)
            for i, peer in enumerate(stage)
        ]
        value = mine[number]
        for i, copy in enumerate(sent):
            copy.wait_recv()
            value = value + inbox[slot + i]
        mine[number + 1] = value
        slot += len(stage)
        copies += sent
    for copy in copies:
        copy.wait_send()
    return slot


def close_kernel(
    grad_part, tokens, grad_middle, gain, gain_two, heads_part,
    grad_tokens, gain_sums, heads_out,
    heads_mine, pair_in, total, ring_in, inbox, sums, small, small_in,
    pair_a, pair_b, ring_a, ring_b, row_a, row_b, heads_a, heads_b, small_a, small_b,
):
    here = neighbours()
    seq, chips = here["seq"], lax.axis_size("seq") // 2
    stretch = tokens.shape[1]
    greet(seq_peers(here) + [here["side"], here["across"], here["corner"]])
    small[0, 0:1] = jnp.zeros_like(small[0, 0:1])
    small[0, 1:2] = gain_two[...]

    def done(half, rows, grad):
        value = tokens[half, rows].astype(jnp.float32)
        scale = norm_scale(value)
        normed = value * scale
        small[0, 0:1] += jnp.sum(normed * grad, axis=0, keepdims=True)
        grad_tokens[half, rows] = grad_middle[half, rows] + norm_back(
            grad * gain[...], normed, scale
        )

    piece = heads_out.shape[1]

    def done_heads(rows, value):
        heads_mine[rows] = value.astype(jnp.bfloat16)

    reduce_steps, finish, drain = reduce_seq_steps(
        here, grad_part, stretch, pair_in, total, ring_in, (pair_a, pair_b), (ring_a, ring_b), done
    )
    heads = reduce_row_steps(here, heads_part, heads_part, inbox, sums, (row_a, row_b), done_heads)
    heads[0]()
    reduce_steps[0]()
    heads[1]()
    for step in reduce_steps[1:]:
        step()
    heads[2]()
    copies = []
    for far in range(1, 2 * chips):
        dest = (seq + far) % (2 * chips)
        rows = pl.ds(pl.multiple_of(dest * piece, piece), piece)
        copies.append(
            send(
                heads_mine.at[rows], heads_out.at[seq], (heads_a, heads_b), far - 1,
                (here["row"], dest),
            )
        )
    for number in range(PARTS):
        finish(number)
    copy_rows(heads_out.at[seq], heads_mine.at[pl.ds(pl.multiple_of(seq * piece, piece), piece)])
    sum_small(here, small, small_in, (small_a, small_b))
    gain_sums[...] = small[2]
    for copy in copies:
        copy.wait()
    drain()


def seq_scratch(chips, stretch, width):
    return [
        pltpu.VMEM((chips, 2, stretch, width), jnp.bfloat16),
        pltpu.VMEM((chips, 2, stretch, width), jnp.bfloat16),
        pltpu.VMEM((chips - 1, 2, stretch, width), jnp.bfloat16),
    ]


def row_scratch(pieces, columns):
    return [
        pltpu.VMEM((6, pieces // 2, columns), jnp.bfloat16),
        pltpu.VMEM((2, pieces // 2, columns), jnp.bfloat16),
    ]


def unpack(units, heads, down, row_size, query_width, key_width):
    seq_size, rows, columns = units.shape
    block = columns // 2 // row_size
    down_rows, width = down.shape

    def kernel(gate, up, heads_ref, down_ref, gate_out, up_out, query, key, value, down_out):
        for source, target in ((gate, gate_out), (up, up_out)):
            for s in range(seq_size):
                target[:, s * block : (s + 1) * block] = source[s].astype(jnp.float32)
        down_out[...] = down_ref[...].astype(jnp.float32)

        @pl.when(pl.program_id(0) == 0)
        def _():
            start = 0
            for target, size in ((query, query_width), (key, key_width), (value, key_width)):
                target[...] = jnp.concatenate(
                    [
                        heads_ref[s, :, start : start + size].astype(jnp.float32)
                        for s in range(seq_size)
                    ],
                    axis=1,
                )
                start += size

    whole = full(rows, seq_size * columns // 2)
    head_shapes = [full(rows, seq_size * w) for w in (query_width, key_width, key_width)]
    down_block = pl.BlockSpec((down_rows // row_size, width), lambda r: (r, 0))
    return pl.pallas_call(
        kernel,
        grid=(row_size,),
        out_shape=[whole, whole] + head_shapes + [full(down_rows, width)],
        in_specs=[
            pl.BlockSpec((seq_size, rows, block), lambda r: (0, 0, r)),
            pl.BlockSpec((seq_size, rows, block), lambda r: (0, 0, row_size + r)),
            pl.BlockSpec(heads.shape, lambda r: (0, 0, 0)),
            down_block,
        ],
        out_specs=[pl.BlockSpec((rows, seq_size * block), lambda r: (0, r))] * 2
        + [pl.BlockSpec(x.shape, lambda r: (0, 0)) for x in head_shapes]
        + [down_block],
    )(units, units, heads, down)


BOTH = ("row", "seq")


def gather(piece, axis_name, axis):
    return lax.all_gather(piece, axis_name, axis=axis, tiled=True)


def scatter(whole, axis_name, axis):
    return lax.psum_scatter(whole, axis_name, scatter_dimension=axis, tiled=True)


def sharded_layer(
    tokens,
    cotangent,
    doc_lengths,
    attn_gain,
    w_query,
    w_key,
    w_value,
    w_out,
    mlp_gain,
    w_gate,
    w_up,
    w_down,
):
    row_size, seq_size = lax.axis_size("row"), lax.axis_size("seq")
    rows, stretch, width = tokens.shape
    length = stretch * seq_size
    count = rows * length
    piece_rows = w_query.shape[0]
    key_heads = w_key.shape[1] // HEAD_DIM // seq_size
    heads = w_query.shape[1] // HEAD_DIM // seq_size
    groups = heads // key_heads
    query_width, key_width = heads * HEAD_DIM, key_heads * HEAD_DIM
    unit_block = w_down.shape[0]
    units = unit_block * row_size
    scale = HEAD_DIM ** (-0.5)

    place = jnp.arange(length, dtype=jnp.int32)
    ends = jnp.cumsum(doc_lengths, axis=1)
    first = jnp.max(
        jnp.where(ends[:, None, :] <= place[None, :, None], ends[:, None, :], 0), axis=2
    )
    table = jnp.asarray(rope_table(HEAD_DIM), jnp.float32)
    angle = (place[None, :] - first).astype(jnp.float32)[..., None] * table
    cosine = jnp.concatenate([jnp.cos(angle), jnp.cos(angle)], axis=-1)[:, :, None, :]
    sine = jnp.concatenate([jnp.sin(angle), jnp.sin(angle)], axis=-1)[:, :, None, :]

    total = row_size * seq_size
    shift_back = [((i % row_size) * seq_size + i // row_size, i) for i in range(total)]

    def head_columns(weight, columns):
        return weight.reshape(piece_rows, seq_size, columns).transpose(1, 0, 2)

    head_width = query_width + 2 * key_width
    spare = -(head_width + 2) % 128
    gain_columns = jnp.stack([attn_gain, mlp_gain], axis=1)
    gain_columns = jnp.pad(gain_columns, ((0, 0), (0, spare)))
    heads_pack = jnp.concatenate(
        [
            head_columns(w_query, query_width),
            head_columns(w_key, key_width),
            head_columns(w_value, key_width),
            jnp.broadcast_to(gain_columns, (seq_size, piece_rows, spare + 2)),
        ],
        axis=2,
    )
    pack_width = head_width + 2 + spare
    chips = seq_size // 2
    pieces = piece_rows * seq_size
    early_cotangent = gather(cotangent[:1], "seq", 1)
    all_tokens, heads_all, units_pack, out_part = call(
        open_kernel,
        (tokens, heads_pack, w_gate, w_up, w_out),
        [
            low(rows, length, width),
            low(row_size, pieces, pack_width),
            low(seq_size, piece_rows, 2 * units),
            low(row_size, piece_rows, width),
        ],
        sem_pairs(2 * chips * PARTS) * 2 + sem_pairs(seq_size - 1) + sem_pairs(4) * 2 + sem_pairs(1),
        0,
    )
    units_mine = lax.all_to_all(units_pack, "seq", 0, 0, tiled=True).reshape(pieces, 2 * units)
    late_down, all_tokens = lax.optimization_barrier((w_down, all_tokens))
    down_part = gather(late_down, "row", 0)
    all_tokens = all_tokens.reshape(count, width)
    heads_all = heads_all.reshape(width, pack_width)
    w_qkv = heads_all[:, :head_width]
    gains = heads_all[:, head_width : head_width + 2].astype(jnp.float32).T
    out_part = out_part.reshape(query_width, width)

    inputs = all_tokens.astype(jnp.float32)
    hidden_one = (inputs * norm_scale(inputs) * gains[0]).astype(jnp.bfloat16)
    qkv = jnp.dot(hidden_one, w_qkv, preferred_element_type=jnp.float32)
    queries = rotate(
        qkv[:, :query_width].reshape(rows, length, heads, HEAD_DIM), cosine, sine
    ).astype(jnp.bfloat16).reshape(rows, length, key_heads, groups, HEAD_DIM)
    keys = rotate(
        qkv[:, query_width : query_width + key_width].reshape(rows, length, key_heads, HEAD_DIM),
        cosine,
        sine,
    ).astype(jnp.bfloat16)
    values = (
        qkv[:, query_width + key_width :]
        .astype(jnp.bfloat16)
        .reshape(rows, length, key_heads, HEAD_DIM)
    )
    raw = jnp.einsum("rqhgd,rkhd->rhgqk", queries, keys, preferred_element_type=jnp.float32)
    allowed = (place[None, None, :] <= place[None, :, None]) & (
        place[None, None, :] >= first[:, :, None]
    )
    probs = jax.nn.softmax(jnp.where(allowed[:, None, None], raw * scale, -1e30), axis=-1)
    probs_low = probs.astype(jnp.bfloat16)
    mixed = (
        jnp.einsum("rhgqk,rkhd->rqhgd", probs_low, values, preferred_element_type=jnp.float32)
        .astype(jnp.bfloat16)
        .reshape(count, query_width)
    )
    branch = jnp.dot(mixed, out_part, preferred_element_type=jnp.float32).astype(jnp.bfloat16)
    middle, hidden_two, w_units = call(
        middle_kernel,
        (branch.reshape(rows, length, width), tokens, gains[1:2], units_mine),
        [full(rows, stretch, width), low(rows, length, width), low(row_size, pieces, 2 * units)],
        seq_scratch(chips, stretch, width)
        + sem_pairs(2 * chips)
        + sem_pairs(2 * PARTS * (chips - 1))
        + sem_pairs(2 * chips * PARTS) * 2
        + sem_pairs(4)
        + [pltpu.SemaphoreType.DMA],
        1,
        far_out=(2,),
    )
    late_cotangent, hidden_two = lax.optimization_barrier((cotangent[1:], hidden_two))
    all_cotangent = jnp.concatenate([early_cotangent, gather(late_cotangent, "seq", 1)])
    all_cotangent = all_cotangent.reshape(count, width)
    hidden_two = hidden_two.reshape(count, width)
    w_units = w_units.reshape(width, 2 * units)
    both = jnp.dot(hidden_two, w_units, preferred_element_type=jnp.float32)
    gate_sum, up_sum = both[:, :units], both[:, units:]
    sigma = jax.nn.sigmoid(gate_sum)
    silu_value = gate_sum * sigma
    active = (silu_value * up_sum).astype(jnp.bfloat16)
    mlp_branch = jnp.dot(active, down_part, preferred_element_type=jnp.float32)
    mlp_branch, down_part = lax.optimization_barrier((mlp_branch.astype(jnp.bfloat16), down_part))
    mlp_branch = scatter(mlp_branch.reshape(rows, length, width), "seq", 1)
    output = (middle + mlp_branch.astype(jnp.float32)).astype(jnp.bfloat16)

    grad_active = contract_last(all_cotangent, down_part)
    grad_down = contract_first(active, all_cotangent).astype(jnp.bfloat16)
    grad_up_low = (grad_active * silu_value).astype(jnp.bfloat16)
    grad_gate_low = (grad_active * up_sum * sigma * (1.0 + gate_sum * (1.0 - sigma))).astype(
        jnp.bfloat16
    )
    both_grads = jnp.concatenate([grad_gate_low, grad_up_low], axis=1)
    grad_hidden = contract_last(both_grads, w_units).astype(jnp.bfloat16)
    grad_units = contract_first(hidden_two, both_grads).astype(jnp.bfloat16)
    grad_hidden, mlp_branch, grad_down = lax.optimization_barrier(
        (grad_hidden, mlp_branch, grad_down)
    )
    grad_middle, grad_branch, grad_gain_two, units_mine = call(
        back_kernel,
        (
            grad_hidden.reshape(rows, length, width),
            cotangent,
            middle,
            gains[1:2],
            grad_units.reshape(row_size, pieces, 2 * units),
        ),
        [
            full(rows, stretch, width),
            low(rows, length, width),
            full(1, width),
            low(pieces, 2 * units),
        ],
        seq_scratch(chips, stretch, width)
        + row_scratch(pieces, 2 * units)
        + [pltpu.VMEM((row_size, pieces, 2 * units), jnp.bfloat16)]
        + sem_pairs(2 * chips)
        + sem_pairs(2 * PARTS * (chips - 1))
        + sem_pairs(2 * chips * PARTS) * 2
        + sem_pairs(6)
        + [pltpu.SemaphoreType.DMA],
        2,
        far_in=(4,),
    )
    grad_branch, grad_down = lax.optimization_barrier((grad_branch, grad_down))
    grad_down = scatter(grad_down, "row", 0)
    grad_units = lax.all_to_all(
        units_mine.reshape(seq_size, piece_rows, 2 * units), "seq", 0, 0, tiled=True
    )
    grad_branch = grad_branch.reshape(count, width)
    grad_mixed = contract_last(grad_branch, out_part).astype(jnp.bfloat16)
    grad_out = scatter(contract_first(mixed, grad_branch).astype(jnp.bfloat16), "row", 0)
    grad_out = lax.ppermute(grad_out, BOTH, shift_back).astype(jnp.float32)
    grad_grouped = grad_mixed.reshape(rows, length, key_heads, groups, HEAD_DIM)
    grad_probs = jnp.einsum(
        "rqhgd,rkhd->rhgqk", grad_grouped, values, preferred_element_type=jnp.float32
    )
    delta = jnp.sum(probs * grad_probs, axis=-1, keepdims=True)
    grad_raw = (scale * probs * (grad_probs - delta)).astype(jnp.bfloat16)
    grad_queries = jnp.einsum(
        "rhgqk,rkhd->rqhgd", grad_raw, keys, preferred_element_type=jnp.float32
    )
    grad_keys = jnp.einsum(
        "rhgqk,rqhgd->rkhd", grad_raw, queries, preferred_element_type=jnp.float32
    )
    grad_values = jnp.einsum(
        "rhgqk,rqhgd->rkhd", probs_low, grad_grouped, preferred_element_type=jnp.float32
    )
    grad_qkv_low = jnp.concatenate(
        [
            rotate_back(grad_queries.reshape(rows, length, heads, HEAD_DIM), cosine, sine).reshape(
                count, query_width
            ),
            rotate_back(grad_keys, cosine, sine).reshape(count, key_width),
            grad_values.reshape(count, key_width),
        ],
        axis=1,
    ).astype(jnp.bfloat16)
    grad_qkv = contract_first(hidden_one, grad_qkv_low).astype(jnp.bfloat16)
    grad_hidden = contract_last(grad_qkv_low, w_qkv).astype(jnp.bfloat16)
    grad_tokens, gain_sums, grad_qkv = call(
        close_kernel,
        (
            grad_hidden.reshape(rows, length, width),
            tokens,
            grad_middle,
            gains[0:1],
            grad_gain_two,
            grad_qkv.reshape(row_size, pieces, head_width),
        ),
        [
            full(rows, stretch, width),
            full(2, width),
            low(seq_size, piece_rows, head_width),
        ],
        [pltpu.VMEM((pieces, head_width), jnp.bfloat16)]
        + seq_scratch(chips, stretch, width)
        + row_scratch(pieces, head_width)
        + [pltpu.VMEM((3, 2, width), jnp.float32)]
        + [pltpu.VMEM((seq_size + row_size - 2, 2, width), jnp.float32)]
        + sem_pairs(2 * chips)
        + sem_pairs(2 * PARTS * (chips - 1))
        + sem_pairs(6)
        + sem_pairs(seq_size - 1)
        + sem_pairs(seq_size + row_size - 2),
        3,
    )

    grad_gate, grad_up, grad_query, grad_key, grad_value, grad_down = unpack(
        grad_units, grad_qkv, grad_down, row_size, query_width, key_width
    )
    own = (lax.axis_index("row") * seq_size + lax.axis_index("seq")) * piece_rows
    grad_gains = lax.dynamic_slice_in_dim(gain_sums, own, piece_rows, 1)
    return (
        output,
        grad_tokens,
        grad_gains[0],
        grad_query,
        grad_key,
        grad_value,
        grad_out,
        grad_gains[1],
        grad_gate,
        grad_up,
        grad_down,
    )


def local(tokens, cotangent, doc_lengths, attn_gain, w_query, w_key, w_value, *rest):
    whole_heads = w_key.shape[1] % (HEAD_DIM * lax.axis_size("seq")) == 0
    layer = sharded_layer if whole_heads else gathered_layer
    return layer(tokens, cotangent, doc_lengths, attn_gain, w_query, w_key, w_value, *rest)


def solution(mesh):
    return jax.shard_map(
        local,
        mesh=mesh,
        in_specs=(
            P("row", "seq", None),
            P("row", "seq", None),
            P("row", None),
            P(("row", "seq")),
            P(("row", "seq"), None),
            P(("row", "seq"), None),
            P(("row", "seq"), None),
            P(("row", "seq"), None),
            P(("row", "seq")),
            P(("row", "seq"), None),
            P(("row", "seq"), None),
            P(("row", "seq"), None),
        ),
        out_specs=(
            P("row", "seq", None),
            P("row", "seq", None),
            P(("row", "seq")),
            P(("row", "seq"), None),
            P(("row", "seq"), None),
            P(("row", "seq"), None),
            P(("row", "seq"), None),
            P(("row", "seq")),
            P(("row", "seq"), None),
            P(("row", "seq"), None),
            P(("row", "seq"), None),
        ),
        check_vma=False,
    )
```

```python
import math

import jax
import jax.numpy as jnp
import numpy as np
from jax import lax
from jax.experimental import pallas as pl
from jax.experimental.pallas import tpu as pltpu
from jax.sharding import PartitionSpec as P

HEAD_DIM = 64


EPSILON = 1e-05
THETA = 500000.0


def rope_table(head_size):
    half_size = head_size // 2
    plain = THETA ** (-(np.arange(half_size) * 2.0) / head_size)
    factor, low_factor, high_factor, old_span = (32.0, 1.0, 4.0, 8192.0)
    wavelength = 2.0 * math.pi / plain
    smooth = (old_span / wavelength - low_factor) / (high_factor - low_factor)
    blended = (1.0 - smooth) * plain / factor + smooth * plain
    return np.where(
        wavelength < old_span / high_factor,
        plain,
        np.where(wavelength > old_span / low_factor, plain / factor, blended),
    )


def norm_scale(values):
    return lax.rsqrt(jnp.mean(values * values, axis=-1, keepdims=True) + EPSILON)


def norm_back(grad_normed, normed, scale):
    return scale * (grad_normed - normed * jnp.mean(grad_normed * normed, axis=-1, keepdims=True))


def rotate(values, cosine, sine):
    half_size = values.shape[-1] // 2
    turned = jnp.concatenate([-values[..., half_size:], values[..., :half_size]], axis=-1)
    return values * cosine + turned * sine


def rotate_back(grad, cosine, sine):
    half_size = grad.shape[-1] // 2
    turned = grad * sine
    return grad * cosine + jnp.concatenate(
        [turned[..., half_size:], -turned[..., :half_size]], axis=-1
    )


def contract_last(left, right):
    return lax.dot_general(
        left, right, (((1,), (1,)), ((), ())), preferred_element_type=jnp.float32
    )


def contract_first(left, right):
    return lax.dot_general(
        left, right, (((0,), (0,)), ((), ())), preferred_element_type=jnp.float32
    )


def gathered_layer(
    tokens,
    cotangent,
    doc_lengths,
    attn_gain,
    w_query,
    w_key,
    w_value,
    w_out,
    mlp_gain,
    w_gate,
    w_up,
    w_down,
):
    rows, stretch, width = tokens.shape
    count = rows * stretch
    key_width = w_key.shape[1]
    hidden_width = w_gate.shape[1]
    key_heads = key_width // HEAD_DIM
    heads = width // HEAD_DIM
    groups = heads // key_heads
    length = stretch * lax.axis_size("seq")
    block = math.gcd(length, 512)
    scale = HEAD_DIM ** (-0.5)
    table = jnp.asarray(rope_table(HEAD_DIM), jnp.float32)
    place = lax.axis_index("seq") * stretch + jnp.arange(stretch, dtype=jnp.int32)
    live_blocks = ((lax.axis_index("seq") + 1) * stretch + block - 1) // block
    ends = jnp.cumsum(doc_lengths, axis=1)
    first = jnp.max(
        jnp.where(ends[:, None, :] <= place[None, :, None], ends[:, None, :], 0), axis=2
    )
    angle = (place[None, :] - first).astype(jnp.float32)[..., None] * table
    cosine = jnp.concatenate([jnp.cos(angle), jnp.cos(angle)], axis=-1)[:, :, None, :]
    sine = jnp.concatenate([jnp.sin(angle), jnp.sin(angle)], axis=-1)[:, :, None, :]
    inputs = tokens.reshape(count, width).astype(jnp.float32)
    scale_one = norm_scale(inputs)
    normed_one = inputs * scale_one
    gain_piece = lax.all_gather(attn_gain, ("row", "seq"), axis=0, tiled=True)
    query_piece = lax.all_gather(w_query, ("row", "seq"), axis=0, tiled=True)
    key_piece = lax.all_gather(w_key, ("row", "seq"), axis=0, tiled=True)
    value_piece = lax.all_gather(w_value, ("row", "seq"), axis=0, tiled=True)
    hidden_piece = (normed_one * gain_piece.astype(jnp.float32)).astype(jnp.bfloat16)
    query_sum = jnp.dot(hidden_piece, query_piece, preferred_element_type=jnp.float32)
    key_sum = jnp.dot(hidden_piece, key_piece, preferred_element_type=jnp.float32)
    value_sum = jnp.dot(hidden_piece, value_piece, preferred_element_type=jnp.float32)
    hidden_one = hidden_piece
    queries = rotate(query_sum.reshape(rows, stretch, heads, HEAD_DIM), cosine, sine).astype(
        jnp.bfloat16
    )
    keys = rotate(key_sum.reshape(rows, stretch, key_heads, HEAD_DIM), cosine, sine).astype(
        jnp.bfloat16
    )
    values = value_sum.astype(jnp.bfloat16)
    query_grouped = queries.reshape(rows, stretch, key_heads, groups, HEAD_DIM)

    def gather_keys():
        return (
            lax.all_gather(keys.reshape(rows, stretch, key_width), "seq", axis=1, tiled=True),
            lax.all_gather(values.reshape(rows, stretch, key_width), "seq", axis=1, tiled=True),
        )

    key_all, value_all = gather_keys()

    def block_rows(source, index):
        return lax.dynamic_slice_in_dim(source, index * block, block, 1).reshape(
            rows, block, key_heads, HEAD_DIM
        )

    def block_scores(key_block, index):
        raw = jnp.einsum(
            "rqhgd,rkhd->rhgqk", query_grouped, key_block, preferred_element_type=jnp.float32
        )
        key_place = index * block + jnp.arange(block, dtype=jnp.int32)
        allowed = (key_place[None, None, :] <= place[None, :, None]) & (
            key_place[None, None, :] >= first[:, :, None]
        )
        return jnp.where(allowed[:, None, None], raw * scale, -1e30)

    def total_step(index, carry):
        running_max, running_total = carry
        scores = block_scores(block_rows(key_all, index), index)
        new_max = jnp.maximum(running_max, jnp.max(scores, axis=-1))
        new_total = running_total * jnp.exp(running_max - new_max) + jnp.sum(
            jnp.exp(scores - new_max[..., None]), axis=-1
        )
        return (new_max, new_total)

    stat_shape = (rows, key_heads, groups, stretch)
    running_max, running_total = lax.fori_loop(
        0,
        live_blocks,
        total_step,
        (jnp.full(stat_shape, -1e30, jnp.float32), jnp.zeros(stat_shape, jnp.float32)),
    )
    log_total = running_max + jnp.log(running_total)

    def mix_step(index, mixed_sum):
        probs = jnp.exp(block_scores(block_rows(key_all, index), index) - log_total[..., None])
        return mixed_sum + jnp.einsum(
            "rhgqk,rkhd->rqhgd",
            probs.astype(jnp.bfloat16),
            block_rows(value_all, index),
            preferred_element_type=jnp.float32,
        )

    mixed_sum = lax.fori_loop(
        0,
        live_blocks,
        mix_step,
        jnp.zeros((rows, stretch, key_heads, groups, HEAD_DIM), jnp.float32),
    )
    mixed = mixed_sum.reshape(count, width).astype(jnp.bfloat16)
    attn_branch = jnp.dot(
        mixed,
        lax.all_gather(w_out, ("row", "seq"), axis=0, tiled=True),
        preferred_element_type=jnp.float32,
    )
    middle = inputs + attn_branch
    scale_two = norm_scale(middle)
    normed_two = middle * scale_two
    gain_piece = lax.all_gather(mlp_gain, ("row", "seq"), axis=0, tiled=True)
    gate_piece = lax.all_gather(w_gate, ("row", "seq"), axis=0, tiled=True)
    up_piece = lax.all_gather(w_up, ("row", "seq"), axis=0, tiled=True)
    hidden_piece = (normed_two * gain_piece.astype(jnp.float32)).astype(jnp.bfloat16)
    gate_sum, up_sum, hidden_two = (
        jnp.dot(hidden_piece, gate_piece, preferred_element_type=jnp.float32),
        jnp.dot(hidden_piece, up_piece, preferred_element_type=jnp.float32),
        hidden_piece,
    )
    sigma = jax.nn.sigmoid(gate_sum)
    silu_value = gate_sum * sigma
    active = (silu_value * up_sum).astype(jnp.bfloat16)
    mlp_branch = jnp.dot(
        active,
        lax.all_gather(w_down, ("row", "seq"), axis=0, tiled=True),
        preferred_element_type=jnp.float32,
    )
    output = (middle + mlp_branch).astype(jnp.bfloat16).reshape(rows, stretch, width)
    grad_out_low = cotangent.reshape(count, width)
    grad_active = contract_last(
        grad_out_low, lax.all_gather(w_down, ("row", "seq"), axis=0, tiled=True)
    )
    grad_down = lax.psum_scatter(
        contract_first(active, grad_out_low), ("row", "seq"), scatter_dimension=0, tiled=True
    )
    grad_up_low = (grad_active * silu_value).astype(jnp.bfloat16)
    grad_gate_low = (grad_active * up_sum * sigma * (1.0 + gate_sum * (1.0 - sigma))).astype(
        jnp.bfloat16
    )
    both_grads = jnp.concatenate([grad_gate_low, grad_up_low], axis=1)
    gain_piece = lax.all_gather(mlp_gain, ("row", "seq"), axis=0, tiled=True)
    gate_piece = lax.all_gather(w_gate, ("row", "seq"), axis=0, tiled=True)
    up_piece = lax.all_gather(w_up, ("row", "seq"), axis=0, tiled=True)
    grad_piece = contract_last(grad_gate_low, gate_piece) + contract_last(grad_up_low, up_piece)
    normed_piece = normed_two
    grad_normed_two = grad_piece * gain_piece.astype(jnp.float32)
    grad_gain_two = jnp.sum(normed_piece * grad_piece, axis=0)
    grad_gate_up = lax.psum_scatter(
        contract_first(hidden_two, both_grads), ("row", "seq"), scatter_dimension=0, tiled=True
    )
    grad_gate = grad_gate_up[:, :hidden_width]
    grad_up = grad_gate_up[:, hidden_width:]
    grad_middle = grad_out_low.astype(jnp.float32) + norm_back(
        grad_normed_two, normed_two, scale_two
    )
    grad_branch_low = grad_middle.astype(jnp.bfloat16)
    grad_mixed = contract_last(
        grad_branch_low, lax.all_gather(w_out, ("row", "seq"), axis=0, tiled=True)
    ).astype(jnp.bfloat16)
    grad_out = lax.psum_scatter(
        contract_first(mixed, grad_branch_low), ("row", "seq"), scatter_dimension=0, tiled=True
    )
    grad_grouped = grad_mixed.reshape(rows, stretch, key_heads, groups, HEAD_DIM)
    key_back, value_back = gather_keys()

    def delta_step(index, total):
        probs = jnp.exp(block_scores(block_rows(key_back, index), index) - log_total[..., None])
        grad_probs = jnp.einsum(
            "rqhgd,rkhd->rhgqk",
            grad_grouped,
            block_rows(value_back, index),
            preferred_element_type=jnp.float32,
        )
        return total + jnp.sum(probs * grad_probs, axis=-1)

    delta = lax.fori_loop(0, live_blocks, delta_step, jnp.zeros(stat_shape, jnp.float32))

    def grad_step(index, carry):
        grad_queries, grad_key_all, grad_value_all = carry
        key_block = block_rows(key_back, index)
        probs = jnp.exp(block_scores(key_block, index) - log_total[..., None])
        grad_probs = jnp.einsum(
            "rqhgd,rkhd->rhgqk",
            grad_grouped,
            block_rows(value_back, index),
            preferred_element_type=jnp.float32,
        )
        grad_raw = (scale * probs * (grad_probs - delta[..., None])).astype(jnp.bfloat16)
        grad_queries = grad_queries + jnp.einsum(
            "rhgqk,rkhd->rqhgd", grad_raw, key_block, preferred_element_type=jnp.float32
        )
        key_part = jnp.einsum(
            "rhgqk,rqhgd->rkhd", grad_raw, query_grouped, preferred_element_type=jnp.float32
        ).reshape(rows, block, key_width)
        value_part = jnp.einsum(
            "rhgqk,rqhgd->rkhd",
            probs.astype(jnp.bfloat16),
            grad_grouped,
            preferred_element_type=jnp.float32,
        ).reshape(rows, block, key_width)
        return (
            grad_queries,
            lax.dynamic_update_slice_in_dim(grad_key_all, key_part, index * block, 1),
            lax.dynamic_update_slice_in_dim(grad_value_all, value_part, index * block, 1),
        )

    grad_queries, grad_key_all, grad_value_all = lax.fori_loop(
        0,
        live_blocks,
        grad_step,
        (
            jnp.zeros((rows, stretch, key_heads, groups, HEAD_DIM), jnp.float32),
            jnp.zeros((rows, length, key_width), jnp.float32),
            jnp.zeros((rows, length, key_width), jnp.float32),
        ),
    )
    grad_key_sum, grad_value_sum = (
        lax.psum_scatter(
            grad_key_all.astype(jnp.bfloat16), "seq", scatter_dimension=1, tiled=True
        ).astype(jnp.float32),
        lax.psum_scatter(
            grad_value_all.astype(jnp.bfloat16), "seq", scatter_dimension=1, tiled=True
        ).astype(jnp.float32),
    )
    grad_query_low = (
        rotate_back(grad_queries.reshape(rows, stretch, heads, HEAD_DIM), cosine, sine)
        .reshape(count, width)
        .astype(jnp.bfloat16)
    )
    grad_key_low = (
        rotate_back(grad_key_sum.reshape(rows, stretch, key_heads, HEAD_DIM), cosine, sine)
        .reshape(count, key_width)
        .astype(jnp.bfloat16)
    )
    grad_value_low = grad_value_sum.reshape(count, key_width).astype(jnp.bfloat16)
    gain_piece = lax.all_gather(attn_gain, ("row", "seq"), axis=0, tiled=True)
    query_piece = lax.all_gather(w_query, ("row", "seq"), axis=0, tiled=True)
    key_piece = lax.all_gather(w_key, ("row", "seq"), axis=0, tiled=True)
    value_piece = lax.all_gather(w_value, ("row", "seq"), axis=0, tiled=True)
    grad_piece = (
        contract_last(grad_query_low, query_piece)
        + contract_last(grad_key_low, key_piece)
        + contract_last(grad_value_low, value_piece)
    )
    normed_piece = normed_one
    grad_normed_one = grad_piece * gain_piece.astype(jnp.float32)
    grad_gain_one = jnp.sum(normed_piece * grad_piece, axis=0)
    grad_query, grad_key, grad_value, grad_attn_gain, grad_mlp_gain = (
        lax.psum_scatter(
            contract_first(hidden_one, grad_query_low),
            ("row", "seq"),
            scatter_dimension=0,
            tiled=True,
        ),
        lax.psum_scatter(
            contract_first(hidden_one, grad_key_low),
            ("row", "seq"),
            scatter_dimension=0,
            tiled=True,
        ),
        lax.psum_scatter(
            contract_first(hidden_one, grad_value_low),
            ("row", "seq"),
            scatter_dimension=0,
            tiled=True,
        ),
        lax.psum_scatter(grad_gain_one, ("row", "seq"), scatter_dimension=0, tiled=True),
        lax.psum_scatter(grad_gain_two, ("row", "seq"), scatter_dimension=0, tiled=True),
    )
    grad_tokens = (grad_middle + norm_back(grad_normed_one, normed_one, scale_one)).reshape(
        rows, stretch, width
    )
    return (
        output,
        grad_tokens,
        grad_attn_gain,
        grad_query,
        grad_key,
        grad_value,
        grad_out,
        grad_mlp_gain,
        grad_gate,
        grad_up,
        grad_down,
    )


MESH = pl.DeviceIdType.MESH
VMEM_LIMIT = 60 * 1024 * 1024
PARTS = 2


def neighbours():
    row, seq = lax.axis_index("row"), lax.axis_index("seq")
    row_size, seq_size = lax.axis_size("row"), lax.axis_size("seq")
    return dict(
        row=row,
        seq=seq,
        z=seq // 2,
        core=seq % 2,
        up=(row, (seq + 2) % seq_size),
        down=(row, (seq + seq_size - 2) % seq_size),
        pair=(row, seq + 1 - 2 * (seq % 2)),
        side=(row + 1 - 2 * (row % 2), seq),
        across=((row + row_size // 2) % row_size, seq),
        corner=((row + 1 - 2 * (row % 2) + row_size // 2) % row_size, seq),
        side_row=row + 1 - 2 * (row % 2),
        across_row=(row + row_size // 2) % row_size,
    )


def greet(peers, route=None):
    barrier = pltpu.get_barrier_semaphore()
    for peer in peers:
        pl.semaphore_signal(barrier, inc=1, device_id=peer, device_id_type=MESH)
    amount = len(peers)
    if route is not None:
        moves, *ends = route

        @pl.when(moves)
        def _():
            for peer in ends:
                pl.semaphore_signal(barrier, inc=1, device_id=peer, device_id_type=MESH)

        amount = amount + jnp.where(moves, len(ends), 0)
    pl.semaphore_wait(barrier, amount)


def send(source, target, sems, index, peer):
    copy = pltpu.make_async_remote_copy(
        src_ref=source,
        dst_ref=target,
        send_sem=sems[0].at[index],
        recv_sem=sems[1].at[index],
        device_id=peer,
        device_id_type=MESH,
    )
    copy.start()
    return copy


def sem_pairs(amount):
    return [pltpu.SemaphoreType.DMA((amount,)), pltpu.SemaphoreType.DMA((amount,))]


def by_rows(amount, step, body):
    def one(i, carry):
        body(pl.ds(pl.multiple_of(i * step, step), step))
        return carry

    lax.fori_loop(0, amount // step, one, 0)


def copy_rows(target, source):
    def one(rows):
        target[rows] = source[rows]

    by_rows(source.shape[0], 16, one)


def gather_seq_steps(here, whole, stretch, pair_sems, ring_sems):
    seq, chips = here["seq"], lax.axis_size("seq") // 2
    seq_size = 2 * chips
    piece = stretch // PARTS
    rings, pairs, last = [], [], {}

    def spot(owner, part):
        return pl.ds(pl.multiple_of(owner * stretch + part * piece, piece), piece)

    def ring(step, part):
        owners = (seq + seq_size - 2 * step) % seq_size, (seq + 2 * step) % seq_size
        for half, peer in ((0, "up"), (1, "down")):
            view = whole.at[half, spot(owners[half], part)]
            slot = (step * PARTS + part) * 2 + half
            if step > 0:
                last[half, part].wait_recv()
            if step < chips - 1:
                last[half, part] = send(view, view, ring_sems, slot, here[peer])
                rings.append(last[half, part])
            pairs.append(send(view, view, pair_sems, slot, here["pair"]))

    def both(step):
        for part in range(PARTS):
            ring(step, part)

    def finish():
        for copy in pairs:
            copy.wait()
        for copy in rings:
            copy.wait_send()

    return ring, [lambda step=step: both(step) for step in range(chips)] + [finish]


def reduce_seq_steps(here, part, stretch, pair_in, total, ring_in, pair_sems, ring_sems, done):
    z, core, chips = here["z"], here["core"], lax.axis_size("seq") // 2
    piece = stretch // PARTS
    copies, pair_copies, last = [], {}, {}
    order = [spot for t in range(chips - 1) for spot in ((chips - 1 - t, 0), (1 + t, 1))]
    order += [(0, 0), (0, 1)]

    def place(far):
        return (z + far) % chips

    def each(number, body):
        def one(rows):
            body(pl.ds(pl.multiple_of(number * piece + rows.start, 16), 16))

        by_rows(piece, 16, one)

    def pair_sum(far, half, number):
        chip = place(far)
        base = (2 * chip + core) * stretch
        if number == 0:
            pair_copies[far, half].wait_recv()

        def add(rows):
            mine = part[half, pl.ds(pl.multiple_of(base + rows.start, 16), 16)]
            other = pair_in[chip, half, rows]
            total[chip, half, rows] = (
                mine.astype(jnp.float32) + other.astype(jnp.float32)
            ).astype(jnp.bfloat16)

        each(number, add)

    def ring_send(step, half, number):
        far, peer = ((chips - 1 - step, "up"), (1 + step, "down"))[half]
        chip = place(far)
        if step == 0:
            pair_sum(far, half, number)
        else:
            last[half, number].wait_recv()
            arrived = ring_in.at[step - 1, half]

            def add(rows):
                total[chip, half, rows] = (
                    total[chip, half, rows].astype(jnp.float32)
                    + arrived[rows].astype(jnp.float32)
                ).astype(jnp.bfloat16)

            each(number, add)
        rows = pl.ds(number * piece, piece)
        last[half, number] = send(
            total.at[chip, half, rows],
            ring_in.at[step, half, rows],
            ring_sems,
            (step * PARTS + number) * 2 + half,
            here[peer],
        )
        copies.append(last[half, number])

    def ring(step):
        for number in range(PARTS):
            for half in range(2):
                ring_send(step, half, number)

    def first_step():
        for index, (far, half) in enumerate(order):
            chip = place(far)
            spot = pl.ds(pl.multiple_of((2 * chip + 1 - core) * stretch, stretch), stretch)
            pair_copies[far, half] = send(
                part.at[half, spot], pair_in.at[chip, half], pair_sems, index, here["pair"]
            )
        ring(0)
        for far, half in order[2:]:
            for number in range(PARTS):
                pair_sum(far, half, number)

    def finish(number):
        for half in range(2):
            last[half, number].wait_recv()
            arrived = ring_in.at[chips - 2, half]

            def close(rows):
                done(
                    half,
                    rows,
                    total[z, half, rows].astype(jnp.float32) + arrived[rows].astype(jnp.float32),
                )

            each(number, close)

    def drain():
        for copy in list(pair_copies.values()) + copies:
            copy.wait_send()

    steps = [first_step] + [lambda step=step: ring(step) for step in range(1, chips - 1)]
    return steps, finish, drain


def gather_row_steps(here, own, whole, sems):
    half = whole.shape[1] // 2
    row, side, across = here["row"], here["side_row"], here["across_row"]
    state = []

    def first_step():
        state.append(send(own, whole.at[row], sems, 0, here["side"]))
        state.append(send(own, whole.at[row], sems, 1, here["across"]))

    def second_step():
        low, high = pl.ds(0, half), pl.ds(half, half)
        state[0].wait_recv()
        state.append(send(whole.at[side, low], whole.at[side, low], sems, 2, here["across"]))
        state[1].wait_recv()
        state.append(send(whole.at[across, high], whole.at[across, high], sems, 3, here["side"]))

    def finish():
        for copy in state[2:]:
            copy.wait_recv()
        for copy in state:
            copy.wait_send()

    return [first_step, second_step, finish]


def reduce_row_steps(here, source, part, inbox, sums, sems, done):
    half = part.shape[1] // 2
    row, side, across = here["row"], here["side_row"], here["across_row"]
    corner = (side + 2) % 4
    state = []

    def first_step():
        low, high = pl.ds(0, half), pl.ds(half, half)
        for index, (owner, rows, peer) in enumerate(
            (
                (corner, low, "side"),
                (corner, high, "across"),
                (side, low, "side"),
                (across, high, "across"),
            )
        ):
            state.append(send(source.at[owner, rows], inbox.at[index], sems, index, here[peer]))

    def add(owner, offset, index):
        def run(rows):
            spot = pl.ds(pl.multiple_of(offset + rows.start, 16), 16)
            sums[index, rows] = (
                part[owner, spot].astype(jnp.float32) + inbox[index, rows].astype(jnp.float32)
            ).astype(jnp.bfloat16)

        by_rows(half, 16, run)

    def second_step():
        state[0].wait_recv()
        add(across, 0, 0)
        state.append(send(sums.at[0], inbox.at[4], sems, 4, here["across"]))
        state[1].wait_recv()
        add(side, half, 1)
        state.append(send(sums.at[1], inbox.at[5], sems, 5, here["side"]))
        state[2].wait_recv()
        state[3].wait_recv()

    def finish():
        for offset, one, two in ((0, 2, 4), (half, 3, 5)):
            state[two].wait_recv()

            def close(rows):
                spot = pl.ds(pl.multiple_of(offset + rows.start, 16), 16)
                done(
                    spot,
                    part[row, spot].astype(jnp.float32)
                    + inbox[one, rows].astype(jnp.float32)
                    + inbox[two, rows].astype(jnp.float32),
                )

            by_rows(half, 16, close)
        for copy in state:
            copy.wait_send()

    return [first_step, second_step, finish]


def exchange_seq(here, source, target_of, sems):
    seq, seq_size = here["seq"], lax.axis_size("seq")
    copies = []
    for far in range(1, seq_size):
        dest = (seq + far) % seq_size
        copies.append(
            send(source.at[dest], target_of(seq), sems, far - 1, (here["row"], dest))
        )
    return copies


def seq_peers(here):
    seq_size = lax.axis_size("seq")
    return [(here["row"], (here["seq"] + far) % seq_size) for far in range(1, seq_size)]


def call(kernel, args, out_shape, scratch, collective_id, far_in=(), far_out=()):
    near, far = (pl.BlockSpec(memory_space=space) for space in (pltpu.VMEM, pl.ANY))
    return pl.pallas_call(
        kernel,
        out_shape=out_shape,
        in_specs=[far if i in far_in else near for i in range(len(args))],
        out_specs=[far if i in far_out else near for i in range(len(out_shape))],
        scratch_shapes=scratch,
        compiler_params=pltpu.CompilerParams(
            collective_id=collective_id, has_side_effects=True, vmem_limit_bytes=VMEM_LIMIT
        ),
    )(*args)


def low(*shape):
    return jax.ShapeDtypeStruct(shape, jnp.bfloat16)


def full(*shape):
    return jax.ShapeDtypeStruct(shape, jnp.float32)


def shift_route(here):
    row_size, seq_size = lax.axis_size("row"), lax.axis_size("seq")
    index = here["row"] * seq_size + here["seq"]
    origin = here["seq"] * row_size + here["row"]
    target = index % row_size, index // row_size
    return target, (origin // seq_size, origin % seq_size), index != origin


def open_kernel(
    tokens, heads_pack, w_gate, w_up, out_piece,
    all_tokens, heads_all, units_pack, out_all,
    packed, pair_a, pair_b, ring_a, ring_b, heads_a, heads_b, row_a, row_b, out_a, out_b,
    shift_a, shift_b, local_sems,
):
    here = neighbours()
    seq, row = here["seq"], here["row"]
    stretch = tokens.shape[1]
    piece = heads_pack.shape[1]
    target, origin, moves = shift_route(here)
    greet(seq_peers(here) + [here["side"], here["across"]], (moves, target, origin))

    def spot(owner):
        return pl.ds(pl.multiple_of(owner * piece, piece), piece)

    def shift():
        return pltpu.make_async_remote_copy(
            src_ref=out_piece,
            dst_ref=out_all.at[target[0]],
            send_sem=shift_a.at[0],
            recv_sem=shift_b.at[0],
            device_id=target,
            device_id_type=MESH,
        )

    heads = exchange_seq(here, heads_pack, lambda s: heads_all.at[row, spot(s)], (heads_a, heads_b))

    @pl.when(moves)
    def _():
        shift().start()

    for half in range(2):
        own = pl.ds(pl.multiple_of(seq * stretch, stretch), stretch)
        copy_rows(all_tokens.at[half, own], tokens.at[half])
    gather_out = gather_row_steps(here, out_all.at[row], out_all, (out_a, out_b))
    gather_heads = gather_row_steps(here, heads_all.at[row], heads_all, (row_a, row_b))
    _, steps = gather_seq_steps(here, all_tokens, stretch, (pair_a, pair_b), (ring_a, ring_b))
    steps[0]()
    own_heads = pltpu.make_async_copy(
        heads_pack.at[seq], heads_all.at[row, spot(seq)], local_sems.at[0]
    )
    own_heads.start()
    own_out = pltpu.make_async_copy(out_piece, out_all.at[row], local_sems.at[1])

    @pl.when(jnp.logical_not(moves))
    def _():
        own_out.start()

    for copy in heads:
        copy.wait_recv()
    own_heads.wait()
    gather_heads[0]()

    @pl.when(moves)
    def _():
        shift().wait()

    @pl.when(jnp.logical_not(moves))
    def _():
        own_out.wait()

    gather_out[0]()
    seq_size, row_size = lax.axis_size("seq"), lax.axis_size("row")
    block = w_gate.shape[1] // (seq_size * row_size)
    for number, weight in enumerate((w_gate, w_up)):
        for r in range(row_size):
            for s in range(seq_size):
                source = (r * seq_size + s) * block
                place = (number * row_size + r) * block
                packed[s, :, place : place + block] = weight[:, source : source + block]
    units_copy = pltpu.make_async_copy(packed, units_pack, local_sems.at[2])
    units_copy.start()
    steps[1]()
    gather_heads[1]()
    gather_out[1]()
    for step in steps[2:]:
        step()
    gather_heads[2]()
    gather_out[2]()
    for copy in heads:
        copy.wait_send()
    units_copy.wait()


def middle_kernel(
    branch, tokens, gain, units_mine,
    middle, hidden, units_all,
    pair_in, total, ring_in, pair_a, pair_b, ring_a, ring_b,
    gpair_a, gpair_b, gring_a, gring_b, row_a, row_b, own_sem,
):
    here = neighbours()
    seq = here["seq"]
    stretch = tokens.shape[1]
    own_copy = pltpu.make_async_copy(units_mine, units_all.at[here["row"]], own_sem)
    own_copy.start()
    greet([here["up"], here["down"], here["pair"], here["side"], here["across"]])

    def done(half, rows, value):
        value = tokens[half, rows].astype(jnp.float32) + value
        middle[half, rows] = value
        normed = value * norm_scale(value)
        spot = pl.ds(pl.multiple_of(seq * stretch + rows.start, 16), 16)
        hidden[half, spot] = (normed * gain[...]).astype(jnp.bfloat16)

    reduce_steps, finish, drain = reduce_seq_steps(
        here, branch, stretch, pair_in, total, ring_in, (pair_a, pair_b), (ring_a, ring_b), done
    )
    units = gather_row_steps(here, units_mine, units_all, (row_a, row_b))
    units[0]()
    for step in reduce_steps:
        step()
    ring, gather_steps = gather_seq_steps(
        here, hidden, stretch, (gpair_a, gpair_b), (gring_a, gring_b)
    )
    for number in range(PARTS):
        finish(number)
        ring(0, number)
    gather_steps[1]()
    units[1]()
    for step in gather_steps[2:]:
        step()
    units[2]()
    drain()
    own_copy.wait()


def back_kernel(
    grad_part, cotangent, middle, gain, units_part,
    grad_middle, grad_low, gain_grad, units_out,
    pair_in, total, ring_in, inbox, sums, units_near, pair_a, pair_b, ring_a, ring_b,
    gpair_a, gpair_b, gring_a, gring_b, row_a, row_b, near_sem,
):
    here = neighbours()
    seq = here["seq"]
    stretch = cotangent.shape[1]
    near_copy = pltpu.make_async_copy(units_part, units_near, near_sem)
    near_copy.start()
    greet([here["up"], here["down"], here["pair"], here["side"], here["across"]])
    gain_grad[...] = jnp.zeros_like(gain_grad)

    def done(half, rows, grad):
        value = middle[half, rows]
        scale = norm_scale(value)
        normed = value * scale
        gain_grad[...] += jnp.sum(normed * grad, axis=0, keepdims=True)
        back = cotangent[half, rows].astype(jnp.float32) + norm_back(
            grad * gain[...], normed, scale
        )
        grad_middle[half, rows] = back
        spot = pl.ds(pl.multiple_of(seq * stretch + rows.start, 16), 16)
        grad_low[half, spot] = back.astype(jnp.bfloat16)

    def done_units(rows, value):
        units_out[rows] = value.astype(jnp.bfloat16)

    reduce_steps, finish, drain = reduce_seq_steps(
        here, grad_part, stretch, pair_in, total, ring_in, (pair_a, pair_b), (ring_a, ring_b), done
    )
    units = reduce_row_steps(
        here, units_part, units_near, inbox, sums, (row_a, row_b), done_units
    )
    units[0]()
    for step in reduce_steps:
        step()
    ring, gather_steps = gather_seq_steps(
        here, grad_low, stretch, (gpair_a, gpair_b), (gring_a, gring_b)
    )
    for number in range(PARTS):
        finish(number)
        ring(0, number)
    near_copy.wait()
    units[1]()
    for step in gather_steps[1:]:
        step()
    units[2]()
    drain()


def sum_small(here, mine, inbox, sems):
    slot = 0
    stages = [seq_peers(here), [here["side"], here["across"], here["corner"]]]
    copies = []
    for number, stage in enumerate(stages):
        sent = [
            send(mine.at[number], inbox.at[slot + i], sems, slot + i, peer)
            for i, peer in enumerate(stage)
        ]
        value = mine[number]
        for i, copy in enumerate(sent):
            copy.wait_recv()
            value = value + inbox[slot + i]
        mine[number + 1] = value
        slot += len(stage)
        copies += sent
    for copy in copies:
        copy.wait_send()
    return slot


def close_kernel(
    grad_part, tokens, grad_middle, gain, gain_two, heads_part, out_part,
    grad_tokens, gain_sums, heads_out, out_out,
    heads_mine, pair_in, total, ring_in, inbox, sums, out_inbox, out_sums, out_mine, small, small_in,
    pair_a, pair_b, ring_a, ring_b, row_a, row_b, heads_a, heads_b, out_a, out_b,
    shift_a, shift_b, small_a, small_b,
):
    here = neighbours()
    seq, chips = here["seq"], lax.axis_size("seq") // 2
    stretch = tokens.shape[1]
    target, origin, moves = shift_route(here)
    greet(
        seq_peers(here) + [here["side"], here["across"], here["corner"]], (moves, target, origin)
    )
    small[0, 0:1] = jnp.zeros_like(small[0, 0:1])
    small[0, 1:2] = gain_two[...]

    def done(half, rows, grad):
        value = tokens[half, rows].astype(jnp.float32)
        scale = norm_scale(value)
        normed = value * scale
        small[0, 0:1] += jnp.sum(normed * grad, axis=0, keepdims=True)
        grad_tokens[half, rows] = grad_middle[half, rows] + norm_back(
            grad * gain[...], normed, scale
        )

    piece = heads_out.shape[1]

    def done_heads(rows, value):
        heads_mine[rows] = value.astype(jnp.bfloat16)

    reduce_steps, finish, drain = reduce_seq_steps(
        here, grad_part, stretch, pair_in, total, ring_in, (pair_a, pair_b), (ring_a, ring_b), done
    )
    def done_out(rows, value):
        out_mine[rows] = value.astype(jnp.bfloat16)

    def shift():
        return pltpu.make_async_remote_copy(
            src_ref=out_mine,
            dst_ref=out_out,
            send_sem=shift_a.at[0],
            recv_sem=shift_b.at[0],
            device_id=origin,
            device_id_type=MESH,
        )

    outs = reduce_row_steps(here, out_part, out_part, out_inbox, out_sums, (out_a, out_b), done_out)
    heads = reduce_row_steps(here, heads_part, heads_part, inbox, sums, (row_a, row_b), done_heads)
    heads[0]()
    outs[0]()
    reduce_steps[0]()
    heads[1]()
    outs[1]()
    for step in reduce_steps[1:]:
        step()
    heads[2]()
    copies = []
    for far in range(1, 2 * chips):
        dest = (seq + far) % (2 * chips)
        rows = pl.ds(pl.multiple_of(dest * piece, piece), piece)
        copies.append(
            send(
                heads_mine.at[rows], heads_out.at[seq], (heads_a, heads_b), far - 1,
                (here["row"], dest),
            )
        )
    outs[2]()

    @pl.when(moves)
    def _():
        shift().start()

    @pl.when(jnp.logical_not(moves))
    def _():
        copy_rows(out_out, out_mine)

    for number in range(PARTS):
        finish(number)
    copy_rows(heads_out.at[seq], heads_mine.at[pl.ds(pl.multiple_of(seq * piece, piece), piece)])
    sum_small(here, small, small_in, (small_a, small_b))
    gain_sums[...] = small[2]
    for copy in copies:
        copy.wait()

    @pl.when(moves)
    def _():
        shift().wait()

    drain()


def seq_scratch(chips, stretch, width):
    return [
        pltpu.VMEM((chips, 2, stretch, width), jnp.bfloat16),
        pltpu.VMEM((chips, 2, stretch, width), jnp.bfloat16),
        pltpu.VMEM((chips - 1, 2, stretch, width), jnp.bfloat16),
    ]


def row_scratch(pieces, columns):
    return [
        pltpu.VMEM((6, pieces // 2, columns), jnp.bfloat16),
        pltpu.VMEM((2, pieces // 2, columns), jnp.bfloat16),
    ]


def unpack(units, heads, down, out, row_size, query_width, key_width):
    seq_size, rows, columns = units.shape
    block = columns // 2 // row_size
    down_rows, width = down.shape

    def kernel(
        gate, up, heads_ref, down_ref, out_ref, gate_out, up_out, query, key, value, down_out, out_out
    ):
        for source, target in ((gate, gate_out), (up, up_out)):
            for s in range(seq_size):
                target[:, s * block : (s + 1) * block] = source[s].astype(jnp.float32)
        down_out[...] = down_ref[...].astype(jnp.float32)

        @pl.when(pl.program_id(0) == 0)
        def _():
            out_out[...] = out_ref[...].astype(jnp.float32)
            start = 0
            for target, size in ((query, query_width), (key, key_width), (value, key_width)):
                target[...] = jnp.concatenate(
                    [
                        heads_ref[s, :, start : start + size].astype(jnp.float32)
                        for s in range(seq_size)
                    ],
                    axis=1,
                )
                start += size

    whole = full(rows, seq_size * columns // 2)
    head_shapes = [full(rows, seq_size * w) for w in (query_width, key_width, key_width)]
    down_block = pl.BlockSpec((down_rows // row_size, width), lambda r: (r, 0))
    return pl.pallas_call(
        kernel,
        grid=(row_size,),
        out_shape=[whole, whole] + head_shapes + [full(down_rows, width), full(*out.shape)],
        in_specs=[
            pl.BlockSpec((seq_size, rows, block), lambda r: (0, 0, r)),
            pl.BlockSpec((seq_size, rows, block), lambda r: (0, 0, row_size + r)),
            pl.BlockSpec(heads.shape, lambda r: (0, 0, 0)),
            down_block,
            pl.BlockSpec(out.shape, lambda r: (0, 0)),
        ],
        out_specs=[pl.BlockSpec((rows, seq_size * block), lambda r: (0, r))] * 2
        + [pl.BlockSpec(x.shape, lambda r: (0, 0)) for x in head_shapes]
        + [down_block, pl.BlockSpec(out.shape, lambda r: (0, 0))],
    )(units, units, heads, down, out)


BOTH = ("row", "seq")


def gather(piece, axis_name, axis):
    return lax.all_gather(piece, axis_name, axis=axis, tiled=True)


def scatter(whole, axis_name, axis):
    return lax.psum_scatter(whole, axis_name, scatter_dimension=axis, tiled=True)


def sharded_layer(
    tokens,
    cotangent,
    doc_lengths,
    attn_gain,
    w_query,
    w_key,
    w_value,
    w_out,
    mlp_gain,
    w_gate,
    w_up,
    w_down,
):
    row_size, seq_size = lax.axis_size("row"), lax.axis_size("seq")
    rows, stretch, width = tokens.shape
    length = stretch * seq_size
    count = rows * length
    piece_rows = w_query.shape[0]
    key_heads = w_key.shape[1] // HEAD_DIM // seq_size
    heads = w_query.shape[1] // HEAD_DIM // seq_size
    groups = heads // key_heads
    query_width, key_width = heads * HEAD_DIM, key_heads * HEAD_DIM
    unit_block = w_down.shape[0]
    units = unit_block * row_size
    scale = HEAD_DIM ** (-0.5)

    place = jnp.arange(length, dtype=jnp.int32)
    ends = jnp.cumsum(doc_lengths, axis=1)
    first = jnp.max(
        jnp.where(ends[:, None, :] <= place[None, :, None], ends[:, None, :], 0), axis=2
    )
    table = jnp.asarray(rope_table(HEAD_DIM), jnp.float32)
    angle = (place[None, :] - first).astype(jnp.float32)[..., None] * table
    cosine = jnp.concatenate([jnp.cos(angle), jnp.cos(angle)], axis=-1)[:, :, None, :]
    sine = jnp.concatenate([jnp.sin(angle), jnp.sin(angle)], axis=-1)[:, :, None, :]

    def head_columns(weight, columns):
        return weight.reshape(piece_rows, seq_size, columns).transpose(1, 0, 2)

    head_width = query_width + 2 * key_width
    spare = -(head_width + 2) % 128
    gain_columns = jnp.stack([attn_gain, mlp_gain], axis=1)
    gain_columns = jnp.pad(gain_columns, ((0, 0), (0, spare)))
    heads_pack = jnp.concatenate(
        [
            head_columns(w_query, query_width),
            head_columns(w_key, key_width),
            head_columns(w_value, key_width),
            jnp.broadcast_to(gain_columns, (seq_size, piece_rows, spare + 2)),
        ],
        axis=2,
    )
    pack_width = head_width + 2 + spare
    chips = seq_size // 2
    pieces = piece_rows * seq_size
    early_cotangent = gather(cotangent[:1], "seq", 1)
    all_tokens, heads_all, units_pack, out_part = call(
        open_kernel,
        (tokens, heads_pack, w_gate, w_up, w_out),
        [
            low(rows, length, width),
            low(row_size, pieces, pack_width),
            low(seq_size, piece_rows, 2 * units),
            low(row_size, piece_rows, width),
        ],
        [pltpu.VMEM((seq_size, piece_rows, 2 * units), jnp.bfloat16)]
        + sem_pairs(2 * chips * PARTS) * 2
        + sem_pairs(seq_size - 1)
        + sem_pairs(4) * 2
        + sem_pairs(1)
        + [pltpu.SemaphoreType.DMA((3,))],
        0,
        far_out=(1, 2, 3),
    )
    units_mine = lax.all_to_all(units_pack, "seq", 0, 0, tiled=True).reshape(pieces, 2 * units)
    late_down, all_tokens = lax.optimization_barrier((w_down, all_tokens))
    down_part = gather(late_down, "row", 0)
    all_tokens = all_tokens.reshape(count, width)
    heads_all = heads_all.reshape(width, pack_width)
    w_qkv = heads_all[:, :head_width]
    gains = heads_all[:, head_width : head_width + 2].astype(jnp.float32).T
    out_part = out_part.reshape(query_width, width)

    inputs = all_tokens.astype(jnp.float32)
    hidden_one = (inputs * norm_scale(inputs) * gains[0]).astype(jnp.bfloat16)
    qkv = jnp.dot(hidden_one, w_qkv, preferred_element_type=jnp.float32)
    queries = rotate(
        qkv[:, :query_width].reshape(rows, length, heads, HEAD_DIM), cosine, sine
    ).astype(jnp.bfloat16).reshape(rows, length, key_heads, groups, HEAD_DIM)
    keys = rotate(
        qkv[:, query_width : query_width + key_width].reshape(rows, length, key_heads, HEAD_DIM),
        cosine,
        sine,
    ).astype(jnp.bfloat16)
    values = (
        qkv[:, query_width + key_width :]
        .astype(jnp.bfloat16)
        .reshape(rows, length, key_heads, HEAD_DIM)
    )
    raw = jnp.einsum("rqhgd,rkhd->rhgqk", queries, keys, preferred_element_type=jnp.float32)
    allowed = (place[None, None, :] <= place[None, :, None]) & (
        place[None, None, :] >= first[:, :, None]
    )
    probs = jax.nn.softmax(jnp.where(allowed[:, None, None], raw * scale, -1e30), axis=-1)
    probs_low = probs.astype(jnp.bfloat16)
    mixed = (
        jnp.einsum("rhgqk,rkhd->rqhgd", probs_low, values, preferred_element_type=jnp.float32)
        .astype(jnp.bfloat16)
        .reshape(count, query_width)
    )
    branch = jnp.dot(mixed, out_part, preferred_element_type=jnp.float32).astype(jnp.bfloat16)
    middle, hidden_two, w_units = call(
        middle_kernel,
        (branch.reshape(rows, length, width), tokens, gains[1:2], units_mine),
        [full(rows, stretch, width), low(rows, length, width), low(row_size, pieces, 2 * units)],
        seq_scratch(chips, stretch, width)
        + sem_pairs(2 * chips)
        + sem_pairs(2 * PARTS * (chips - 1))
        + sem_pairs(2 * chips * PARTS) * 2
        + sem_pairs(4)
        + [pltpu.SemaphoreType.DMA],
        1,
        far_out=(2,),
    )
    late_cotangent, hidden_two = lax.optimization_barrier((cotangent[1:], hidden_two))
    late_cotangent = gather(late_cotangent, "seq", 1)
    all_cotangent = jnp.concatenate([early_cotangent, late_cotangent]).reshape(count, width)
    hidden_two = hidden_two.reshape(count, width)
    w_units = w_units.reshape(width, 2 * units)
    both = jnp.dot(hidden_two, w_units, preferred_element_type=jnp.float32)
    gate_sum, up_sum = both[:, :units], both[:, units:]
    sigma = jax.nn.sigmoid(gate_sum)
    silu_value = gate_sum * sigma
    active = (silu_value * up_sum).astype(jnp.bfloat16)
    mlp_branch = jnp.dot(active, down_part, preferred_element_type=jnp.float32)
    mlp_branch, down_part = lax.optimization_barrier((mlp_branch.astype(jnp.bfloat16), down_part))
    mlp_branch = scatter(mlp_branch.reshape(rows, length, width), "seq", 1)
    output = (middle + mlp_branch.astype(jnp.float32)).astype(jnp.bfloat16)

    grad_active = contract_last(all_cotangent, down_part)
    grad_down = (
        contract_first(active[:length], early_cotangent[0])
        + contract_first(active[length:], late_cotangent.reshape(-1, width))
    ).astype(jnp.bfloat16)
    grad_up_low = (grad_active * silu_value).astype(jnp.bfloat16)
    grad_gate_low = (grad_active * up_sum * sigma * (1.0 + gate_sum * (1.0 - sigma))).astype(
        jnp.bfloat16
    )
    both_grads = jnp.concatenate([grad_gate_low, grad_up_low], axis=1)
    grad_hidden = contract_last(both_grads, w_units).astype(jnp.bfloat16)
    grad_units = contract_first(hidden_two, both_grads).astype(jnp.bfloat16)
    grad_hidden, mlp_branch, grad_down = lax.optimization_barrier(
        (grad_hidden, mlp_branch, grad_down)
    )
    grad_middle, grad_branch, grad_gain_two, units_mine = call(
        back_kernel,
        (
            grad_hidden.reshape(rows, length, width),
            cotangent,
            middle,
            gains[1:2],
            grad_units.reshape(row_size, pieces, 2 * units),
        ),
        [
            full(rows, stretch, width),
            low(rows, length, width),
            full(1, width),
            low(pieces, 2 * units),
        ],
        seq_scratch(chips, stretch, width)
        + row_scratch(pieces, 2 * units)
        + [pltpu.VMEM((row_size, pieces, 2 * units), jnp.bfloat16)]
        + sem_pairs(2 * chips)
        + sem_pairs(2 * PARTS * (chips - 1))
        + sem_pairs(2 * chips * PARTS) * 2
        + sem_pairs(6)
        + [pltpu.SemaphoreType.DMA],
        2,
        far_in=(4,),
    )
    grad_branch, grad_down = lax.optimization_barrier((grad_branch, grad_down))
    grad_down = scatter(grad_down, "row", 0)
    grad_units = lax.all_to_all(
        units_mine.reshape(seq_size, piece_rows, 2 * units), "seq", 0, 0, tiled=True
    )
    grad_branch = grad_branch.reshape(count, width)
    grad_mixed = contract_last(grad_branch, out_part).astype(jnp.bfloat16)
    grad_out = contract_first(mixed, grad_branch).astype(jnp.bfloat16)
    grad_grouped = grad_mixed.reshape(rows, length, key_heads, groups, HEAD_DIM)
    grad_probs = jnp.einsum(
        "rqhgd,rkhd->rhgqk", grad_grouped, values, preferred_element_type=jnp.float32
    )
    delta = jnp.sum(probs * grad_probs, axis=-1, keepdims=True)
    grad_raw = (scale * probs * (grad_probs - delta)).astype(jnp.bfloat16)
    grad_queries = jnp.einsum(
        "rhgqk,rkhd->rqhgd", grad_raw, keys, preferred_element_type=jnp.float32
    )
    grad_keys = jnp.einsum(
        "rhgqk,rqhgd->rkhd", grad_raw, queries, preferred_element_type=jnp.float32
    )
    grad_values = jnp.einsum(
        "rhgqk,rqhgd->rkhd", probs_low, grad_grouped, preferred_element_type=jnp.float32
    )
    grad_qkv_low = jnp.concatenate(
        [
            rotate_back(grad_queries.reshape(rows, length, heads, HEAD_DIM), cosine, sine).reshape(
                count, query_width
            ),
            rotate_back(grad_keys, cosine, sine).reshape(count, key_width),
            grad_values.reshape(count, key_width),
        ],
        axis=1,
    ).astype(jnp.bfloat16)
    grad_qkv = contract_first(hidden_one, grad_qkv_low).astype(jnp.bfloat16)
    grad_hidden = contract_last(grad_qkv_low, w_qkv).astype(jnp.bfloat16)
    grad_tokens, gain_sums, grad_qkv, grad_out = call(
        close_kernel,
        (
            grad_hidden.reshape(rows, length, width),
            tokens,
            grad_middle,
            gains[0:1],
            grad_gain_two,
            grad_qkv.reshape(row_size, pieces, head_width),
            grad_out.reshape(row_size, piece_rows, width),
        ),
        [
            full(rows, stretch, width),
            full(2, width),
            low(seq_size, piece_rows, head_width),
            low(piece_rows, width),
        ],
        [pltpu.VMEM((pieces, head_width), jnp.bfloat16)]
        + seq_scratch(chips, stretch, width)
        + row_scratch(pieces, head_width)
        + row_scratch(piece_rows, width)
        + [pltpu.VMEM((piece_rows, width), jnp.bfloat16)]
        + [pltpu.VMEM((3, 2, width), jnp.float32)]
        + [pltpu.VMEM((seq_size + row_size - 2, 2, width), jnp.float32)]
        + sem_pairs(2 * chips)
        + sem_pairs(2 * PARTS * (chips - 1))
        + sem_pairs(6)
        + sem_pairs(seq_size - 1)
        + sem_pairs(6)
        + sem_pairs(1)
        + sem_pairs(seq_size + row_size - 2),
        3,
    )

    grad_gate, grad_up, grad_query, grad_key, grad_value, grad_down, grad_out = unpack(
        grad_units, grad_qkv, grad_down, grad_out, row_size, query_width, key_width
    )
    own = (lax.axis_index("row") * seq_size + lax.axis_index("seq")) * piece_rows
    grad_gains = lax.dynamic_slice_in_dim(gain_sums, own, piece_rows, 1)
    return (
        output,
        grad_tokens,
        grad_gains[0],
        grad_query,
        grad_key,
        grad_value,
        grad_out,
        grad_gains[1],
        grad_gate,
        grad_up,
        grad_down,
    )


def local(tokens, cotangent, doc_lengths, attn_gain, w_query, w_key, w_value, *rest):
    whole_heads = w_key.shape[1] % (HEAD_DIM * lax.axis_size("seq")) == 0
    layer = sharded_layer if whole_heads else gathered_layer
    return layer(tokens, cotangent, doc_lengths, attn_gain, w_query, w_key, w_value, *rest)


def solution(mesh):
    return jax.shard_map(
        local,
        mesh=mesh,
        in_specs=(
            P("row", "seq", None),
            P("row", "seq", None),
            P("row", None),
            P(("row", "seq")),
            P(("row", "seq"), None),
            P(("row", "seq"), None),
            P(("row", "seq"), None),
            P(("row", "seq"), None),
            P(("row", "seq")),
            P(("row", "seq"), None),
            P(("row", "seq"), None),
            P(("row", "seq"), None),
        ),
        out_specs=(
            P("row", "seq", None),
            P("row", "seq", None),
            P(("row", "seq")),
            P(("row", "seq"), None),
            P(("row", "seq"), None),
            P(("row", "seq"), None),
            P(("row", "seq"), None),
            P(("row", "seq")),
            P(("row", "seq"), None),
            P(("row", "seq"), None),
            P(("row", "seq"), None),
        ),
        check_vma=False,
    )
```

```python
import math

import jax
import jax.numpy as jnp
import numpy as np
from jax import lax
from jax.experimental import pallas as pl
from jax.experimental.pallas import tpu as pltpu
from jax.sharding import PartitionSpec as P

HEAD_DIM = 64


EPSILON = 1e-05
THETA = 500000.0


def rope_table(head_size):
    half_size = head_size // 2
    plain = THETA ** (-(np.arange(half_size) * 2.0) / head_size)
    factor, low_factor, high_factor, old_span = (32.0, 1.0, 4.0, 8192.0)
    wavelength = 2.0 * math.pi / plain
    smooth = (old_span / wavelength - low_factor) / (high_factor - low_factor)
    blended = (1.0 - smooth) * plain / factor + smooth * plain
    return np.where(
        wavelength < old_span / high_factor,
        plain,
        np.where(wavelength > old_span / low_factor, plain / factor, blended),
    )


def norm_scale(values):
    return lax.rsqrt(jnp.mean(values * values, axis=-1, keepdims=True) + EPSILON)


def norm_back(grad_normed, normed, scale):
    return scale * (grad_normed - normed * jnp.mean(grad_normed * normed, axis=-1, keepdims=True))


def rotate(values, cosine, sine):
    half_size = values.shape[-1] // 2
    turned = jnp.concatenate([-values[..., half_size:], values[..., :half_size]], axis=-1)
    return values * cosine + turned * sine


def rotate_back(grad, cosine, sine):
    half_size = grad.shape[-1] // 2
    turned = grad * sine
    return grad * cosine + jnp.concatenate(
        [turned[..., half_size:], -turned[..., :half_size]], axis=-1
    )


def contract_last(left, right):
    return lax.dot_general(
        left, right, (((1,), (1,)), ((), ())), preferred_element_type=jnp.float32
    )


def contract_first(left, right):
    return lax.dot_general(
        left, right, (((0,), (0,)), ((), ())), preferred_element_type=jnp.float32
    )


def gathered_layer(
    tokens,
    cotangent,
    doc_lengths,
    attn_gain,
    w_query,
    w_key,
    w_value,
    w_out,
    mlp_gain,
    w_gate,
    w_up,
    w_down,
):
    rows, stretch, width = tokens.shape
    count = rows * stretch
    key_width = w_key.shape[1]
    hidden_width = w_gate.shape[1]
    key_heads = key_width // HEAD_DIM
    heads = width // HEAD_DIM
    groups = heads // key_heads
    length = stretch * lax.axis_size("seq")
    block = math.gcd(length, 512)
    scale = HEAD_DIM ** (-0.5)
    table = jnp.asarray(rope_table(HEAD_DIM), jnp.float32)
    place = lax.axis_index("seq") * stretch + jnp.arange(stretch, dtype=jnp.int32)
    live_blocks = ((lax.axis_index("seq") + 1) * stretch + block - 1) // block
    ends = jnp.cumsum(doc_lengths, axis=1)
    first = jnp.max(
        jnp.where(ends[:, None, :] <= place[None, :, None], ends[:, None, :], 0), axis=2
    )
    angle = (place[None, :] - first).astype(jnp.float32)[..., None] * table
    cosine = jnp.concatenate([jnp.cos(angle), jnp.cos(angle)], axis=-1)[:, :, None, :]
    sine = jnp.concatenate([jnp.sin(angle), jnp.sin(angle)], axis=-1)[:, :, None, :]
    inputs = tokens.reshape(count, width).astype(jnp.float32)
    scale_one = norm_scale(inputs)
    normed_one = inputs * scale_one
    gain_piece = lax.all_gather(attn_gain, ("row", "seq"), axis=0, tiled=True)
    query_piece = lax.all_gather(w_query, ("row", "seq"), axis=0, tiled=True)
    key_piece = lax.all_gather(w_key, ("row", "seq"), axis=0, tiled=True)
    value_piece = lax.all_gather(w_value, ("row", "seq"), axis=0, tiled=True)
    hidden_piece = (normed_one * gain_piece.astype(jnp.float32)).astype(jnp.bfloat16)
    query_sum = jnp.dot(hidden_piece, query_piece, preferred_element_type=jnp.float32)
    key_sum = jnp.dot(hidden_piece, key_piece, preferred_element_type=jnp.float32)
    value_sum = jnp.dot(hidden_piece, value_piece, preferred_element_type=jnp.float32)
    hidden_one = hidden_piece
    queries = rotate(query_sum.reshape(rows, stretch, heads, HEAD_DIM), cosine, sine).astype(
        jnp.bfloat16
    )
    keys = rotate(key_sum.reshape(rows, stretch, key_heads, HEAD_DIM), cosine, sine).astype(
        jnp.bfloat16
    )
    values = value_sum.astype(jnp.bfloat16)
    query_grouped = queries.reshape(rows, stretch, key_heads, groups, HEAD_DIM)

    def gather_keys():
        return (
            lax.all_gather(keys.reshape(rows, stretch, key_width), "seq", axis=1, tiled=True),
            lax.all_gather(values.reshape(rows, stretch, key_width), "seq", axis=1, tiled=True),
        )

    key_all, value_all = gather_keys()

    def block_rows(source, index):
        return lax.dynamic_slice_in_dim(source, index * block, block, 1).reshape(
            rows, block, key_heads, HEAD_DIM
        )

    def block_scores(key_block, index):
        raw = jnp.einsum(
            "rqhgd,rkhd->rhgqk", query_grouped, key_block, preferred_element_type=jnp.float32
        )
        key_place = index * block + jnp.arange(block, dtype=jnp.int32)
        allowed = (key_place[None, None, :] <= place[None, :, None]) & (
            key_place[None, None, :] >= first[:, :, None]
        )
        return jnp.where(allowed[:, None, None], raw * scale, -1e30)

    def total_step(index, carry):
        running_max, running_total = carry
        scores = block_scores(block_rows(key_all, index), index)
        new_max = jnp.maximum(running_max, jnp.max(scores, axis=-1))
        new_total = running_total * jnp.exp(running_max - new_max) + jnp.sum(
            jnp.exp(scores - new_max[..., None]), axis=-1
        )
        return (new_max, new_total)

    stat_shape = (rows, key_heads, groups, stretch)
    running_max, running_total = lax.fori_loop(
        0,
        live_blocks,
        total_step,
        (jnp.full(stat_shape, -1e30, jnp.float32), jnp.zeros(stat_shape, jnp.float32)),
    )
    log_total = running_max + jnp.log(running_total)

    def mix_step(index, mixed_sum):
        probs = jnp.exp(block_scores(block_rows(key_all, index), index) - log_total[..., None])
        return mixed_sum + jnp.einsum(
            "rhgqk,rkhd->rqhgd",
            probs.astype(jnp.bfloat16),
            block_rows(value_all, index),
            preferred_element_type=jnp.float32,
        )

    mixed_sum = lax.fori_loop(
        0,
        live_blocks,
        mix_step,
        jnp.zeros((rows, stretch, key_heads, groups, HEAD_DIM), jnp.float32),
    )
    mixed = mixed_sum.reshape(count, width).astype(jnp.bfloat16)
    attn_branch = jnp.dot(
        mixed,
        lax.all_gather(w_out, ("row", "seq"), axis=0, tiled=True),
        preferred_element_type=jnp.float32,
    )
    middle = inputs + attn_branch
    scale_two = norm_scale(middle)
    normed_two = middle * scale_two
    gain_piece = lax.all_gather(mlp_gain, ("row", "seq"), axis=0, tiled=True)
    gate_piece = lax.all_gather(w_gate, ("row", "seq"), axis=0, tiled=True)
    up_piece = lax.all_gather(w_up, ("row", "seq"), axis=0, tiled=True)
    hidden_piece = (normed_two * gain_piece.astype(jnp.float32)).astype(jnp.bfloat16)
    gate_sum, up_sum, hidden_two = (
        jnp.dot(hidden_piece, gate_piece, preferred_element_type=jnp.float32),
        jnp.dot(hidden_piece, up_piece, preferred_element_type=jnp.float32),
        hidden_piece,
    )
    sigma = jax.nn.sigmoid(gate_sum)
    silu_value = gate_sum * sigma
    active = (silu_value * up_sum).astype(jnp.bfloat16)
    mlp_branch = jnp.dot(
        active,
        lax.all_gather(w_down, ("row", "seq"), axis=0, tiled=True),
        preferred_element_type=jnp.float32,
    )
    output = (middle + mlp_branch).astype(jnp.bfloat16).reshape(rows, stretch, width)
    grad_out_low = cotangent.reshape(count, width)
    grad_active = contract_last(
        grad_out_low, lax.all_gather(w_down, ("row", "seq"), axis=0, tiled=True)
    )
    grad_down = lax.psum_scatter(
        contract_first(active, grad_out_low), ("row", "seq"), scatter_dimension=0, tiled=True
    )
    grad_up_low = (grad_active * silu_value).astype(jnp.bfloat16)
    grad_gate_low = (grad_active * up_sum * sigma * (1.0 + gate_sum * (1.0 - sigma))).astype(
        jnp.bfloat16
    )
    both_grads = jnp.concatenate([grad_gate_low, grad_up_low], axis=1)
    gain_piece = lax.all_gather(mlp_gain, ("row", "seq"), axis=0, tiled=True)
    gate_piece = lax.all_gather(w_gate, ("row", "seq"), axis=0, tiled=True)
    up_piece = lax.all_gather(w_up, ("row", "seq"), axis=0, tiled=True)
    grad_piece = contract_last(grad_gate_low, gate_piece) + contract_last(grad_up_low, up_piece)
    normed_piece = normed_two
    grad_normed_two = grad_piece * gain_piece.astype(jnp.float32)
    grad_gain_two = jnp.sum(normed_piece * grad_piece, axis=0)
    grad_gate_up = lax.psum_scatter(
        contract_first(hidden_two, both_grads), ("row", "seq"), scatter_dimension=0, tiled=True
    )
    grad_gate = grad_gate_up[:, :hidden_width]
    grad_up = grad_gate_up[:, hidden_width:]
    grad_middle = grad_out_low.astype(jnp.float32) + norm_back(
        grad_normed_two, normed_two, scale_two
    )
    grad_branch_low = grad_middle.astype(jnp.bfloat16)
    grad_mixed = contract_last(
        grad_branch_low, lax.all_gather(w_out, ("row", "seq"), axis=0, tiled=True)
    ).astype(jnp.bfloat16)
    grad_out = lax.psum_scatter(
        contract_first(mixed, grad_branch_low), ("row", "seq"), scatter_dimension=0, tiled=True
    )
    grad_grouped = grad_mixed.reshape(rows, stretch, key_heads, groups, HEAD_DIM)
    key_back, value_back = gather_keys()

    def delta_step(index, total):
        probs = jnp.exp(block_scores(block_rows(key_back, index), index) - log_total[..., None])
        grad_probs = jnp.einsum(
            "rqhgd,rkhd->rhgqk",
            grad_grouped,
            block_rows(value_back, index),
            preferred_element_type=jnp.float32,
        )
        return total + jnp.sum(probs * grad_probs, axis=-1)

    delta = lax.fori_loop(0, live_blocks, delta_step, jnp.zeros(stat_shape, jnp.float32))

    def grad_step(index, carry):
        grad_queries, grad_key_all, grad_value_all = carry
        key_block = block_rows(key_back, index)
        probs = jnp.exp(block_scores(key_block, index) - log_total[..., None])
        grad_probs = jnp.einsum(
            "rqhgd,rkhd->rhgqk",
            grad_grouped,
            block_rows(value_back, index),
            preferred_element_type=jnp.float32,
        )
        grad_raw = (scale * probs * (grad_probs - delta[..., None])).astype(jnp.bfloat16)
        grad_queries = grad_queries + jnp.einsum(
            "rhgqk,rkhd->rqhgd", grad_raw, key_block, preferred_element_type=jnp.float32
        )
        key_part = jnp.einsum(
            "rhgqk,rqhgd->rkhd", grad_raw, query_grouped, preferred_element_type=jnp.float32
        ).reshape(rows, block, key_width)
        value_part = jnp.einsum(
            "rhgqk,rqhgd->rkhd",
            probs.astype(jnp.bfloat16),
            grad_grouped,
            preferred_element_type=jnp.float32,
        ).reshape(rows, block, key_width)
        return (
            grad_queries,
            lax.dynamic_update_slice_in_dim(grad_key_all, key_part, index * block, 1),
            lax.dynamic_update_slice_in_dim(grad_value_all, value_part, index * block, 1),
        )

    grad_queries, grad_key_all, grad_value_all = lax.fori_loop(
        0,
        live_blocks,
        grad_step,
        (
            jnp.zeros((rows, stretch, key_heads, groups, HEAD_DIM), jnp.float32),
            jnp.zeros((rows, length, key_width), jnp.float32),
            jnp.zeros((rows, length, key_width), jnp.float32),
        ),
    )
    grad_key_sum, grad_value_sum = (
        lax.psum_scatter(
            grad_key_all.astype(jnp.bfloat16), "seq", scatter_dimension=1, tiled=True
        ).astype(jnp.float32),
        lax.psum_scatter(
            grad_value_all.astype(jnp.bfloat16), "seq", scatter_dimension=1, tiled=True
        ).astype(jnp.float32),
    )
    grad_query_low = (
        rotate_back(grad_queries.reshape(rows, stretch, heads, HEAD_DIM), cosine, sine)
        .reshape(count, width)
        .astype(jnp.bfloat16)
    )
    grad_key_low = (
        rotate_back(grad_key_sum.reshape(rows, stretch, key_heads, HEAD_DIM), cosine, sine)
        .reshape(count, key_width)
        .astype(jnp.bfloat16)
    )
    grad_value_low = grad_value_sum.reshape(count, key_width).astype(jnp.bfloat16)
    gain_piece = lax.all_gather(attn_gain, ("row", "seq"), axis=0, tiled=True)
    query_piece = lax.all_gather(w_query, ("row", "seq"), axis=0, tiled=True)
    key_piece = lax.all_gather(w_key, ("row", "seq"), axis=0, tiled=True)
    value_piece = lax.all_gather(w_value, ("row", "seq"), axis=0, tiled=True)
    grad_piece = (
        contract_last(grad_query_low, query_piece)
        + contract_last(grad_key_low, key_piece)
        + contract_last(grad_value_low, value_piece)
    )
    normed_piece = normed_one
    grad_normed_one = grad_piece * gain_piece.astype(jnp.float32)
    grad_gain_one = jnp.sum(normed_piece * grad_piece, axis=0)
    grad_query, grad_key, grad_value, grad_attn_gain, grad_mlp_gain = (
        lax.psum_scatter(
            contract_first(hidden_one, grad_query_low),
            ("row", "seq"),
            scatter_dimension=0,
            tiled=True,
        ),
        lax.psum_scatter(
            contract_first(hidden_one, grad_key_low),
            ("row", "seq"),
            scatter_dimension=0,
            tiled=True,
        ),
        lax.psum_scatter(
            contract_first(hidden_one, grad_value_low),
            ("row", "seq"),
            scatter_dimension=0,
            tiled=True,
        ),
        lax.psum_scatter(grad_gain_one, ("row", "seq"), scatter_dimension=0, tiled=True),
        lax.psum_scatter(grad_gain_two, ("row", "seq"), scatter_dimension=0, tiled=True),
    )
    grad_tokens = (grad_middle + norm_back(grad_normed_one, normed_one, scale_one)).reshape(
        rows, stretch, width
    )
    return (
        output,
        grad_tokens,
        grad_attn_gain,
        grad_query,
        grad_key,
        grad_value,
        grad_out,
        grad_mlp_gain,
        grad_gate,
        grad_up,
        grad_down,
    )


MESH = pl.DeviceIdType.MESH
VMEM_LIMIT = 60 * 1024 * 1024
PARTS = 2


def neighbours():
    row, seq = lax.axis_index("row"), lax.axis_index("seq")
    row_size, seq_size = lax.axis_size("row"), lax.axis_size("seq")
    return dict(
        row=row,
        seq=seq,
        z=seq // 2,
        core=seq % 2,
        up=(row, (seq + 2) % seq_size),
        down=(row, (seq + seq_size - 2) % seq_size),
        pair=(row, seq + 1 - 2 * (seq % 2)),
        side=(row + 1 - 2 * (row % 2), seq),
        across=((row + row_size // 2) % row_size, seq),
        corner=((row + 1 - 2 * (row % 2) + row_size // 2) % row_size, seq),
        side_row=row + 1 - 2 * (row % 2),
        across_row=(row + row_size // 2) % row_size,
    )


def greet(peers, route=None):
    barrier = pltpu.get_barrier_semaphore()
    for peer in peers:
        pl.semaphore_signal(barrier, inc=1, device_id=peer, device_id_type=MESH)
    amount = len(peers)
    if route is not None:
        moves, *ends = route

        @pl.when(moves)
        def _():
            for peer in ends:
                pl.semaphore_signal(barrier, inc=1, device_id=peer, device_id_type=MESH)

        amount = amount + jnp.where(moves, len(ends), 0)
    pl.semaphore_wait(barrier, amount)


def send(source, target, sems, index, peer):
    copy = pltpu.make_async_remote_copy(
        src_ref=source,
        dst_ref=target,
        send_sem=sems[0].at[index],
        recv_sem=sems[1].at[index],
        device_id=peer,
        device_id_type=MESH,
    )
    copy.start()
    return copy


def sem_pairs(amount):
    return [pltpu.SemaphoreType.DMA((amount,)), pltpu.SemaphoreType.DMA((amount,))]


def by_rows(amount, step, body):
    def one(i, carry):
        body(pl.ds(pl.multiple_of(i * step, step), step))
        return carry

    lax.fori_loop(0, amount // step, one, 0)


def copy_rows(target, source):
    def one(rows):
        target[rows] = source[rows]

    by_rows(source.shape[0], 16, one)


def gather_seq_steps(here, whole, stretch, pair_sems, ring_sems):
    seq, chips = here["seq"], lax.axis_size("seq") // 2
    seq_size = 2 * chips
    piece = stretch // PARTS
    rings, pairs, last = [], [], {}

    def spot(owner, part):
        return pl.ds(pl.multiple_of(owner * stretch + part * piece, piece), piece)

    def ring(step, part):
        owners = (seq + seq_size - 2 * step) % seq_size, (seq + 2 * step) % seq_size
        for half, peer in ((0, "up"), (1, "down")):
            view = whole.at[half, spot(owners[half], part)]
            slot = (step * PARTS + part) * 2 + half
            if step > 0:
                last[half, part].wait_recv()
            if step < chips - 1:
                last[half, part] = send(view, view, ring_sems, slot, here[peer])
                rings.append(last[half, part])
            pairs.append(send(view, view, pair_sems, slot, here["pair"]))

    def both(step):
        for part in range(PARTS):
            ring(step, part)

    def finish():
        for copy in pairs:
            copy.wait()
        for copy in rings:
            copy.wait_send()

    return ring, [lambda step=step: both(step) for step in range(chips)] + [finish]


def reduce_seq_steps(here, part, stretch, pair_in, total, ring_in, pair_sems, ring_sems, done):
    z, core, chips = here["z"], here["core"], lax.axis_size("seq") // 2
    piece = stretch // PARTS
    copies, pair_copies, last = [], {}, {}
    order = [spot for t in range(chips - 1) for spot in ((chips - 1 - t, 0), (1 + t, 1))]
    order += [(0, 0), (0, 1)]

    def place(far):
        return (z + far) % chips

    def each(number, body):
        def one(rows):
            body(pl.ds(pl.multiple_of(number * piece + rows.start, 16), 16))

        by_rows(piece, 16, one)

    def pair_sum(far, half, number):
        chip = place(far)
        base = (2 * chip + core) * stretch
        if number == 0:
            pair_copies[far, half].wait_recv()

        def add(rows):
            mine = part[half, pl.ds(pl.multiple_of(base + rows.start, 16), 16)]
            other = pair_in[chip, half, rows]
            total[chip, half, rows] = (
                mine.astype(jnp.float32) + other.astype(jnp.float32)
            ).astype(jnp.bfloat16)

        each(number, add)

    def ring_send(step, half, number):
        far, peer = ((chips - 1 - step, "up"), (1 + step, "down"))[half]
        chip = place(far)
        if step == 0:
            pair_sum(far, half, number)
        else:
            last[half, number].wait_recv()
            arrived = ring_in.at[step - 1, half]

            def add(rows):
                total[chip, half, rows] = (
                    total[chip, half, rows].astype(jnp.float32)
                    + arrived[rows].astype(jnp.float32)
                ).astype(jnp.bfloat16)

            each(number, add)
        rows = pl.ds(number * piece, piece)
        last[half, number] = send(
            total.at[chip, half, rows],
            ring_in.at[step, half, rows],
            ring_sems,
            (step * PARTS + number) * 2 + half,
            here[peer],
        )
        copies.append(last[half, number])

    def ring(step):
        for number in range(PARTS):
            for half in range(2):
                ring_send(step, half, number)

    def first_step():
        for index, (far, half) in enumerate(order):
            chip = place(far)
            spot = pl.ds(pl.multiple_of((2 * chip + 1 - core) * stretch, stretch), stretch)
            pair_copies[far, half] = send(
                part.at[half, spot], pair_in.at[chip, half], pair_sems, index, here["pair"]
            )
        ring(0)
        for far, half in order[2:]:
            for number in range(PARTS):
                pair_sum(far, half, number)

    def finish(number):
        for half in range(2):
            last[half, number].wait_recv()
            arrived = ring_in.at[chips - 2, half]

            def close(rows):
                done(
                    half,
                    rows,
                    total[z, half, rows].astype(jnp.float32) + arrived[rows].astype(jnp.float32),
                )

            each(number, close)

    def drain():
        for copy in list(pair_copies.values()) + copies:
            copy.wait_send()

    steps = [first_step] + [lambda step=step: ring(step) for step in range(1, chips - 1)]
    return steps, finish, drain


def gather_row_steps(here, own, whole, sems):
    half = whole.shape[1] // 2
    row, side, across = here["row"], here["side_row"], here["across_row"]
    state = []

    def first_step():
        state.append(send(own, whole.at[row], sems, 0, here["side"]))
        state.append(send(own, whole.at[row], sems, 1, here["across"]))

    def second_step():
        low, high = pl.ds(0, half), pl.ds(half, half)
        state[0].wait_recv()
        state.append(send(whole.at[side, low], whole.at[side, low], sems, 2, here["across"]))
        state[1].wait_recv()
        state.append(send(whole.at[across, high], whole.at[across, high], sems, 3, here["side"]))

    def finish():
        for copy in state[2:]:
            copy.wait_recv()
        for copy in state:
            copy.wait_send()

    return [first_step, second_step, finish]


def reduce_row_steps(here, source, part, inbox, sums, sems, done):
    half = part.shape[1] // 2
    row, side, across = here["row"], here["side_row"], here["across_row"]
    corner = (side + 2) % 4
    state = []

    def first_step():
        low, high = pl.ds(0, half), pl.ds(half, half)
        for index, (owner, rows, peer) in enumerate(
            (
                (corner, low, "side"),
                (corner, high, "across"),
                (side, low, "side"),
                (across, high, "across"),
            )
        ):
            state.append(send(source.at[owner, rows], inbox.at[index], sems, index, here[peer]))

    def add(owner, offset, index):
        def run(rows):
            spot = pl.ds(pl.multiple_of(offset + rows.start, 16), 16)
            sums[index, rows] = (
                part[owner, spot].astype(jnp.float32) + inbox[index, rows].astype(jnp.float32)
            ).astype(jnp.bfloat16)

        by_rows(half, 16, run)

    def second_step():
        state[0].wait_recv()
        add(across, 0, 0)
        state.append(send(sums.at[0], inbox.at[4], sems, 4, here["across"]))
        state[1].wait_recv()
        add(side, half, 1)
        state.append(send(sums.at[1], inbox.at[5], sems, 5, here["side"]))
        state[2].wait_recv()
        state[3].wait_recv()

    def finish():
        for offset, one, two in ((0, 2, 4), (half, 3, 5)):
            state[two].wait_recv()

            def close(rows):
                spot = pl.ds(pl.multiple_of(offset + rows.start, 16), 16)
                done(
                    spot,
                    part[row, spot].astype(jnp.float32)
                    + inbox[one, rows].astype(jnp.float32)
                    + inbox[two, rows].astype(jnp.float32),
                )

            by_rows(half, 16, close)
        for copy in state:
            copy.wait_send()

    return [first_step, second_step, finish]


def exchange_seq(here, source, target_of, sems):
    seq, seq_size = here["seq"], lax.axis_size("seq")
    copies = []
    for far in range(1, seq_size):
        dest = (seq + far) % seq_size
        copies.append(
            send(source.at[dest], target_of(seq), sems, far - 1, (here["row"], dest))
        )
    return copies


def seq_peers(here):
    seq_size = lax.axis_size("seq")
    return [(here["row"], (here["seq"] + far) % seq_size) for far in range(1, seq_size)]


def call(kernel, args, out_shape, scratch, collective_id, far_in=(), far_out=(), grant=None):
    near, far = (pl.BlockSpec(memory_space=space) for space in (pltpu.VMEM, pl.ANY))
    return pl.pallas_call(
        kernel,
        out_shape=out_shape,
        in_specs=[far if i in far_in else near for i in range(len(args))],
        out_specs=[far if i in far_out else near for i in range(len(out_shape))],
        scratch_shapes=scratch,
        compiler_params=pltpu.CompilerParams(
            collective_id=collective_id, has_side_effects=True, vmem_limit_bytes=grant or VMEM_LIMIT
        ),
    )(*args)


def low(*shape):
    return jax.ShapeDtypeStruct(shape, jnp.bfloat16)


def full(*shape):
    return jax.ShapeDtypeStruct(shape, jnp.float32)


def shift_route(here):
    row_size, seq_size = lax.axis_size("row"), lax.axis_size("seq")
    index = here["row"] * seq_size + here["seq"]
    origin = here["seq"] * row_size + here["row"]
    target = index % row_size, index // row_size
    return target, (origin // seq_size, origin % seq_size), index != origin


def open_kernel(
    tokens, heads_pack, w_gate, w_up, out_piece,
    all_tokens, heads_all, units_pack, out_all,
    packed, pair_a, pair_b, ring_a, ring_b, heads_a, heads_b, row_a, row_b, out_a, out_b,
    shift_a, shift_b, local_sems,
):
    here = neighbours()
    seq, row = here["seq"], here["row"]
    stretch = tokens.shape[1]
    piece = heads_pack.shape[1]
    target, origin, moves = shift_route(here)
    greet(seq_peers(here) + [here["side"], here["across"]], (moves, target, origin))

    def spot(owner):
        return pl.ds(pl.multiple_of(owner * piece, piece), piece)

    def shift():
        return pltpu.make_async_remote_copy(
            src_ref=out_piece,
            dst_ref=out_all.at[target[0]],
            send_sem=shift_a.at[0],
            recv_sem=shift_b.at[0],
            device_id=target,
            device_id_type=MESH,
        )

    heads = exchange_seq(here, heads_pack, lambda s: heads_all.at[row, spot(s)], (heads_a, heads_b))

    @pl.when(moves)
    def _():
        shift().start()

    for half in range(2):
        own = pl.ds(pl.multiple_of(seq * stretch, stretch), stretch)
        copy_rows(all_tokens.at[half, own], tokens.at[half])
    gather_out = gather_row_steps(here, out_all.at[row], out_all, (out_a, out_b))
    gather_heads = gather_row_steps(here, heads_all.at[row], heads_all, (row_a, row_b))
    _, steps = gather_seq_steps(here, all_tokens, stretch, (pair_a, pair_b), (ring_a, ring_b))
    steps[0]()
    own_heads = pltpu.make_async_copy(
        heads_pack.at[seq], heads_all.at[row, spot(seq)], local_sems.at[0]
    )
    own_heads.start()
    own_out = pltpu.make_async_copy(out_piece, out_all.at[row], local_sems.at[1])

    @pl.when(jnp.logical_not(moves))
    def _():
        own_out.start()

    for copy in heads:
        copy.wait_recv()
    own_heads.wait()
    gather_heads[0]()

    @pl.when(moves)
    def _():
        shift().wait()

    @pl.when(jnp.logical_not(moves))
    def _():
        own_out.wait()

    gather_out[0]()
    seq_size, row_size = lax.axis_size("seq"), lax.axis_size("row")
    block = w_gate.shape[1] // (seq_size * row_size)
    for number, weight in enumerate((w_gate, w_up)):
        for r in range(row_size):
            for s in range(seq_size):
                source = (r * seq_size + s) * block
                place = (number * row_size + r) * block
                packed[s, :, place : place + block] = weight[:, source : source + block]
    units_copy = pltpu.make_async_copy(packed, units_pack, local_sems.at[2])
    units_copy.start()
    steps[1]()
    gather_heads[1]()
    gather_out[1]()
    for step in steps[2:]:
        step()
    gather_heads[2]()
    gather_out[2]()
    for copy in heads:
        copy.wait_send()
    units_copy.wait()


def middle_kernel(
    branch, tokens, gain, units_mine,
    middle, hidden, units_all,
    pair_in, total, ring_in, pair_a, pair_b, ring_a, ring_b,
    gpair_a, gpair_b, gring_a, gring_b, row_a, row_b, own_sem,
):
    here = neighbours()
    seq = here["seq"]
    stretch = tokens.shape[1]
    own_copy = pltpu.make_async_copy(units_mine, units_all.at[here["row"]], own_sem)
    own_copy.start()
    greet([here["up"], here["down"], here["pair"], here["side"], here["across"]])

    def done(half, rows, value):
        value = tokens[half, rows].astype(jnp.float32) + value
        middle[half, rows] = value
        normed = value * norm_scale(value)
        spot = pl.ds(pl.multiple_of(seq * stretch + rows.start, 16), 16)
        hidden[half, spot] = (normed * gain[...]).astype(jnp.bfloat16)

    reduce_steps, finish, drain = reduce_seq_steps(
        here, branch, stretch, pair_in, total, ring_in, (pair_a, pair_b), (ring_a, ring_b), done
    )
    units = gather_row_steps(here, units_mine, units_all, (row_a, row_b))
    units[0]()
    for step in reduce_steps:
        step()
    ring, gather_steps = gather_seq_steps(
        here, hidden, stretch, (gpair_a, gpair_b), (gring_a, gring_b)
    )
    for number in range(PARTS):
        finish(number)
        ring(0, number)
    gather_steps[1]()
    units[1]()
    for step in gather_steps[2:]:
        step()
    units[2]()
    drain()
    own_copy.wait()


def back_kernel(
    grad_part, cotangent, middle, gain, units_part,
    grad_middle, grad_low, gain_grad, units_out,
    pair_in, total, ring_in, inbox, sums, units_near, pair_a, pair_b, ring_a, ring_b,
    gpair_a, gpair_b, gring_a, gring_b, row_a, row_b, near_sem,
):
    here = neighbours()
    seq = here["seq"]
    stretch = cotangent.shape[1]
    near_copy = pltpu.make_async_copy(units_part, units_near, near_sem)
    near_copy.start()
    greet([here["up"], here["down"], here["pair"], here["side"], here["across"]])
    gain_grad[...] = jnp.zeros_like(gain_grad)

    def done(half, rows, grad):
        value = middle[half, rows]
        scale = norm_scale(value)
        normed = value * scale
        gain_grad[...] += jnp.sum(normed * grad, axis=0, keepdims=True)
        back = cotangent[half, rows].astype(jnp.float32) + norm_back(
            grad * gain[...], normed, scale
        )
        grad_middle[half, rows] = back
        spot = pl.ds(pl.multiple_of(seq * stretch + rows.start, 16), 16)
        grad_low[half, spot] = back.astype(jnp.bfloat16)

    def done_units(rows, value):
        units_out[rows] = value.astype(jnp.bfloat16)

    reduce_steps, finish, drain = reduce_seq_steps(
        here, grad_part, stretch, pair_in, total, ring_in, (pair_a, pair_b), (ring_a, ring_b), done
    )
    units = reduce_row_steps(
        here, units_part, units_near, inbox, sums, (row_a, row_b), done_units
    )
    units[0]()
    for step in reduce_steps:
        step()
    ring, gather_steps = gather_seq_steps(
        here, grad_low, stretch, (gpair_a, gpair_b), (gring_a, gring_b)
    )
    for number in range(PARTS):
        finish(number)
        ring(0, number)
    near_copy.wait()
    units[1]()
    for step in gather_steps[1:]:
        step()
    units[2]()
    drain()


def sum_small(here, mine, inbox, sems):
    slot = 0
    stages = [seq_peers(here), [here["side"], here["across"], here["corner"]]]
    copies = []
    for number, stage in enumerate(stages):
        sent = [
            send(mine.at[number], inbox.at[slot + i], sems, slot + i, peer)
            for i, peer in enumerate(stage)
        ]
        value = mine[number]
        for i, copy in enumerate(sent):
            copy.wait_recv()
            value = value + inbox[slot + i]
        mine[number + 1] = value
        slot += len(stage)
        copies += sent
    for copy in copies:
        copy.wait_send()
    return slot


def close_kernel(
    grad_part, tokens, grad_middle, gain, gain_two, heads_part, out_part,
    grad_tokens, gain_sums, heads_out, out_out,
    heads_mine, pair_in, total, ring_in, inbox, sums, out_inbox, out_sums, out_mine, small, small_in,
    pair_a, pair_b, ring_a, ring_b, row_a, row_b, heads_a, heads_b, out_a, out_b,
    shift_a, shift_b, small_a, small_b,
):
    here = neighbours()
    seq, chips = here["seq"], lax.axis_size("seq") // 2
    stretch = tokens.shape[1]
    target, origin, moves = shift_route(here)
    greet(
        seq_peers(here) + [here["side"], here["across"], here["corner"]], (moves, target, origin)
    )
    small[0, 0:1] = jnp.zeros_like(small[0, 0:1])
    small[0, 1:2] = gain_two[...]

    def done(half, rows, grad):
        value = tokens[half, rows].astype(jnp.float32)
        scale = norm_scale(value)
        normed = value * scale
        small[0, 0:1] += jnp.sum(normed * grad, axis=0, keepdims=True)
        grad_tokens[half, rows] = grad_middle[half, rows] + norm_back(
            grad * gain[...], normed, scale
        )

    piece = heads_out.shape[1]

    def done_heads(rows, value):
        heads_mine[rows] = value.astype(jnp.bfloat16)

    reduce_steps, finish, drain = reduce_seq_steps(
        here, grad_part, stretch, pair_in, total, ring_in, (pair_a, pair_b), (ring_a, ring_b), done
    )
    def done_out(rows, value):
        out_mine[rows] = value.astype(jnp.bfloat16)

    def shift():
        return pltpu.make_async_remote_copy(
            src_ref=out_mine,
            dst_ref=out_out,
            send_sem=shift_a.at[0],
            recv_sem=shift_b.at[0],
            device_id=origin,
            device_id_type=MESH,
        )

    outs = reduce_row_steps(here, out_part, out_part, out_inbox, out_sums, (out_a, out_b), done_out)
    heads = reduce_row_steps(here, heads_part, heads_part, inbox, sums, (row_a, row_b), done_heads)
    heads[0]()
    outs[0]()
    reduce_steps[0]()
    heads[1]()
    outs[1]()
    for step in reduce_steps[1:]:
        step()
    heads[2]()
    copies = []
    for far in range(1, 2 * chips):
        dest = (seq + far) % (2 * chips)
        rows = pl.ds(pl.multiple_of(dest * piece, piece), piece)
        copies.append(
            send(
                heads_mine.at[rows], heads_out.at[seq], (heads_a, heads_b), far - 1,
                (here["row"], dest),
            )
        )
    outs[2]()

    @pl.when(moves)
    def _():
        shift().start()

    @pl.when(jnp.logical_not(moves))
    def _():
        copy_rows(out_out, out_mine)

    for number in range(PARTS):
        finish(number)
    copy_rows(heads_out.at[seq], heads_mine.at[pl.ds(pl.multiple_of(seq * piece, piece), piece)])
    sum_small(here, small, small_in, (small_a, small_b))
    gain_sums[...] = small[2]
    for copy in copies:
        copy.wait()

    @pl.when(moves)
    def _():
        shift().wait()

    drain()


def seq_scratch(chips, stretch, width):
    return [
        pltpu.VMEM((chips, 2, stretch, width), jnp.bfloat16),
        pltpu.VMEM((chips, 2, stretch, width), jnp.bfloat16),
        pltpu.VMEM((chips - 1, 2, stretch, width), jnp.bfloat16),
    ]


def row_scratch(pieces, columns):
    return [
        pltpu.VMEM((6, pieces // 2, columns), jnp.bfloat16),
        pltpu.VMEM((2, pieces // 2, columns), jnp.bfloat16),
    ]


def unpack(units, heads, down, out, row_size, query_width, key_width):
    seq_size, rows, columns = units.shape
    block = columns // 2 // row_size
    down_rows, width = down.shape

    def kernel(
        gate, up, heads_ref, down_ref, out_ref, gate_out, up_out, query, key, value, down_out, out_out
    ):
        for source, target in ((gate, gate_out), (up, up_out)):
            for s in range(seq_size):
                target[:, s * block : (s + 1) * block] = source[s].astype(jnp.float32)
        down_out[...] = down_ref[...].astype(jnp.float32)

        @pl.when(pl.program_id(0) == 0)
        def _():
            out_out[...] = out_ref[...].astype(jnp.float32)
            start = 0
            for target, size in ((query, query_width), (key, key_width), (value, key_width)):
                target[...] = jnp.concatenate(
                    [
                        heads_ref[s, :, start : start + size].astype(jnp.float32)
                        for s in range(seq_size)
                    ],
                    axis=1,
                )
                start += size

    whole = full(rows, seq_size * columns // 2)
    head_shapes = [full(rows, seq_size * w) for w in (query_width, key_width, key_width)]
    down_block = pl.BlockSpec((down_rows // row_size, width), lambda r: (r, 0))
    return pl.pallas_call(
        kernel,
        grid=(row_size,),
        out_shape=[whole, whole] + head_shapes + [full(down_rows, width), full(*out.shape)],
        in_specs=[
            pl.BlockSpec((seq_size, rows, block), lambda r: (0, 0, r)),
            pl.BlockSpec((seq_size, rows, block), lambda r: (0, 0, row_size + r)),
            pl.BlockSpec(heads.shape, lambda r: (0, 0, 0)),
            down_block,
            pl.BlockSpec(out.shape, lambda r: (0, 0)),
        ],
        out_specs=[pl.BlockSpec((rows, seq_size * block), lambda r: (0, r))] * 2
        + [pl.BlockSpec(x.shape, lambda r: (0, 0)) for x in head_shapes]
        + [down_block, pl.BlockSpec(out.shape, lambda r: (0, 0))],
    )(units, units, heads, down, out)


BOTH = ("row", "seq")


def gather(piece, axis_name, axis):
    return lax.all_gather(piece, axis_name, axis=axis, tiled=True)


def scatter(whole, axis_name, axis):
    return lax.psum_scatter(whole, axis_name, scatter_dimension=axis, tiled=True)


def sharded_layer(
    tokens,
    cotangent,
    doc_lengths,
    attn_gain,
    w_query,
    w_key,
    w_value,
    w_out,
    mlp_gain,
    w_gate,
    w_up,
    w_down,
):
    row_size, seq_size = lax.axis_size("row"), lax.axis_size("seq")
    rows, stretch, width = tokens.shape
    length = stretch * seq_size
    count = rows * length
    piece_rows = w_query.shape[0]
    key_heads = w_key.shape[1] // HEAD_DIM // seq_size
    heads = w_query.shape[1] // HEAD_DIM // seq_size
    groups = heads // key_heads
    query_width, key_width = heads * HEAD_DIM, key_heads * HEAD_DIM
    unit_block = w_down.shape[0]
    units = unit_block * row_size
    scale = HEAD_DIM ** (-0.5)

    place = jnp.arange(length, dtype=jnp.int32)
    ends = jnp.cumsum(doc_lengths, axis=1)
    first = jnp.max(
        jnp.where(ends[:, None, :] <= place[None, :, None], ends[:, None, :], 0), axis=2
    )
    table = jnp.asarray(rope_table(HEAD_DIM), jnp.float32)
    angle = (place[None, :] - first).astype(jnp.float32)[..., None] * table
    cosine = jnp.concatenate([jnp.cos(angle), jnp.cos(angle)], axis=-1)[:, :, None, :]
    sine = jnp.concatenate([jnp.sin(angle), jnp.sin(angle)], axis=-1)[:, :, None, :]

    def head_columns(weight, columns):
        return weight.reshape(piece_rows, seq_size, columns).transpose(1, 0, 2)

    head_width = query_width + 2 * key_width
    spare = -(head_width + 2) % 128
    gain_columns = jnp.stack([attn_gain, mlp_gain], axis=1)
    gain_columns = jnp.pad(gain_columns, ((0, 0), (0, spare)))
    heads_pack = jnp.concatenate(
        [
            head_columns(w_query, query_width),
            head_columns(w_key, key_width),
            head_columns(w_value, key_width),
            jnp.broadcast_to(gain_columns, (seq_size, piece_rows, spare + 2)),
        ],
        axis=2,
    )
    pack_width = head_width + 2 + spare
    chips = seq_size // 2
    pieces = piece_rows * seq_size
    early_cotangent = gather(cotangent[:1], "seq", 1)
    all_tokens, heads_all, units_pack, out_part = call(
        open_kernel,
        (tokens, heads_pack, w_gate, w_up, w_out),
        [
            low(rows, length, width),
            low(row_size, pieces, pack_width),
            low(seq_size, piece_rows, 2 * units),
            low(row_size, piece_rows, width),
        ],
        [pltpu.VMEM((seq_size, piece_rows, 2 * units), jnp.bfloat16)]
        + sem_pairs(2 * chips * PARTS) * 2
        + sem_pairs(seq_size - 1)
        + sem_pairs(4) * 2
        + sem_pairs(1)
        + [pltpu.SemaphoreType.DMA((3,))],
        0,
        far_out=(1, 2, 3),
    )
    units_mine = lax.all_to_all(units_pack, "seq", 0, 0, tiled=True).reshape(pieces, 2 * units)
    late_down, all_tokens = lax.optimization_barrier((w_down, all_tokens))
    down_part = gather(late_down, "row", 0)
    all_tokens = all_tokens.reshape(count, width)
    heads_all = heads_all.reshape(width, pack_width)
    w_qkv = heads_all[:, :head_width]
    gains = heads_all[:, head_width : head_width + 2].astype(jnp.float32).T
    out_part = out_part.reshape(query_width, width)

    inputs = all_tokens.astype(jnp.float32)
    hidden_one = (inputs * norm_scale(inputs) * gains[0]).astype(jnp.bfloat16)
    qkv = jnp.dot(hidden_one, w_qkv, preferred_element_type=jnp.float32)
    queries = rotate(
        qkv[:, :query_width].reshape(rows, length, heads, HEAD_DIM), cosine, sine
    ).astype(jnp.bfloat16).reshape(rows, length, key_heads, groups, HEAD_DIM)
    keys = rotate(
        qkv[:, query_width : query_width + key_width].reshape(rows, length, key_heads, HEAD_DIM),
        cosine,
        sine,
    ).astype(jnp.bfloat16)
    values = (
        qkv[:, query_width + key_width :]
        .astype(jnp.bfloat16)
        .reshape(rows, length, key_heads, HEAD_DIM)
    )
    raw = jnp.einsum("rqhgd,rkhd->rhgqk", queries, keys, preferred_element_type=jnp.float32)
    allowed = (place[None, None, :] <= place[None, :, None]) & (
        place[None, None, :] >= first[:, :, None]
    )
    probs = jax.nn.softmax(jnp.where(allowed[:, None, None], raw * scale, -1e30), axis=-1)
    probs_low = probs.astype(jnp.bfloat16)
    mixed = (
        jnp.einsum("rhgqk,rkhd->rqhgd", probs_low, values, preferred_element_type=jnp.float32)
        .astype(jnp.bfloat16)
        .reshape(count, query_width)
    )
    branch = jnp.dot(mixed, out_part, preferred_element_type=jnp.float32).astype(jnp.bfloat16)
    middle, hidden_two, w_units = call(
        middle_kernel,
        (branch.reshape(rows, length, width), tokens, gains[1:2], units_mine),
        [full(rows, stretch, width), low(rows, length, width), low(row_size, pieces, 2 * units)],
        seq_scratch(chips, stretch, width)
        + sem_pairs(2 * chips)
        + sem_pairs(2 * PARTS * (chips - 1))
        + sem_pairs(2 * chips * PARTS) * 2
        + sem_pairs(4)
        + [pltpu.SemaphoreType.DMA],
        1,
        far_out=(2,),
    )
    late_cotangent, hidden_two = lax.optimization_barrier((cotangent[1:], hidden_two))
    late_cotangent = gather(late_cotangent, "seq", 1)
    all_cotangent = jnp.concatenate([early_cotangent, late_cotangent]).reshape(count, width)
    hidden_two = hidden_two.reshape(count, width)
    w_units = w_units.reshape(width, 2 * units)
    both = jnp.dot(hidden_two, w_units, preferred_element_type=jnp.float32)
    gate_sum, up_sum = both[:, :units], both[:, units:]
    sigma = jax.nn.sigmoid(gate_sum)
    silu_value = gate_sum * sigma
    active = (silu_value * up_sum).astype(jnp.bfloat16)
    mlp_branch = jnp.dot(active, down_part, preferred_element_type=jnp.float32)
    mlp_branch, down_part = lax.optimization_barrier((mlp_branch.astype(jnp.bfloat16), down_part))
    mlp_branch = scatter(mlp_branch.reshape(rows, length, width), "seq", 1)
    output = (middle + mlp_branch.astype(jnp.float32)).astype(jnp.bfloat16)

    grad_active = contract_last(all_cotangent, down_part)
    grad_down = (
        contract_first(active[:length], early_cotangent[0])
        + contract_first(active[length:], late_cotangent.reshape(-1, width))
    ).astype(jnp.bfloat16)
    grad_up_low = (grad_active * silu_value).astype(jnp.bfloat16)
    grad_gate_low = (grad_active * up_sum * sigma * (1.0 + gate_sum * (1.0 - sigma))).astype(
        jnp.bfloat16
    )
    both_grads = jnp.concatenate([grad_gate_low, grad_up_low], axis=1)
    grad_hidden = contract_last(both_grads, w_units).astype(jnp.bfloat16)
    grad_units = contract_first(hidden_two, both_grads).astype(jnp.bfloat16)
    grad_hidden, mlp_branch, grad_down = lax.optimization_barrier(
        (grad_hidden, mlp_branch, grad_down)
    )
    grad_middle, grad_branch, grad_gain_two, units_mine = call(
        back_kernel,
        (
            grad_hidden.reshape(rows, length, width),
            cotangent,
            middle,
            gains[1:2],
            grad_units.reshape(row_size, pieces, 2 * units),
        ),
        [
            full(rows, stretch, width),
            low(rows, length, width),
            full(1, width),
            low(pieces, 2 * units),
        ],
        seq_scratch(chips, stretch, width)
        + row_scratch(pieces, 2 * units)
        + [pltpu.VMEM((row_size, pieces, 2 * units), jnp.bfloat16)]
        + sem_pairs(2 * chips)
        + sem_pairs(2 * PARTS * (chips - 1))
        + sem_pairs(2 * chips * PARTS) * 2
        + sem_pairs(6)
        + [pltpu.SemaphoreType.DMA],
        2,
        far_in=(4,),
    )
    grad_branch, grad_down = lax.optimization_barrier((grad_branch, grad_down))
    grad_down = scatter(grad_down, "row", 0)
    grad_units = lax.all_to_all(
        units_mine.reshape(seq_size, piece_rows, 2 * units), "seq", 0, 0, tiled=True
    )
    grad_branch = grad_branch.reshape(count, width)
    grad_mixed = contract_last(grad_branch, out_part).astype(jnp.bfloat16)
    grad_out = contract_first(mixed, grad_branch).astype(jnp.bfloat16)
    grad_grouped = grad_mixed.reshape(rows, length, key_heads, groups, HEAD_DIM)
    grad_probs = jnp.einsum(
        "rqhgd,rkhd->rhgqk", grad_grouped, values, preferred_element_type=jnp.float32
    )
    delta = jnp.sum(probs * grad_probs, axis=-1, keepdims=True)
    grad_raw = (scale * probs * (grad_probs - delta)).astype(jnp.bfloat16)
    grad_queries = jnp.einsum(
        "rhgqk,rkhd->rqhgd", grad_raw, keys, preferred_element_type=jnp.float32
    )
    grad_keys = jnp.einsum(
        "rhgqk,rqhgd->rkhd", grad_raw, queries, preferred_element_type=jnp.float32
    )
    grad_values = jnp.einsum(
        "rhgqk,rqhgd->rkhd", probs_low, grad_grouped, preferred_element_type=jnp.float32
    )
    grad_qkv_low = jnp.concatenate(
        [
            rotate_back(grad_queries.reshape(rows, length, heads, HEAD_DIM), cosine, sine).reshape(
                count, query_width
            ),
            rotate_back(grad_keys, cosine, sine).reshape(count, key_width),
            grad_values.reshape(count, key_width),
        ],
        axis=1,
    ).astype(jnp.bfloat16)
    grad_qkv = contract_first(hidden_one, grad_qkv_low).astype(jnp.bfloat16)
    grad_hidden = contract_last(grad_qkv_low, w_qkv).astype(jnp.bfloat16)
    grad_tokens, gain_sums, grad_qkv, grad_out = call(
        close_kernel,
        (
            grad_hidden.reshape(rows, length, width),
            tokens,
            grad_middle,
            gains[0:1],
            grad_gain_two,
            grad_qkv.reshape(row_size, pieces, head_width),
            grad_out.reshape(row_size, piece_rows, width),
        ),
        [
            full(rows, stretch, width),
            full(2, width),
            low(seq_size, piece_rows, head_width),
            low(piece_rows, width),
        ],
        [pltpu.VMEM((pieces, head_width), jnp.bfloat16)]
        + seq_scratch(chips, stretch, width)
        + row_scratch(pieces, head_width)
        + row_scratch(piece_rows, width)
        + [pltpu.VMEM((piece_rows, width), jnp.bfloat16)]
        + [pltpu.VMEM((3, 2, width), jnp.float32)]
        + [pltpu.VMEM((seq_size + row_size - 2, 2, width), jnp.float32)]
        + sem_pairs(2 * chips)
        + sem_pairs(2 * PARTS * (chips - 1))
        + sem_pairs(6)
        + sem_pairs(seq_size - 1)
        + sem_pairs(6)
        + sem_pairs(1)
        + sem_pairs(seq_size + row_size - 2),
        3,
        grant=VMEM_LIMIT // 2,
    )

    grad_gate, grad_up, grad_query, grad_key, grad_value, grad_down, grad_out = unpack(
        grad_units, grad_qkv, grad_down, grad_out, row_size, query_width, key_width
    )
    own = (lax.axis_index("row") * seq_size + lax.axis_index("seq")) * piece_rows
    grad_gains = lax.dynamic_slice_in_dim(gain_sums, own, piece_rows, 1)
    return (
        output,
        grad_tokens,
        grad_gains[0],
        grad_query,
        grad_key,
        grad_value,
        grad_out,
        grad_gains[1],
        grad_gate,
        grad_up,
        grad_down,
    )


def local(tokens, cotangent, doc_lengths, attn_gain, w_query, w_key, w_value, *rest):
    whole_heads = w_key.shape[1] % (HEAD_DIM * lax.axis_size("seq")) == 0
    layer = sharded_layer if whole_heads else gathered_layer
    return layer(tokens, cotangent, doc_lengths, attn_gain, w_query, w_key, w_value, *rest)


def solution(mesh):
    return jax.shard_map(
        local,
        mesh=mesh,
        in_specs=(
            P("row", "seq", None),
            P("row", "seq", None),
            P("row", None),
            P(("row", "seq")),
            P(("row", "seq"), None),
            P(("row", "seq"), None),
            P(("row", "seq"), None),
            P(("row", "seq"), None),
            P(("row", "seq")),
            P(("row", "seq"), None),
            P(("row", "seq"), None),
            P(("row", "seq"), None),
        ),
        out_specs=(
            P("row", "seq", None),
            P("row", "seq", None),
            P(("row", "seq")),
            P(("row", "seq"), None),
            P(("row", "seq"), None),
            P(("row", "seq"), None),
            P(("row", "seq"), None),
            P(("row", "seq")),
            P(("row", "seq"), None),
            P(("row", "seq"), None),
            P(("row", "seq"), None),
        ),
        check_vma=False,
    )
```
